32 devices in a mesh: dp: 2 (over y), fsdp: 16 (over z, x, core).
Axes of the slice: x: 2, y: 2, z: 4, core: 2. Of those that a mesh axis runs over, the one named last changes fastest.
Arguments:
- tile_embeddings: bfloat16 [32, 256, 768], P(('dp', 'fsdp')), may hold values from -6 to 6
- horizon_indices: int32 [32], P(('dp', 'fsdp')), may hold values from 0 to 39
- horizon_tallies: int32 [40], replicated, may hold values from 1 to 8
- member_guesses: bfloat16 [32, 256, 3, 4416], P(('dp', 'fsdp')), may hold values from -6 to 6
- adjoint_of_mixture: bfloat16 [32, 256, 4416], P(('dp', 'fsdp')), may hold values from -6 to 6
- triple_projection_matrix: bfloat16 [768, 2304], P(('dp', 'fsdp')), may hold values from -0.21875 to 0.21875
- attention_outward_matrix: bfloat16 [768, 768], P(('dp', 'fsdp')), may hold values from -0.875 to 0.875
- widening_matrix: bfloat16 [768, 3072], P(('dp', 'fsdp')), may hold values from -0.21875 to 0.21875
- narrowing_matrix: bfloat16 [3072, 768], P(('dp', 'fsdp')), may hold values from -0.109375 to 0.109375
- gating_matrix: bfloat16 [768, 13248], P(('dp', 'fsdp')), may hold values from -0.109375 to 0.109375
- horizon_embedding_matrix: bfloat16 [768, 40], P(('dp', 'fsdp')), may hold values from -3 to 3
- normalization_scales: bfloat16 [768, 2], P(('dp', 'fsdp')), may hold values from 0.5 to 1.5
- channel_offsets: bfloat16 [768, 4], P(('dp', 'fsdp')), may hold values from -0.59765625 to 0.59765625
- triple_projection_offset: bfloat16 [768, 2], P(('dp', 'fsdp')), may hold values from -0.59765625 to 0.59765625
- hidden_offset: bfloat16 [3072], P(('dp', 'fsdp')), may hold values from -0.59765625 to 0.59765625
Outputs:
- combined_result: bfloat16 [32, 256, 4416], P(('dp', 'fsdp'))
- regularizer_cost: float32 [], replicated
- grad_tokens: bfloat16 [32, 256, 768], P(('dp', 'fsdp'))
- grad_qkv_weight: float32 [768, 2304], P(('dp', 'fsdp'))
- grad_proj_weight: float32 [768, 768], P(('dp', 'fsdp'))
- grad_fc1_weight: float32 [768, 3072], P(('dp', 'fsdp'))
- grad_fc2_weight: float32 [3072, 768], P(('dp', 'fsdp'))
- grad_head_weight: float32 [768, 13248], P(('dp', 'fsdp'))
- grad_lead_table: float32 [768, 40], P(('dp', 'fsdp'))
- grad_norm_gains: float32 [768, 2], P(('dp', 'fsdp'))
- grad_width_biases: float32 [768, 4], P(('dp', 'fsdp'))
- grad_qkv_bias: float32 [768, 2], P(('dp', 'fsdp'))
- grad_fc1_bias: float32 [3072], P(('dp', 'fsdp'))
The draws below stay inside these ranges and needn't reach their ends.
All inputs are finite; a program needn't handle non-finite values.
Results may differ from the reference program's by a relative error of at most 0.022.
Values may be sent and summed in bfloat16 or wider, within the bound.
No kernel may reach another device: no remote copies, remote signals or barrier semaphores. Data moves between devices by JAX's collectives and lax.ppermute only.
A program may use at most 256 MiB of HBM per device.

```python
import jax
import jax.numpy as jnp
from jax import lax

D = 768
HEADS = 12
HD = 64
FF = 3072
MODEL_COUNT = 3
TILE_SAMPLES = 4416
LEADS = 40
TILE_COUNT = 256
SNAPSHOT_TOTAL = 32


def plant(result, own_key, low, largest):
    longest = result.shape.index(max(result.shape))
    spots = []
    for shift in (0, 1):
        where = [jax.random.randint(jax.random.fold_in(own_key, axis), (), 0, length) for axis, length in enumerate(result.shape)]
        where[longest] = (where[longest] + shift) % result.shape[longest]
        spots.append(tuple(where))
    return result.at[spots[0]].set(low).at[spots[1]].set(largest)


def level_of(own_key, extent, shards, smallest, high):
    level = 1.0
    for axis_at, parts in shards:
        draws = jax.random.uniform(jax.random.fold_in(jax.random.fold_in(own_key, 6), axis_at), (parts,), jnp.float32, smallest / len(shards), high / len(shards))
        level = level * jnp.repeat(jnp.exp(draws), extent[axis_at] // parts).reshape((-1,) + (1,) * (len(extent) - 1 - axis_at))
    return level


def gaussian(own_key, shape, spread, reach, cuts=(), kind=jnp.bfloat16):
    level = level_of(own_key, shape, cuts, -0.22, 0.18) if cuts else 1.0
    result = jax.random.normal(own_key, shape, jnp.float32) * spread * level
    return jnp.minimum(jnp.maximum(result, -reach), reach).astype(kind)


def setup_inputs(seed: int = 0) -> dict:
    streams_of = jax.random.split(jax.random.key(seed), 16)
    tile_embeddings = gaussian(streams_of[0], (SNAPSHOT_TOTAL, TILE_COUNT, D), 1.0, 6.0, ((0, 32),))
    horizon_indices = plant(jax.random.randint(streams_of[1], (SNAPSHOT_TOTAL,), 0, LEADS), jax.random.fold_in(streams_of[1], 1), 0, LEADS - 1).astype(jnp.int32)
    horizon_tallies = plant(jax.random.randint(streams_of[2], (LEADS,), 1, 9), jax.random.fold_in(streams_of[2], 1), 1, 8).astype(jnp.int32)
    member_guesses = gaussian(streams_of[3], (SNAPSHOT_TOTAL, TILE_COUNT, MODEL_COUNT, TILE_SAMPLES), 1.0, 6.0, ((0, 32),))
    adjoint_of_mixture = gaussian(streams_of[4], (SNAPSHOT_TOTAL, TILE_COUNT, TILE_SAMPLES), 1.0, 6.0, ((0, 32),))
    triple_projection_matrix = gaussian(streams_of[5], (D, 3 * D), D ** -0.5, 0.21875, ((0, 32),))
    attention_outward_matrix = gaussian(streams_of[6], (D, D), (D // 16) ** -0.5, 0.875, ((0, 32),))
    widening_matrix = gaussian(streams_of[7], (D, FF), D ** -0.5, 0.21875, ((0, 32),))
    narrowing_matrix = gaussian(streams_of[8], (FF, D), FF ** -0.5, 0.109375, ((0, 32),))
    gating_matrix = gaussian(streams_of[9], (D, MODEL_COUNT * TILE_SAMPLES), (4 * D) ** -0.5, 0.109375, ((0, 32),))
    horizon_embedding_matrix = gaussian(streams_of[10], (D, LEADS), 0.5, 3.0, ((0, 32),))
    normalization_scales = jnp.clip(1.0 + 0.1 * jax.random.normal(streams_of[11], (D, 2), jnp.float32), 0.5, 1.5).astype(jnp.bfloat16)
    channel_offsets = gaussian(streams_of[12], (D, 4), 0.1, 0.59765625, ((0, 32),))
    triple_projection_offset = gaussian(streams_of[13], (D, 2), 0.1, 0.59765625, ((0, 32),))
    hidden_offset = gaussian(streams_of[14], (FF,), 0.1, 0.59765625, ((0, 32),))
    return dict(tile_embeddings=tile_embeddings, horizon_indices=horizon_indices, horizon_tallies=horizon_tallies, member_guesses=member_guesses, adjoint_of_mixture=adjoint_of_mixture, triple_projection_matrix=triple_projection_matrix, attention_outward_matrix=attention_outward_matrix, widening_matrix=widening_matrix, narrowing_matrix=narrowing_matrix, gating_matrix=gating_matrix, horizon_embedding_matrix=horizon_embedding_matrix, normalization_scales=normalization_scales, channel_offsets=channel_offsets, triple_projection_offset=triple_projection_offset, hidden_offset=hidden_offset)


EPS = 1e-06
HIGHEST = lax.Precision.HIGHEST

@jax.custom_vjp
def low(v):
    return lax.optimization_barrier(v.astype(jnp.bfloat16)).astype(jnp.float32)

@jax.custom_vjp
def low_back(v):
    return v

def low_keep(v):
    return (low(v), None)

def low_pass(kept, grad):
    return (grad,)

def back_keep(v):
    return (v, None)

def back_low(kept, grad):
    return (low(grad),)
low.defvjp(low_keep, low_pass)
low_back.defvjp(back_keep, back_low)

def layer_norm(values, norm_gain, norm_shift):
    row_mean = lax.optimization_barrier(jnp.mean(values, axis=-1, keepdims=True))
    centred = values - row_mean
    row_var = lax.optimization_barrier(jnp.mean(centred * centred, axis=-1, keepdims=True))
    return centred * lax.rsqrt(row_var + EPS) * norm_gain + norm_shift

def exact_gelu(values):
    return jax.nn.gelu(values, approximate=False)

def blend_head(unnormalized_scores, member_outlook, regularizer_strength):
    log_weight = jax.nn.log_softmax(unnormalized_scores, axis=1)
    mixing_share = jnp.exp(log_weight)
    combined_outlook = lax.optimization_barrier(jnp.sum(mixing_share * member_outlook, axis=1))
    shannon_measure = -lax.optimization_barrier(jnp.sum(mixing_share * log_weight, axis=1))
    return (combined_outlook, jnp.sum(shannon_measure) * regularizer_strength)

def matmul(left, right):
    return jnp.dot(left, right, precision=HIGHEST)

def frame_forward(parameter_tuple, frame, horizon_indicator, member_outlook, regularizer_strength):
    qkv_w, proj_w, fc1_w, fc2_w, head_w, lead_w, norm_gain, width_bias, qkv_b, fc1_b = parameter_tuple
    started = frame + matmul(lead_w, horizon_indicator)[None, :]
    normed = low(layer_norm(started, norm_gain[:, 0], width_bias[:, 0]))
    full_offset = jnp.concatenate([qkv_b[:, 0], jnp.zeros_like(qkv_b[:, 0]), qkv_b[:, 1]])
    joined = low(low_back(matmul(normed, qkv_w) + full_offset))
    queries = joined[:, :D].reshape(TILE_COUNT, HEADS, HD)
    keys_all = joined[:, D:2 * D].reshape(TILE_COUNT, HEADS, HD)
    values_all = joined[:, 2 * D:].reshape(TILE_COUNT, HEADS, HD)
    scores = low_back(jnp.einsum('qhd,khd->hqk', queries, keys_all, precision=HIGHEST) * HD ** (-0.5))
    probs = low(jax.nn.softmax(scores, axis=-1))
    attended = low(low_back(jnp.einsum('hqk,khd->qhd', probs, values_all, precision=HIGHEST))).reshape(TILE_COUNT, D)
    attn_out = low_back(matmul(attended, proj_w) + width_bias[:, 1])
    middle = started + attn_out
    normed_two = low(layer_norm(middle, norm_gain[:, 1], width_bias[:, 2]))
    pre_act = low_back(matmul(normed_two, fc1_w) + fc1_b)
    hidden = low(exact_gelu(pre_act))
    branch = low_back(matmul(hidden, fc2_w) + width_bias[:, 3])
    final_sum = middle + branch
    unnormalized_scores = low_back(matmul(low(final_sum), head_w)).reshape(TILE_COUNT, MODEL_COUNT, TILE_SAMPLES)
    return blend_head(unnormalized_scores, member_outlook.astype(jnp.float32), regularizer_strength)

def reference(tile_embeddings, horizon_indices, horizon_tallies, member_guesses, adjoint_of_mixture, triple_projection_matrix, attention_outward_matrix, widening_matrix, narrowing_matrix, gating_matrix, horizon_embedding_matrix, normalization_scales, channel_offsets, triple_projection_offset, hidden_offset):
    parameter_tuple = tuple((weight_arg.astype(jnp.float32) for weight_arg in (triple_projection_matrix, attention_outward_matrix, widening_matrix, narrowing_matrix, gating_matrix, horizon_embedding_matrix, normalization_scales, channel_offsets, triple_projection_offset, hidden_offset)))
    snapshots_float = tile_embeddings.astype(jnp.float32)
    horizon_indicator = (horizon_indices[:, None] == jnp.arange(LEADS, dtype=jnp.int32)[None, :]).astype(jnp.float32)
    frame_count = lax.optimization_barrier(jnp.sum(horizon_indicator * horizon_tallies.astype(jnp.float32)[None, :], axis=1))
    regularizer_strength = 1.0 / (frame_count * (LEADS * TILE_COUNT * TILE_SAMPLES))

    def complete_batch(params_in, given_snapshots):

        def solitary_snapshot(frame_item):
            return frame_forward(params_in, *frame_item)
        combined_outlook, regularizer_amounts = lax.map(jax.checkpoint(solitary_snapshot), (given_snapshots, horizon_indicator, member_guesses, regularizer_strength))
        return (combined_outlook, jnp.sum(regularizer_amounts))
    (combined_outlook, regularizer_cost), adjoint_function = jax.vjp(complete_batch, parameter_tuple, snapshots_float)
    parameter_derivatives, snapshot_derivative = adjoint_function((adjoint_of_mixture.astype(combined_outlook.dtype), jnp.ones((), regularizer_cost.dtype)))
    return (combined_outlook.astype(jnp.bfloat16), regularizer_cost, snapshot_derivative.astype(jnp.bfloat16), parameter_derivatives[0], parameter_derivatives[1], parameter_derivatives[2], parameter_derivatives[3], parameter_derivatives[4], parameter_derivatives[5], parameter_derivatives[6], parameter_derivatives[7], parameter_derivatives[8], parameter_derivatives[9])
```

```python
import functools

import jax
import jax.numpy as jnp
from jax import lax
from jax.experimental import pallas as pl
from jax.experimental.pallas import tpu as pltpu
from jax.sharding import PartitionSpec as P

D = 768
HEADS = 12
HD = 64
FF = 3072
MODEL_COUNT = 3
TILE_SAMPLES = 4416
LEADS = 40
TILE_COUNT = 256
EPS = 1e-06
LANES = 128
HALF = 2304
PADDED = 2 * HALF
VMEM = 56 * 1024 * 1024

AXES = ("dp", "fsdp")
RING = [(z, 0) for z in range(4)] + [(z, 1) for z in (3, 2, 1, 0)]


def ring_pairs(step):
    pairs = []
    for spot, (z, x) in enumerate(RING):
        to_z, to_x = RING[(spot + step) % 8]
        for core in range(2):
            pairs.append((z * 4 + x * 2 + core, to_z * 4 + to_x * 2 + core))
    return pairs


def forth(value):
    return lax.ppermute(value, "fsdp", ring_pairs(1))


def back(value):
    return lax.ppermute(value, "fsdp", ring_pairs(-1))


def across(value):
    return lax.ppermute(value, "dp", [(0, 1), (1, 0)])


def sibling(value):
    return lax.ppermute(value, "fsdp", [(i, i ^ 1) for i in range(16)])


def places():
    y = lax.axis_index("dp")
    f = lax.axis_index("fsdp")
    z, x, core = f // 4, (f // 2) % 2, f % 2
    spot = jnp.where(x == 0, z, 7 - z)
    i = lax.iota(jnp.int32, 32)
    seat = (spot + (i // 2) % 8) % 8
    pair = jnp.where(seat < 4, seat * 2, (7 - seat) * 2 + 1)
    return ((y + i // 16) % 2) * 16 + pair * 2 + (core + i) % 2


def slot(other_row, distance, other_core):
    return other_row * 16 + (distance % 8) * 2 + other_core


def gather_pieces(own, share, half):
    r, n = own.shape
    rest = n - share
    found = []
    over = across(own)
    first = own
    if rest:
        first = jnp.concatenate([own, over[:, share:]], axis=1)
    wide = n + rest
    rights, lefts = [first], [first]
    for _ in range(3):
        rights.append(forth(rights[-1]))
        lefts.append(back(lefts[-1]))
    rows_half, cols_half = half
    if cols_half:
        far = [
            (forth(rights[3][:, :cols_half]), 0, 0),
            (back(lefts[3][:, cols_half:]), 0, cols_half),
        ]
    else:
        far = [
            (forth(rights[3][:rows_half]), 0, 0),
            (back(lefts[3][rows_half:]), rows_half, 0),
        ]
    held = []
    held.append((own, 0, 0, 0, False))
    held.append((over, 0, 0, 0, True))
    for k in range(1, 4):
        held.append((rights[k], -k, 0, 0, False))
        held.append((lefts[k], k, 0, 0, False))
        pair = jnp.concatenate([rights[k][:, :share], lefts[k][:, :share]], axis=0)
        held.append((across(pair), k, 0, 0, True))
    for array, row, col in far:
        held.append((array, 4, row, col, False))
        stop = min(share, col + array.shape[1])
        if stop > col:
            held.append((across(array[:, : stop - col]), 4, row, col, True))
    for array, distance, row, col, swapped in held:
        for other_core in (0, 1):
            source = sibling(array) if other_core else array
            if swapped and array.shape[0] == 2 * r:
                found.append((source, (0, r), (0, share), slot(1, -distance, other_core), 0, 0))
                found.append((source, (r, 2 * r), (0, share), slot(1, distance, other_core), 0, 0))
                continue
            rows = (0, array.shape[0])
            if swapped:
                found.append((source, rows, (0, array.shape[1]), slot(1, distance, other_core), row, col))
                continue
            stop = col + array.shape[1]
            if col < n:
                found.append((source, rows, (0, min(stop, n) - col), slot(0, distance, other_core), row, col))
            if stop > n:
                begin = max(col, n)
                found.append(
                    (source, rows, (begin - col, stop - col), slot(1, distance, other_core), row, share + begin - n)
                )
    return found


def place(found, fields, table, shards):
    layout, shapes = fields
    sources = []
    for item in found:
        if not any(item[0] is s for s in sources):
            sources.append(item[0])
    moves = []
    for source, rows, cols, where, row, col in found:
        at = [i for i, s in enumerate(sources) if s is source][0]
        for (f0, f1), (g0, g1), out, out_row, out_col in layout:
            top, bottom = max(row, f0), min(row + rows[1] - rows[0], f1)
            left, right = max(col, g0), min(col + cols[1] - cols[0], g1)
            if top < bottom and left < right:
                moves.append(
                    (
                        at,
                        (rows[0] + top - row, cols[0] + left - col),
                        (bottom - top, right - left),
                        where,
                        out,
                        (out_row + top - f0, out_col + left - g0),
                    )
                )

    def body(table_ref, *refs):
        ins, outs, sems = refs[: len(sources)], refs[len(sources) : -1], refs[-1]
        copies = []
        for i, (at, (sr, sc), (nr, nc), where, out, (dr, dc)) in enumerate(moves):
            copy = pltpu.make_async_copy(
                ins[at].at[pl.ds(sr, nr), pl.ds(sc, nc)],
                outs[out].at[table_ref[where], pl.ds(dr, nr), pl.ds(dc, nc)],
                sems.at[i],
            )
            copy.start()
            copies.append(copy)
        for copy in copies:
            copy.wait()

    return pl.pallas_call(
        body,
        grid_spec=pltpu.PrefetchScalarGridSpec(
            num_scalar_prefetch=1,
            grid=(1,),
            in_specs=[pl.BlockSpec(memory_space=pl.ANY)] * len(sources),
            out_specs=[pl.BlockSpec(memory_space=pl.ANY)] * len(shapes),
            scratch_shapes=[pltpu.SemaphoreType.DMA((len(moves),))],
        ),
        out_shape=[jax.ShapeDtypeStruct((shards,) + s, jnp.bfloat16) for s in shapes],
        name="place",
    )(table, *sources)


def add_low(left, right):
    return (left.astype(jnp.float32) + right.astype(jnp.float32)).astype(jnp.bfloat16)


def scatter_sum(blocks, share, table):
    def near(k):
        return blocks(table[slot(0, k, 0)] // 2)

    def far(k):
        return blocks(table[slot(1, k, 0)] // 2)

    nears = {k: near(k) for k in (4, 3, -3, 2, -2, 1, -1, 0)}
    fars = {k: far(k) for k in nears}
    r, n = nears[0].shape
    rest = n - share
    wide = n + rest
    half = (wide // 256) * 128

    def joined(k, met):
        first = add_low(nears[k][:, :share], met)
        if rest:
            return jnp.concatenate([first, nears[k][:, share:], fars[k][:, share:]], axis=1)
        return first

    ready = {4: joined(4, across(fars[4][:, :share]))}
    for k in (3, 2, 1):
        both = across(jnp.concatenate([fars[k][:, :share], fars[-k][:, :share]], axis=0))
        ready[k] = joined(k, both[:r])
        ready[-k] = joined(-k, both[r:])
    ready[0] = joined(0, across(fars[0][:, :share]))
    right, left = forth(ready[4][:, :half]), back(ready[4][:, half:])
    go_right = jnp.concatenate([add_low(ready[3][:, :half], right), ready[3][:, half:]], axis=1)
    go_left = jnp.concatenate([ready[-3][:, :half], add_low(ready[-3][:, half:], left)], axis=1)
    for k in (2, 1):
        right, left = forth(go_right), back(go_left)
        go_right, go_left = add_low(ready[k], right), add_low(ready[-k], left)
    right, left = forth(go_right), back(go_left)
    total = (
        ready[0].astype(jnp.float32) + right.astype(jnp.float32) + left.astype(jnp.float32)
    )
    if not rest:
        return total
    met = across(total[:, n:].astype(jnp.bfloat16))
    return jnp.concatenate([total[:, :share], total[:, share:n] + met.astype(jnp.float32)], axis=1)


def layer_norm(values, norm_gain, norm_shift):
    row_mean = jnp.mean(values, axis=-1, keepdims=True)
    centred = values - row_mean
    row_var = jnp.mean(centred * centred, axis=-1, keepdims=True)
    return centred * lax.rsqrt(row_var + EPS) * norm_gain + norm_shift


def exact_gelu(values):
    return jax.nn.gelu(values, approximate=False)


def plain_dot(left, right):
    return jnp.dot(left, right, preferred_element_type=jnp.float32)


def times_transpose(left, right):
    return lax.dot_general(
        left, right, (((1,), (1,)), ((), ())), preferred_element_type=jnp.float32
    )


def transpose_times(left, right):
    return lax.dot_general(
        left, right, (((0,), (0,)), ((), ())), preferred_element_type=jnp.float32
    )


HEAD_TILE = 768
ROWS = 16
COLS = 384


def head_body(weight_ref, x_ref, w0_ref, w1_ref, w2_ref, guess_ref, adj_ref, comb_ref, dl_ref, df_ref, ent_ref, logit_ref):
    j = pl.program_id(0)
    strength = weight_ref[0]

    @pl.when(j == 0)
    def _():
        df_ref[...] = jnp.zeros_like(df_ref)
        ent_ref[...] = jnp.zeros_like(ent_ref)

    x = x_ref[...]
    weights = (w0_ref, w1_ref, w2_ref)
    for e in range(MODEL_COUNT):
        logit_ref[e] = jnp.dot(x, weights[e][...], preferred_element_type=jnp.float32)

    for part in range(HEAD_TILE // COLS):
        cols = pl.ds(part * COLS, COLS)
        pixel = j * HEAD_TILE + part * COLS + lax.broadcasted_iota(jnp.int32, (ROWS, COLS), 1)
        real = pixel < TILE_SAMPLES

        def chunk(i, total):
            rows = pl.ds(pl.multiple_of(i * ROWS, ROWS), ROWS)
            l0, l1, l2 = (logit_ref[e, rows, cols] for e in range(3))
            top = jnp.maximum(jnp.maximum(l0, l1), l2)
            l0, l1, l2 = l0 - top, l1 - top, l2 - top
            e0, e1, e2 = jnp.exp(l0), jnp.exp(l1), jnp.exp(l2)
            norm = e0 + e1 + e2
            inverse = 1.0 / norm
            log_norm = jnp.log(norm)
            b0, b1, b2 = e0 * inverse, e1 * inverse, e2 * inverse
            l0, l1, l2 = l0 - log_norm, l1 - log_norm, l2 - log_norm
            minus_h = b0 * l0 + b1 * l1 + b2 * l2
            g0, g1, g2 = (guess_ref[e, rows, cols].astype(jnp.float32) for e in range(3))
            mixed = b0 * g0 + b1 * g1 + b2 * g2
            comb_ref[rows, cols] = mixed.astype(jnp.bfloat16)
            adj = adj_ref[rows, cols].astype(jnp.float32)
            for e, (b, l, g) in enumerate(((b0, l0, g0), (b1, l1, g1), (b2, l2, g2))):
                d = b * (adj * (g - mixed) - strength * (l - minus_h))
                dl_ref[0, e, rows, cols] = jnp.where(real, d, 0.0).astype(jnp.bfloat16)
            return total - jnp.where(real, minus_h, 0.0)

        total = lax.fori_loop(
            0, TILE_COUNT // ROWS, chunk, jnp.zeros((ROWS, COLS), jnp.float32)
        )
        gathered = total[:, :LANES]
        for k in range(1, COLS // LANES):
            gathered = gathered + total[:, k * LANES : (k + 1) * LANES]
        ent_ref[...] += gathered[:8] + gathered[8:]

    part = None
    for e in range(MODEL_COUNT):
        piece = lax.dot_general(
            dl_ref[0, e], weights[e][...], (((1,), (1,)), ((), ())), preferred_element_type=jnp.float32
        )
        part = piece if part is None else part + piece
    df_ref[...] += part


def head_pass(strength, final_low, head_w, guesses, adjoint):
    steps = PADDED // HEAD_TILE
    tile = HEAD_TILE

    def weight_spec(e):
        return pl.BlockSpec((D, tile), lambda j, s: (0, e * steps + j))

    return pl.pallas_call(
        head_body,
        grid_spec=pltpu.PrefetchScalarGridSpec(
            num_scalar_prefetch=1,
            grid=(steps,),
            in_specs=[
                pl.BlockSpec((TILE_COUNT, D), lambda j, s: (0, 0)),
                weight_spec(0),
                weight_spec(1),
                weight_spec(2),
                pl.BlockSpec((MODEL_COUNT, TILE_COUNT, tile), lambda j, s: (0, 0, j)),
                pl.BlockSpec((TILE_COUNT, tile), lambda j, s: (0, j)),
            ],
            out_specs=[
                pl.BlockSpec((TILE_COUNT, tile), lambda j, s: (0, j)),
                pl.BlockSpec(
                    (1, MODEL_COUNT, TILE_COUNT, tile),
                    lambda j, s: (j // (steps // 2), 0, 0, j % (steps // 2)),
                ),
                pl.BlockSpec((TILE_COUNT, D), lambda j, s: (0, 0)),
                pl.BlockSpec((8, LANES), lambda j, s: (0, 0)),
            ],
            scratch_shapes=[pltpu.VMEM((MODEL_COUNT, TILE_COUNT, tile), jnp.float32)],
        ),
        out_shape=[
            jax.ShapeDtypeStruct((TILE_COUNT, TILE_SAMPLES), jnp.bfloat16),
            jax.ShapeDtypeStruct((2, MODEL_COUNT, TILE_COUNT, HALF), jnp.bfloat16),
            jax.ShapeDtypeStruct((TILE_COUNT, D), jnp.float32),
            jax.ShapeDtypeStruct((8, LANES), jnp.float32),
        ],
        compiler_params=pltpu.CompilerParams(
            dimension_semantics=("arbitrary",), vmem_limit_bytes=VMEM
        ),
        name="head_pass",
    )(strength, final_low, head_w, head_w, head_w, guesses, adjoint)


def head_grad_body(core_ref, x_mine_ref, x_other_ref, d_mine_ref, d_other_ref, out_ref):
    value = lax.dot_general(
        x_mine_ref[...], d_mine_ref[0, 0], (((0,), (0,)), ((), ())), preferred_element_type=jnp.float32
    )
    value += lax.dot_general(
        x_other_ref[...], d_other_ref[0], (((0,), (0,)), ((), ())), preferred_element_type=jnp.float32
    )
    out_ref[...] = value.astype(jnp.bfloat16)


def head_grad(core, x_mine, x_other, d_mine, d_other):
    tile = 768
    steps = HALF // tile
    return pl.pallas_call(
        head_grad_body,
        grid_spec=pltpu.PrefetchScalarGridSpec(
            num_scalar_prefetch=1,
            grid=(MODEL_COUNT, steps),
            in_specs=[
                pl.BlockSpec((TILE_COUNT, D), lambda e, j, c: (0, 0)),
                pl.BlockSpec((TILE_COUNT, D), lambda e, j, c: (0, 0)),
                pl.BlockSpec((1, 1, TILE_COUNT, tile), lambda e, j, c: (c[0], e, 0, j)),
                pl.BlockSpec((1, TILE_COUNT, tile), lambda e, j, c: (e, 0, j)),
            ],
            out_specs=pl.BlockSpec((D, tile), lambda e, j, c: (0, e * steps + j)),
        ),
        out_shape=jax.ShapeDtypeStruct((D, MODEL_COUNT * HALF), jnp.bfloat16),
        compiler_params=pltpu.CompilerParams(
            dimension_semantics=("arbitrary", "arbitrary"), vmem_limit_bytes=VMEM
        ),
        name="head_grad",
    )(core, x_mine, x_other, d_mine, d_other)


def pack_small(lead_w, gains, biases, qkv_b, fc1_b, rows):
    value = jnp.concatenate([lead_w, gains, biases, qkv_b, fc1_b.reshape(4, rows).T], axis=1)
    return jnp.pad(value, ((0, 0), (0, LANES - value.shape[1])))


def split_small(small):
    at, found = 0, []
    for width in (LEADS, 2, 4, 2, 4):
        found.append(small[:, at : at + width])
        at += width
    return found


def pad_experts(value):
    value = value.reshape(value.shape[0], MODEL_COUNT, TILE_SAMPLES)
    value = jnp.pad(value, ((0, 0), (0, 0), (0, PADDED - TILE_SAMPLES)))
    return value.reshape(value.shape[0], MODEL_COUNT * PADDED)


DIGITS = 16
BASE = 8.0


def digits_of(value):
    powers = jnp.asarray([BASE**k for k in range(DIGITS + 1)], jnp.float32)
    floors = jnp.floor(value * 32.0 * powers)
    return floors[1:] - BASE * floors[:-1]


def value_of(digits):
    powers = jnp.asarray([BASE ** -(k + 1) / 32.0 for k in range(DIGITS)], jnp.float32)
    return jnp.sum(digits * powers)


HEAD_SHARE = 29 * LANES
HEAD_BACK_SHARE = 14 * LANES


class Paired:
    def __init__(self):
        self.table = places()
        self.core = lax.axis_index("fsdp") % 2

    def gather_first(self, qkv, proj, small):
        r = qkv.shape[0]
        own = jnp.concatenate([qkv, proj, small], axis=1)
        found = gather_pieces(own, own.shape[1], (0, 13 * LANES))
        n = 3 * D
        layout = [
            ((0, r), (0, n), 0, 0, 0),
            ((0, r), (n, n + D), 1, 0, 0),
            ((0, r), (n + D, n + D + LANES), 2, 0, 0),
        ]
        qkv, proj, small = place(found, (layout, [(r, n), (r, D), (r, LANES)]), self.table, 32)
        return qkv.reshape(D, n), proj.reshape(D, D), small.reshape(D, LANES)

    def gather_second(self, fc1, fc2):
        r = fc1.shape[0]
        own = jnp.concatenate([fc2] + [fc1[:, k * D : (k + 1) * D] for k in range(4)], axis=0)
        found = gather_pieces(own, D, (4 * r, 0))
        layout = [((0, 4 * r), (0, D), 1, 0, 0)]
        for k in range(4):
            layout.append((((4 + k) * r, (5 + k) * r), (0, D), 0, 0, k * D))
        fc1, fc2 = place(found, (layout, [(r, FF), (4 * r, D)]), self.table, 32)
        return fc1.reshape(D, FF), fc2.reshape(FF, D)

    def gather_head(self, head):
        r = head.shape[0]
        own = pad_experts(head)
        n = own.shape[1]
        wide = 2 * n - HEAD_SHARE
        found = gather_pieces(own, HEAD_SHARE, (0, wide // 256 * LANES))
        (value,) = place(found, ([((0, r), (0, n), 0, 0, 0)], [(r, n)]), self.table, 32)
        return value.reshape(D, n)

    def half(self, value):
        n = value.shape[1] // 2
        low, high = value[:, :n], value[:, n:]
        first = self.core == 0
        return jnp.where(first, low, high), jnp.where(first, high, low)

    def with_sibling(self, value):
        return jnp.concatenate([value, sibling(value)], axis=0)

    def paired_grad(self, left, right):
        mine, other = self.half(right)
        joint = jnp.concatenate([mine, sibling(other)], axis=0)
        return transpose_times(left, joint).astype(jnp.bfloat16)

    def finish(self, total, rows):
        own = jnp.where(self.core == 0, rows(total, 0), rows(total, 1))
        other = jnp.where(self.core == 0, rows(total, 1), rows(total, 0))
        met = sibling(other.astype(jnp.bfloat16)).astype(jnp.float32)
        first = self.core == 0
        return jnp.where(first, own, met), jnp.where(first, met, own)


def on_device(
    tile_embeddings,
    horizon_indices,
    horizon_tallies,
    member_guesses,
    adjoint_of_mixture,
    triple_projection_matrix,
    attention_outward_matrix,
    widening_matrix,
    narrowing_matrix,
    gating_matrix,
    horizon_embedding_matrix,
    normalization_scales,
    channel_offsets,
    triple_projection_offset,
    hidden_offset,
    *,
    paired,
):
    rows = triple_projection_matrix.shape[0]
    small = pack_small(
        horizon_embedding_matrix,
        normalization_scales,
        channel_offsets,
        triple_projection_offset,
        hidden_offset,
        rows,
    )
    if paired:
        net = Paired()
        qkv_w, proj_w, small_all = net.gather_first(
            triple_projection_matrix, attention_outward_matrix, small
        )
        fc1_w, fc2_w = net.gather_second(widening_matrix, narrowing_matrix)
        head_w = net.gather_head(gating_matrix)
    else:
        whole = functools.partial(lax.all_gather, axis_name=AXES, axis=0, tiled=True)
        qkv_w = whole(triple_projection_matrix)
        proj_w = whole(attention_outward_matrix)
        fc1_w = whole(widening_matrix)
        fc2_w = whole(narrowing_matrix)
        small_all = whole(small)
        head_w = whole(pad_experts(gating_matrix))
    lead_w, gain_all, bias_all, qkv_b, fc1_b = split_small(small_all)
    fc1_b_f = (
        fc1_b.astype(jnp.float32).reshape(D // rows, rows, 4).transpose(0, 2, 1).reshape(FF)
    )
    gain_f = gain_all.astype(jnp.float32)
    bias_f = bias_all.astype(jnp.float32)
    qkv_b_f = qkv_b.astype(jnp.float32)
    full_offset = jnp.concatenate([qkv_b_f[:, 0], jnp.zeros_like(qkv_b_f[:, 0]), qkv_b_f[:, 1]])
    guesses = jnp.transpose(member_guesses[0], (1, 0, 2))
    adjoint = adjoint_of_mixture[0]
    frame = tile_embeddings[0].astype(jnp.float32)
    horizon_indicator = (horizon_indices[0] == lax.iota(jnp.int32, LEADS)).astype(jnp.float32)
    frame_count = jnp.sum(horizon_indicator * horizon_tallies.astype(jnp.float32))
    regularizer_strength = 1.0 / (frame_count * (LEADS * TILE_COUNT * TILE_SAMPLES))
    lead_vector = jnp.sum(lead_w.astype(jnp.float32) * horizon_indicator[None, :], axis=1)
    started = frame + lead_vector[None, :]
    normed_f, norm_one_back = jax.vjp(layer_norm, started, gain_f[:, 0], bias_f[:, 0])
    normed = normed_f.astype(jnp.bfloat16)
    joined = (plain_dot(normed, qkv_w) + full_offset).astype(jnp.bfloat16)
    queries = joined[:, :D].reshape(TILE_COUNT, HEADS, HD)
    keys_all = joined[:, D : 2 * D].reshape(TILE_COUNT, HEADS, HD)
    values_all = joined[:, 2 * D :].reshape(TILE_COUNT, HEADS, HD)
    score_scale = HD ** (-0.5)
    scores = (
        jnp.einsum("qhd,khd->hqk", queries, keys_all, preferred_element_type=jnp.float32)
        * score_scale
    )
    row_top = jnp.max(scores, axis=-1, keepdims=True)
    expd = jnp.exp(scores - row_top)
    prob_full = expd / jnp.sum(expd, axis=-1, keepdims=True)
    probs_low = prob_full.astype(jnp.bfloat16)
    attended = (
        jnp.einsum("hqk,khd->qhd", probs_low, values_all, preferred_element_type=jnp.float32)
        .astype(jnp.bfloat16)
        .reshape(TILE_COUNT, D)
    )
    middle = started + plain_dot(attended, proj_w) + bias_f[:, 1]
    normed_two_f, norm_two_back = jax.vjp(layer_norm, middle, gain_f[:, 1], bias_f[:, 2])
    normed_two = normed_two_f.astype(jnp.bfloat16)
    pre_act = plain_dot(normed_two, fc1_w) + fc1_b_f
    hidden_f, gelu_back = jax.vjp(exact_gelu, pre_act)
    hidden = hidden_f.astype(jnp.bfloat16)
    final_sum = middle + plain_dot(hidden, fc2_w) + bias_f[:, 3]
    final_low = final_sum.astype(jnp.bfloat16)

    combined, d_logits, d_final, entropy = head_pass(
        regularizer_strength.reshape(1), final_low, head_w, guesses, adjoint
    )
    combined_result = combined[None]
    contribution = jnp.sum(entropy) * regularizer_strength

    if paired:
        sent = lax.dynamic_index_in_dim(d_logits, 1 - net.core, 0, keepdims=False)
        d_logits_other = sibling(sent)
        final_other = sibling(final_low)
        grad_head = head_grad(
            net.core.reshape(1), final_low, final_other, d_logits, d_logits_other
        ).reshape(16, 2 * rows, MODEL_COUNT * HALF)
        normed_pair, attended_pair, normed_two_pair, hidden_pair = (
            net.with_sibling(v) for v in (normed, attended, normed_two, hidden)
        )

    d_branch = d_final.astype(jnp.bfloat16)
    grad_fc2_bias = jnp.sum(d_branch.astype(jnp.float32), axis=0)
    d_hidden = times_transpose(d_branch, fc2_w)
    d_pre = gelu_back(d_hidden)[0].astype(jnp.bfloat16)
    grad_fc1_bias = jnp.sum(d_pre.astype(jnp.float32), axis=0)
    d_normed_two = times_transpose(d_pre, fc1_w)
    d_mid_part, grad_gain_two, grad_shift_two = norm_two_back(d_normed_two)
    d_middle = d_final + d_mid_part
    d_attn = d_middle.astype(jnp.bfloat16)
    grad_proj_bias = jnp.sum(d_attn.astype(jnp.float32), axis=0)
    d_attended = times_transpose(d_attn, proj_w).astype(jnp.bfloat16).reshape(TILE_COUNT, HEADS, HD)
    d_values = jnp.einsum("hqk,qhd->khd", probs_low, d_attended, preferred_element_type=jnp.float32)
    d_prob = jnp.einsum("qhd,khd->hqk", d_attended, values_all, preferred_element_type=jnp.float32)
    d_score = (
        prob_full * (d_prob - jnp.sum(prob_full * d_prob, axis=-1, keepdims=True))
    ).astype(jnp.bfloat16)
    d_queries = (
        jnp.einsum("hqk,khd->qhd", d_score, keys_all, preferred_element_type=jnp.float32)
        * score_scale
    )
    d_keys = (
        jnp.einsum("hqk,qhd->khd", d_score, queries, preferred_element_type=jnp.float32)
        * score_scale
    )
    d_joined = jnp.concatenate(
        [v.reshape(TILE_COUNT, D) for v in (d_queries, d_keys, d_values)], axis=1
    ).astype(jnp.bfloat16)
    joined_sums = jnp.sum(d_joined.astype(jnp.float32), axis=0)
    d_normed = times_transpose(d_joined, qkv_w)
    d_start_part, grad_gain_one, grad_shift_one = norm_one_back(d_normed)
    d_started = d_middle + d_start_part
    grad_tokens = d_started.astype(jnp.bfloat16)[None]

    columns = jnp.stack(
        [
            grad_gain_one,
            grad_gain_two,
            grad_shift_one,
            grad_proj_bias,
            grad_shift_two,
            grad_fc2_bias,
            joined_sums[:D],
            joined_sums[2 * D :],
        ],
        axis=1,
    )
    hidden_columns = (
        grad_fc1_bias.reshape(D // rows, 4, rows).transpose(0, 2, 1).reshape(D, 4)
    )
    small_grad = jnp.concatenate(
        [
            jnp.sum(d_started, axis=0)[:, None] * horizon_indicator[None, :],
            columns,
            hidden_columns,
            jnp.broadcast_to(digits_of(contribution)[None, :], (D, DIGITS)),
            jnp.zeros((D, LANES - LEADS - 12 - DIGITS), jnp.float32),
        ],
        axis=1,
    ).astype(jnp.bfloat16)

    if paired:
        head_total = scatter_sum(
            lambda i: lax.dynamic_index_in_dim(grad_head, i, 0, keepdims=False),
            HEAD_BACK_SHARE,
            net.table,
        )

        def low_or_high(value, core):
            return value[core * rows : (core + 1) * rows]

        low, high = net.finish(head_total, low_or_high)
        low, high = (v.reshape(rows, MODEL_COUNT, HALF) for v in (low, high))
        out_head = jnp.concatenate([low, high[:, :, : TILE_SAMPLES - HALF]], axis=2).reshape(
            rows, MODEL_COUNT * TILE_SAMPLES
        )

        fc2_half = net.paired_grad(hidden_pair, d_branch).reshape(16, 8 * rows, D // 2)
        fc1_half = net.paired_grad(normed_two_pair, d_pre).reshape(16, 2 * rows, FF // 2)

        def second_block(i):
            one = lax.dynamic_index_in_dim(fc1_half, i, 0, keepdims=False)
            two = lax.dynamic_index_in_dim(fc2_half, i, 0, keepdims=False)
            wide = D // 2
            return jnp.concatenate(
                [two] + [one[:, k * wide : (k + 1) * wide] for k in range(4)], axis=0
            )

        total = scatter_sum(second_block, D // 2, net.table)

        def fc2_rows(value, core):
            return value[core * 4 * rows : (core + 1) * 4 * rows]

        def fc1_rows(value, core):
            begin = 8 * rows + core * rows
            return jnp.concatenate(
                [value[begin + 2 * k * rows : begin + (2 * k + 1) * rows] for k in range(4)], axis=1
            )

        out_fc2 = jnp.concatenate(net.finish(total, fc2_rows), axis=1)
        out_fc1 = jnp.concatenate(net.finish(total, fc1_rows), axis=1)

        qkv_half = net.paired_grad(normed_pair, d_joined).reshape(16, 2 * rows, 3 * D // 2)
        proj_half = net.paired_grad(attended_pair, d_attn).reshape(16, 2 * rows, D // 2)
        small_pair = add_low(small_grad, sibling(small_grad)).reshape(16, 2 * rows, LANES)

        def first_block(i):
            return jnp.concatenate(
                [
                    lax.dynamic_index_in_dim(v, i, 0, keepdims=False)
                    for v in (qkv_half, proj_half, small_pair)
                ],
                axis=1,
            )

        total = scatter_sum(first_block, 2 * D + LANES, net.table)
        out_small = jnp.where(net.core == 0, total[:rows, 2 * D :], total[rows:, 2 * D :])
        low, high = net.finish(total[:, : 2 * D], low_or_high)
        n = 3 * D // 2
        out_qkv = jnp.concatenate([low[:, :n], high[:, :n]], axis=1)
        out_proj = jnp.concatenate([low[:, n:], high[:, n:]], axis=1)
    else:

        def summed(value):
            return lax.psum_scatter(
                value.astype(jnp.bfloat16), AXES, scatter_dimension=0, tiled=True
            ).astype(jnp.float32)

        flat = d_logits.transpose(2, 1, 0, 3).reshape(TILE_COUNT, MODEL_COUNT * PADDED)
        out_head = summed(transpose_times(final_low, flat))
        out_head = out_head.reshape(rows, MODEL_COUNT, PADDED)[:, :, :TILE_SAMPLES]
        out_head = out_head.reshape(rows, MODEL_COUNT * TILE_SAMPLES)
        out_fc2 = summed(transpose_times(hidden, d_branch))
        out_fc1 = summed(transpose_times(normed_two, d_pre))
        out_qkv = summed(transpose_times(normed, d_joined))
        out_proj = summed(transpose_times(attended, d_attn))
        out_small = summed(small_grad)
        cost = lax.psum(contribution, AXES)

    out_lead = out_small[:, :LEADS]
    out_gains = out_small[:, LEADS : LEADS + 2]
    out_biases = out_small[:, LEADS + 2 : LEADS + 6]
    out_qkv_bias = out_small[:, LEADS + 6 : LEADS + 8]
    out_fc1_bias = out_small[:, LEADS + 8 : LEADS + 12].T.reshape(4 * rows)
    if paired:
        cost = value_of(out_small[0, LEADS + 12 : LEADS + 12 + DIGITS])
    return (
        combined_result,
        cost,
        grad_tokens,
        out_qkv,
        out_proj,
        out_fc1,
        out_fc2,
        out_head,
        out_lead,
        out_gains,
        out_biases,
        out_qkv_bias,
        out_fc1_bias,
    )


def solution(mesh):
    split = P(AXES)
    paired = mesh.shape["dp"] == 2 and mesh.shape["fsdp"] == 16
    return jax.shard_map(
        functools.partial(on_device, paired=paired),
        mesh=mesh,
        in_specs=(split, split, P()) + (split,) * 12,
        out_specs=(split, P()) + (split,) * 11,
        check_vma=False,
    )
```

```python
import functools

import jax
import jax.numpy as jnp
from jax import lax
from jax.experimental import pallas as pl
from jax.experimental.pallas import tpu as pltpu
from jax.sharding import PartitionSpec as P

D = 768
HEADS = 12
HD = 64
FF = 3072
MODEL_COUNT = 3
TILE_SAMPLES = 4416
LEADS = 40
TILE_COUNT = 256
EPS = 1e-06
LANES = 128
HALF = 2304
PADDED = 2 * HALF
VMEM = 56 * 1024 * 1024

AXES = ("dp", "fsdp")
RING = [(z, 0) for z in range(4)] + [(z, 1) for z in (3, 2, 1, 0)]


def ring_pairs(step):
    pairs = []
    for spot, (z, x) in enumerate(RING):
        to_z, to_x = RING[(spot + step) % 8]
        for core in range(2):
            pairs.append((z * 4 + x * 2 + core, to_z * 4 + to_x * 2 + core))
    return pairs


def forth(value):
    return lax.ppermute(value, "fsdp", ring_pairs(1))


def back(value):
    return lax.ppermute(value, "fsdp", ring_pairs(-1))


def across(value):
    return lax.ppermute(value, "dp", [(0, 1), (1, 0)])


def sibling(value):
    return lax.ppermute(value, "fsdp", [(i, i ^ 1) for i in range(16)])


def places():
    y = lax.axis_index("dp")
    f = lax.axis_index("fsdp")
    z, x, core = f // 4, (f // 2) % 2, f % 2
    spot = jnp.where(x == 0, z, 7 - z)
    i = lax.iota(jnp.int32, 32)
    seat = (spot + (i // 2) % 8) % 8
    pair = jnp.where(seat < 4, seat * 2, (7 - seat) * 2 + 1)
    return ((y + i // 16) % 2) * 16 + pair * 2 + (core + i) % 2


def slot(other_row, distance, other_core):
    return other_row * 16 + (distance % 8) * 2 + other_core


def gather_pieces(own, share, half):
    r, n = own.shape
    rest = n - share
    found = []
    over = across(own)
    first = own
    if rest:
        first = jnp.concatenate([own, over[:, share:]], axis=1)
    wide = n + rest
    rights, lefts = [first], [first]
    for _ in range(3):
        rights.append(forth(rights[-1]))
        lefts.append(back(lefts[-1]))
    rows_half, cols_half = half
    if cols_half:
        far = [
            (forth(rights[3][:, :cols_half]), 0, 0),
            (back(lefts[3][:, cols_half:]), 0, cols_half),
        ]
    else:
        far = [
            (forth(rights[3][:rows_half]), 0, 0),
            (back(lefts[3][rows_half:]), rows_half, 0),
        ]
    held = []
    held.append((own, 0, 0, 0, False))
    held.append((over, 0, 0, 0, True))
    for k in range(1, 4):
        held.append((rights[k], -k, 0, 0, False))
        held.append((lefts[k], k, 0, 0, False))
        pair = jnp.concatenate([rights[k][:, :share], lefts[k][:, :share]], axis=0)
        held.append((across(pair), k, 0, 0, True))
    for array, row, col in far:
        held.append((array, 4, row, col, False))
        stop = min(share, col + array.shape[1])
        if stop > col:
            held.append((across(array[:, : stop - col]), 4, row, col, True))
    for array, distance, row, col, swapped in held:
        for other_core in (0, 1):
            source = sibling(array) if other_core else array
            if swapped and array.shape[0] == 2 * r:
                found.append((source, (0, r), (0, share), slot(1, -distance, other_core), 0, 0))
                found.append((source, (r, 2 * r), (0, share), slot(1, distance, other_core), 0, 0))
                continue
            rows = (0, array.shape[0])
            if swapped:
                found.append((source, rows, (0, array.shape[1]), slot(1, distance, other_core), row, col))
                continue
            stop = col + array.shape[1]
            if col < n:
                found.append((source, rows, (0, min(stop, n) - col), slot(0, distance, other_core), row, col))
            if stop > n:
                begin = max(col, n)
                found.append(
                    (source, rows, (begin - col, stop - col), slot(1, distance, other_core), row, share + begin - n)
                )
    return found


def plan_moves(found, fields):
    layout = fields[0]
    sources = []
    for item in found:
        if not any(item[0] is s for s in sources):
            sources.append(item[0])
    moves = []
    for source, rows, cols, where, row, col in found:
        at = [i for i, s in enumerate(sources) if s is source][0]
        for (f0, f1), (g0, g1), out, out_row, out_col in layout:
            top, bottom = max(row, f0), min(row + rows[1] - rows[0], f1)
            left, right = max(col, g0), min(col + cols[1] - cols[0], g1)
            if top < bottom and left < right:
                moves.append(
                    (
                        at,
                        (rows[0] + top - row, cols[0] + left - col),
                        (bottom - top, right - left),
                        where,
                        out,
                        (out_row + top - f0, out_col + left - g0),
                    )
                )
    return sources, moves


def place(found, fields, table, shards):
    sources, moves = plan_moves(found, fields)
    shapes = fields[1]

    def body(table_ref, *refs):
        ins, outs = refs[: len(sources)], refs[len(sources) : len(sources) + len(shapes)]
        held, sems, out_sems = refs[len(sources) + len(shapes) : -2], refs[-2], refs[-1]
        run_moves(moves, table_ref, ins, held, sems)
        copies = [
            pltpu.make_async_copy(held[i], outs[i], out_sems.at[i]) for i in range(len(shapes))
        ]
        for copy in copies:
            copy.start()
        for copy in copies:
            copy.wait()

    whole = [(shards,) + s for s in shapes]
    return pl.pallas_call(
        body,
        grid_spec=pltpu.PrefetchScalarGridSpec(
            num_scalar_prefetch=1,
            grid=(1,),
            in_specs=[pl.BlockSpec(memory_space=pl.ANY)] * len(sources),
            out_specs=[pl.BlockSpec(memory_space=pl.ANY)] * len(shapes),
            scratch_shapes=[pltpu.VMEM(s, jnp.bfloat16) for s in whole]
            + [
                pltpu.SemaphoreType.DMA((len(moves),)),
                pltpu.SemaphoreType.DMA((len(shapes),)),
            ],
        ),
        out_shape=[jax.ShapeDtypeStruct(s, jnp.bfloat16) for s in whole],
        compiler_params=pltpu.CompilerParams(vmem_limit_bytes=VMEM),
        name="place",
    )(table, *sources)


def run_moves(moves, table_ref, ins, outs, sems):
    copies = []
    for i, (at, (sr, sc), (nr, nc), where, out, (dr, dc)) in enumerate(moves):
        copy = pltpu.make_async_copy(
            ins[at].at[pl.ds(sr, nr), pl.ds(sc, nc)],
            outs[out].at[table_ref[where], pl.ds(dr, nr), pl.ds(dc, nc)],
            sems.at[i],
        )
        copy.start()
        copies.append(copy)
    for copy in copies:
        copy.wait()


def add_low(left, right):
    return (left.astype(jnp.float32) + right.astype(jnp.float32)).astype(jnp.bfloat16)


def scatter_sum(blocks, share):
    nears = {k: blocks(k % 8) for k in (4, 3, -3, 2, -2, 1, -1, 0)}
    fars = {k: blocks(8 + k % 8) for k in nears}
    r, n = nears[0].shape
    rest = n - share
    wide = n + rest
    half = (wide // 256) * 128

    def joined(k, met):
        first = add_low(nears[k][:, :share], met)
        if rest:
            return jnp.concatenate([first, nears[k][:, share:], fars[k][:, share:]], axis=1)
        return first

    ready = {4: joined(4, across(fars[4][:, :share]))}
    for k in (3, 2, 1):
        both = across(jnp.concatenate([fars[k][:, :share], fars[-k][:, :share]], axis=0))
        ready[k] = joined(k, both[:r])
        ready[-k] = joined(-k, both[r:])
    ready[0] = joined(0, across(fars[0][:, :share]))
    right, left = forth(ready[4][:, :half]), back(ready[4][:, half:])
    go_right = jnp.concatenate([add_low(ready[3][:, :half], right), ready[3][:, half:]], axis=1)
    go_left = jnp.concatenate([ready[-3][:, :half], add_low(ready[-3][:, half:], left)], axis=1)
    for k in (2, 1):
        right, left = forth(go_right), back(go_left)
        go_right, go_left = add_low(ready[k], right), add_low(ready[-k], left)
    right, left = forth(go_right), back(go_left)
    total = (
        ready[0].astype(jnp.float32) + right.astype(jnp.float32) + left.astype(jnp.float32)
    )
    if not rest:
        return total
    met = across(total[:, n:].astype(jnp.bfloat16))
    return jnp.concatenate([total[:, :share], total[:, share:n] + met.astype(jnp.float32)], axis=1)


def layer_norm(values, norm_gain, norm_shift):
    row_mean = jnp.mean(values, axis=-1, keepdims=True)
    centred = values - row_mean
    row_var = jnp.mean(centred * centred, axis=-1, keepdims=True)
    return centred * lax.rsqrt(row_var + EPS) * norm_gain + norm_shift


def exact_gelu(values):
    return jax.nn.gelu(values, approximate=False)


def plain_dot(left, right):
    return jnp.dot(left, right, preferred_element_type=jnp.float32)


def times_transpose(left, right):
    return lax.dot_general(
        left, right, (((1,), (1,)), ((), ())), preferred_element_type=jnp.float32
    )


def transpose_times(left, right):
    return lax.dot_general(
        left, right, (((0,), (0,)), ((), ())), preferred_element_type=jnp.float32
    )


HEAD_TILE = 768
ROWS = 16
COLS = 384


def head_body(moves, weight_ref, table_ref, x_ref, guess_ref, adj_ref, *refs):
    ins, refs = refs[:-7], refs[-7:]
    comb_ref, dl_ref, df_ref, ent_ref, logit_ref, held_ref, sems = refs
    j = pl.program_id(0)
    strength = weight_ref[0]

    @pl.when(j == 0)
    def _():
        df_ref[...] = jnp.zeros_like(df_ref)
        ent_ref[...] = jnp.zeros_like(ent_ref)
        run_moves(moves, table_ref, ins, [held_ref], sems)

    x = x_ref[...]

    def weight(e):
        begin = pl.multiple_of(e * PADDED + j * HEAD_TILE, LANES)
        return held_ref[:, :, pl.ds(begin, HEAD_TILE)].reshape(D, HEAD_TILE)

    for e in range(MODEL_COUNT):
        logit_ref[e] = jnp.dot(x, weight(e), preferred_element_type=jnp.float32)

    for part in range(HEAD_TILE // COLS):
        cols = pl.ds(part * COLS, COLS)
        pixel = j * HEAD_TILE + part * COLS + lax.broadcasted_iota(jnp.int32, (ROWS, COLS), 1)
        real = pixel < TILE_SAMPLES

        def chunk(i, total):
            rows = pl.ds(pl.multiple_of(i * ROWS, ROWS), ROWS)
            l0, l1, l2 = (logit_ref[e, rows, cols] for e in range(3))
            top = jnp.maximum(jnp.maximum(l0, l1), l2)
            l0, l1, l2 = l0 - top, l1 - top, l2 - top
            e0, e1, e2 = jnp.exp(l0), jnp.exp(l1), jnp.exp(l2)
            norm = e0 + e1 + e2
            inverse = 1.0 / norm
            log_norm = jnp.log(norm)
            b0, b1, b2 = e0 * inverse, e1 * inverse, e2 * inverse
            l0, l1, l2 = l0 - log_norm, l1 - log_norm, l2 - log_norm
            minus_h = b0 * l0 + b1 * l1 + b2 * l2
            g0, g1, g2 = (guess_ref[e, rows, cols].astype(jnp.float32) for e in range(3))
            mixed = b0 * g0 + b1 * g1 + b2 * g2
            comb_ref[rows, cols] = mixed.astype(jnp.bfloat16)
            adj = adj_ref[rows, cols].astype(jnp.float32)
            for e, (b, l, g) in enumerate(((b0, l0, g0), (b1, l1, g1), (b2, l2, g2))):
                d = b * (adj * (g - mixed) - strength * (l - minus_h))
                dl_ref[0, e, rows, cols] = jnp.where(real, d, 0.0).astype(jnp.bfloat16)
            return total - jnp.where(real, minus_h, 0.0)

        total = lax.fori_loop(
            0, TILE_COUNT // ROWS, chunk, jnp.zeros((ROWS, COLS), jnp.float32)
        )
        gathered = total[:, :LANES]
        for k in range(1, COLS // LANES):
            gathered = gathered + total[:, k * LANES : (k + 1) * LANES]
        ent_ref[...] += gathered[:8] + gathered[8:]

    part = None
    for e in range(MODEL_COUNT):
        piece = lax.dot_general(
            dl_ref[0, e], weight(e), (((1,), (1,)), ((), ())), preferred_element_type=jnp.float32
        )
        part = piece if part is None else part + piece
    df_ref[...] += part


def head_pass(strength, table, final_low, sources, moves, held_shape, guesses, adjoint):
    steps = PADDED // HEAD_TILE
    tile = HEAD_TILE
    return pl.pallas_call(
        functools.partial(head_body, moves),
        grid_spec=pltpu.PrefetchScalarGridSpec(
            num_scalar_prefetch=2,
            grid=(steps,),
            in_specs=[
                pl.BlockSpec((TILE_COUNT, D), lambda j, s, t: (0, 0)),
                pl.BlockSpec((MODEL_COUNT, TILE_COUNT, tile), lambda j, s, t: (0, 0, j)),
                pl.BlockSpec((TILE_COUNT, tile), lambda j, s, t: (0, j)),
            ]
            + [pl.BlockSpec(memory_space=pl.ANY)] * len(sources),
            out_specs=[
                pl.BlockSpec((TILE_COUNT, tile), lambda j, s, t: (0, j)),
                pl.BlockSpec(
                    (1, MODEL_COUNT, TILE_COUNT, tile),
                    lambda j, s, t: (j // (steps // 2), 0, 0, j % (steps // 2)),
                ),
                pl.BlockSpec((TILE_COUNT, D), lambda j, s, t: (0, 0)),
                pl.BlockSpec((8, LANES), lambda j, s, t: (0, 0)),
            ],
            scratch_shapes=[
                pltpu.VMEM((MODEL_COUNT, TILE_COUNT, tile), jnp.float32),
                pltpu.VMEM(held_shape, jnp.bfloat16),
                pltpu.SemaphoreType.DMA((len(moves),)),
            ],
        ),
        out_shape=[
            jax.ShapeDtypeStruct((TILE_COUNT, TILE_SAMPLES), jnp.bfloat16),
            jax.ShapeDtypeStruct((2, MODEL_COUNT, TILE_COUNT, HALF), jnp.bfloat16),
            jax.ShapeDtypeStruct((TILE_COUNT, D), jnp.float32),
            jax.ShapeDtypeStruct((8, LANES), jnp.float32),
        ],
        compiler_params=pltpu.CompilerParams(
            dimension_semantics=("arbitrary",), vmem_limit_bytes=VMEM
        ),
        name="head_pass",
    )(strength, table, final_low, guesses, adjoint, *sources)


def head_grad_body(core_ref, chips_ref, x_mine_ref, x_other_ref, d_mine_ref, d_other_ref, out_ref, sum_ref):
    value = lax.dot_general(
        x_mine_ref[...], d_mine_ref[0, 0], (((0,), (0,)), ((), ())), preferred_element_type=jnp.float32
    )
    value += lax.dot_general(
        x_other_ref[...], d_other_ref[0], (((0,), (0,)), ((), ())), preferred_element_type=jnp.float32
    )
    sum_ref[...] = value.reshape(sum_ref.shape)
    for i in range(16):
        out_ref[i] = sum_ref[chips_ref[i]].astype(jnp.bfloat16)


def head_grad(core, chips, x_mine, x_other, d_mine, d_other):
    tile = 768
    steps = HALF // tile
    r = D // 16
    return pl.pallas_call(
        head_grad_body,
        grid_spec=pltpu.PrefetchScalarGridSpec(
            num_scalar_prefetch=2,
            grid=(MODEL_COUNT, steps),
            in_specs=[
                pl.BlockSpec((TILE_COUNT, D), lambda e, j, c, t: (0, 0)),
                pl.BlockSpec((TILE_COUNT, D), lambda e, j, c, t: (0, 0)),
                pl.BlockSpec((1, 1, TILE_COUNT, tile), lambda e, j, c, t: (c[0], e, 0, j)),
                pl.BlockSpec((1, TILE_COUNT, tile), lambda e, j, c, t: (e, 0, j)),
            ],
            out_specs=pl.BlockSpec((16, r, tile), lambda e, j, c, t: (0, 0, e * steps + j)),
            scratch_shapes=[pltpu.VMEM((16, r, tile), jnp.float32)],
        ),
        out_shape=jax.ShapeDtypeStruct((16, r, MODEL_COUNT * HALF), jnp.bfloat16),
        compiler_params=pltpu.CompilerParams(
            dimension_semantics=("arbitrary", "arbitrary"), vmem_limit_bytes=VMEM
        ),
        name="head_grad",
    )(core, chips, x_mine, x_other, d_mine, d_other)


def pack_small(lead_w, gains, biases, qkv_b, fc1_b, rows):
    value = jnp.concatenate([lead_w, gains, biases, qkv_b, fc1_b.reshape(4, rows).T], axis=1)
    return jnp.pad(value, ((0, 0), (0, LANES - value.shape[1])))


def split_small(small):
    at, found = 0, []
    for width in (LEADS, 2, 4, 2, 4):
        found.append(small[:, at : at + width])
        at += width
    return found


def pad_experts(value):
    value = value.reshape(value.shape[0], MODEL_COUNT, TILE_SAMPLES)
    value = jnp.pad(value, ((0, 0), (0, 0), (0, PADDED - TILE_SAMPLES)))
    return value.reshape(value.shape[0], MODEL_COUNT * PADDED)


DIGITS = 16
BASE = 8.0


def digits_of(value):
    powers = jnp.asarray([BASE**k for k in range(DIGITS + 1)], jnp.float32)
    floors = jnp.floor(value * 32.0 * powers)
    return floors[1:] - BASE * floors[:-1]


def value_of(digits):
    powers = jnp.asarray([BASE ** -(k + 1) / 32.0 for k in range(DIGITS)], jnp.float32)
    return jnp.sum(digits * powers)


HEAD_SHARE = 29 * LANES
HEAD_BACK_SHARE = 14 * LANES


class Paired:
    def __init__(self):
        self.table = places()
        self.core = lax.axis_index("fsdp") % 2
        self.chips = self.table[::2] // 2
        self.chip_of = self.chips.astype(jnp.uint32)

    def block(self, value, i):
        zero = jnp.uint32(0)
        return lax.dynamic_slice(value, (self.chip_of[i], zero, zero), (1,) + value.shape[1:])[0]

    def gather_first(self, qkv, proj, small):
        r = qkv.shape[0]
        own = jnp.concatenate([qkv, proj, small], axis=1)
        found = gather_pieces(own, own.shape[1], (0, 13 * LANES))
        n = 3 * D
        layout = [
            ((0, r), (0, n), 0, 0, 0),
            ((0, r), (n, n + D), 1, 0, 0),
            ((0, r), (n + D, n + D + LANES), 2, 0, 0),
        ]
        qkv, proj, small = place(found, (layout, [(r, n), (r, D), (r, LANES)]), self.table, 32)
        return qkv.reshape(D, n), proj.reshape(D, D), small.reshape(D, LANES)

    def gather_second(self, fc1, fc2):
        r = fc1.shape[0]
        own = jnp.concatenate([fc2] + [fc1[:, k * D : (k + 1) * D] for k in range(4)], axis=0)
        found = gather_pieces(own, D, (4 * r, 0))
        layout = [((0, 4 * r), (0, D), 1, 0, 0)]
        for k in range(4):
            layout.append((((4 + k) * r, (5 + k) * r), (0, D), 0, 0, k * D))
        fc1, fc2 = place(found, (layout, [(r, FF), (4 * r, D)]), self.table, 32)
        return fc1.reshape(D, FF), fc2.reshape(FF, D)

    def gather_head(self, head):
        r = head.shape[0]
        own = pad_experts(head)
        n = own.shape[1]
        wide = 2 * n - HEAD_SHARE
        found = gather_pieces(own, HEAD_SHARE, (0, wide // 256 * LANES))
        return plan_moves(found, ([((0, r), (0, n), 0, 0, 0)], [(r, n)]))

    def half(self, value):
        n = value.shape[1] // 2
        low, high = value[:, :n], value[:, n:]
        first = self.core == 0
        return jnp.where(first, low, high), jnp.where(first, high, low)

    def with_sibling(self, value):
        return jnp.concatenate([value, sibling(value)], axis=0)

    def paired_grad(self, left, right):
        mine, other = self.half(right)
        joint = jnp.concatenate([mine, sibling(other)], axis=0)
        return transpose_times(left, joint).astype(jnp.bfloat16)

    def finish(self, total, rows):
        own = jnp.where(self.core == 0, rows(total, 0), rows(total, 1))
        other = jnp.where(self.core == 0, rows(total, 1), rows(total, 0))
        met = sibling(other.astype(jnp.bfloat16)).astype(jnp.float32)
        first = self.core == 0
        return jnp.where(first, own, met), jnp.where(first, met, own)


def on_device(
    tile_embeddings,
    horizon_indices,
    horizon_tallies,
    member_guesses,
    adjoint_of_mixture,
    triple_projection_matrix,
    attention_outward_matrix,
    widening_matrix,
    narrowing_matrix,
    gating_matrix,
    horizon_embedding_matrix,
    normalization_scales,
    channel_offsets,
    triple_projection_offset,
    hidden_offset,
    *,
    paired,
):
    rows = triple_projection_matrix.shape[0]
    small = pack_small(
        horizon_embedding_matrix,
        normalization_scales,
        channel_offsets,
        triple_projection_offset,
        hidden_offset,
        rows,
    )
    if paired:
        net = Paired()
        qkv_w, proj_w, small_all = net.gather_first(
            triple_projection_matrix, attention_outward_matrix, small
        )
        fc1_w, fc2_w = net.gather_second(widening_matrix, narrowing_matrix)
        head_sources, head_moves = net.gather_head(gating_matrix)
        table = net.table
        held_shape = (32, rows, MODEL_COUNT * PADDED)
    else:
        whole = functools.partial(lax.all_gather, axis_name=AXES, axis=0, tiled=True)
        qkv_w = whole(triple_projection_matrix)
        proj_w = whole(attention_outward_matrix)
        fc1_w = whole(widening_matrix)
        fc2_w = whole(narrowing_matrix)
        small_all = whole(small)
        head_sources = [whole(pad_experts(gating_matrix))]
        held_shape = (1, D, MODEL_COUNT * PADDED)
        head_moves = [(0, (0, 0), held_shape[1:], 0, 0, (0, 0))]
        table = jnp.zeros((1,), jnp.int32)
    lead_w, gain_all, bias_all, qkv_b, fc1_b = split_small(small_all)
    fc1_b_f = (
        fc1_b.astype(jnp.float32).reshape(D // rows, rows, 4).transpose(0, 2, 1).reshape(FF)
    )
    gain_f = gain_all.astype(jnp.float32)
    bias_f = bias_all.astype(jnp.float32)
    qkv_b_f = qkv_b.astype(jnp.float32)
    full_offset = jnp.concatenate([qkv_b_f[:, 0], jnp.zeros_like(qkv_b_f[:, 0]), qkv_b_f[:, 1]])
    guesses = jnp.transpose(member_guesses[0], (1, 0, 2))
    adjoint = adjoint_of_mixture[0]
    frame = tile_embeddings[0].astype(jnp.float32)
    horizon_indicator = (horizon_indices[0] == lax.iota(jnp.int32, LEADS)).astype(jnp.float32)
    frame_count = jnp.sum(horizon_indicator * horizon_tallies.astype(jnp.float32))
    regularizer_strength = 1.0 / (frame_count * (LEADS * TILE_COUNT * TILE_SAMPLES))
    lead_vector = jnp.sum(lead_w.astype(jnp.float32) * horizon_indicator[None, :], axis=1)
    started = frame + lead_vector[None, :]
    normed_f, norm_one_back = jax.vjp(layer_norm, started, gain_f[:, 0], bias_f[:, 0])
    normed = normed_f.astype(jnp.bfloat16)
    joined = (plain_dot(normed, qkv_w) + full_offset).astype(jnp.bfloat16)
    queries = joined[:, :D].reshape(TILE_COUNT, HEADS, HD)
    keys_all = joined[:, D : 2 * D].reshape(TILE_COUNT, HEADS, HD)
    values_all = joined[:, 2 * D :].reshape(TILE_COUNT, HEADS, HD)
    score_scale = HD ** (-0.5)
    scores = (
        jnp.einsum("qhd,khd->hqk", queries, keys_all, preferred_element_type=jnp.float32)
        * score_scale
    )
    row_top = jnp.max(scores, axis=-1, keepdims=True)
    expd = jnp.exp(scores - row_top)
    prob_full = expd / jnp.sum(expd, axis=-1, keepdims=True)
    probs_low = prob_full.astype(jnp.bfloat16)
    attended = (
        jnp.einsum("hqk,khd->qhd", probs_low, values_all, preferred_element_type=jnp.float32)
        .astype(jnp.bfloat16)
        .reshape(TILE_COUNT, D)
    )
    middle = started + plain_dot(attended, proj_w) + bias_f[:, 1]
    normed_two_f, norm_two_back = jax.vjp(layer_norm, middle, gain_f[:, 1], bias_f[:, 2])
    normed_two = normed_two_f.astype(jnp.bfloat16)
    pre_act = plain_dot(normed_two, fc1_w) + fc1_b_f
    hidden_f, gelu_back = jax.vjp(exact_gelu, pre_act)
    hidden = hidden_f.astype(jnp.bfloat16)
    final_sum = middle + plain_dot(hidden, fc2_w) + bias_f[:, 3]
    final_low = final_sum.astype(jnp.bfloat16)

    combined, d_logits, d_final, entropy = head_pass(
        regularizer_strength.reshape(1), table, final_low, head_sources, head_moves, held_shape, guesses, adjoint
    )
    combined_result = combined[None]
    contribution = jnp.sum(entropy) * regularizer_strength

    if paired:
        sent = lax.dynamic_index_in_dim(d_logits, 1 - net.core, 0, keepdims=False)
        d_logits_other = sibling(sent)
        final_other = sibling(final_low)
        grad_head = head_grad(
            net.core.reshape(1), net.chips, final_low, final_other, d_logits, d_logits_other
        )
        normed_pair, attended_pair, normed_two_pair, hidden_pair = (
            net.with_sibling(v) for v in (normed, attended, normed_two, hidden)
        )

    d_branch = d_final.astype(jnp.bfloat16)
    grad_fc2_bias = jnp.sum(d_branch.astype(jnp.float32), axis=0)
    d_hidden = times_transpose(d_branch, fc2_w)
    d_pre = gelu_back(d_hidden)[0].astype(jnp.bfloat16)
    if paired:
        d_pre, grad_head = lax.optimization_barrier((d_pre, grad_head))
    grad_fc1_bias = jnp.sum(d_pre.astype(jnp.float32), axis=0)
    d_normed_two = times_transpose(d_pre, fc1_w)
    d_mid_part, grad_gain_two, grad_shift_two = norm_two_back(d_normed_two)
    d_middle = d_final + d_mid_part
    d_attn = d_middle.astype(jnp.bfloat16)
    grad_proj_bias = jnp.sum(d_attn.astype(jnp.float32), axis=0)
    d_attended = times_transpose(d_attn, proj_w).astype(jnp.bfloat16).reshape(TILE_COUNT, HEADS, HD)
    d_values = jnp.einsum("hqk,qhd->khd", probs_low, d_attended, preferred_element_type=jnp.float32)
    d_prob = jnp.einsum("qhd,khd->hqk", d_attended, values_all, preferred_element_type=jnp.float32)
    d_score = (
        prob_full * (d_prob - jnp.sum(prob_full * d_prob, axis=-1, keepdims=True))
    ).astype(jnp.bfloat16)
    d_queries = (
        jnp.einsum("hqk,khd->qhd", d_score, keys_all, preferred_element_type=jnp.float32)
        * score_scale
    )
    d_keys = (
        jnp.einsum("hqk,qhd->khd", d_score, queries, preferred_element_type=jnp.float32)
        * score_scale
    )
    d_joined = jnp.concatenate(
        [v.reshape(TILE_COUNT, D) for v in (d_queries, d_keys, d_values)], axis=1
    ).astype(jnp.bfloat16)
    joined_sums = jnp.sum(d_joined.astype(jnp.float32), axis=0)
    d_normed = times_transpose(d_joined, qkv_w)
    d_start_part, grad_gain_one, grad_shift_one = norm_one_back(d_normed)
    d_started = d_middle + d_start_part
    grad_tokens = d_started.astype(jnp.bfloat16)[None]

    columns = jnp.stack(
        [
            grad_gain_one,
            grad_gain_two,
            grad_shift_one,
            grad_proj_bias,
            grad_shift_two,
            grad_fc2_bias,
            joined_sums[:D],
            joined_sums[2 * D :],
        ],
        axis=1,
    )
    hidden_columns = (
        grad_fc1_bias.reshape(D // rows, 4, rows).transpose(0, 2, 1).reshape(D, 4)
    )
    small_grad = jnp.concatenate(
        [
            jnp.sum(d_started, axis=0)[:, None] * horizon_indicator[None, :],
            columns,
            hidden_columns,
            jnp.broadcast_to(digits_of(contribution)[None, :], (D, DIGITS)),
            jnp.zeros((D, LANES - LEADS - 12 - DIGITS), jnp.float32),
        ],
        axis=1,
    ).astype(jnp.bfloat16)

    if paired:
        head_total = scatter_sum(lambda i: grad_head[i], HEAD_BACK_SHARE)

        def low_or_high(value, core):
            return value[core * rows : (core + 1) * rows]

        low, high = net.finish(head_total, low_or_high)
        low, high = (v.reshape(rows, MODEL_COUNT, HALF) for v in (low, high))
        out_head = jnp.concatenate([low, high[:, :, : TILE_SAMPLES - HALF]], axis=2).reshape(
            rows, MODEL_COUNT * TILE_SAMPLES
        )

        fc2_half = net.paired_grad(hidden_pair, d_branch).reshape(16, 8 * rows, D // 2)
        fc1_half = net.paired_grad(normed_two_pair, d_pre).reshape(16, 2 * rows, FF // 2)

        def second_block(i):
            one = net.block(fc1_half, i)
            two = net.block(fc2_half, i)
            wide = D // 2
            return jnp.concatenate(
                [two] + [one[:, k * wide : (k + 1) * wide] for k in range(4)], axis=0
            )

        total = scatter_sum(second_block, D // 2)

        def fc2_rows(value, core):
            return value[core * 4 * rows : (core + 1) * 4 * rows]

        def fc1_rows(value, core):
            begin = 8 * rows + core * rows
            return jnp.concatenate(
                [value[begin + 2 * k * rows : begin + (2 * k + 1) * rows] for k in range(4)], axis=1
            )

        out_fc2 = jnp.concatenate(net.finish(total, fc2_rows), axis=1)
        out_fc1 = jnp.concatenate(net.finish(total, fc1_rows), axis=1)

        qkv_half = net.paired_grad(normed_pair, d_joined).reshape(16, 2 * rows, 3 * D // 2)
        proj_half = net.paired_grad(attended_pair, d_attn).reshape(16, 2 * rows, D // 2)
        small_pair = add_low(small_grad, sibling(small_grad)).reshape(16, 2 * rows, LANES)

        def first_block(i):
            return jnp.concatenate(
                [
                    net.block(v, i)
                    for v in (qkv_half, proj_half, small_pair)
                ],
                axis=1,
            )

        total = scatter_sum(first_block, 2 * D + LANES)
        out_small = jnp.where(net.core == 0, total[:rows, 2 * D :], total[rows:, 2 * D :])
        low, high = net.finish(total[:, : 2 * D], low_or_high)
        n = 3 * D // 2
        out_qkv = jnp.concatenate([low[:, :n], high[:, :n]], axis=1)
        out_proj = jnp.concatenate([low[:, n:], high[:, n:]], axis=1)
    else:

        def summed(value):
            return lax.psum_scatter(
                value.astype(jnp.bfloat16), AXES, scatter_dimension=0, tiled=True
            ).astype(jnp.float32)

        flat = d_logits.transpose(2, 1, 0, 3).reshape(TILE_COUNT, MODEL_COUNT * PADDED)
        out_head = summed(transpose_times(final_low, flat))
        out_head = out_head.reshape(rows, MODEL_COUNT, PADDED)[:, :, :TILE_SAMPLES]
        out_head = out_head.reshape(rows, MODEL_COUNT * TILE_SAMPLES)
        out_fc2 = summed(transpose_times(hidden, d_branch))
        out_fc1 = summed(transpose_times(normed_two, d_pre))
        out_qkv = summed(transpose_times(normed, d_joined))
        out_proj = summed(transpose_times(attended, d_attn))
        out_small = summed(small_grad)
        cost = lax.psum(contribution, AXES)

    out_lead = out_small[:, :LEADS]
    out_gains = out_small[:, LEADS : LEADS + 2]
    out_biases = out_small[:, LEADS + 2 : LEADS + 6]
    out_qkv_bias = out_small[:, LEADS + 6 : LEADS + 8]
    out_fc1_bias = out_small[:, LEADS + 8 : LEADS + 12].T.reshape(4 * rows)
    if paired:
        cost = value_of(out_small[0, LEADS + 12 : LEADS + 12 + DIGITS])
    return (
        combined_result,
        cost,
        grad_tokens,
        out_qkv,
        out_proj,
        out_fc1,
        out_fc2,
        out_head,
        out_lead,
        out_gains,
        out_biases,
        out_qkv_bias,
        out_fc1_bias,
    )


def solution(mesh):
    split = P(AXES)
    paired = mesh.shape["dp"] == 2 and mesh.shape["fsdp"] == 16
    return jax.shard_map(
        functools.partial(on_device, paired=paired),
        mesh=mesh,
        in_specs=(split, split, P()) + (split,) * 12,
        out_specs=(split, P()) + (split,) * 11,
        check_vma=False,
    )
```

```python
import functools

import jax
import jax.numpy as jnp
from jax import lax
from jax.experimental import pallas as pl
from jax.experimental.pallas import tpu as pltpu
from jax.sharding import PartitionSpec as P

D = 768
HEADS = 12
HD = 64
FF = 3072
MODEL_COUNT = 3
TILE_SAMPLES = 4416
LEADS = 40
TILE_COUNT = 256
EPS = 1e-06
LANES = 128
HALF = 2304
PADDED = 2 * HALF
VMEM = 56 * 1024 * 1024

AXES = ("dp", "fsdp")
RING = [(z, 0) for z in range(4)] + [(z, 1) for z in (3, 2, 1, 0)]


def ring_pairs(step):
    pairs = []
    for spot, (z, x) in enumerate(RING):
        to_z, to_x = RING[(spot + step) % 8]
        for core in range(2):
            pairs.append((z * 4 + x * 2 + core, to_z * 4 + to_x * 2 + core))
    return pairs


def forth(value):
    return lax.ppermute(value, "fsdp", ring_pairs(1))


def back(value):
    return lax.ppermute(value, "fsdp", ring_pairs(-1))


def across(value):
    return lax.ppermute(value, "dp", [(0, 1), (1, 0)])


def sibling(value):
    return lax.ppermute(value, "fsdp", [(i, i ^ 1) for i in range(16)])


def places():
    y = lax.axis_index("dp")
    f = lax.axis_index("fsdp")
    z, x, core = f // 4, (f // 2) % 2, f % 2
    spot = jnp.where(x == 0, z, 7 - z)
    i = lax.iota(jnp.int32, 32)
    seat = (spot + (i // 2) % 8) % 8
    pair = jnp.where(seat < 4, seat * 2, (7 - seat) * 2 + 1)
    return ((y + i // 16) % 2) * 16 + pair * 2 + (core + i) % 2


def slot(other_row, distance, other_core):
    return other_row * 16 + (distance % 8) * 2 + other_core


def ring_run(first, right, left):
    rights, lefts = [first], [first]
    for k in range(max(right, left)):
        if k < right:
            rights.append(forth(rights[-1]))
        if k < left:
            lefts.append(back(lefts[-1]))
    return rights, lefts


def gather_round_first(own, longer):
    r = own.shape[0]
    right, left = (4, 3) if longer > 0 else (3, 4)
    rights, lefts = ring_run(own, right, left)
    last = rights[4] if longer > 0 else lefts[4]
    batches = [
        (jnp.concatenate([own, rights[1], lefts[1], rights[2], lefts[2]], axis=0), (0, -1, 1, -2, 2)),
        (jnp.concatenate([rights[3], lefts[3], last], axis=0), (-3, 3, 4)),
    ]
    found = []
    for batch, distances in batches:
        for other_row, array in ((0, batch), (1, across(batch))):
            for other_core, source in ((0, array), (1, sibling(array))):
                for i, k in enumerate(distances):
                    found.append((source, (i * r, (i + 1) * r), slot(other_row, k, other_core)))
    return found


def gather_across_first(own):
    r = own.shape[0]
    first = jnp.concatenate([own, across(own)], axis=0)
    rights, lefts = ring_run(first, 3, 3)
    held = [(first, 0)]
    for k in range(1, 4):
        held += [(rights[k], -k), (lefts[k], k)]
    found = []
    for array, k in held:
        for other_core, source in ((0, array), (1, sibling(array))):
            for other_row in (0, 1):
                rows = (other_row * r, (other_row + 1) * r)
                found.append((source, rows, slot(other_row, k, other_core)))
    for other_row, array in ((0, forth(rights[3][:r])), (1, back(lefts[3][r:]))):
        for other_core, source in ((0, array), (1, sibling(array))):
            found.append((source, (0, r), slot(other_row, 4, other_core)))
    return found


def plan_moves(found, fields):
    sources, moves = [], []
    for source, rows, where in found:
        at = [i for i, s in enumerate(sources) if s is source]
        if not at:
            at = [len(sources)]
            sources.append(source)
        for (f0, f1), (g0, g1), out, out_row, out_col in fields:
            moves.append(
                (at[0], (rows[0] + f0, g0), (f1 - f0, g1 - g0), where, out, (out_row, out_col))
            )
    return sources, moves


def place(found, fields, shapes, table, shards):
    sources, moves = plan_moves(found, fields)

    def body(table_ref, *refs):
        ins, outs = refs[: len(sources)], refs[len(sources) : len(sources) + len(shapes)]
        held, sems, out_sems = refs[len(sources) + len(shapes) : -2], refs[-2], refs[-1]
        run_moves(moves, table_ref, ins, held, sems)
        copies = [
            pltpu.make_async_copy(held[i], outs[i], out_sems.at[i]) for i in range(len(shapes))
        ]
        for copy in copies:
            copy.start()
        for copy in copies:
            copy.wait()

    whole = [(shards,) + s for s in shapes]
    return pl.pallas_call(
        body,
        grid_spec=pltpu.PrefetchScalarGridSpec(
            num_scalar_prefetch=1,
            grid=(1,),
            in_specs=[pl.BlockSpec(memory_space=pl.ANY)] * len(sources),
            out_specs=[pl.BlockSpec(memory_space=pl.ANY)] * len(shapes),
            scratch_shapes=[pltpu.VMEM(s, jnp.bfloat16) for s in whole]
            + [
                pltpu.SemaphoreType.DMA((len(moves),)),
                pltpu.SemaphoreType.DMA((len(shapes),)),
            ],
        ),
        out_shape=[jax.ShapeDtypeStruct(s, jnp.bfloat16) for s in whole],
        compiler_params=pltpu.CompilerParams(vmem_limit_bytes=VMEM),
        name="place",
    )(table, *sources)


def run_moves(moves, table_ref, ins, outs, sems):
    copies = []
    for i, (at, (sr, sc), (nr, nc), where, out, (dr, dc)) in enumerate(moves):
        copy = pltpu.make_async_copy(
            ins[at].at[pl.ds(sr, nr), pl.ds(sc, nc)],
            outs[out].at[table_ref[where], pl.ds(dr, nr), pl.ds(dc, nc)],
            sems.at[i],
        )
        copy.start()
        copies.append(copy)
    for copy in copies:
        copy.wait()


def add_low(*values):
    total = values[0].astype(jnp.float32)
    for value in values[1:]:
        total = total + value.astype(jnp.float32)
    return total.astype(jnp.bfloat16)


ORDER_FIRST = (4, 3, -3)
ORDER_LAST = (2, -2, 1, -1, 0)


def sum_across_first(near, far, longer):
    met = [across(v) for v in far]
    ready = {}
    for part, order in enumerate((ORDER_FIRST, ORDER_LAST)):
        for i, k in enumerate(order):
            ready[k] = (near[part][i], met[part][i])
    go = {1: None, -1: None}
    for k in (4, 3, 2, 1):
        for way in (1, -1):
            if k == 4 and way != longer:
                continue
            mine = ready[4] if k == 4 else ready[way * k]
            value = add_low(*mine) if go[way] is None else add_low(*mine, go[way])
            go[way] = forth(value) if way > 0 else back(value)
    return sum(v.astype(jnp.float32) for v in ready[0] + (go[1], go[-1]))


def sum_round_first(blocks, far_near, far_far):
    r = far_near.shape[0]
    right, left = forth(far_near), back(far_far)
    go_right = jnp.concatenate([add_low(blocks[3][:r], right), blocks[3][r:]], axis=0)
    go_left = jnp.concatenate([blocks[-3][:r], add_low(blocks[-3][r:], left)], axis=0)
    for k in (2, 1):
        right, left = forth(go_right), back(go_left)
        go_right, go_left = add_low(blocks[k], right), add_low(blocks[-k], left)
    right, left = forth(go_right), back(go_left)
    sent = add_low(blocks[0][r:], right[r:], left[r:])
    met = across(sent)
    return sum(v.astype(jnp.float32) for v in (blocks[0][:r], right[:r], left[:r], met))


def layer_norm(values, norm_gain, norm_shift):
    row_mean = jnp.mean(values, axis=-1, keepdims=True)
    centred = values - row_mean
    row_var = jnp.mean(centred * centred, axis=-1, keepdims=True)
    return centred * lax.rsqrt(row_var + EPS) * norm_gain + norm_shift


def exact_gelu(values):
    return jax.nn.gelu(values, approximate=False)


def plain_dot(left, right):
    return jnp.dot(left, right, preferred_element_type=jnp.float32)


def times_transpose(left, right):
    return lax.dot_general(
        left, right, (((1,), (1,)), ((), ())), preferred_element_type=jnp.float32
    )


def transpose_times(left, right):
    return lax.dot_general(
        left, right, (((0,), (0,)), ((), ())), preferred_element_type=jnp.float32
    )


HEAD_TILE = 768
ROWS = 16
COLS = 384


def head_body(moves, weight_ref, table_ref, x_ref, guess_ref, adj_ref, *refs):
    ins, refs = refs[:-7], refs[-7:]
    comb_ref, dl_ref, df_ref, ent_ref, logit_ref, held_ref, sems = refs
    j = pl.program_id(0)
    strength = weight_ref[0]
    spot = pixel_tile(j, table_ref)

    @pl.when(j == 0)
    def _():
        df_ref[...] = jnp.zeros_like(df_ref)
        ent_ref[...] = jnp.zeros_like(ent_ref)
        run_moves(moves, table_ref, ins, [held_ref], sems)

    x = x_ref[...]

    def weight(e):
        begin = pl.multiple_of(e * PADDED + spot * HEAD_TILE, LANES)
        return held_ref[:, :, pl.ds(begin, HEAD_TILE)].reshape(D, HEAD_TILE)

    for e in range(MODEL_COUNT):
        logit_ref[e] = jnp.dot(x, weight(e), preferred_element_type=jnp.float32)

    for part in range(HEAD_TILE // COLS):
        cols = pl.ds(part * COLS, COLS)
        pixel = spot * HEAD_TILE + part * COLS + lax.broadcasted_iota(jnp.int32, (ROWS, COLS), 1)
        real = pixel < TILE_SAMPLES

        def chunk(i, total):
            rows = pl.ds(pl.multiple_of(i * ROWS, ROWS), ROWS)
            l0, l1, l2 = (logit_ref[e, rows, cols] for e in range(3))
            top = jnp.maximum(jnp.maximum(l0, l1), l2)
            l0, l1, l2 = l0 - top, l1 - top, l2 - top
            e0, e1, e2 = jnp.exp(l0), jnp.exp(l1), jnp.exp(l2)
            norm = e0 + e1 + e2
            inverse = 1.0 / norm
            log_norm = jnp.log(norm)
            b0, b1, b2 = e0 * inverse, e1 * inverse, e2 * inverse
            l0, l1, l2 = l0 - log_norm, l1 - log_norm, l2 - log_norm
            minus_h = b0 * l0 + b1 * l1 + b2 * l2
            g0, g1, g2 = (guess_ref[e, rows, cols].astype(jnp.float32) for e in range(3))
            mixed = b0 * g0 + b1 * g1 + b2 * g2
            comb_ref[rows, cols] = mixed.astype(jnp.bfloat16)
            adj = adj_ref[rows, cols].astype(jnp.float32)
            for e, (b, l, g) in enumerate(((b0, l0, g0), (b1, l1, g1), (b2, l2, g2))):
                d = b * (adj * (g - mixed) - strength * (l - minus_h))
                dl_ref[0, e, rows, cols] = jnp.where(real, d, 0.0).astype(jnp.bfloat16)
            return total - jnp.where(real, minus_h, 0.0)

        total = lax.fori_loop(
            0, TILE_COUNT // ROWS, chunk, jnp.zeros((ROWS, COLS), jnp.float32)
        )
        gathered = total[:, :LANES]
        for k in range(1, COLS // LANES):
            gathered = gathered + total[:, k * LANES : (k + 1) * LANES]
        ent_ref[...] += gathered[:8] + gathered[8:]

    part = None
    for e in range(MODEL_COUNT):
        piece = lax.dot_general(
            dl_ref[0, e], weight(e), (((1,), (1,)), ((), ())), preferred_element_type=jnp.float32
        )
        part = piece if part is None else part + piece
    df_ref[...] += part


HEAD_STEPS = PADDED // HEAD_TILE


def pixel_tile(j, table_ref):
    half = HEAD_STEPS // 2
    core = table_ref[table_ref.shape[0] - 1]
    return jnp.where(j < half, (1 - core) * half + j, core * half + j - half)


def head_pass(strength, table, final_low, sources, moves, held_shape, guesses, adjoint):
    steps = HEAD_STEPS
    tile = HEAD_TILE
    return pl.pallas_call(
        functools.partial(head_body, moves),
        grid_spec=pltpu.PrefetchScalarGridSpec(
            num_scalar_prefetch=2,
            grid=(steps,),
            in_specs=[
                pl.BlockSpec((TILE_COUNT, D), lambda j, s, t: (0, 0)),
                pl.BlockSpec((MODEL_COUNT, TILE_COUNT, tile), lambda j, s, t: (0, 0, pixel_tile(j, t))),
                pl.BlockSpec((TILE_COUNT, tile), lambda j, s, t: (0, pixel_tile(j, t))),
            ]
            + [pl.BlockSpec(memory_space=pl.ANY)] * len(sources),
            out_specs=[
                pl.BlockSpec((TILE_COUNT, tile), lambda j, s, t: (0, pixel_tile(j, t))),
                pl.BlockSpec(
                    (1, MODEL_COUNT, TILE_COUNT, tile),
                    lambda j, s, t: (j // (steps // 2), 0, 0, j % (steps // 2)),
                ),
                pl.BlockSpec((TILE_COUNT, D), lambda j, s, t: (0, 0)),
                pl.BlockSpec((8, LANES), lambda j, s, t: (0, 0)),
            ],
            scratch_shapes=[
                pltpu.VMEM((MODEL_COUNT, TILE_COUNT, tile), jnp.float32),
                pltpu.VMEM(held_shape, jnp.bfloat16),
                pltpu.SemaphoreType.DMA((len(moves),)),
            ],
        ),
        out_shape=[
            jax.ShapeDtypeStruct((TILE_COUNT, TILE_SAMPLES), jnp.bfloat16),
            jax.ShapeDtypeStruct((2, MODEL_COUNT, TILE_COUNT, HALF), jnp.bfloat16),
            jax.ShapeDtypeStruct((TILE_COUNT, D), jnp.float32),
            jax.ShapeDtypeStruct((8, LANES), jnp.float32),
        ],
        compiler_params=pltpu.CompilerParams(
            dimension_semantics=("arbitrary",), vmem_limit_bytes=VMEM
        ),
        name="head_pass",
    )(strength, table, final_low, guesses, adjoint, *sources)


def dot_tokens(left, right):
    return lax.dot_general(left, right, (((0,), (0,)), ((), ())), preferred_element_type=jnp.float32)


def chip_at(marks_ref, other_row, distance):
    return marks_ref[1 + other_row * 8 + distance % 8]


HEAD_ORDER = (0, 1, -1, 2, -2, 3, -3)


def head_grad_body(marks_ref, x_mine_ref, x_other_ref, d_mine_ref, d_other_ref, *refs):
    outs, near_ref, far_ref, sum_ref = refs[:7], refs[7], refs[8], refs[9]
    value = dot_tokens(x_mine_ref[...], d_mine_ref[0, 0]) + dot_tokens(x_other_ref[...], d_other_ref[0])
    sum_ref[...] = value.reshape(sum_ref.shape)
    r = sum_ref.shape[1]
    for k, out in zip(HEAD_ORDER, outs):
        for other_row in (0, 1):
            block = sum_ref[chip_at(marks_ref, other_row, k)].astype(jnp.bfloat16)
            out[other_row * r : (other_row + 1) * r, :] = block
    near_ref[...] = sum_ref[chip_at(marks_ref, 0, 4)].astype(jnp.bfloat16)
    far_ref[...] = sum_ref[chip_at(marks_ref, 1, 4)].astype(jnp.bfloat16)


def head_grad(marks, x_mine, x_other, d_both, d_other):
    tile = 768
    steps = HALF // tile
    r = D // 16
    n = MODEL_COUNT * HALF
    tall = [2 * r] * 7 + [r] * 2
    outs = pl.pallas_call(
        head_grad_body,
        grid_spec=pltpu.PrefetchScalarGridSpec(
            num_scalar_prefetch=1,
            grid=(MODEL_COUNT, steps),
            in_specs=[
                pl.BlockSpec((TILE_COUNT, D), lambda e, j, c: (0, 0)),
                pl.BlockSpec((TILE_COUNT, D), lambda e, j, c: (0, 0)),
                pl.BlockSpec((1, 1, TILE_COUNT, tile), lambda e, j, c: (1, e, 0, j)),
                pl.BlockSpec((1, TILE_COUNT, tile), lambda e, j, c: (e, 0, j)),
            ],
            out_specs=[pl.BlockSpec((h, tile), lambda e, j, c: (0, e * steps + j)) for h in tall],
            scratch_shapes=[pltpu.VMEM((16, r, tile), jnp.float32)],
        ),
        out_shape=[jax.ShapeDtypeStruct((h, n), jnp.bfloat16) for h in tall],
        compiler_params=pltpu.CompilerParams(
            dimension_semantics=("arbitrary", "arbitrary"), vmem_limit_bytes=VMEM
        ),
        name="head_grad",
    )(marks, x_mine, x_other, d_both, d_other)
    return dict(zip(HEAD_ORDER, outs[:7])), outs[7], outs[8]


def ring_rows(marks_ref, outs, write):
    for other_row in (0, 1):
        for part, order in enumerate((ORDER_FIRST, ORDER_LAST)):
            for i, k in enumerate(order):
                write(outs[2 * other_row + part], i, chip_at(marks_ref, other_row, k))


def core_half(ref, marks_ref):
    n = ref.shape[1] // 2
    return ref[:, pl.ds(pl.multiple_of(marks_ref[0] * n, LANES), n)]


def paired_product(marks_ref, x, x_other, d, d_other):
    return dot_tokens(x[...], core_half(d, marks_ref)) + dot_tokens(
        x_other[...], core_half(d_other, marks_ref)
    )


def second_grad_body(marks_ref, *refs):
    ins, outs, (fc2_ref, fc1_ref) = refs[:8], refs[8:12], refs[12:]
    fc2_ref[...] = paired_product(marks_ref, *ins[:4]).reshape(fc2_ref.shape)
    fc1_ref[...] = paired_product(marks_ref, *ins[4:]).reshape(fc1_ref.shape)
    r4, wide = fc2_ref.shape[1:]
    r = fc1_ref.shape[1]

    def write(out, i, chip):
        out[i, :r4, :] = fc2_ref[chip].astype(jnp.bfloat16)
        for k in range(4):
            block = fc1_ref[chip, :, k * wide : (k + 1) * wide].astype(jnp.bfloat16)
            out[i, r4 + k * r : r4 + (k + 1) * r, :] = block

    ring_rows(marks_ref, outs, write)


def first_grad_body(marks_ref, *refs):
    ins, outs, (qkv_ref, proj_ref, small_ref) = refs[:10], refs[10:14], refs[14:]
    qkv_ref[...] = paired_product(marks_ref, *ins[:4]).reshape(qkv_ref.shape)
    proj_ref[...] = paired_product(marks_ref, *ins[4:8]).reshape(proj_ref.shape)
    small = ins[8][...].astype(jnp.float32) + ins[9][...].astype(jnp.float32)
    small_ref[...] = small.reshape(small_ref.shape)
    n, m = qkv_ref.shape[2], qkv_ref.shape[2] + proj_ref.shape[2]

    def write(out, i, chip):
        out[i, :, :n] = qkv_ref[chip].astype(jnp.bfloat16)
        out[i, :, n:m] = proj_ref[chip].astype(jnp.bfloat16)
        out[i, :, m:] = small_ref[chip].astype(jnp.bfloat16)

    ring_rows(marks_ref, outs, write)


def ring_grad(body, marks, ins, block, scratch, name):
    shapes = [(3,) + block, (5,) + block] * 2
    outs = pl.pallas_call(
        body,
        grid_spec=pltpu.PrefetchScalarGridSpec(
            num_scalar_prefetch=1,
            grid=(1,),
            in_specs=[pl.BlockSpec(v.shape, lambda i, m: (0, 0)) for v in ins],
            out_specs=[pl.BlockSpec(s, lambda i, m: (0, 0, 0)) for s in shapes],
            scratch_shapes=[pltpu.VMEM(s, jnp.float32) for s in scratch],
        ),
        out_shape=[jax.ShapeDtypeStruct(s, jnp.bfloat16) for s in shapes],
        compiler_params=pltpu.CompilerParams(vmem_limit_bytes=VMEM),
        name=name,
    )(marks, *ins)
    return outs[:2], outs[2:]


def pack_small(lead_w, gains, biases, qkv_b, fc1_b, rows):
    value = jnp.concatenate([lead_w, gains, biases, qkv_b, fc1_b.reshape(4, rows).T], axis=1)
    return jnp.pad(value, ((0, 0), (0, LANES - value.shape[1])))


def split_small(small):
    at, found = 0, []
    for width in (LEADS, 2, 4, 2, 4):
        found.append(small[:, at : at + width])
        at += width
    return found


def pad_experts(value):
    value = value.reshape(value.shape[0], MODEL_COUNT, TILE_SAMPLES)
    value = jnp.pad(value, ((0, 0), (0, 0), (0, PADDED - TILE_SAMPLES)))
    return value.reshape(value.shape[0], MODEL_COUNT * PADDED)


DIGITS = 16
BASE = 8.0


def digits_of(value):
    powers = jnp.asarray([BASE**k for k in range(DIGITS + 1)], jnp.float32)
    floors = jnp.floor(value * 32.0 * powers)
    return floors[1:] - BASE * floors[:-1]


def value_of(digits):
    powers = jnp.asarray([BASE ** -(k + 1) / 32.0 for k in range(DIGITS)], jnp.float32)
    return jnp.sum(digits * powers)


class Paired:
    def __init__(self):
        self.table = places()
        self.core = lax.axis_index("fsdp") % 2
        self.chips = self.table[::2] // 2
        self.marks = jnp.concatenate([self.core.reshape(1), self.chips])

    def gather_first(self, qkv, proj, small):
        r = qkv.shape[0]
        found = gather_round_first(jnp.concatenate([qkv, proj, small], axis=1), 1)
        n = 3 * D
        fields = [
            ((0, r), (0, n), 0, 0, 0),
            ((0, r), (n, n + D), 1, 0, 0),
            ((0, r), (n + D, n + D + LANES), 2, 0, 0),
        ]
        qkv, proj, small = place(found, fields, [(r, n), (r, D), (r, LANES)], self.table, 32)
        return qkv.reshape(D, n), proj.reshape(D, D), small.reshape(D, LANES)

    def gather_second(self, fc1, fc2):
        r = fc1.shape[0]
        own = jnp.concatenate([fc2] + [fc1[:, k * D : (k + 1) * D] for k in range(4)], axis=0)
        found = gather_round_first(own, -1)
        fields = [((0, 4 * r), (0, D), 1, 0, 0)]
        for k in range(4):
            fields.append((((4 + k) * r, (5 + k) * r), (0, D), 0, 0, k * D))
        fc1, fc2 = place(found, fields, [(r, FF), (4 * r, D)], self.table, 32)
        return fc1.reshape(D, FF), fc2.reshape(FF, D)

    def gather_head(self, head):
        own = pad_experts(head)
        return plan_moves(gather_across_first(own), [((0, own.shape[0]), (0, own.shape[1]), 0, 0, 0)])

    def finish(self, total, rows):
        own = jnp.where(self.core == 0, rows(total, 0), rows(total, 1))
        other = jnp.where(self.core == 0, rows(total, 1), rows(total, 0))
        met = sibling(other.astype(jnp.bfloat16)).astype(jnp.float32)
        first = self.core == 0
        return jnp.where(first, own, met), jnp.where(first, met, own)


def on_device(
    tile_embeddings,
    horizon_indices,
    horizon_tallies,
    member_guesses,
    adjoint_of_mixture,
    triple_projection_matrix,
    attention_outward_matrix,
    widening_matrix,
    narrowing_matrix,
    gating_matrix,
    horizon_embedding_matrix,
    normalization_scales,
    channel_offsets,
    triple_projection_offset,
    hidden_offset,
    *,
    paired,
):
    rows = triple_projection_matrix.shape[0]
    small = pack_small(
        horizon_embedding_matrix,
        normalization_scales,
        channel_offsets,
        triple_projection_offset,
        hidden_offset,
        rows,
    )
    if paired:
        net = Paired()
        qkv_w, proj_w, small_all = net.gather_first(
            triple_projection_matrix, attention_outward_matrix, small
        )
        fc1_w, fc2_w = net.gather_second(widening_matrix, narrowing_matrix)
        head_sources, head_moves = net.gather_head(gating_matrix)
        table = jnp.concatenate([net.table, net.core.reshape(1)])
        held_shape = (32, rows, MODEL_COUNT * PADDED)
    else:
        whole = functools.partial(lax.all_gather, axis_name=AXES, axis=0, tiled=True)
        qkv_w = whole(triple_projection_matrix)
        proj_w = whole(attention_outward_matrix)
        fc1_w = whole(widening_matrix)
        fc2_w = whole(narrowing_matrix)
        small_all = whole(small)
        head_sources = [whole(pad_experts(gating_matrix))]
        held_shape = (1, D, MODEL_COUNT * PADDED)
        head_moves = [(0, (0, 0), held_shape[1:], 0, 0, (0, 0))]
        table = jnp.asarray([0, 1], jnp.int32)
    lead_w, gain_all, bias_all, qkv_b, fc1_b = split_small(small_all)
    fc1_b_f = (
        fc1_b.astype(jnp.float32).reshape(D // rows, rows, 4).transpose(0, 2, 1).reshape(FF)
    )
    gain_f = gain_all.astype(jnp.float32)
    bias_f = bias_all.astype(jnp.float32)
    qkv_b_f = qkv_b.astype(jnp.float32)
    full_offset = jnp.concatenate([qkv_b_f[:, 0], jnp.zeros_like(qkv_b_f[:, 0]), qkv_b_f[:, 1]])
    guesses = jnp.transpose(member_guesses[0], (1, 0, 2))
    adjoint = adjoint_of_mixture[0]
    frame = tile_embeddings[0].astype(jnp.float32)
    horizon_indicator = (horizon_indices[0] == lax.iota(jnp.int32, LEADS)).astype(jnp.float32)
    frame_count = jnp.sum(horizon_indicator * horizon_tallies.astype(jnp.float32))
    regularizer_strength = 1.0 / (frame_count * (LEADS * TILE_COUNT * TILE_SAMPLES))
    lead_vector = jnp.sum(lead_w.astype(jnp.float32) * horizon_indicator[None, :], axis=1)
    started = frame + lead_vector[None, :]
    normed_f, norm_one_back = jax.vjp(layer_norm, started, gain_f[:, 0], bias_f[:, 0])
    normed = normed_f.astype(jnp.bfloat16)
    joined = (plain_dot(normed, qkv_w) + full_offset).astype(jnp.bfloat16)
    queries = joined[:, :D].reshape(TILE_COUNT, HEADS, HD)
    keys_all = joined[:, D : 2 * D].reshape(TILE_COUNT, HEADS, HD)
    values_all = joined[:, 2 * D :].reshape(TILE_COUNT, HEADS, HD)
    score_scale = HD ** (-0.5)
    scores = (
        jnp.einsum("qhd,khd->hqk", queries, keys_all, preferred_element_type=jnp.float32)
        * score_scale
    )
    row_top = jnp.max(scores, axis=-1, keepdims=True)
    expd = jnp.exp(scores - row_top)
    prob_full = expd / jnp.sum(expd, axis=-1, keepdims=True)
    probs_low = prob_full.astype(jnp.bfloat16)
    attended = (
        jnp.einsum("hqk,khd->qhd", probs_low, values_all, preferred_element_type=jnp.float32)
        .astype(jnp.bfloat16)
        .reshape(TILE_COUNT, D)
    )
    middle = started + plain_dot(attended, proj_w) + bias_f[:, 1]
    normed_two_f, norm_two_back = jax.vjp(layer_norm, middle, gain_f[:, 1], bias_f[:, 2])
    normed_two = normed_two_f.astype(jnp.bfloat16)
    pre_act = plain_dot(normed_two, fc1_w) + fc1_b_f
    hidden_f, gelu_back = jax.vjp(exact_gelu, pre_act)
    hidden = hidden_f.astype(jnp.bfloat16)
    final_sum = middle + plain_dot(hidden, fc2_w) + bias_f[:, 3]
    final_low = final_sum.astype(jnp.bfloat16)

    combined, d_logits, d_final, entropy = head_pass(
        regularizer_strength.reshape(1), table, final_low, head_sources, head_moves, held_shape, guesses, adjoint
    )
    combined_result = combined[None]
    contribution = jnp.sum(entropy) * regularizer_strength

    if paired:
        d_logits_other = sibling(d_logits[0])
        final_other = sibling(final_low)
        grad_head = head_grad(net.marks, final_low, final_other, d_logits, d_logits_other)
        normed_other, attended_other, normed_two_other, hidden_other = (
            sibling(v) for v in (normed, attended, normed_two, hidden)
        )

    d_branch = d_final.astype(jnp.bfloat16)
    grad_fc2_bias = jnp.sum(d_branch.astype(jnp.float32), axis=0)
    d_hidden = times_transpose(d_branch, fc2_w)
    d_pre = gelu_back(d_hidden)[0].astype(jnp.bfloat16)
    if paired:
        d_pre, grad_head = lax.optimization_barrier((d_pre, grad_head))
    grad_fc1_bias = jnp.sum(d_pre.astype(jnp.float32), axis=0)
    d_normed_two = times_transpose(d_pre, fc1_w)
    d_mid_part, grad_gain_two, grad_shift_two = norm_two_back(d_normed_two)
    d_middle = d_final + d_mid_part
    d_attn = d_middle.astype(jnp.bfloat16)
    grad_proj_bias = jnp.sum(d_attn.astype(jnp.float32), axis=0)
    d_attended = times_transpose(d_attn, proj_w).astype(jnp.bfloat16).reshape(TILE_COUNT, HEADS, HD)
    d_values = jnp.einsum("hqk,qhd->khd", probs_low, d_attended, preferred_element_type=jnp.float32)
    d_prob = jnp.einsum("qhd,khd->hqk", d_attended, values_all, preferred_element_type=jnp.float32)
    d_score = (
        prob_full * (d_prob - jnp.sum(prob_full * d_prob, axis=-1, keepdims=True))
    ).astype(jnp.bfloat16)
    d_queries = (
        jnp.einsum("hqk,khd->qhd", d_score, keys_all, preferred_element_type=jnp.float32)
        * score_scale
    )
    d_keys = (
        jnp.einsum("hqk,qhd->khd", d_score, queries, preferred_element_type=jnp.float32)
        * score_scale
    )
    d_joined = jnp.concatenate(
        [v.reshape(TILE_COUNT, D) for v in (d_queries, d_keys, d_values)], axis=1
    ).astype(jnp.bfloat16)
    joined_sums = jnp.sum(d_joined.astype(jnp.float32), axis=0)
    d_normed = times_transpose(d_joined, qkv_w)
    d_start_part, grad_gain_one, grad_shift_one = norm_one_back(d_normed)
    d_started = d_middle + d_start_part
    grad_tokens = d_started.astype(jnp.bfloat16)[None]

    columns = jnp.stack(
        [
            grad_gain_one,
            grad_gain_two,
            grad_shift_one,
            grad_proj_bias,
            grad_shift_two,
            grad_fc2_bias,
            joined_sums[:D],
            joined_sums[2 * D :],
        ],
        axis=1,
    )
    hidden_columns = (
        grad_fc1_bias.reshape(D // rows, 4, rows).transpose(0, 2, 1).reshape(D, 4)
    )
    small_grad = jnp.concatenate(
        [
            jnp.sum(d_started, axis=0)[:, None] * horizon_indicator[None, :],
            columns,
            hidden_columns,
            jnp.broadcast_to(digits_of(contribution)[None, :], (D, DIGITS)),
            jnp.zeros((D, LANES - LEADS - 12 - DIGITS), jnp.float32),
        ],
        axis=1,
    ).astype(jnp.bfloat16)

    if paired:
        head_total = sum_round_first(*grad_head)

        def low_or_high(value, core):
            return value[core * rows : (core + 1) * rows]

        low, high = net.finish(head_total, low_or_high)
        low, high = (v.reshape(rows, MODEL_COUNT, HALF) for v in (low, high))
        out_head = jnp.concatenate([low, high[:, :, : TILE_SAMPLES - HALF]], axis=2).reshape(
            rows, MODEL_COUNT * TILE_SAMPLES
        )

        near, far = ring_grad(
            second_grad_body,
            net.marks,
            (hidden, hidden_other, d_branch, sibling(d_branch))
            + (normed_two, normed_two_other, d_pre, sibling(d_pre)),
            (16 * rows, D // 2),
            [(16, 8 * rows, D // 2), (16, 2 * rows, FF // 2)],
            "second_grad",
        )
        total = sum_across_first(near, far, 1)

        def fc2_rows(value, core):
            return value[core * 4 * rows : (core + 1) * 4 * rows]

        def fc1_rows(value, core):
            begin = 8 * rows + core * rows
            return jnp.concatenate(
                [value[begin + 2 * k * rows : begin + (2 * k + 1) * rows] for k in range(4)], axis=1
            )

        out_fc2 = jnp.concatenate(net.finish(total, fc2_rows), axis=1)
        out_fc1 = jnp.concatenate(net.finish(total, fc1_rows), axis=1)

        near, far = ring_grad(
            first_grad_body,
            net.marks,
            (normed, normed_other, d_joined, sibling(d_joined))
            + (attended, attended_other, d_attn, sibling(d_attn))
            + (small_grad, sibling(small_grad)),
            (2 * rows, 2 * D + LANES),
            [(16, 2 * rows, 3 * D // 2), (16, 2 * rows, D // 2), (16, 2 * rows, LANES)],
            "first_grad",
        )
        total = sum_across_first(near, far, -1)
        out_small = jnp.where(net.core == 0, total[:rows, 2 * D :], total[rows:, 2 * D :])
        low, high = net.finish(total[:, : 2 * D], low_or_high)
        n = 3 * D // 2
        out_qkv = jnp.concatenate([low[:, :n], high[:, :n]], axis=1)
        out_proj = jnp.concatenate([low[:, n:], high[:, n:]], axis=1)
    else:

        def summed(value):
            return lax.psum_scatter(
                value.astype(jnp.bfloat16), AXES, scatter_dimension=0, tiled=True
            ).astype(jnp.float32)

        flat = d_logits.transpose(2, 1, 0, 3).reshape(TILE_COUNT, MODEL_COUNT * PADDED)
        out_head = summed(transpose_times(final_low, flat))
        out_head = out_head.reshape(rows, MODEL_COUNT, PADDED)[:, :, :TILE_SAMPLES]
        out_head = out_head.reshape(rows, MODEL_COUNT * TILE_SAMPLES)
        out_fc2 = summed(transpose_times(hidden, d_branch))
        out_fc1 = summed(transpose_times(normed_two, d_pre))
        out_qkv = summed(transpose_times(normed, d_joined))
        out_proj = summed(transpose_times(attended, d_attn))
        out_small = summed(small_grad)
        cost = lax.psum(contribution, AXES)

    out_lead = out_small[:, :LEADS]
    out_gains = out_small[:, LEADS : LEADS + 2]
    out_biases = out_small[:, LEADS + 2 : LEADS + 6]
    out_qkv_bias = out_small[:, LEADS + 6 : LEADS + 8]
    out_fc1_bias = out_small[:, LEADS + 8 : LEADS + 12].T.reshape(4 * rows)
    if paired:
        cost = value_of(out_small[0, LEADS + 12 : LEADS + 12 + DIGITS])
    return (
        combined_result,
        cost,
        grad_tokens,
        out_qkv,
        out_proj,
        out_fc1,
        out_fc2,
        out_head,
        out_lead,
        out_gains,
        out_biases,
        out_qkv_bias,
        out_fc1_bias,
    )


def solution(mesh):
    split = P(AXES)
    paired = mesh.shape["dp"] == 2 and mesh.shape["fsdp"] == 16
    return jax.shard_map(
        functools.partial(on_device, paired=paired),
        mesh=mesh,
        in_specs=(split, split, P()) + (split,) * 12,
        out_specs=(split, P()) + (split,) * 11,
        check_vma=False,
    )
```

```python
import functools

import jax
import jax.numpy as jnp
from jax import lax
from jax.experimental import pallas as pl
from jax.experimental.pallas import tpu as pltpu
from jax.sharding import PartitionSpec as P

D = 768
HEADS = 12
HD = 64
FF = 3072
MODEL_COUNT = 3
TILE_SAMPLES = 4416
LEADS = 40
TILE_COUNT = 256
EPS = 1e-06
LANES = 128
HALF = 2304
PADDED = 2 * HALF
VMEM = 56 * 1024 * 1024

AXES = ("dp", "fsdp")
RING = [(z, 0) for z in range(4)] + [(z, 1) for z in (3, 2, 1, 0)]


def ring_pairs(step):
    pairs = []
    for spot, (z, x) in enumerate(RING):
        to_z, to_x = RING[(spot + step) % 8]
        for core in range(2):
            pairs.append((z * 4 + x * 2 + core, to_z * 4 + to_x * 2 + core))
    return pairs


def forth(value):
    return lax.ppermute(value, "fsdp", ring_pairs(1))


def back(value):
    return lax.ppermute(value, "fsdp", ring_pairs(-1))


def across(value):
    return lax.ppermute(value, "dp", [(0, 1), (1, 0)])


def exchange_rows(value):
    return lax.all_to_all(value, "dp", 0, 0)


def sibling(value):
    return lax.ppermute(value, "fsdp", [(i, i ^ 1) for i in range(16)])


def places(relative):
    y = lax.axis_index("dp") if relative else 0
    f = lax.axis_index("fsdp")
    z, x, core = f // 4, (f // 2) % 2, f % 2
    spot = jnp.where(x == 0, z, 7 - z)
    i = lax.iota(jnp.int32, 32)
    seat = (spot + (i // 2) % 8) % 8
    pair = jnp.where(seat < 4, seat * 2, (7 - seat) * 2 + 1)
    return ((y + i // 16) % 2) * 16 + pair * 2 + (core + i) % 2


def slot(other_row, distance, other_core):
    return other_row * 16 + (distance % 8) * 2 + other_core


def plan_moves(found, fields):
    sources, moves = [], []
    for source, rows, where in found:
        at = [i for i, s in enumerate(sources) if s is source]
        if not at:
            at = [len(sources)]
            sources.append(source)
        for (f0, f1), (g0, g1), out, out_row, out_col in fields:
            moves.append(
                (at[0], (rows[0] + f0, g0), (f1 - f0, g1 - g0), where, out, (out_row, out_col))
            )
    return sources, moves


def place(sources, moves, shapes, table, shards):
    def body(table_ref, *refs):
        ins, outs = refs[: len(sources)], refs[len(sources) : len(sources) + len(shapes)]
        held, sems, out_sems = refs[len(sources) + len(shapes) : -2], refs[-2], refs[-1]
        run_moves(moves, table_ref, ins, held, sems)
        copies = [
            pltpu.make_async_copy(held[i], outs[i], out_sems.at[i]) for i in range(len(shapes))
        ]
        for copy in copies:
            copy.start()
        for copy in copies:
            copy.wait()

    whole = [(shards,) + s for s in shapes]
    return pl.pallas_call(
        body,
        grid_spec=pltpu.PrefetchScalarGridSpec(
            num_scalar_prefetch=1,
            grid=(1,),
            in_specs=[pl.BlockSpec(memory_space=pl.ANY)] * len(sources),
            out_specs=[pl.BlockSpec(memory_space=pl.ANY)] * len(shapes),
            scratch_shapes=[pltpu.VMEM(s, jnp.bfloat16) for s in whole]
            + [
                pltpu.SemaphoreType.DMA((len(moves),)),
                pltpu.SemaphoreType.DMA((len(shapes),)),
            ],
        ),
        out_shape=[jax.ShapeDtypeStruct(s, jnp.bfloat16) for s in whole],
        compiler_params=pltpu.CompilerParams(vmem_limit_bytes=VMEM),
        name="place",
    )(table, *sources)


def run_moves(moves, table_ref, ins, outs, sems, begin=0):
    copies = []
    for i, (at, (sr, sc), (nr, nc), where, out, (dr, dc)) in enumerate(moves):
        copy = pltpu.make_async_copy(
            ins[at].at[pl.ds(sr, nr), pl.ds(begin + sc, nc)],
            outs[out].at[table_ref[where], pl.ds(dr, nr), pl.ds(dc, nc)],
            sems.at[i],
        )
        copy.start()
        copies.append(copy)
    for copy in copies:
        copy.wait()


def add_low(*values):
    total = values[0].astype(jnp.float32)
    for value in values[1:]:
        total = total + value.astype(jnp.float32)
    return total.astype(jnp.bfloat16)


ORDER_FIRST = (4, 3, -3)
ORDER_LAST = (2, -2, 1, -1, 0)


class Sequence:
    def __init__(self, token):
        self.token = token

    def tie(self, *values):
        out = lax.optimization_barrier((self.token,) + values)
        self.token = out[0]
        return out[1] if len(values) == 1 else out[1:]

    def run(self, function, *values):
        values = lax.optimization_barrier((self.token,) + values)
        self.token = values[0]
        return self.tie(function(*values[1:]))


class Around:
    def __init__(self, seq, first):
        self.seq, self.rights, self.lefts = seq, [first], [first]

    def start(self, right=True, left=True):
        if right:
            self.rights.append(forth(self.rights[-1]))
        if left:
            self.lefts.append(back(self.lefts[-1]))

    def arrive(self, right=True, left=True):
        ends = ([self.rights] if right else []) + ([self.lefts] if left else [])
        met = self.seq.tie(*[end[-1] for end in ends])
        for end, value in zip(ends, met if len(ends) > 1 else (met,)):
            end[-1] = value


class RoundFirst(Around):
    def __init__(self, seq, first, longer):
        super().__init__(seq, first)
        self.longer, self.found = longer, []

    def last(self):
        ends = self.rights if self.longer > 0 else self.lefts
        ends.append(forth(ends[-1]) if self.longer > 0 else back(ends[-1]))

    def arrive_last(self):
        self.arrive(self.longer > 0, self.longer < 0)

    def batch(self, early):
        rights, lefts = self.rights, self.lefts
        r = rights[0].shape[0]
        if early:
            parts, distances = (rights[0], rights[1], lefts[1], rights[2], lefts[2]), (0, -1, 1, -2, 2)
        else:
            end = rights[4] if self.longer > 0 else lefts[4]
            parts, distances = (rights[3], lefts[3], end), (-3, 3, 4)
        joint = self.seq.run(lambda *v: jnp.concatenate(v, axis=0), *parts)
        self.found.append((joint, r, 0, 0, distances))
        self.found.append((sibling(joint), r, 0, 1, distances))
        self.over = across(joint), r, distances

    def arrive_over(self):
        over, r, distances = self.over
        over = self.seq.tie(over)
        self.found.append((over, r, 1, 0, distances))
        self.found.append((sibling(over), r, 1, 1, distances))

    def arrive_batches(self):
        met = self.seq.tie(*[v[0] for v in self.found])
        self.found = [(m,) + v[1:] for m, v in zip(met, self.found)]

    def collect(self):
        return [
            (source, (i * r, (i + 1) * r), slot(other_row, k, other_core))
            for source, r, other_row, other_core, distances in self.found
            for i, k in enumerate(distances)
        ]


class AcrossFirst(Around):
    def __init__(self, seq, first):
        super().__init__(seq, first)
        self.found = []

    def note(self, joint, spots):
        r = self.rights[0].shape[0] // 2
        for other_core, source in ((0, joint), (1, sibling(joint))):
            for i, (row, k) in enumerate(spots):
                self.found.append((source, (i * r, (i + 1) * r), slot(row, k, other_core)))

    def early(self):
        rights, lefts = self.rights, self.lefts
        parts, distances = (rights[0], rights[1], lefts[1], rights[2], lefts[2]), (0, -1, 1, -2, 2)
        joint = self.seq.run(lambda *v: jnp.concatenate(v, axis=0), *parts)
        self.note(joint, [(row, k) for k in distances for row in (0, 1)])

    def third(self):
        self.note(self.rights[3], [(0, -3), (1, -3)])
        self.note(self.lefts[3], [(0, 3), (1, 3)])

    def last(self):
        r = self.rights[0].shape[0] // 2
        right, left = self.seq.run(lambda a, b: (a[:r], b[r:]), self.rights[3], self.lefts[3])
        self.far = [forth(right), back(left)]

    def arrive_last(self):
        self.far = list(self.seq.tie(*self.far))
        for row, array in enumerate(self.far):
            self.note(array, [(row, 4)])

    def collect(self):
        return self.found


ORDER_FIRST = (4, 3, -3)
ORDER_LAST = (2, -2, 1, -1, 0)


class SumAcrossFirst:
    def __init__(self, seq, parts, longer):
        self.seq, self.longer, self.ready = seq, longer, {}
        self.parts = parts
        self.met = [None, None]
        self.right = self.left = None

    def go_across(self, part):
        self.met[part] = exchange_rows(self.parts[part])

    def arrive_across(self, part):
        met = self.seq.tie(self.met[part])
        for i, k in enumerate((ORDER_FIRST, ORDER_LAST)[part]):
            self.ready[k] = (met, i)

    def step(self, k):
        if k == 4:
            value = self.seq.run(lambda v: add_low(v[0, 0], v[1, 0]), self.ready[4][0])
            if self.longer > 0:
                self.right = forth(value)
            else:
                self.left = back(value)
            return
        (met, i), (_, j) = self.ready[k], self.ready[-k]

        def add(met, right, left):
            return add_low(met[0, i], met[1, i], *right), add_low(met[0, j], met[1, j], *left)

        right = () if self.right is None else (self.right,)
        left = () if self.left is None else (self.left,)
        go_right, go_left = self.seq.run(add, met, right, left)
        self.right, self.left = forth(go_right), back(go_left)

    def finish(self):
        met, i = self.ready[0]

        def add(met, right, left):
            return sum(v.astype(jnp.float32) for v in (met[0, i], met[1, i], right, left))

        return self.seq.run(add, met, self.right, self.left)


class SumRoundFirst:
    def __init__(self, seq, blocks, far_right, far_left):
        self.seq, self.blocks = seq, blocks
        self.right, self.left = forth(far_right), back(far_left)

    def step(self, k):
        def add_part(one, two, right, left):
            r = right.shape[0]
            return (
                jnp.concatenate([add_low(one[:r], right), one[r:]], axis=0),
                jnp.concatenate([two[:r], add_low(two[r:], left)], axis=0),
            )

        def add(one, two, right, left):
            return add_low(one, right), add_low(two, left)

        go_right, go_left = self.seq.run(
            add_part if k == 3 else add, self.blocks[k], self.blocks[-k], self.right, self.left
        )
        self.right, self.left = forth(go_right), back(go_left)

    def go_across(self):
        def add(block, right, left):
            r = block.shape[0] // 2
            near = sum(v[:r].astype(jnp.float32) for v in (block, right, left))
            return near, add_low(block[r:], right[r:], left[r:])

        self.near, sent = self.seq.run(add, self.blocks[0], self.right, self.left)
        self.met = across(sent)

    def finish(self):
        return self.seq.run(lambda a, b: a + b.astype(jnp.float32), self.near, self.met)


def layer_norm(values, norm_gain, norm_shift):
    row_mean = jnp.mean(values, axis=-1, keepdims=True)
    centred = values - row_mean
    row_var = jnp.mean(centred * centred, axis=-1, keepdims=True)
    return centred * lax.rsqrt(row_var + EPS) * norm_gain + norm_shift


def exact_gelu(values):
    return jax.nn.gelu(values, approximate=False)


def plain_dot(left, right):
    return jnp.dot(left, right, preferred_element_type=jnp.float32)


def times_transpose(left, right):
    return lax.dot_general(
        left, right, (((1,), (1,)), ((), ())), preferred_element_type=jnp.float32
    )


def transpose_times(left, right):
    return lax.dot_general(
        left, right, (((0,), (0,)), ((), ())), preferred_element_type=jnp.float32
    )


CHUNKS = 2
CHUNK = HALF // CHUNKS
HEAD_TILE = 384
HALF_STEPS = CHUNK // HEAD_TILE
ROWS = 16
COLS = 384


def half_of(own, table_ref):
    core = table_ref[table_ref.shape[0] - 1]
    return core if own else 1 - core


def pixel_block(q, own, j, table_ref):
    return half_of(own, table_ref) * (CHUNKS * HALF_STEPS) + q * HALF_STEPS + j


def head_body(q, own, moves, weight_ref, table_ref, x_ref, guess_ref, adj_ref, *refs):
    ins, refs = refs[:-7], refs[-7:]
    comb_ref, dl_ref, df_ref, ent_ref, logit_ref, held_ref, sems = refs
    j = pl.program_id(0)
    strength = weight_ref[0]
    half = half_of(own, table_ref)
    first_pixel = half * HALF + q * CHUNK + j * HEAD_TILE

    @pl.when(j == 0)
    def _():
        df_ref[...] = jnp.zeros_like(df_ref)
        ent_ref[...] = jnp.zeros_like(ent_ref)
        begin = pl.multiple_of((2 * q + half) * WIDE, LANES)
        run_moves(moves, table_ref, ins, [held_ref], sems, begin)

    x = x_ref[...]

    def weight(e):
        begin = pl.multiple_of(e * CHUNK + j * HEAD_TILE, LANES)
        return held_ref[:, :, pl.ds(begin, HEAD_TILE)].reshape(D, HEAD_TILE)

    for e in range(MODEL_COUNT):
        logit_ref[e] = jnp.dot(x, weight(e), preferred_element_type=jnp.float32)

    for part in range(HEAD_TILE // COLS):
        cols = pl.ds(part * COLS, COLS)
        pixel = first_pixel + part * COLS + lax.broadcasted_iota(jnp.int32, (ROWS, COLS), 1)
        real = pixel < TILE_SAMPLES

        def chunk(i, total):
            rows = pl.ds(pl.multiple_of(i * ROWS, ROWS), ROWS)
            l0, l1, l2 = (logit_ref[e, rows, cols] for e in range(3))
            top = jnp.maximum(jnp.maximum(l0, l1), l2)
            l0, l1, l2 = l0 - top, l1 - top, l2 - top
            e0, e1, e2 = jnp.exp(l0), jnp.exp(l1), jnp.exp(l2)
            norm = e0 + e1 + e2
            inverse = 1.0 / norm
            log_norm = jnp.log(norm)
            b0, b1, b2 = e0 * inverse, e1 * inverse, e2 * inverse
            l0, l1, l2 = l0 - log_norm, l1 - log_norm, l2 - log_norm
            minus_h = b0 * l0 + b1 * l1 + b2 * l2
            g0, g1, g2 = (guess_ref[e, rows, cols].astype(jnp.float32) for e in range(3))
            mixed = b0 * g0 + b1 * g1 + b2 * g2
            comb_ref[rows, cols] = mixed.astype(jnp.bfloat16)
            adj = adj_ref[rows, cols].astype(jnp.float32)
            for e, (b, l, g) in enumerate(((b0, l0, g0), (b1, l1, g1), (b2, l2, g2))):
                d = b * (adj * (g - mixed) - strength * (l - minus_h))
                dl_ref[e, rows, cols] = jnp.where(real, d, 0.0).astype(jnp.bfloat16)
            return total - jnp.where(real, minus_h, 0.0)

        total = lax.fori_loop(
            0, TILE_COUNT // ROWS, chunk, jnp.zeros((ROWS, COLS), jnp.float32)
        )
        gathered = total[:, :LANES]
        for k in range(1, COLS // LANES):
            gathered = gathered + total[:, k * LANES : (k + 1) * LANES]
        ent_ref[...] += gathered[:8] + gathered[8:]

    part = None
    for e in range(MODEL_COUNT):
        piece = lax.dot_general(
            dl_ref[e], weight(e), (((1,), (1,)), ((), ())), preferred_element_type=jnp.float32
        )
        part = piece if part is None else part + piece
    df_ref[...] += part


def head_pass(q, own, strength, table, final_low, sources, moves, held_shape, guesses, adjoint, before):
    tile = HEAD_TILE
    extra = [] if before is None else [before]

    def body(*refs):
        refs = refs[:5] + refs[5 + len(extra) :]
        head_body(q, own, moves, *refs)

    d_spec = (MODEL_COUNT, TILE_COUNT, tile)
    return pl.pallas_call(
        body,
        grid_spec=pltpu.PrefetchScalarGridSpec(
            num_scalar_prefetch=2,
            grid=(HALF_STEPS,),
            in_specs=[
                pl.BlockSpec((TILE_COUNT, D), lambda j, s, t: (0, 0)),
                pl.BlockSpec(d_spec, lambda j, s, t: (0, 0, pixel_block(q, own, j, t))),
                pl.BlockSpec((TILE_COUNT, tile), lambda j, s, t: (0, pixel_block(q, own, j, t))),
            ]
            + [pl.BlockSpec(memory_space=pl.ANY)] * (len(extra) + len(sources)),
            out_specs=[
                pl.BlockSpec((TILE_COUNT, tile), lambda j, s, t: (0, pixel_block(q, own, j, t))),
                pl.BlockSpec(d_spec, lambda j, s, t: (0, 0, j)),
                pl.BlockSpec((TILE_COUNT, D), lambda j, s, t: (0, 0)),
                pl.BlockSpec((8, LANES), lambda j, s, t: (0, 0)),
            ],
            scratch_shapes=[
                pltpu.VMEM(d_spec, jnp.float32),
                pltpu.VMEM(held_shape, jnp.bfloat16),
                pltpu.SemaphoreType.DMA((len(moves),)),
            ],
        ),
        out_shape=[
            jax.ShapeDtypeStruct((TILE_COUNT, TILE_SAMPLES), jnp.bfloat16),
            jax.ShapeDtypeStruct((MODEL_COUNT, TILE_COUNT, CHUNK), jnp.bfloat16),
            jax.ShapeDtypeStruct((TILE_COUNT, D), jnp.float32),
            jax.ShapeDtypeStruct((8, LANES), jnp.float32),
        ],
        input_output_aliases={5: 0} if extra else {},
        compiler_params=pltpu.CompilerParams(
            dimension_semantics=("arbitrary",), vmem_limit_bytes=VMEM
        ),
        name="head_pass",
    )(strength, table, final_low, guesses, adjoint, *extra, *sources)


def dot_tokens(left, right):
    return lax.dot_general(left, right, (((0,), (0,)), ((), ())), preferred_element_type=jnp.float32)


def chip_at(marks_ref, row, distance):
    return marks_ref[1 + row * 8 + distance % 8]


HEAD_ORDER = (0, 1, -1, 2, -2, 3, -3)


def head_grad_body(marks_ref, x_mine_ref, x_other_ref, d_mine_ref, d_other_ref, *refs):
    outs, right_ref, left_ref, sum_ref = refs[:7], refs[7], refs[8], refs[9]
    value = dot_tokens(x_mine_ref[...], d_mine_ref[0]) + dot_tokens(x_other_ref[...], d_other_ref[0])
    sum_ref[...] = value.reshape(sum_ref.shape)
    r = sum_ref.shape[1]
    for k, out in zip(HEAD_ORDER, outs):
        for row in (0, 1):
            block = sum_ref[chip_at(marks_ref, row, k)].astype(jnp.bfloat16)
            out[row * r : (row + 1) * r, :] = block
    right_ref[...] = sum_ref[chip_at(marks_ref, 0, 4)].astype(jnp.bfloat16)
    left_ref[...] = sum_ref[chip_at(marks_ref, 1, 4)].astype(jnp.bfloat16)


def head_grad(marks, x_mine, x_other, d_mine, d_other):
    tile = CHUNK
    r = D // 16
    n = MODEL_COUNT * CHUNK
    tall = [2 * r] * 7 + [r] * 2
    outs = pl.pallas_call(
        head_grad_body,
        grid_spec=pltpu.PrefetchScalarGridSpec(
            num_scalar_prefetch=1,
            grid=(MODEL_COUNT,),
            in_specs=[
                pl.BlockSpec((TILE_COUNT, D), lambda e, c: (0, 0)),
                pl.BlockSpec((TILE_COUNT, D), lambda e, c: (0, 0)),
                pl.BlockSpec((1, TILE_COUNT, tile), lambda e, c: (e, 0, 0)),
                pl.BlockSpec((1, TILE_COUNT, tile), lambda e, c: (e, 0, 0)),
            ],
            out_specs=[pl.BlockSpec((h, tile), lambda e, c: (0, e)) for h in tall],
            scratch_shapes=[pltpu.VMEM((16, r, tile), jnp.float32)],
        ),
        out_shape=[jax.ShapeDtypeStruct((h, n), jnp.bfloat16) for h in tall],
        compiler_params=pltpu.CompilerParams(
            dimension_semantics=("arbitrary",), vmem_limit_bytes=VMEM
        ),
        name="head_grad",
    )(marks, x_mine, x_other, d_mine, d_other)
    return dict(zip(HEAD_ORDER, outs[:7])), outs[7], outs[8]


def ring_rows(marks_ref, outs, write):
    for row in (0, 1):
        for out, order in zip(outs, (ORDER_FIRST, ORDER_LAST)):
            for i, k in enumerate(order):
                write(out, row, i, chip_at(marks_ref, row, k))


def core_half(ref, marks_ref):
    n = ref.shape[1] // 2
    return ref[:, pl.ds(pl.multiple_of(marks_ref[0] * n, LANES), n)]


def paired_product(marks_ref, x, x_other, d, d_other):
    return dot_tokens(x[...], core_half(d, marks_ref)) + dot_tokens(
        x_other[...], core_half(d_other, marks_ref)
    )


def second_grad_body(marks_ref, *refs):
    ins, outs, (fc2_ref, fc1_ref) = refs[:8], refs[8:10], refs[10:]
    fc2_ref[...] = paired_product(marks_ref, *ins[:4]).reshape(fc2_ref.shape)
    fc1_ref[...] = paired_product(marks_ref, *ins[4:]).reshape(fc1_ref.shape)
    r4, wide = fc2_ref.shape[1:]
    r = fc1_ref.shape[1]

    def write(out, row, i, chip):
        out[row, i, :r4, :] = fc2_ref[chip].astype(jnp.bfloat16)
        for k in range(4):
            block = fc1_ref[chip, :, k * wide : (k + 1) * wide].astype(jnp.bfloat16)
            out[row, i, r4 + k * r : r4 + (k + 1) * r, :] = block

    ring_rows(marks_ref, outs, write)


def first_grad_body(marks_ref, *refs):
    ins, outs, refs = refs[:12], refs[12:14], refs[14:]
    qkv_ref, proj_ref, small_ref, flat_ref, hidden_ref, block_ref = refs
    qkv_ref[...] = paired_product(marks_ref, *ins[:4]).reshape(qkv_ref.shape)
    proj_ref[...] = paired_product(marks_ref, *ins[4:8]).reshape(proj_ref.shape)
    flat_ref[...] = jnp.zeros_like(flat_ref)
    flat_ref[: ins[8].shape[0], :] = ins[8][...] + ins[9][...]
    small_ref[...] = flat_ref[...].T.reshape(small_ref.shape)
    shards = hidden_ref.shape[0]
    r, wide = qkv_ref.shape[1] // 2, FF // shards
    hidden_ref[...] = jnp.zeros_like(hidden_ref)
    for d in range(shards):
        cols = slice(d * wide, (d + 1) * wide)
        hidden_ref[d : d + 1, :wide] = ins[10][:, cols] + ins[11][:, cols]
    block_ref[...] = jnp.zeros_like(block_ref)
    n, m = qkv_ref.shape[2], qkv_ref.shape[2] + proj_ref.shape[2]

    def write(out, row, i, chip):
        out[row, i, :, :n] = qkv_ref[chip].astype(jnp.bfloat16)
        out[row, i, :, n:m] = proj_ref[chip].astype(jnp.bfloat16)
        out[row, i, :, m : m + LANES] = small_ref[chip].astype(jnp.bfloat16)
        block_ref[0:1, :] = hidden_ref[pl.ds(2 * chip, 1), :]
        block_ref[r : r + 1, :] = hidden_ref[pl.ds(2 * chip + 1, 1), :]
        out[row, i, :, m + LANES :] = block_ref[...].astype(jnp.bfloat16)

    ring_rows(marks_ref, outs, write)


def ring_grad(body, marks, ins, block, scratch, name):
    shapes = [(2, 3) + block, (2, 5) + block]
    return pl.pallas_call(
        body,
        grid_spec=pltpu.PrefetchScalarGridSpec(
            num_scalar_prefetch=1,
            grid=(1,),
            in_specs=[pl.BlockSpec(v.shape, lambda i, m: (0, 0)) for v in ins],
            out_specs=[pl.BlockSpec(s, lambda i, m: (0, 0, 0, 0)) for s in shapes],
            scratch_shapes=[pltpu.VMEM(s, jnp.float32) for s in scratch],
        ),
        out_shape=[jax.ShapeDtypeStruct(s, jnp.bfloat16) for s in shapes],
        compiler_params=pltpu.CompilerParams(vmem_limit_bytes=VMEM),
        name=name,
    )(marks, *ins)


def pack_small(lead_w, gains, biases, qkv_b, fc1_b, rows):
    value = jnp.concatenate([lead_w, gains, biases, qkv_b, fc1_b.reshape(4, rows).T], axis=1)
    return jnp.pad(value, ((0, 0), (0, LANES - value.shape[1])))


def split_small(small):
    at, found = 0, []
    for width in (LEADS, 2, 4, 2, 4):
        found.append(small[:, at : at + width])
        at += width
    return found


WIDE = MODEL_COUNT * CHUNK


def head_chunks(value):
    r = value.shape[0]
    value = value.reshape(r, MODEL_COUNT, TILE_SAMPLES)
    value = jnp.pad(value, ((0, 0), (0, 0), (0, PADDED - TILE_SAMPLES)))
    value = value.reshape(r, MODEL_COUNT, 2, CHUNKS, CHUNK).transpose(0, 2, 1, 3, 4)
    return [value[:, :, :, q].reshape(r, 2 * WIDE) for q in range(CHUNKS)]


def pack_trunk_body(qkv_ref, proj_ref, fc1_ref, fc2_ref, lead_ref, gain_ref, bias_ref, qkv_b_ref, fc1_b_ref, *refs):
    one_ref, two_ref, flat_ref, tall_ref = refs
    r = qkv_ref.shape[0]
    flat_ref[...] = jnp.zeros_like(flat_ref)
    at = LEADS
    for ref in (gain_ref, bias_ref, qkv_b_ref):
        rows = ref.shape[0]
        flat_ref[at : at + rows, :r] = ref[...].astype(jnp.float32)
        at += rows
    tall_ref[...] = flat_ref[...].T
    tall_ref[:r, :LEADS] = lead_ref[...].astype(jnp.float32)
    flat_ref[...] = jnp.zeros_like(flat_ref)
    flat_ref[0:1, : 4 * r] = fc1_b_ref[...].astype(jnp.float32)
    n = 4 * D
    one_ref[:, : 3 * D] = qkv_ref[...]
    one_ref[:, 3 * D : n] = proj_ref[...]
    one_ref[:, n : n + LANES] = tall_ref[:r, :].astype(jnp.bfloat16)
    one_ref[:, n + LANES :] = flat_ref[:r, :].astype(jnp.bfloat16)
    two_ref[: 4 * r, :] = fc2_ref[...]
    for k in range(4):
        two_ref[(4 + k) * r : (5 + k) * r, :] = fc1_ref[:, k * D : (k + 1) * D]


def pack_trunk(qkv, proj, fc1, fc2, lead_w, gains, biases, qkv_b, fc1_b):
    r = qkv.shape[0]
    return pl.pallas_call(
        pack_trunk_body,
        out_shape=[
            jax.ShapeDtypeStruct((r, 4 * D + 2 * LANES), jnp.bfloat16),
            jax.ShapeDtypeStruct((8 * r, D), jnp.bfloat16),
        ],
        scratch_shapes=[pltpu.VMEM((LANES, LANES), jnp.float32)] * 2,
        compiler_params=pltpu.CompilerParams(vmem_limit_bytes=VMEM),
        name="pack_trunk",
    )(qkv, proj, fc1, fc2, lead_w, gains.T, biases.T, qkv_b.T, fc1_b.reshape(1, 4 * r))


def pack_head_body(head_ref, out):
    r = head_ref.shape[0]
    for q in range(CHUNKS):
        for h in range(2):
            first = h * HALF + q * CHUNK
            real = min(CHUNK, TILE_SAMPLES - first)
            for e in range(MODEL_COUNT):
                begin, at = e * TILE_SAMPLES + first, ((2 * q + h) * MODEL_COUNT + e) * CHUNK
                part = head_ref[:, begin : begin + real]
                if real < CHUNK:
                    part = jnp.concatenate([part, jnp.zeros((r, CHUNK - real), part.dtype)], axis=1)
                out[:, at : at + CHUNK] = part


def pack_head(head):
    return pl.pallas_call(
        pack_head_body,
        out_shape=jax.ShapeDtypeStruct((head.shape[0], 2 * CHUNKS * WIDE), jnp.bfloat16),
        compiler_params=pltpu.CompilerParams(vmem_limit_bytes=VMEM),
        name="pack_head",
    )(head)


def head_whole(low, high):
    r = low[0].shape[0]
    parts = [v.reshape(r, MODEL_COUNT, CHUNK) for v in (*low, *high)]
    return jnp.concatenate(parts, axis=2)[:, :, :TILE_SAMPLES].reshape(r, MODEL_COUNT * TILE_SAMPLES)


DIGITS = 16
BASE = 8.0


def digits_of(value):
    powers = jnp.asarray([BASE**k for k in range(DIGITS + 1)], jnp.float32)
    floors = jnp.floor(value * 32.0 * powers)
    return floors[1:] - BASE * floors[:-1]


def value_of(digits):
    powers = jnp.asarray([BASE ** -(k + 1) / 32.0 for k in range(DIGITS)], jnp.float32)
    return jnp.sum(digits * powers)


SCALE = HD ** (-0.5)
ROW_GAIN, ROW_BIAS, ROW_QKV, ROW_DIGIT = LEADS, LEADS + 2, LEADS + 6, LEADS + 8
SMALL_ROWS = 64
FIRST_WIDE = 4 * D + 2 * LANES


def slab(ref, first, n):
    shards, rows = ref.shape[:2]
    return ref[:, :, first : first + n].reshape(shards * rows, n)


def dot_last(left, right):
    return lax.dot_general(left, right, (((1,), (1,)), ((), ())), preferred_element_type=jnp.float32)


def normalised(values):
    centred = values - jnp.mean(values, axis=-1, keepdims=True)
    inverse = lax.rsqrt(jnp.mean(centred * centred, axis=-1, keepdims=True) + EPS)
    return centred * inverse, inverse


def norm_back(values, d_out, gain):
    unit, inverse = normalised(values)
    d_unit = d_out * gain
    mean_one = jnp.mean(d_unit, axis=-1, keepdims=True)
    mean_two = jnp.mean(d_unit * unit, axis=-1, keepdims=True)
    d_values = inverse * (d_unit - mean_one - unit * mean_two)
    return (
        d_values,
        jnp.sum(d_out * unit, axis=0, keepdims=True),
        jnp.sum(d_out, axis=0, keepdims=True),
    )


def head_masks():
    lane = lax.broadcasted_iota(jnp.int32, (1, 2 * HD), 1)
    low = lane < HD
    return low, [m.astype(jnp.float32).astype(jnp.bfloat16) for m in (low, lane >= HD)]


def softmax_of(scores):
    expd = jnp.exp(scores - jnp.max(scores, axis=-1, keepdims=True))
    return expd * (1.0 / jnp.sum(expd, axis=-1, keepdims=True))


def trunk_first_body(moves, table_ref, index_ref, frame_ref, *refs):
    ins, refs = refs[:-9], refs[-9:]
    middle_ref, normed_ref, joined_ref, attended_ref, normed_two_ref, par_ref, fc1_b_ref = refs[:7]
    held_ref, sems = refs[7:]
    run_moves(moves, table_ref, ins, [held_ref], sems)
    par_ref[...] = slab(held_ref, 4 * D, LANES).astype(jnp.float32).T
    shards = held_ref.shape[0]
    wide = FF // shards
    for d in range(shards):
        row = held_ref[d, 0:1, 4 * D + LANES : 4 * D + LANES + wide]
        fc1_b_ref[:, d * wide : (d + 1) * wide] = row.astype(jnp.float32)

    def row(i):
        return par_ref[i : i + 1, :]

    started = frame_ref[...].astype(jnp.float32) + par_ref[pl.ds(index_ref[0], 1), :]
    normed = (normalised(started)[0] * row(ROW_GAIN) + row(ROW_BIAS)).astype(jnp.bfloat16)
    normed_ref[...] = normed
    for i, shift in enumerate((row(ROW_QKV), None, row(ROW_QKV + 1))):
        part = jnp.dot(normed, slab(held_ref, i * D, D), preferred_element_type=jnp.float32)
        part = part if shift is None else part + shift
        joined_ref[:, i * D : (i + 1) * D] = part.astype(jnp.bfloat16)
    low, masks = head_masks()
    for p in range(HEADS // 2):
        at = p * 2 * HD
        q, k, v = (joined_ref[:, i * D + at : i * D + at + 2 * HD] for i in range(3))
        outs = []
        for mask in masks:
            probs = softmax_of(dot_last(q * mask, k) * SCALE).astype(jnp.bfloat16)
            outs.append(jnp.dot(probs, v, preferred_element_type=jnp.float32))
        attended_ref[:, at : at + 2 * HD] = jnp.where(low, *outs).astype(jnp.bfloat16)
    middle = (
        started
        + jnp.dot(attended_ref[...], slab(held_ref, 3 * D, D), preferred_element_type=jnp.float32)
        + row(ROW_BIAS + 1)
    )
    middle_ref[...] = middle
    normed_two = normalised(middle)[0] * row(ROW_GAIN + 1) + row(ROW_BIAS + 2)
    normed_two_ref[...] = normed_two.astype(jnp.bfloat16)


def trunk_call(body, scalars, ins, sources, outs, scratch, name):
    any_spec = pl.BlockSpec(memory_space=pl.ANY)

    def whole(shape):
        return pl.BlockSpec(shape, lambda i, *s: (0,) * len(shape))

    return pl.pallas_call(
        body,
        grid_spec=pltpu.PrefetchScalarGridSpec(
            num_scalar_prefetch=len(scalars),
            grid=(1,),
            in_specs=[whole(v.shape) for v in ins] + [any_spec] * len(sources),
            out_specs=[whole(s) for s, _ in outs],
            scratch_shapes=scratch,
        ),
        out_shape=[jax.ShapeDtypeStruct(*o) for o in outs],
        compiler_params=pltpu.CompilerParams(vmem_limit_bytes=VMEM),
        name=name,
    )(*scalars, *ins, *sources)


def trunk_first(table, index, rows, moves, frame, *sources):
    flat, low, full = (TILE_COUNT, D), jnp.bfloat16, jnp.float32
    return trunk_call(
        functools.partial(trunk_first_body, moves),
        (table, index),
        (frame,),
        sources,
        [
            (flat, full),
            (flat, low),
            ((TILE_COUNT, 3 * D), low),
            (flat, low),
            (flat, low),
            ((LANES, D), full),
            ((1, FF), full),
        ],
        [
            pltpu.VMEM((32, rows, FIRST_WIDE), low),
            pltpu.SemaphoreType.DMA((len(moves),)),
        ],
        "trunk_first",
    )


def trunk_second_body(moves, table_ref, middle_ref, normed_two_ref, par_ref, fc1_b_ref, *refs):
    ins, refs = refs[:-5], refs[-5:]
    hidden_ref, slope_ref, final_ref, held_ref, sems = refs
    run_moves(moves, table_ref, ins, [held_ref], sems)
    total = middle_ref[...] + par_ref[ROW_BIAS + 3 : ROW_BIAS + 4, :]
    normed_two = normed_two_ref[...]
    for k in range(4):
        cols = slice(k * D, (k + 1) * D)
        pre = jnp.dot(normed_two, widening(held_ref, k), preferred_element_type=jnp.float32)
        pre = pre + fc1_b_ref[:, cols]
        share = 0.5 * (1.0 + lax.erf(pre * (0.5**0.5)))
        density = jnp.exp(-0.5 * pre * pre) * ((0.5 / 3.141592653589793) ** 0.5)
        slope_ref[:, cols] = share + pre * density
        hidden = (pre * share).astype(jnp.bfloat16)
        hidden_ref[:, cols] = hidden
        weight = narrowing(held_ref, k)
        total += jnp.dot(hidden, weight, preferred_element_type=jnp.float32)
    final_ref[...] = total.astype(jnp.bfloat16)


def second_scratch(rows):
    return [pltpu.VMEM((32, 8 * rows, D), jnp.bfloat16)]


def narrowing(held_ref, k):
    shards, rows = held_ref.shape[:2]
    return held_ref[k * shards // 4 : (k + 1) * shards // 4, : rows // 2, :].reshape(D, D)


def widening(held_ref, k):
    rows = held_ref.shape[1] // 8
    return held_ref[:, (4 + k) * rows : (5 + k) * rows, :].reshape(D, D)


def trunk_second(table, rows, moves, middle, normed_two, par, fc1_b, *sources):
    return trunk_call(
        functools.partial(trunk_second_body, moves),
        (table,),
        (middle, normed_two, par, fc1_b),
        sources,
        [
            ((TILE_COUNT, FF), jnp.bfloat16),
            ((TILE_COUNT, FF), jnp.float32),
            ((TILE_COUNT, D), jnp.bfloat16),
        ],
        second_scratch(rows) + [pltpu.SemaphoreType.DMA((len(moves),))],
        "trunk_second",
    )


def second_back_body(moves_two, moves_one, n_two, table_ref, slope_ref, middle_ref, par_ref, *refs):
    d_parts, refs = refs[: 2 * CHUNKS], refs[2 * CHUNKS :]
    ins, refs = refs[:-11], refs[-11:]
    branch_ref, pre_ref, middle_d_ref, attn_ref, attended_ref, rows_ref, fc1_b_ref = refs[:7]
    held_ref, proj_ref, sems_two, sems_one = refs[7:]
    run_moves(moves_one, table_ref, ins[n_two:], [proj_ref], sems_one)
    run_moves(moves_two, table_ref, ins[:n_two], [held_ref], sems_two)
    d_final = d_parts[0][...]
    for part in d_parts[1:]:
        d_final = d_final + part[...]
    d_branch = d_final.astype(jnp.bfloat16)
    branch_ref[...] = d_branch
    d_normed = None
    for k in range(4):
        cols = slice(k * D, (k + 1) * D)
        d_hidden = dot_last(d_branch, narrowing(held_ref, k))
        d_pre = (d_hidden * slope_ref[:, cols]).astype(jnp.bfloat16)
        pre_ref[:, cols] = d_pre
        fc1_b_ref[:, cols] = jnp.sum(d_pre.astype(jnp.float32), axis=0, keepdims=True)
        part = dot_last(d_pre, widening(held_ref, k))
        d_normed = part if d_normed is None else d_normed + part
    gain = par_ref[ROW_GAIN + 1 : ROW_GAIN + 2, :]
    d_part, d_gain, d_shift = norm_back(middle_ref[...], d_normed, gain)
    d_middle = d_final + d_part
    middle_d_ref[...] = d_middle
    d_attn = d_middle.astype(jnp.bfloat16)
    attn_ref[...] = d_attn
    attended_ref[...] = dot_last(d_attn, slab(proj_ref, 0, D)).astype(jnp.bfloat16)
    sums = [jnp.sum(v.astype(jnp.float32), axis=0, keepdims=True) for v in (d_attn, d_branch)]
    rows_ref[...] = jnp.zeros_like(rows_ref)
    for i, value in enumerate((d_gain, d_shift, *sums)):
        rows_ref[i : i + 1, :] = value


def second_back(table, rows, moves_two, moves_one, n_two, slope, middle, par, d_parts, *sources):
    flat, low, full = (TILE_COUNT, D), jnp.bfloat16, jnp.float32
    return trunk_call(
        functools.partial(second_back_body, moves_two, moves_one, n_two),
        (table,),
        (slope, middle, par, *d_parts),
        sources,
        [
            (flat, low),
            ((TILE_COUNT, FF), low),
            (flat, full),
            (flat, low),
            (flat, low),
            ((8, D), full),
            ((1, FF), full),
        ],
        second_scratch(rows)
        + [
            pltpu.VMEM((32, rows, D), low),
            pltpu.SemaphoreType.DMA((len(moves_two),)),
            pltpu.SemaphoreType.DMA((len(moves_one),)),
        ],
        "second_back",
    )


def first_back_body(moves, n_ent, table_ref, index_ref, weight_ref, frame_ref, joined_ref, par_ref, middle_d_ref, attended_ref, rows_ref, *refs):
    ents, refs = refs[:n_ent], refs[n_ent:]
    ins, refs = refs[:-5], refs[-5:]
    d_joined_ref, tokens_ref, small_ref, qkv_ref, sems = refs
    run_moves(moves, table_ref, ins, [qkv_ref], sems)
    small_ref[...] = jnp.zeros_like(small_ref)
    _, masks = head_masks()
    for p in range(HEADS // 2):
        at = p * 2 * HD
        q, k, v = (joined_ref[:, i * D + at : i * D + at + 2 * HD] for i in range(3))
        d_out = attended_ref[:, at : at + 2 * HD]
        totals = [None] * 3
        for mask in masks:
            q_one, k_one, d_one = q * mask, k * mask, d_out * mask
            probs = softmax_of(dot_last(q_one, k) * SCALE)
            d_probs = dot_last(d_one, v)
            inner = jnp.sum(probs * d_probs, axis=-1, keepdims=True)
            d_scores = (probs * (d_probs - inner)).astype(jnp.bfloat16)
            parts = (
                jnp.dot(d_scores, k_one, preferred_element_type=jnp.float32),
                dot_tokens(d_scores, q_one),
                dot_tokens(probs.astype(jnp.bfloat16), d_one),
            )
            totals = [a if b is None else a + b for a, b in zip(parts, totals)]
        for i, scale in enumerate((SCALE, SCALE, 1.0)):
            d_joined_ref[:, i * D + at : i * D + at + 2 * HD] = (totals[i] * scale).astype(
                jnp.bfloat16
            )
    d_normed = None
    for i in range(3):
        block = d_joined_ref[:, i * D : (i + 1) * D]
        if i != 1:
            at = ROW_QKV + i // 2
            total = jnp.sum(block.astype(jnp.float32), axis=0, keepdims=True)
            small_ref[at : at + 1, :] = total
        part = dot_last(block, slab(qkv_ref, i * D, D))
        d_normed = part if d_normed is None else d_normed + part
    started = frame_ref[...].astype(jnp.float32) + par_ref[pl.ds(index_ref[0], 1), :]
    gain = par_ref[ROW_GAIN : ROW_GAIN + 1, :]
    d_part, d_gain, d_shift = norm_back(started, d_normed, gain)
    d_started = middle_d_ref[...] + d_part
    tokens_ref[...] = d_started.astype(jnp.bfloat16)
    small_ref[pl.ds(index_ref[0], 1), :] = jnp.sum(d_started, axis=0, keepdims=True)
    small_ref[ROW_GAIN : ROW_GAIN + 1, :] = d_gain
    small_ref[ROW_BIAS : ROW_BIAS + 1, :] = d_shift
    small_ref[ROW_GAIN + 1 : ROW_GAIN + 2, :] = rows_ref[0:1, :]
    small_ref[ROW_BIAS + 2 : ROW_BIAS + 3, :] = rows_ref[1:2, :]
    small_ref[ROW_BIAS + 1 : ROW_BIAS + 2, :] = rows_ref[2:3, :]
    small_ref[ROW_BIAS + 3 : ROW_BIAS + 4, :] = rows_ref[3:4, :]
    entropy = ents[0][...]
    for ent in ents[1:]:
        entropy = entropy + ent[...]
    entropy = jnp.sum(jnp.sum(entropy, axis=0, keepdims=True), axis=1, keepdims=True)
    value = jnp.broadcast_to(entropy * weight_ref[0] * 32.0, (1, D))
    before = jnp.floor(value)
    for k in range(DIGITS):
        value = value * BASE
        floor = jnp.floor(value)
        small_ref[ROW_DIGIT + k : ROW_DIGIT + k + 1, :] = floor - BASE * before
        before = floor


def first_back(table, index, strength, rows, moves, frame, joined, par, d_middle, d_attended, d_rows, ents, *sources):
    return trunk_call(
        functools.partial(first_back_body, moves, len(ents)),
        (table, index, strength),
        (frame, joined, par, d_middle, d_attended, d_rows, *ents),
        sources,
        [
            ((TILE_COUNT, 3 * D), jnp.bfloat16),
            ((TILE_COUNT, D), jnp.bfloat16),
            ((SMALL_ROWS, D), jnp.float32),
        ],
        [
            pltpu.VMEM((32, rows, 3 * D), jnp.bfloat16),
            pltpu.SemaphoreType.DMA((len(moves),)),
        ],
        "first_back",
    )


def low_or_high(value, core, rows):
    return value[core * rows : (core + 1) * rows]


def fc2_rows(value, core, rows):
    return value[core * 4 * rows : (core + 1) * 4 * rows]


def fc1_rows(value, core, rows):
    begin = 8 * rows + core * rows
    return jnp.concatenate(
        [value[begin + 2 * k * rows : begin + (2 * k + 1) * rows] for k in range(4)], axis=1
    )


class Parameters:
    def __init__(self, small_all, rows):
        lead_w, gain_all, bias_all, qkv_b, fc1_b = split_small(small_all)
        self.lead = lead_w.astype(jnp.float32)
        self.gain = gain_all.astype(jnp.float32)
        self.bias = bias_all.astype(jnp.float32)
        qkv_b = qkv_b.astype(jnp.float32)
        self.offset = jnp.concatenate([qkv_b[:, 0], jnp.zeros_like(qkv_b[:, 0]), qkv_b[:, 1]])
        self.fc1 = (
            fc1_b.astype(jnp.float32).reshape(D // rows, rows, 4).transpose(0, 2, 1).reshape(FF)
        )


    def parts(self):
        return self.lead, self.gain, self.bias, self.offset, self.fc1


def attention_input(frame, lead_vector, gain, bias, offset, qkv_w):
    started = frame.astype(jnp.float32) + lead_vector[None, :]
    normed = layer_norm(started, gain, bias).astype(jnp.bfloat16)
    joined = (plain_dot(normed, qkv_w) + offset).astype(jnp.bfloat16)
    return started, normed, joined


def heads_of(joined):
    return [joined[:, i * D : (i + 1) * D].reshape(TILE_COUNT, HEADS, HD) for i in range(3)]


def attention(joined):
    queries, keys, values = heads_of(joined)
    scores = jnp.einsum("qhd,khd->hqk", queries, keys, preferred_element_type=jnp.float32) * SCALE
    row_top = jnp.max(scores, axis=-1, keepdims=True)
    expd = jnp.exp(scores - row_top)
    prob_full = expd / jnp.sum(expd, axis=-1, keepdims=True)
    probs_low = prob_full.astype(jnp.bfloat16)
    attended = jnp.einsum("hqk,khd->qhd", probs_low, values, preferred_element_type=jnp.float32)
    return prob_full, attended.astype(jnp.bfloat16).reshape(TILE_COUNT, D)


def mlp_input(started, attended, proj_w, proj_bias, gain, bias):
    middle = started + plain_dot(attended, proj_w) + proj_bias
    return middle, layer_norm(middle, gain, bias).astype(jnp.bfloat16)


def mlp(middle, normed_two, fc1_w, fc1_b, fc2_w, fc2_b):
    pre_act = plain_dot(normed_two, fc1_w) + fc1_b
    hidden = exact_gelu(pre_act).astype(jnp.bfloat16)
    final_sum = middle + plain_dot(hidden, fc2_w) + fc2_b
    return pre_act, hidden, final_sum.astype(jnp.bfloat16)


def mlp_back(d_parts, pre_act, fc2_w):
    d_final = sum(d_parts)
    d_branch = d_final.astype(jnp.bfloat16)
    d_hidden = times_transpose(d_branch, fc2_w)
    _, gelu_back = jax.vjp(exact_gelu, pre_act)
    return d_final, d_branch, gelu_back(d_hidden)[0].astype(jnp.bfloat16)


def mlp_input_back(d_final, d_pre, fc1_w, middle, gain, bias, proj_w):
    d_normed_two = times_transpose(d_pre, fc1_w)
    _, norm_back = jax.vjp(layer_norm, middle, gain, bias)
    d_part, d_gain, d_shift = norm_back(d_normed_two)
    d_middle = d_final + d_part
    d_attn = d_middle.astype(jnp.bfloat16)
    d_attended = times_transpose(d_attn, proj_w).astype(jnp.bfloat16)
    return d_middle, d_attn, d_attended, d_gain, d_shift


def attention_back(joined, prob_full, d_attended):
    queries, keys, values = heads_of(joined)
    d_attended = d_attended.reshape(TILE_COUNT, HEADS, HD)
    probs_low = prob_full.astype(jnp.bfloat16)
    d_values = jnp.einsum("hqk,qhd->khd", probs_low, d_attended, preferred_element_type=jnp.float32)
    d_prob = jnp.einsum("qhd,khd->hqk", d_attended, values, preferred_element_type=jnp.float32)
    d_score = (
        prob_full * (d_prob - jnp.sum(prob_full * d_prob, axis=-1, keepdims=True))
    ).astype(jnp.bfloat16)
    d_queries = (
        jnp.einsum("hqk,khd->qhd", d_score, keys, preferred_element_type=jnp.float32) * SCALE
    )
    d_keys = (
        jnp.einsum("hqk,qhd->khd", d_score, queries, preferred_element_type=jnp.float32) * SCALE
    )
    return jnp.concatenate(
        [v.reshape(TILE_COUNT, D) for v in (d_queries, d_keys, d_values)], axis=1
    ).astype(jnp.bfloat16)


def attention_input_back(d_middle, d_joined, qkv_w, started, gain, bias):
    d_normed = times_transpose(d_joined, qkv_w)
    _, norm_back = jax.vjp(layer_norm, started, gain, bias)
    d_part, d_gain, d_shift = norm_back(d_normed)
    return d_middle + d_part, d_gain, d_shift


def small_gradient(rows, horizon_indicator, contribution, d_started, d_joined, d_attn, d_branch, d_pre, gains, shifts):
    def column_sum(value):
        return jnp.sum(value.astype(jnp.float32), axis=0)

    joined_sums = column_sum(d_joined)
    columns = jnp.stack(
        [
            *gains,
            shifts[0],
            column_sum(d_attn),
            shifts[1],
            column_sum(d_branch),
            joined_sums[:D],
            joined_sums[2 * D :],
        ],
        axis=1,
    )
    hidden_columns = column_sum(d_pre).reshape(D // rows, 4, rows).transpose(0, 2, 1).reshape(D, 4)
    return jnp.concatenate(
        [
            jnp.sum(d_started, axis=0)[:, None] * horizon_indicator[None, :],
            columns,
            hidden_columns,
            jnp.broadcast_to(digits_of(contribution)[None, :], (D, DIGITS)),
            jnp.zeros((D, LANES - LEADS - 12 - DIGITS), jnp.float32),
        ],
        axis=1,
    ).astype(jnp.bfloat16)


def small_outputs(value, rows):
    return (
        value[:, :LEADS],
        value[:, LEADS : LEADS + 2],
        value[:, LEADS + 2 : LEADS + 6],
        value[:, LEADS + 6 : LEADS + 8],
        value[:, LEADS + 8 : LEADS + 12].T.reshape(4 * rows),
    )


def frame_scalars(horizon_indices, horizon_tallies):
    indicator = (horizon_indices[0] == lax.iota(jnp.int32, LEADS)).astype(jnp.float32)
    frame_count = jnp.sum(indicator * horizon_tallies.astype(jnp.float32))
    return indicator, 1.0 / (frame_count * (LEADS * TILE_COUNT * TILE_SAMPLES))


def plain_step(
    tile_embeddings,
    horizon_indices,
    horizon_tallies,
    member_guesses,
    adjoint_of_mixture,
    triple_projection_matrix,
    attention_outward_matrix,
    widening_matrix,
    narrowing_matrix,
    gating_matrix,
    *small_parts,
):
    rows = triple_projection_matrix.shape[0]
    whole = functools.partial(lax.all_gather, axis_name=AXES, axis=0, tiled=True)

    def summed(value):
        return lax.psum_scatter(
            value.astype(jnp.bfloat16), AXES, scatter_dimension=0, tiled=True
        ).astype(jnp.float32)

    qkv_w, proj_w = whole(triple_projection_matrix), whole(attention_outward_matrix)
    fc1_w, fc2_w = whole(widening_matrix), whole(narrowing_matrix)
    par = Parameters(whole(pack_small(*small_parts, rows)), rows)
    indicator, strength = frame_scalars(horizon_indices, horizon_tallies)
    guesses = jnp.transpose(member_guesses[0], (1, 0, 2))
    lead_vector = jnp.sum(par.lead * indicator[None, :], axis=1)
    started, normed, joined = attention_input(
        tile_embeddings[0], lead_vector, par.gain[:, 0], par.bias[:, 0], par.offset, qkv_w
    )
    prob_full, attended = attention(joined)
    middle, normed_two = mlp_input(
        started, attended, proj_w, par.bias[:, 1], par.gain[:, 1], par.bias[:, 2]
    )
    pre_act, hidden, final_low = mlp(middle, normed_two, fc1_w, par.fc1, fc2_w, par.bias[:, 3])
    table = jnp.asarray([0, 1], jnp.int32)
    held_shape = (1, D, WIDE)
    combined, head_grads, d_parts, entropies = None, [], [], []
    head_w = whole(jnp.concatenate(head_chunks(gating_matrix), axis=1))
    for q in range(CHUNKS):
        halves = []
        for own in (False, True):
            combined, d_logits, d_part, entropy = head_pass(
                q,
                own,
                strength.reshape(1),
                table,
                final_low,
                [head_w],
                [(0, (0, 0), held_shape[1:], 0, 0, (0, 0))],
                held_shape,
                guesses,
                adjoint_of_mixture[0],
                combined,
            )
            flat = d_logits.transpose(1, 0, 2).reshape(TILE_COUNT, WIDE)
            halves.append(summed(transpose_times(final_low, flat)))
            d_parts.append(d_part)
            entropies.append(entropy)
        head_grads.append(halves)
    contribution = jnp.sum(sum(entropies)) * strength
    d_final, d_branch, d_pre = mlp_back(d_parts, pre_act, fc2_w)
    d_middle, d_attn, d_attended, gain_two, shift_two = mlp_input_back(
        d_final, d_pre, fc1_w, middle, par.gain[:, 1], par.bias[:, 2], proj_w
    )
    d_joined = attention_back(joined, prob_full, d_attended)
    d_started, gain_one, shift_one = attention_input_back(
        d_middle, d_joined, qkv_w, started, par.gain[:, 0], par.bias[:, 0]
    )
    small_grad = small_gradient(
        rows,
        indicator,
        contribution,
        d_started,
        d_joined,
        d_attn,
        d_branch,
        d_pre,
        (gain_one, gain_two),
        (shift_one, shift_two),
    )
    return (
        combined[None],
        lax.psum(contribution, AXES),
        d_started.astype(jnp.bfloat16)[None],
        summed(transpose_times(normed, d_joined)),
        summed(transpose_times(attended, d_attn)),
        summed(transpose_times(normed_two, d_pre)),
        summed(transpose_times(hidden, d_branch)),
        head_whole(*zip(*head_grads)),
        *small_outputs(summed(small_grad), rows),
    )


def paired_step(
    tile_embeddings,
    horizon_indices,
    horizon_tallies,
    member_guesses,
    adjoint_of_mixture,
    triple_projection_matrix,
    attention_outward_matrix,
    widening_matrix,
    narrowing_matrix,
    gating_matrix,
    *small_parts,
):
    rows = triple_projection_matrix.shape[0]
    core = lax.axis_index("fsdp") % 2
    table = places(True)
    marks = jnp.concatenate([core.reshape(1), places(False)[::2] // 2])
    head_marks = jnp.concatenate([core.reshape(1), table[::2] // 2])
    head_table = jnp.concatenate([table, core.reshape(1)])
    seq = Sequence(horizon_tallies)
    indicator, strength = frame_scalars(horizon_indices, horizon_tallies)

    first_own, second_own = seq.run(
        pack_trunk,
        triple_projection_matrix,
        attention_outward_matrix,
        widening_matrix,
        narrowing_matrix,
        *small_parts,
    )
    one, two = RoundFirst(seq, first_own, 1), RoundFirst(seq, second_own, -1)
    one.start()
    two.start()
    head_own = seq.run(pack_head, gating_matrix)
    over = across(head_own)
    one.arrive()
    one.start()
    two.arrive()
    two.start()
    one.arrive()
    one.start()
    one.batch(True)
    two.arrive()
    two.start()
    head_first = seq.run(
        lambda a, b: jnp.concatenate([a, b], axis=0), head_own, over
    )
    one.arrive()
    one.last()
    two.arrive()
    two.last()
    three = AcrossFirst(seq, head_first)
    three.start()
    one.arrive_over()
    one.arrive_last()
    one.batch(False)
    two.arrive_last()
    two.batch(True)
    one.arrive_over()
    one.arrive_batches()
    whole_one = [((0, rows), (0, FIRST_WIDE), 0, 0, 0)]
    whole_two = [((0, 8 * rows), (0, D), 0, 0, 0)]
    index = horizon_indices
    sources_one, moves = plan_moves(one.collect(), whole_one)
    middle, normed, joined, attended, normed_two, par, fc1_b = seq.run(
        functools.partial(trunk_first, table, index, rows, moves), tile_embeddings[0], *sources_one
    )
    three.arrive()
    three.start()
    guesses = seq.run(
        lambda v: lax.optimization_barrier(jnp.transpose(v[0], (1, 0, 2))), member_guesses
    )
    two.arrive_over()
    two.batch(False)
    adjoint = seq.run(lambda v: lax.optimization_barrier(v[0]), adjoint_of_mixture)
    three.arrive()
    three.start()
    two.arrive_over()
    two.arrive_batches()
    three.early()
    three.arrive()
    three.last()
    sources_two, moves_two = plan_moves(two.collect(), whole_two)
    hidden, slope, final_low = seq.run(
        functools.partial(trunk_second, table, rows, moves_two),
        middle,
        normed_two,
        par,
        fc1_b,
        *sources_two,
    )
    three.arrive_last()
    three.third()
    final_other = sibling(final_low)
    normed_other, attended_other = sibling(normed), sibling(attended)
    normed_two_other, hidden_other = sibling(normed_two), sibling(hidden)

    held_shape = (32, rows, WIDE)
    head_fields = [((0, rows), (0, WIDE), 0, 0, 0)]
    state = dict(combined=None, d_parts=[], entropies=[])

    def head(q, own, around):
        sources, moves = plan_moves(around.collect(), head_fields)
        before = () if state["combined"] is None else (state["combined"],)

        def function(final_low, before, *sources):
            return head_pass(
                q,
                own,
                strength.reshape(1),
                head_table,
                final_low,
                list(sources),
                moves,
                held_shape,
                guesses,
                adjoint,
                before[0] if before else None,
            )

        state["combined"], d_logits, d_part, entropy = seq.run(
            function, final_low, before, *sources
        )
        state["d_parts"].append(d_part)
        state["entropies"].append(entropy)
        return d_logits

    make_grad = functools.partial(head_grad, head_marks)
    send = sibling(head(0, False, three))
    own = head(0, True, three)
    sum_one = SumRoundFirst(seq, *seq.run(make_grad, final_low, final_other, own, send))
    send = sibling(head(1, False, three))
    sum_one.step(3)
    own = head(1, True, three)
    sum_one.step(2)
    moves_proj = plan_moves(one.collect(), [((0, rows), (3 * D, 4 * D), 0, 0, 0)])[1]
    moves_qkv = plan_moves(one.collect(), [((0, rows), (0, 3 * D), 0, 0, 0)])[1]
    d_branch, d_pre, d_middle, d_attn, d_attended, d_rows, d_fc1_b = seq.run(
        functools.partial(second_back, table, rows, moves_two, moves_proj, len(sources_two)),
        slope,
        middle,
        par,
        state["d_parts"],
        *sources_two,
        *sources_one,
    )
    d_attn_other, d_fc1_b_other = sibling(d_attn), sibling(d_fc1_b)
    d_branch_other, d_pre_other = sibling(d_branch), sibling(d_pre)
    sum_one.step(1)
    sum_two = SumRoundFirst(seq, *seq.run(make_grad, final_low, final_other, own, send))
    parts = seq.run(
        lambda *ins: ring_grad(
            second_grad_body,
            marks,
            ins,
            (16 * rows, D // 2),
            [(16, 8 * rows, D // 2), (16, 2 * rows, FF // 2)],
            "second_grad",
        ),
        *(hidden, hidden_other, d_branch, d_branch_other),
        *(normed_two, normed_two_other, d_pre, d_pre_other),
    )
    sum_three = SumAcrossFirst(seq, parts, 1)
    sum_three.go_across(0)
    sum_two.step(3)
    sum_one.go_across()
    d_joined, tokens, small_grad = seq.run(
        functools.partial(first_back, table, index, strength.reshape(1), rows, moves_qkv),
        tile_embeddings[0],
        joined,
        par,
        d_middle,
        d_attended,
        d_rows,
        state["entropies"],
        *sources_one,
    )
    d_joined_other, small_other = sibling(d_joined), sibling(small_grad)
    sum_two.step(2)
    sum_three.arrive_across(0)
    sum_three.go_across(1)
    sum_three.step(4)
    parts = seq.run(
        lambda *ins: ring_grad(
            first_grad_body,
            marks,
            ins,
            (2 * rows, 2 * D + 2 * LANES),
            [(16, 2 * rows, 3 * D // 2), (16, 2 * rows, D // 2), (16, 2 * rows, LANES)]
            + [(LANES, D), (32, LANES), (2 * rows, LANES)],
            "first_grad",
        ),
        *(normed, normed_other, d_joined, d_joined_other),
        *(attended, attended_other, d_attn, d_attn_other),
        *(small_grad, small_other, d_fc1_b, d_fc1_b_other),
    )
    sum_four = SumAcrossFirst(seq, parts, -1)
    sum_three.step(3)
    sum_two.step(1)
    combined_result = seq.run(lambda v: lax.optimization_barrier(v[None]), state["combined"])
    total_one = sum_one.finish()
    sum_three.arrive_across(1)
    sum_four.go_across(0)
    sum_three.step(2)
    sum_two.go_across()
    sum_four.arrive_across(0)
    sum_four.go_across(1)
    sum_four.step(4)
    sum_three.step(1)
    sum_four.step(3)
    grad_tokens = tokens[None]
    first = core == 0

    def finish(total, rows_of):
        low, high = rows_of(total, 0, rows), rows_of(total, 1, rows)
        own, other = jnp.where(first, low, high), jnp.where(first, high, low)
        met = sibling(other.astype(jnp.bfloat16)).astype(jnp.float32)
        return jnp.where(first, own, met), jnp.where(first, met, own)

    head_one = finish(total_one, low_or_high)
    sum_four.arrive_across(1)
    sum_four.step(2)
    total = sum_three.finish()
    out_fc2 = jnp.concatenate(finish(total, fc2_rows), axis=1)
    out_fc1 = jnp.concatenate(finish(total, fc1_rows), axis=1)
    sum_four.step(1)
    head_two = finish(sum_two.finish(), low_or_high)
    out_head = head_whole(*zip(head_one, head_two))
    total = sum_four.finish()
    out_small = jnp.where(first, total[:rows, 2 * D :], total[rows:, 2 * D :])
    low, high = finish(total[:, : 2 * D], low_or_high)
    n = 3 * D // 2
    out_fc1_b = out_small[0, LANES : LANES + 4 * rows]
    return (
        combined_result,
        value_of(out_small[0, ROW_DIGIT : ROW_DIGIT + DIGITS]),
        grad_tokens,
        jnp.concatenate([low[:, :n], high[:, :n]], axis=1),
        jnp.concatenate([low[:, n:], high[:, n:]], axis=1),
        out_fc1,
        out_fc2,
        out_head,
        out_small[:, :LEADS],
        out_small[:, ROW_GAIN:ROW_BIAS],
        out_small[:, ROW_BIAS:ROW_QKV],
        out_small[:, ROW_QKV:ROW_DIGIT],
        out_fc1_b,
    )


def solution(mesh):
    split = P(AXES)
    paired = mesh.shape["dp"] == 2 and mesh.shape["fsdp"] == 16
    return jax.shard_map(
        paired_step if paired else plain_step,
        mesh=mesh,
        in_specs=(split, split, P()) + (split,) * 12,
        out_specs=(split, P()) + (split,) * 11,
        check_vma=False,
    )
```

```python
import functools

import jax
import jax.numpy as jnp
from jax import lax
from jax.experimental import pallas as pl
from jax.experimental.pallas import tpu as pltpu
from jax.sharding import PartitionSpec as P

D = 768
HEADS = 12
HD = 64
FF = 3072
MODEL_COUNT = 3
TILE_SAMPLES = 4416
LEADS = 40
TILE_COUNT = 256
EPS = 1e-06
LANES = 128
HALF = 2304
PADDED = 2 * HALF
VMEM = 56 * 1024 * 1024

AXES = ("dp", "fsdp")
RING = [(z, 0) for z in range(4)] + [(z, 1) for z in (3, 2, 1, 0)]


def ring_pairs(step):
    pairs = []
    for spot, (z, x) in enumerate(RING):
        to_z, to_x = RING[(spot + step) % 8]
        for core in range(2):
            pairs.append((z * 4 + x * 2 + core, to_z * 4 + to_x * 2 + core))
    return pairs


def forth(value):
    return lax.ppermute(value, "fsdp", ring_pairs(1))


def back(value):
    return lax.ppermute(value, "fsdp", ring_pairs(-1))


def across(value):
    return lax.ppermute(value, "dp", [(0, 1), (1, 0)])


def exchange_rows(value):
    return lax.all_to_all(value, "dp", 0, 0)


def sibling(value):
    return lax.ppermute(value, "fsdp", [(i, i ^ 1) for i in range(16)])


def places(relative):
    y = lax.axis_index("dp") if relative else 0
    f = lax.axis_index("fsdp")
    z, x, core = f // 4, (f // 2) % 2, f % 2
    spot = jnp.where(x == 0, z, 7 - z)
    i = lax.iota(jnp.int32, 32)
    seat = (spot + (i // 2) % 8) % 8
    pair = jnp.where(seat < 4, seat * 2, (7 - seat) * 2 + 1)
    return ((y + i // 16) % 2) * 16 + pair * 2 + (core + i) % 2


def slot(other_row, distance, other_core):
    return other_row * 16 + (distance % 8) * 2 + other_core


def plan_moves(found, fields):
    sources, moves = [], []
    for source, rows, where in found:
        at = [i for i, s in enumerate(sources) if s is source]
        if not at:
            at = [len(sources)]
            sources.append(source)
        for (f0, f1), (g0, g1), out, out_row, out_col in fields:
            moves.append(
                (at[0], (rows[0] + f0, g0), (f1 - f0, g1 - g0), where, out, (out_row, out_col))
            )
    return sources, moves


def place(sources, moves, shapes, table, shards):
    def body(table_ref, *refs):
        ins, outs = refs[: len(sources)], refs[len(sources) : len(sources) + len(shapes)]
        held, sems, out_sems = refs[len(sources) + len(shapes) : -2], refs[-2], refs[-1]
        run_moves(moves, table_ref, ins, held, sems)
        copies = [
            pltpu.make_async_copy(held[i], outs[i], out_sems.at[i]) for i in range(len(shapes))
        ]
        for copy in copies:
            copy.start()
        for copy in copies:
            copy.wait()

    whole = [(shards,) + s for s in shapes]
    return pl.pallas_call(
        body,
        grid_spec=pltpu.PrefetchScalarGridSpec(
            num_scalar_prefetch=1,
            grid=(1,),
            in_specs=[pl.BlockSpec(memory_space=pl.ANY)] * len(sources),
            out_specs=[pl.BlockSpec(memory_space=pl.ANY)] * len(shapes),
            scratch_shapes=[pltpu.VMEM(s, jnp.bfloat16) for s in whole]
            + [
                pltpu.SemaphoreType.DMA((len(moves),)),
                pltpu.SemaphoreType.DMA((len(shapes),)),
            ],
        ),
        out_shape=[jax.ShapeDtypeStruct(s, jnp.bfloat16) for s in whole],
        compiler_params=pltpu.CompilerParams(vmem_limit_bytes=VMEM),
        name="place",
    )(table, *sources)


def run_moves(moves, table_ref, ins, outs, sems, begin=0):
    copies = []
    for i, (at, (sr, sc), (nr, nc), where, out, (dr, dc)) in enumerate(moves):
        copy = pltpu.make_async_copy(
            ins[at].at[pl.ds(sr, nr), pl.ds(begin + sc, nc)],
            outs[out].at[table_ref[where], pl.ds(dr, nr), pl.ds(dc, nc)],
            sems.at[i],
        )
        copy.start()
        copies.append(copy)
    for copy in copies:
        copy.wait()


def add_low(*values):
    total = values[0].astype(jnp.float32)
    for value in values[1:]:
        total = total + value.astype(jnp.float32)
    return total.astype(jnp.bfloat16)


class Sequence:
    def __init__(self, token):
        self.token = token

    def tie(self, *values):
        out = lax.optimization_barrier((self.token,) + values)
        self.token = out[0]
        return out[1] if len(values) == 1 else out[1:]

    def run(self, function, *values):
        values = lax.optimization_barrier((self.token,) + values)
        self.token = values[0]
        return self.tie(function(*values[1:]))


class Around:
    def __init__(self, seq, first):
        self.seq, self.rights, self.lefts = seq, [first], [first]

    def start(self, right=True, left=True):
        if right:
            self.rights.append(forth(self.rights[-1]))
        if left:
            self.lefts.append(back(self.lefts[-1]))

    def arrive(self, right=True, left=True):
        ends = ([self.rights] if right else []) + ([self.lefts] if left else [])
        met = self.seq.tie(*[end[-1] for end in ends])
        for end, value in zip(ends, met if len(ends) > 1 else (met,)):
            end[-1] = value


class RoundFirst(Around):
    def __init__(self, seq, first, longer):
        super().__init__(seq, first)
        self.longer, self.found = longer, []

    def last(self):
        ends = self.rights if self.longer > 0 else self.lefts
        ends.append(forth(ends[-1]) if self.longer > 0 else back(ends[-1]))

    def arrive_last(self):
        self.arrive(self.longer > 0, self.longer < 0)

    def batch(self, early):
        rights, lefts = self.rights, self.lefts
        r = rights[0].shape[0]
        if early:
            parts, distances = (rights[0], rights[1], lefts[1], rights[2], lefts[2]), (0, -1, 1, -2, 2)
        else:
            end = rights[4] if self.longer > 0 else lefts[4]
            parts, distances = (rights[3], lefts[3], end), (-3, 3, 4)
        joint = self.seq.run(lambda *v: jnp.concatenate(v, axis=0), *parts)
        self.found.append((joint, r, 0, 0, distances))
        self.found.append((sibling(joint), r, 0, 1, distances))
        self.over = across(joint), r, distances

    def arrive_over(self):
        over, r, distances = self.over
        over = self.seq.tie(over)
        self.found.append((over, r, 1, 0, distances))
        self.found.append((sibling(over), r, 1, 1, distances))

    def arrive_batches(self):
        met = self.seq.tie(*[v[0] for v in self.found])
        self.found = [(m,) + v[1:] for m, v in zip(met, self.found)]

    def collect(self):
        return [
            (source, (i * r, (i + 1) * r), slot(other_row, k, other_core))
            for source, r, other_row, other_core, distances in self.found
            for i, k in enumerate(distances)
        ]


class AcrossFirst(Around):
    def __init__(self, seq, first):
        super().__init__(seq, first)
        self.found = []
        self.note(first, [(0, 0), (1, 0)])

    def note(self, joint, spots):
        r = self.rights[0].shape[0] // 2
        for other_core, source in ((0, joint), (1, sibling(joint))):
            for i, (row, k) in enumerate(spots):
                self.found.append((source, (i * r, (i + 1) * r), slot(row, k, other_core)))

    def arrive(self):
        super().arrive()
        k = len(self.rights) - 1
        self.note(self.rights[k], [(0, -k), (1, -k)])
        self.note(self.lefts[k], [(0, k), (1, k)])

    def last(self):
        r = self.rights[0].shape[0] // 2
        right, left = self.seq.run(lambda a, b: (a[:r], b[r:]), self.rights[3], self.lefts[3])
        self.far = [forth(right), back(left)]

    def arrive_last(self):
        self.far = list(self.seq.tie(*self.far))
        for row, array in enumerate(self.far):
            self.note(array, [(row, 4)])

    def collect(self):
        return self.found


ORDER_FIRST = (4, 3, -3)
ORDER_LAST = (2, -2, 1, -1, 0)


class SumAcrossFirst:
    def __init__(self, seq, parts, longer):
        self.seq, self.longer, self.ready = seq, longer, {}
        self.parts = parts
        self.met = [None, None]
        self.right = self.left = None

    def go_across(self, part):
        self.met[part] = exchange_rows(self.parts[part])

    def arrive_across(self, part):
        met = self.seq.tie(self.met[part])
        for i, k in enumerate((ORDER_FIRST, ORDER_LAST)[part]):
            self.ready[k] = (met, i)

    def arrive(self):
        if self.right is None:
            self.left = self.seq.tie(self.left)
        elif self.left is None:
            self.right = self.seq.tie(self.right)
        else:
            self.right, self.left = self.seq.tie(self.right, self.left)

    def step(self, k):
        if k == 4:
            value = self.seq.run(lambda v: add_low(v[0, 0], v[1, 0]), self.ready[4][0])
            if self.longer > 0:
                self.right = forth(value)
            else:
                self.left = back(value)
            return
        (met, i), (_, j) = self.ready[k], self.ready[-k]

        def add(met, right, left):
            return add_low(met[0, i], met[1, i], *right), add_low(met[0, j], met[1, j], *left)

        right = () if self.right is None else (self.right,)
        left = () if self.left is None else (self.left,)
        go_right, go_left = self.seq.run(add, met, right, left)
        self.right, self.left = forth(go_right), back(go_left)

    def finish(self):
        met, i = self.ready[0]

        def add(met, right, left):
            return sum(v.astype(jnp.float32) for v in (met[0, i], met[1, i], right, left))

        return self.seq.run(add, met, self.right, self.left)


class SumRoundFirst:
    def __init__(self, seq, blocks, far_right, far_left):
        self.seq, self.blocks = seq, blocks
        self.right, self.left = forth(far_right), back(far_left)

    def arrive(self):
        self.right, self.left = self.seq.tie(self.right, self.left)

    def step(self, k):
        def add_part(one, two, right, left):
            r = right.shape[0]
            return (
                jnp.concatenate([add_low(one[:r], right), one[r:]], axis=0),
                jnp.concatenate([two[:r], add_low(two[r:], left)], axis=0),
            )

        def add(one, two, right, left):
            return add_low(one, right), add_low(two, left)

        go_right, go_left = self.seq.run(
            add_part if k == 3 else add, self.blocks[k], self.blocks[-k], self.right, self.left
        )
        self.right, self.left = forth(go_right), back(go_left)

    def go_across(self):
        def add(block, right, left):
            r = block.shape[0] // 2
            near = sum(v[:r].astype(jnp.float32) for v in (block, right, left))
            return near, add_low(block[r:], right[r:], left[r:])

        self.near, sent = self.seq.run(add, self.blocks[0], self.right, self.left)
        self.met = across(sent)

    def finish(self):
        return self.seq.run(lambda a, b: a + b.astype(jnp.float32), self.near, self.met)


def layer_norm(values, norm_gain, norm_shift):
    row_mean = jnp.mean(values, axis=-1, keepdims=True)
    centred = values - row_mean
    row_var = jnp.mean(centred * centred, axis=-1, keepdims=True)
    return centred * lax.rsqrt(row_var + EPS) * norm_gain + norm_shift


def exact_gelu(values):
    return jax.nn.gelu(values, approximate=False)


def plain_dot(left, right):
    return jnp.dot(left, right, preferred_element_type=jnp.float32)


def times_transpose(left, right):
    return lax.dot_general(
        left, right, (((1,), (1,)), ((), ())), preferred_element_type=jnp.float32
    )


def transpose_times(left, right):
    return lax.dot_general(
        left, right, (((0,), (0,)), ((), ())), preferred_element_type=jnp.float32
    )


CHUNKS = 2
CHUNK = HALF // CHUNKS
HEAD_TILE = 384
HALF_STEPS = CHUNK // HEAD_TILE
ROWS = 16
COLS = 384


def half_of(own, table_ref):
    core = table_ref[table_ref.shape[0] - 1]
    return core if own else 1 - core


def pixel_block(q, own, j, table_ref):
    return half_of(own, table_ref) * (CHUNKS * HALF_STEPS) + q * HALF_STEPS + j


def head_body(q, own, moves, weight_ref, table_ref, x_ref, guess_ref, adj_ref, *refs):
    ins, refs = refs[:-7], refs[-7:]
    comb_ref, dl_ref, df_ref, ent_ref, logit_ref, held_ref, sems = refs
    j = pl.program_id(0)
    strength = weight_ref[0]
    half = half_of(own, table_ref)
    first_pixel = half * HALF + q * CHUNK + j * HEAD_TILE

    @pl.when(j == 0)
    def _():
        df_ref[...] = jnp.zeros_like(df_ref)
        ent_ref[...] = jnp.zeros_like(ent_ref)
        begin = pl.multiple_of((2 * q + half) * WIDE, LANES)
        run_moves(moves, table_ref, ins, [held_ref], sems, begin)

    x = x_ref[...]

    def weight(e):
        begin = pl.multiple_of(e * CHUNK + j * HEAD_TILE, LANES)
        return held_ref[:, :, pl.ds(begin, HEAD_TILE)].reshape(D, HEAD_TILE)

    for e in range(MODEL_COUNT):
        logit_ref[e] = jnp.dot(x, weight(e), preferred_element_type=jnp.float32)

    for part in range(HEAD_TILE // COLS):
        cols = pl.ds(part * COLS, COLS)
        pixel = first_pixel + part * COLS + lax.broadcasted_iota(jnp.int32, (ROWS, COLS), 1)
        real = pixel < TILE_SAMPLES

        def chunk(i, total):
            rows = pl.ds(pl.multiple_of(i * ROWS, ROWS), ROWS)
            l0, l1, l2 = (logit_ref[e, rows, cols] for e in range(3))
            top = jnp.maximum(jnp.maximum(l0, l1), l2)
            l0, l1, l2 = l0 - top, l1 - top, l2 - top
            e0, e1, e2 = jnp.exp(l0), jnp.exp(l1), jnp.exp(l2)
            norm = e0 + e1 + e2
            inverse = 1.0 / norm
            log_norm = jnp.log(norm)
            b0, b1, b2 = e0 * inverse, e1 * inverse, e2 * inverse
            l0, l1, l2 = l0 - log_norm, l1 - log_norm, l2 - log_norm
            minus_h = b0 * l0 + b1 * l1 + b2 * l2
            g0, g1, g2 = (guess_ref[e, rows, cols].astype(jnp.float32) for e in range(3))
            mixed = b0 * g0 + b1 * g1 + b2 * g2
            comb_ref[rows, cols] = mixed.astype(jnp.bfloat16)
            adj = adj_ref[rows, cols].astype(jnp.float32)
            for e, (b, l, g) in enumerate(((b0, l0, g0), (b1, l1, g1), (b2, l2, g2))):
                d = b * (adj * (g - mixed) - strength * (l - minus_h))
                dl_ref[e, rows, cols] = jnp.where(real, d, 0.0).astype(jnp.bfloat16)
            return total - jnp.where(real, minus_h, 0.0)

        total = lax.fori_loop(
            0,
            TILE_COUNT // ROWS,
            chunk,
            jnp.zeros((ROWS, COLS), jnp.float32),
            unroll=True,
        )
        gathered = total[:, :LANES]
        for k in range(1, COLS // LANES):
            gathered = gathered + total[:, k * LANES : (k + 1) * LANES]
        ent_ref[...] += gathered[:8] + gathered[8:]

    part = None
    for e in range(MODEL_COUNT):
        piece = lax.dot_general(
            dl_ref[e], weight(e), (((1,), (1,)), ((), ())), preferred_element_type=jnp.float32
        )
        part = piece if part is None else part + piece
    df_ref[...] += part


def head_pass(q, own, strength, table, final_low, sources, moves, held_shape, guesses, adjoint, before):
    tile = HEAD_TILE
    extra = [] if before is None else [before]

    def body(*refs):
        refs = refs[:5] + refs[5 + len(extra) :]
        head_body(q, own, moves, *refs)

    d_spec = (MODEL_COUNT, TILE_COUNT, tile)
    return pl.pallas_call(
        body,
        grid_spec=pltpu.PrefetchScalarGridSpec(
            num_scalar_prefetch=2,
            grid=(HALF_STEPS,),
            in_specs=[
                pl.BlockSpec((TILE_COUNT, D), lambda j, s, t: (0, 0)),
                pl.BlockSpec(d_spec, lambda j, s, t: (0, 0, pixel_block(q, own, j, t))),
                pl.BlockSpec((TILE_COUNT, tile), lambda j, s, t: (0, pixel_block(q, own, j, t))),
            ]
            + [pl.BlockSpec(memory_space=pl.ANY)] * (len(extra) + len(sources)),
            out_specs=[
                pl.BlockSpec((TILE_COUNT, tile), lambda j, s, t: (0, pixel_block(q, own, j, t))),
                pl.BlockSpec(d_spec, lambda j, s, t: (0, 0, j)),
                pl.BlockSpec((TILE_COUNT, D), lambda j, s, t: (0, 0)),
                pl.BlockSpec((8, LANES), lambda j, s, t: (0, 0)),
            ],
            scratch_shapes=[
                pltpu.VMEM(d_spec, jnp.float32),
                pltpu.VMEM(held_shape, jnp.bfloat16),
                pltpu.SemaphoreType.DMA((len(moves),)),
            ],
        ),
        out_shape=[
            jax.ShapeDtypeStruct((TILE_COUNT, TILE_SAMPLES), jnp.bfloat16),
            jax.ShapeDtypeStruct((MODEL_COUNT, TILE_COUNT, CHUNK), jnp.bfloat16),
            jax.ShapeDtypeStruct((TILE_COUNT, D), jnp.float32),
            jax.ShapeDtypeStruct((8, LANES), jnp.float32),
        ],
        input_output_aliases={5: 0} if extra else {},
        compiler_params=pltpu.CompilerParams(
            dimension_semantics=("arbitrary",), vmem_limit_bytes=VMEM
        ),
        name="head_pass",
    )(strength, table, final_low, guesses, adjoint, *extra, *sources)


def dot_tokens(left, right):
    return lax.dot_general(left, right, (((0,), (0,)), ((), ())), preferred_element_type=jnp.float32)


def chip_at(marks_ref, row, distance):
    return marks_ref[1 + row * 8 + distance % 8]


HEAD_ORDER = (0, 1, -1, 2, -2, 3, -3)


def head_grad_body(marks_ref, x_mine_ref, x_other_ref, d_mine_ref, d_other_ref, *refs):
    outs, right_ref, left_ref, sum_ref = refs[:7], refs[7], refs[8], refs[9]
    value = dot_tokens(x_mine_ref[...], d_mine_ref[0]) + dot_tokens(x_other_ref[...], d_other_ref[0])
    sum_ref[...] = value.reshape(sum_ref.shape)
    r = sum_ref.shape[1]
    for k, out in zip(HEAD_ORDER, outs):
        for row in (0, 1):
            block = sum_ref[chip_at(marks_ref, row, k)].astype(jnp.bfloat16)
            out[row * r : (row + 1) * r, :] = block
    right_ref[...] = sum_ref[chip_at(marks_ref, 0, 4)].astype(jnp.bfloat16)
    left_ref[...] = sum_ref[chip_at(marks_ref, 1, 4)].astype(jnp.bfloat16)


def head_grad(marks, x_mine, x_other, d_mine, d_other):
    tile = CHUNK
    r = D // 16
    n = MODEL_COUNT * CHUNK
    tall = [2 * r] * 7 + [r] * 2
    outs = pl.pallas_call(
        head_grad_body,
        grid_spec=pltpu.PrefetchScalarGridSpec(
            num_scalar_prefetch=1,
            grid=(MODEL_COUNT,),
            in_specs=[
                pl.BlockSpec((TILE_COUNT, D), lambda e, c: (0, 0)),
                pl.BlockSpec((TILE_COUNT, D), lambda e, c: (0, 0)),
                pl.BlockSpec((1, TILE_COUNT, tile), lambda e, c: (e, 0, 0)),
                pl.BlockSpec((1, TILE_COUNT, tile), lambda e, c: (e, 0, 0)),
            ],
            out_specs=[pl.BlockSpec((h, tile), lambda e, c: (0, e)) for h in tall],
            scratch_shapes=[pltpu.VMEM((16, r, tile), jnp.float32)],
        ),
        out_shape=[jax.ShapeDtypeStruct((h, n), jnp.bfloat16) for h in tall],
        compiler_params=pltpu.CompilerParams(
            dimension_semantics=("arbitrary",), vmem_limit_bytes=VMEM
        ),
        name="head_grad",
    )(marks, x_mine, x_other, d_mine, d_other)
    return dict(zip(HEAD_ORDER, outs[:7])), outs[7], outs[8]


def ring_rows(marks_ref, outs, write):
    for row in (0, 1):
        for out, order in zip(outs, (ORDER_FIRST, ORDER_LAST)):
            for i, k in enumerate(order):
                write(out, row, i, chip_at(marks_ref, row, k))


def core_half(ref, marks_ref):
    n = ref.shape[1] // 2
    return ref[:, pl.ds(pl.multiple_of(marks_ref[0] * n, LANES), n)]


def paired_product(marks_ref, x, x_other, d, d_other):
    return dot_tokens(x[...], core_half(d, marks_ref)) + dot_tokens(
        x_other[...], core_half(d_other, marks_ref)
    )


def second_grad_body(marks_ref, *refs):
    ins, outs, (fc2_ref, fc1_ref) = refs[:8], refs[8:10], refs[10:]
    fc2_ref[...] = paired_product(marks_ref, *ins[:4]).reshape(fc2_ref.shape)
    fc1_ref[...] = paired_product(marks_ref, *ins[4:]).reshape(fc1_ref.shape)
    r4, wide = fc2_ref.shape[1:]
    r = fc1_ref.shape[1]

    def write(out, row, i, chip):
        out[row, i, :r4, :] = fc2_ref[chip].astype(jnp.bfloat16)
        for k in range(4):
            block = fc1_ref[chip, :, k * wide : (k + 1) * wide].astype(jnp.bfloat16)
            out[row, i, r4 + k * r : r4 + (k + 1) * r, :] = block

    ring_rows(marks_ref, outs, write)


def first_grad_body(marks_ref, *refs):
    ins, outs, refs = refs[:12], refs[12:21], refs[21:]
    qkv_ref, proj_ref, small_ref, flat_ref, hidden_ref, block_ref = refs
    qkv_ref[...] = paired_product(marks_ref, *ins[:4]).reshape(qkv_ref.shape)
    proj_ref[...] = paired_product(marks_ref, *ins[4:8]).reshape(proj_ref.shape)
    flat_ref[...] = jnp.zeros_like(flat_ref)
    flat_ref[: ins[8].shape[0], :] = ins[8][...] + ins[9][...]
    small_ref[...] = flat_ref[...].T.reshape(small_ref.shape)
    shards = hidden_ref.shape[0]
    r, wide = qkv_ref.shape[1] // 2, FF // shards
    hidden_ref[...] = jnp.zeros_like(hidden_ref)
    for d in range(shards):
        cols = slice(d * wide, (d + 1) * wide)
        hidden_ref[d : d + 1, :wide] = ins[10][:, cols] + ins[11][:, cols]
    block_ref[...] = jnp.zeros_like(block_ref)
    n, m = qkv_ref.shape[2], qkv_ref.shape[2] + proj_ref.shape[2]

    def write(out, at, chip):
        rows = slice(at, at + 2 * r)
        out[rows, :n] = qkv_ref[chip].astype(jnp.bfloat16)
        out[rows, n:m] = proj_ref[chip].astype(jnp.bfloat16)
        out[rows, m : m + LANES] = small_ref[chip].astype(jnp.bfloat16)
        block_ref[0:1, :] = hidden_ref[pl.ds(2 * chip, 1), :]
        block_ref[r : r + 1, :] = hidden_ref[pl.ds(2 * chip + 1, 1), :]
        out[rows, m + LANES :] = block_ref[...].astype(jnp.bfloat16)

    for k, out in zip(HEAD_ORDER, outs):
        for row in (0, 1):
            write(out, row * 2 * r, chip_at(marks_ref, row, k))
    for row, out in enumerate(outs[7:]):
        write(out, 0, chip_at(marks_ref, row, 4))


def round_grad(body, marks, ins, block, scratch, name):
    r, n = block
    shapes = [(2 * r, n)] * 7 + [(r, n)] * 2
    outs = pl.pallas_call(
        body,
        grid_spec=pltpu.PrefetchScalarGridSpec(
            num_scalar_prefetch=1,
            grid=(1,),
            in_specs=[pl.BlockSpec(v.shape, lambda i, m: (0, 0)) for v in ins],
            out_specs=[pl.BlockSpec(s, lambda i, m: (0, 0)) for s in shapes],
            scratch_shapes=[pltpu.VMEM(s, jnp.float32) for s in scratch],
        ),
        out_shape=[jax.ShapeDtypeStruct(s, jnp.bfloat16) for s in shapes],
        compiler_params=pltpu.CompilerParams(vmem_limit_bytes=VMEM),
        name=name,
    )(marks, *ins)
    return dict(zip(HEAD_ORDER, outs[:7])), outs[7], outs[8]


def ring_grad(body, marks, ins, block, scratch, name):
    shapes = [(2, 3) + block, (2, 5) + block]
    return pl.pallas_call(
        body,
        grid_spec=pltpu.PrefetchScalarGridSpec(
            num_scalar_prefetch=1,
            grid=(1,),
            in_specs=[pl.BlockSpec(v.shape, lambda i, m: (0, 0)) for v in ins],
            out_specs=[pl.BlockSpec(s, lambda i, m: (0, 0, 0, 0)) for s in shapes],
            scratch_shapes=[pltpu.VMEM(s, jnp.float32) for s in scratch],
        ),
        out_shape=[jax.ShapeDtypeStruct(s, jnp.bfloat16) for s in shapes],
        compiler_params=pltpu.CompilerParams(vmem_limit_bytes=VMEM),
        name=name,
    )(marks, *ins)


def pack_small(lead_w, gains, biases, qkv_b, fc1_b, rows):
    value = jnp.concatenate([lead_w, gains, biases, qkv_b, fc1_b.reshape(4, rows).T], axis=1)
    return jnp.pad(value, ((0, 0), (0, LANES - value.shape[1])))


def split_small(small):
    at, found = 0, []
    for width in (LEADS, 2, 4, 2, 4):
        found.append(small[:, at : at + width])
        at += width
    return found


WIDE = MODEL_COUNT * CHUNK


def head_chunks(value):
    r = value.shape[0]
    value = value.reshape(r, MODEL_COUNT, TILE_SAMPLES)
    value = jnp.pad(value, ((0, 0), (0, 0), (0, PADDED - TILE_SAMPLES)))
    value = value.reshape(r, MODEL_COUNT, 2, CHUNKS, CHUNK).transpose(0, 2, 1, 3, 4)
    return [value[:, :, :, q].reshape(r, 2 * WIDE) for q in range(CHUNKS)]


def pack_trunk_body(qkv_ref, proj_ref, fc1_ref, fc2_ref, lead_ref, gain_ref, bias_ref, qkv_b_ref, fc1_b_ref, *refs):
    one_ref, two_ref, flat_ref, tall_ref = refs
    r = qkv_ref.shape[0]
    flat_ref[...] = jnp.zeros_like(flat_ref)
    at = LEADS
    for ref in (gain_ref, bias_ref, qkv_b_ref):
        rows = ref.shape[0]
        flat_ref[at : at + rows, :r] = ref[...].astype(jnp.float32)
        at += rows
    tall_ref[...] = flat_ref[...].T
    tall_ref[:r, :LEADS] = lead_ref[...].astype(jnp.float32)
    flat_ref[...] = jnp.zeros_like(flat_ref)
    flat_ref[0:1, : 4 * r] = fc1_b_ref[...].astype(jnp.float32)
    n = 4 * D
    one_ref[:, : 3 * D] = qkv_ref[...]
    one_ref[:, 3 * D : n] = proj_ref[...]
    one_ref[:, n : n + LANES] = tall_ref[:r, :].astype(jnp.bfloat16)
    one_ref[:, n + LANES :] = flat_ref[:r, :].astype(jnp.bfloat16)
    two_ref[: 4 * r, :] = fc2_ref[...]
    for k in range(4):
        two_ref[(4 + k) * r : (5 + k) * r, :] = fc1_ref[:, k * D : (k + 1) * D]


def pack_trunk(qkv, proj, fc1, fc2, lead_w, gains, biases, qkv_b, fc1_b):
    r = qkv.shape[0]
    return pl.pallas_call(
        pack_trunk_body,
        out_shape=[
            jax.ShapeDtypeStruct((r, 4 * D + 2 * LANES), jnp.bfloat16),
            jax.ShapeDtypeStruct((8 * r, D), jnp.bfloat16),
        ],
        scratch_shapes=[pltpu.VMEM((LANES, LANES), jnp.float32)] * 2,
        compiler_params=pltpu.CompilerParams(vmem_limit_bytes=VMEM),
        name="pack_trunk",
    )(qkv, proj, fc1, fc2, lead_w, gains.T, biases.T, qkv_b.T, fc1_b.reshape(1, 4 * r))


def pack_head_body(head_ref, out):
    r = head_ref.shape[0]
    for q in range(CHUNKS):
        for h in range(2):
            first = h * HALF + q * CHUNK
            real = min(CHUNK, TILE_SAMPLES - first)
            for e in range(MODEL_COUNT):
                begin, at = e * TILE_SAMPLES + first, ((2 * q + h) * MODEL_COUNT + e) * CHUNK
                part = head_ref[:, begin : begin + real]
                if real < CHUNK:
                    part = jnp.concatenate([part, jnp.zeros((r, CHUNK - real), part.dtype)], axis=1)
                out[:, at : at + CHUNK] = part


def pack_head(head):
    return pl.pallas_call(
        pack_head_body,
        out_shape=jax.ShapeDtypeStruct((head.shape[0], 2 * CHUNKS * WIDE), jnp.bfloat16),
        compiler_params=pltpu.CompilerParams(vmem_limit_bytes=VMEM),
        name="pack_head",
    )(head)


def head_whole(low, high):
    r = low[0].shape[0]
    parts = [v.reshape(r, MODEL_COUNT, CHUNK) for v in (*low, *high)]
    return jnp.concatenate(parts, axis=2)[:, :, :TILE_SAMPLES].reshape(r, MODEL_COUNT * TILE_SAMPLES)


DIGITS = 16
BASE = 8.0


def digits_of(value):
    powers = jnp.asarray([BASE**k for k in range(DIGITS + 1)], jnp.float32)
    floors = jnp.floor(value * 32.0 * powers)
    return floors[1:] - BASE * floors[:-1]


def value_of(digits):
    powers = jnp.asarray([BASE ** -(k + 1) / 32.0 for k in range(DIGITS)], jnp.float32)
    return jnp.sum(digits * powers)


SCALE = HD ** (-0.5)
ROW_GAIN, ROW_BIAS, ROW_QKV, ROW_DIGIT = LEADS, LEADS + 2, LEADS + 6, LEADS + 8
SMALL_ROWS = 64
FIRST_WIDE = 4 * D + 2 * LANES


def slab(ref, first, n):
    shards, rows = ref.shape[:2]
    return ref[:, :, first : first + n].reshape(shards * rows, n)


def dot_last(left, right):
    return lax.dot_general(left, right, (((1,), (1,)), ((), ())), preferred_element_type=jnp.float32)


def normalised(values):
    centred = values - jnp.mean(values, axis=-1, keepdims=True)
    inverse = lax.rsqrt(jnp.mean(centred * centred, axis=-1, keepdims=True) + EPS)
    return centred * inverse, inverse


def norm_back(values, d_out, gain):
    unit, inverse = normalised(values)
    d_unit = d_out * gain
    mean_one = jnp.mean(d_unit, axis=-1, keepdims=True)
    mean_two = jnp.mean(d_unit * unit, axis=-1, keepdims=True)
    d_values = inverse * (d_unit - mean_one - unit * mean_two)
    return (
        d_values,
        jnp.sum(d_out * unit, axis=0, keepdims=True),
        jnp.sum(d_out, axis=0, keepdims=True),
    )


def head_masks():
    lane = lax.broadcasted_iota(jnp.int32, (1, 2 * HD), 1)
    low = lane < HD
    return low, [m.astype(jnp.float32).astype(jnp.bfloat16) for m in (low, lane >= HD)]


def softmax_of(scores):
    expd = jnp.exp(scores - jnp.max(scores, axis=-1, keepdims=True))
    return expd * (1.0 / jnp.sum(expd, axis=-1, keepdims=True))


def trunk_first_body(moves, table_ref, index_ref, frame_ref, *refs):
    ins, refs = refs[:-9], refs[-9:]
    middle_ref, normed_ref, joined_ref, attended_ref, normed_two_ref, par_ref, fc1_b_ref = refs[:7]
    held_ref, sems = refs[7:]
    run_moves(moves, table_ref, ins, [held_ref], sems)
    par_ref[...] = slab(held_ref, 4 * D, LANES).astype(jnp.float32).T
    shards = held_ref.shape[0]
    wide = FF // shards
    for d in range(shards):
        row = held_ref[d, 0:1, 4 * D + LANES : 4 * D + LANES + wide]
        fc1_b_ref[:, d * wide : (d + 1) * wide] = row.astype(jnp.float32)

    def row(i):
        return par_ref[i : i + 1, :]

    started = frame_ref[...].astype(jnp.float32) + par_ref[pl.ds(index_ref[0], 1), :]
    normed = (normalised(started)[0] * row(ROW_GAIN) + row(ROW_BIAS)).astype(jnp.bfloat16)
    normed_ref[...] = normed
    for i, shift in enumerate((row(ROW_QKV), None, row(ROW_QKV + 1))):
        part = jnp.dot(normed, slab(held_ref, i * D, D), preferred_element_type=jnp.float32)
        part = part if shift is None else part + shift
        joined_ref[:, i * D : (i + 1) * D] = part.astype(jnp.bfloat16)
    low, masks = head_masks()
    for p in range(HEADS // 2):
        at = p * 2 * HD
        q, k, v = (joined_ref[:, i * D + at : i * D + at + 2 * HD] for i in range(3))
        outs = []
        for mask in masks:
            probs = softmax_of(dot_last(q * mask, k) * SCALE).astype(jnp.bfloat16)
            outs.append(jnp.dot(probs, v, preferred_element_type=jnp.float32))
        attended_ref[:, at : at + 2 * HD] = jnp.where(low, *outs).astype(jnp.bfloat16)
    middle = (
        started
        + jnp.dot(attended_ref[...], slab(held_ref, 3 * D, D), preferred_element_type=jnp.float32)
        + row(ROW_BIAS + 1)
    )
    middle_ref[...] = middle
    normed_two = normalised(middle)[0] * row(ROW_GAIN + 1) + row(ROW_BIAS + 2)
    normed_two_ref[...] = normed_two.astype(jnp.bfloat16)


def trunk_call(body, scalars, ins, sources, outs, scratch, name):
    any_spec = pl.BlockSpec(memory_space=pl.ANY)

    def whole(shape):
        return pl.BlockSpec(shape, lambda i, *s: (0,) * len(shape))

    return pl.pallas_call(
        body,
        grid_spec=pltpu.PrefetchScalarGridSpec(
            num_scalar_prefetch=len(scalars),
            grid=(1,),
            in_specs=[whole(v.shape) for v in ins] + [any_spec] * len(sources),
            out_specs=[whole(s) for s, _ in outs],
            scratch_shapes=scratch,
        ),
        out_shape=[jax.ShapeDtypeStruct(*o) for o in outs],
        compiler_params=pltpu.CompilerParams(vmem_limit_bytes=VMEM),
        name=name,
    )(*scalars, *ins, *sources)


def trunk_first(table, index, rows, moves, frame, *sources):
    flat, low, full = (TILE_COUNT, D), jnp.bfloat16, jnp.float32
    return trunk_call(
        functools.partial(trunk_first_body, moves),
        (table, index),
        (frame,),
        sources,
        [
            (flat, full),
            (flat, low),
            ((TILE_COUNT, 3 * D), low),
            (flat, low),
            (flat, low),
            ((LANES, D), full),
            ((1, FF), full),
        ],
        [
            pltpu.VMEM((32, rows, FIRST_WIDE), low),
            pltpu.SemaphoreType.DMA((len(moves),)),
        ],
        "trunk_first",
    )


def trunk_second_body(moves, table_ref, middle_ref, normed_two_ref, par_ref, fc1_b_ref, *refs):
    ins, refs = refs[:-5], refs[-5:]
    hidden_ref, slope_ref, final_ref, held_ref, sems = refs
    run_moves(moves, table_ref, ins, [held_ref], sems)
    total = middle_ref[...] + par_ref[ROW_BIAS + 3 : ROW_BIAS + 4, :]
    normed_two = normed_two_ref[...]
    for k in range(4):
        cols = slice(k * D, (k + 1) * D)
        pre = jnp.dot(normed_two, widening(held_ref, k), preferred_element_type=jnp.float32)
        pre = pre + fc1_b_ref[:, cols]
        share = 0.5 * (1.0 + lax.erf(pre * (0.5**0.5)))
        density = jnp.exp(-0.5 * pre * pre) * ((0.5 / 3.141592653589793) ** 0.5)
        slope_ref[:, cols] = share + pre * density
        hidden = (pre * share).astype(jnp.bfloat16)
        hidden_ref[:, cols] = hidden
        weight = narrowing(held_ref, k)
        total += jnp.dot(hidden, weight, preferred_element_type=jnp.float32)
    final_ref[...] = total.astype(jnp.bfloat16)


def second_scratch(rows):
    return [pltpu.VMEM((32, 8 * rows, D), jnp.bfloat16)]


def narrowing(held_ref, k):
    shards, rows = held_ref.shape[:2]
    return held_ref[k * shards // 4 : (k + 1) * shards // 4, : rows // 2, :].reshape(D, D)


def widening(held_ref, k):
    rows = held_ref.shape[1] // 8
    return held_ref[:, (4 + k) * rows : (5 + k) * rows, :].reshape(D, D)


def trunk_second(table, rows, moves, middle, normed_two, par, fc1_b, *sources):
    return trunk_call(
        functools.partial(trunk_second_body, moves),
        (table,),
        (middle, normed_two, par, fc1_b),
        sources,
        [
            ((TILE_COUNT, FF), jnp.bfloat16),
            ((TILE_COUNT, FF), jnp.float32),
            ((TILE_COUNT, D), jnp.bfloat16),
        ],
        second_scratch(rows) + [pltpu.SemaphoreType.DMA((len(moves),))],
        "trunk_second",
    )


def second_back_body(moves_two, moves_one, n_two, table_ref, slope_ref, middle_ref, par_ref, *refs):
    d_parts, refs = refs[: 2 * CHUNKS], refs[2 * CHUNKS :]
    ins, refs = refs[:-11], refs[-11:]
    branch_ref, pre_ref, middle_d_ref, attn_ref, attended_ref, rows_ref, fc1_b_ref = refs[:7]
    held_ref, proj_ref, sems_two, sems_one = refs[7:]
    run_moves(moves_one, table_ref, ins[n_two:], [proj_ref], sems_one)
    run_moves(moves_two, table_ref, ins[:n_two], [held_ref], sems_two)
    d_final = d_parts[0][...]
    for part in d_parts[1:]:
        d_final = d_final + part[...]
    d_branch = d_final.astype(jnp.bfloat16)
    branch_ref[...] = d_branch
    d_normed = None
    for k in range(4):
        cols = slice(k * D, (k + 1) * D)
        d_hidden = dot_last(d_branch, narrowing(held_ref, k))
        d_pre = (d_hidden * slope_ref[:, cols]).astype(jnp.bfloat16)
        pre_ref[:, cols] = d_pre
        fc1_b_ref[:, cols] = jnp.sum(d_pre.astype(jnp.float32), axis=0, keepdims=True)
        part = dot_last(d_pre, widening(held_ref, k))
        d_normed = part if d_normed is None else d_normed + part
    gain = par_ref[ROW_GAIN + 1 : ROW_GAIN + 2, :]
    d_part, d_gain, d_shift = norm_back(middle_ref[...], d_normed, gain)
    d_middle = d_final + d_part
    middle_d_ref[...] = d_middle
    d_attn = d_middle.astype(jnp.bfloat16)
    attn_ref[...] = d_attn
    attended_ref[...] = dot_last(d_attn, slab(proj_ref, 0, D)).astype(jnp.bfloat16)
    sums = [jnp.sum(v.astype(jnp.float32), axis=0, keepdims=True) for v in (d_attn, d_branch)]
    rows_ref[...] = jnp.zeros_like(rows_ref)
    for i, value in enumerate((d_gain, d_shift, *sums)):
        rows_ref[i : i + 1, :] = value


def second_back(table, rows, moves_two, moves_one, n_two, slope, middle, par, d_parts, *sources):
    flat, low, full = (TILE_COUNT, D), jnp.bfloat16, jnp.float32
    return trunk_call(
        functools.partial(second_back_body, moves_two, moves_one, n_two),
        (table,),
        (slope, middle, par, *d_parts),
        sources,
        [
            (flat, low),
            ((TILE_COUNT, FF), low),
            (flat, full),
            (flat, low),
            (flat, low),
            ((8, D), full),
            ((1, FF), full),
        ],
        second_scratch(rows)
        + [
            pltpu.VMEM((32, rows, D), low),
            pltpu.SemaphoreType.DMA((len(moves_two),)),
            pltpu.SemaphoreType.DMA((len(moves_one),)),
        ],
        "second_back",
    )


def first_back_body(moves, n_ent, table_ref, index_ref, weight_ref, frame_ref, joined_ref, par_ref, middle_d_ref, attended_ref, rows_ref, *refs):
    ents, refs = refs[:n_ent], refs[n_ent:]
    ins, refs = refs[:-5], refs[-5:]
    d_joined_ref, tokens_ref, small_ref, qkv_ref, sems = refs
    run_moves(moves, table_ref, ins, [qkv_ref], sems)
    small_ref[...] = jnp.zeros_like(small_ref)
    _, masks = head_masks()
    for p in range(HEADS // 2):
        at = p * 2 * HD
        q, k, v = (joined_ref[:, i * D + at : i * D + at + 2 * HD] for i in range(3))
        d_out = attended_ref[:, at : at + 2 * HD]
        totals = [None] * 3
        for mask in masks:
            q_one, k_one, d_one = q * mask, k * mask, d_out * mask
            probs = softmax_of(dot_last(q_one, k) * SCALE)
            d_probs = dot_last(d_one, v)
            inner = jnp.sum(probs * d_probs, axis=-1, keepdims=True)
            d_scores = (probs * (d_probs - inner)).astype(jnp.bfloat16)
            parts = (
                jnp.dot(d_scores, k_one, preferred_element_type=jnp.float32),
                dot_tokens(d_scores, q_one),
                dot_tokens(probs.astype(jnp.bfloat16), d_one),
            )
            totals = [a if b is None else a + b for a, b in zip(parts, totals)]
        for i, scale in enumerate((SCALE, SCALE, 1.0)):
            d_joined_ref[:, i * D + at : i * D + at + 2 * HD] = (totals[i] * scale).astype(
                jnp.bfloat16
            )
    d_normed = None
    for i in range(3):
        block = d_joined_ref[:, i * D : (i + 1) * D]
        if i != 1:
            at = ROW_QKV + i // 2
            total = jnp.sum(block.astype(jnp.float32), axis=0, keepdims=True)
            small_ref[at : at + 1, :] = total
        part = dot_last(block, slab(qkv_ref, i * D, D))
        d_normed = part if d_normed is None else d_normed + part
    started = frame_ref[...].astype(jnp.float32) + par_ref[pl.ds(index_ref[0], 1), :]
    gain = par_ref[ROW_GAIN : ROW_GAIN + 1, :]
    d_part, d_gain, d_shift = norm_back(started, d_normed, gain)
    d_started = middle_d_ref[...] + d_part
    tokens_ref[...] = d_started.astype(jnp.bfloat16)
    small_ref[pl.ds(index_ref[0], 1), :] = jnp.sum(d_started, axis=0, keepdims=True)
    small_ref[ROW_GAIN : ROW_GAIN + 1, :] = d_gain
    small_ref[ROW_BIAS : ROW_BIAS + 1, :] = d_shift
    small_ref[ROW_GAIN + 1 : ROW_GAIN + 2, :] = rows_ref[0:1, :]
    small_ref[ROW_BIAS + 2 : ROW_BIAS + 3, :] = rows_ref[1:2, :]
    small_ref[ROW_BIAS + 1 : ROW_BIAS + 2, :] = rows_ref[2:3, :]
    small_ref[ROW_BIAS + 3 : ROW_BIAS + 4, :] = rows_ref[3:4, :]
    entropy = ents[0][...]
    for ent in ents[1:]:
        entropy = entropy + ent[...]
    entropy = jnp.sum(jnp.sum(entropy, axis=0, keepdims=True), axis=1, keepdims=True)
    value = jnp.broadcast_to(entropy * weight_ref[0] * 32.0, (1, D))
    before = jnp.floor(value)
    for k in range(DIGITS):
        value = value * BASE
        floor = jnp.floor(value)
        small_ref[ROW_DIGIT + k : ROW_DIGIT + k + 1, :] = floor - BASE * before
        before = floor


def first_back(table, index, strength, rows, moves, frame, joined, par, d_middle, d_attended, d_rows, ents, *sources):
    return trunk_call(
        functools.partial(first_back_body, moves, len(ents)),
        (table, index, strength),
        (frame, joined, par, d_middle, d_attended, d_rows, *ents),
        sources,
        [
            ((TILE_COUNT, 3 * D), jnp.bfloat16),
            ((TILE_COUNT, D), jnp.bfloat16),
            ((SMALL_ROWS, D), jnp.float32),
        ],
        [
            pltpu.VMEM((32, rows, 3 * D), jnp.bfloat16),
            pltpu.SemaphoreType.DMA((len(moves),)),
        ],
        "first_back",
    )


def low_or_high(value, core, rows):
    return value[core * rows : (core + 1) * rows]


def fc2_rows(value, core, rows):
    return value[core * 4 * rows : (core + 1) * 4 * rows]


def fc1_rows(value, core, rows):
    begin = 8 * rows + core * rows
    return jnp.concatenate(
        [value[begin + 2 * k * rows : begin + (2 * k + 1) * rows] for k in range(4)], axis=1
    )


class Parameters:
    def __init__(self, small_all, rows):
        lead_w, gain_all, bias_all, qkv_b, fc1_b = split_small(small_all)
        self.lead = lead_w.astype(jnp.float32)
        self.gain = gain_all.astype(jnp.float32)
        self.bias = bias_all.astype(jnp.float32)
        qkv_b = qkv_b.astype(jnp.float32)
        self.offset = jnp.concatenate([qkv_b[:, 0], jnp.zeros_like(qkv_b[:, 0]), qkv_b[:, 1]])
        self.fc1 = (
            fc1_b.astype(jnp.float32).reshape(D // rows, rows, 4).transpose(0, 2, 1).reshape(FF)
        )


    def parts(self):
        return self.lead, self.gain, self.bias, self.offset, self.fc1


def attention_input(frame, lead_vector, gain, bias, offset, qkv_w):
    started = frame.astype(jnp.float32) + lead_vector[None, :]
    normed = layer_norm(started, gain, bias).astype(jnp.bfloat16)
    joined = (plain_dot(normed, qkv_w) + offset).astype(jnp.bfloat16)
    return started, normed, joined


def heads_of(joined):
    return [joined[:, i * D : (i + 1) * D].reshape(TILE_COUNT, HEADS, HD) for i in range(3)]


def attention(joined):
    queries, keys, values = heads_of(joined)
    scores = jnp.einsum("qhd,khd->hqk", queries, keys, preferred_element_type=jnp.float32) * SCALE
    row_top = jnp.max(scores, axis=-1, keepdims=True)
    expd = jnp.exp(scores - row_top)
    prob_full = expd / jnp.sum(expd, axis=-1, keepdims=True)
    probs_low = prob_full.astype(jnp.bfloat16)
    attended = jnp.einsum("hqk,khd->qhd", probs_low, values, preferred_element_type=jnp.float32)
    return prob_full, attended.astype(jnp.bfloat16).reshape(TILE_COUNT, D)


def mlp_input(started, attended, proj_w, proj_bias, gain, bias):
    middle = started + plain_dot(attended, proj_w) + proj_bias
    return middle, layer_norm(middle, gain, bias).astype(jnp.bfloat16)


def mlp(middle, normed_two, fc1_w, fc1_b, fc2_w, fc2_b):
    pre_act = plain_dot(normed_two, fc1_w) + fc1_b
    hidden = exact_gelu(pre_act).astype(jnp.bfloat16)
    final_sum = middle + plain_dot(hidden, fc2_w) + fc2_b
    return pre_act, hidden, final_sum.astype(jnp.bfloat16)


def mlp_back(d_parts, pre_act, fc2_w):
    d_final = sum(d_parts)
    d_branch = d_final.astype(jnp.bfloat16)
    d_hidden = times_transpose(d_branch, fc2_w)
    _, gelu_back = jax.vjp(exact_gelu, pre_act)
    return d_final, d_branch, gelu_back(d_hidden)[0].astype(jnp.bfloat16)


def mlp_input_back(d_final, d_pre, fc1_w, middle, gain, bias, proj_w):
    d_normed_two = times_transpose(d_pre, fc1_w)
    _, norm_back = jax.vjp(layer_norm, middle, gain, bias)
    d_part, d_gain, d_shift = norm_back(d_normed_two)
    d_middle = d_final + d_part
    d_attn = d_middle.astype(jnp.bfloat16)
    d_attended = times_transpose(d_attn, proj_w).astype(jnp.bfloat16)
    return d_middle, d_attn, d_attended, d_gain, d_shift


def attention_back(joined, prob_full, d_attended):
    queries, keys, values = heads_of(joined)
    d_attended = d_attended.reshape(TILE_COUNT, HEADS, HD)
    probs_low = prob_full.astype(jnp.bfloat16)
    d_values = jnp.einsum("hqk,qhd->khd", probs_low, d_attended, preferred_element_type=jnp.float32)
    d_prob = jnp.einsum("qhd,khd->hqk", d_attended, values, preferred_element_type=jnp.float32)
    d_score = (
        prob_full * (d_prob - jnp.sum(prob_full * d_prob, axis=-1, keepdims=True))
    ).astype(jnp.bfloat16)
    d_queries = (
        jnp.einsum("hqk,khd->qhd", d_score, keys, preferred_element_type=jnp.float32) * SCALE
    )
    d_keys = (
        jnp.einsum("hqk,qhd->khd", d_score, queries, preferred_element_type=jnp.float32) * SCALE
    )
    return jnp.concatenate(
        [v.reshape(TILE_COUNT, D) for v in (d_queries, d_keys, d_values)], axis=1
    ).astype(jnp.bfloat16)


def attention_input_back(d_middle, d_joined, qkv_w, started, gain, bias):
    d_normed = times_transpose(d_joined, qkv_w)
    _, norm_back = jax.vjp(layer_norm, started, gain, bias)
    d_part, d_gain, d_shift = norm_back(d_normed)
    return d_middle + d_part, d_gain, d_shift


def small_gradient(rows, horizon_indicator, contribution, d_started, d_joined, d_attn, d_branch, d_pre, gains, shifts):
    def column_sum(value):
        return jnp.sum(value.astype(jnp.float32), axis=0)

    joined_sums = column_sum(d_joined)
    columns = jnp.stack(
        [
            *gains,
            shifts[0],
            column_sum(d_attn),
            shifts[1],
            column_sum(d_branch),
            joined_sums[:D],
            joined_sums[2 * D :],
        ],
        axis=1,
    )
    hidden_columns = column_sum(d_pre).reshape(D // rows, 4, rows).transpose(0, 2, 1).reshape(D, 4)
    return jnp.concatenate(
        [
            jnp.sum(d_started, axis=0)[:, None] * horizon_indicator[None, :],
            columns,
            hidden_columns,
            jnp.broadcast_to(digits_of(contribution)[None, :], (D, DIGITS)),
            jnp.zeros((D, LANES - LEADS - 12 - DIGITS), jnp.float32),
        ],
        axis=1,
    ).astype(jnp.bfloat16)


def small_outputs(value, rows):
    return (
        value[:, :LEADS],
        value[:, LEADS : LEADS + 2],
        value[:, LEADS + 2 : LEADS + 6],
        value[:, LEADS + 6 : LEADS + 8],
        value[:, LEADS + 8 : LEADS + 12].T.reshape(4 * rows),
    )


def frame_scalars(horizon_indices, horizon_tallies):
    indicator = (horizon_indices[0] == lax.iota(jnp.int32, LEADS)).astype(jnp.float32)
    frame_count = jnp.sum(indicator * horizon_tallies.astype(jnp.float32))
    return indicator, 1.0 / (frame_count * (LEADS * TILE_COUNT * TILE_SAMPLES))


def plain_step(
    tile_embeddings,
    horizon_indices,
    horizon_tallies,
    member_guesses,
    adjoint_of_mixture,
    triple_projection_matrix,
    attention_outward_matrix,
    widening_matrix,
    narrowing_matrix,
    gating_matrix,
    *small_parts,
):
    rows = triple_projection_matrix.shape[0]
    whole = functools.partial(lax.all_gather, axis_name=AXES, axis=0, tiled=True)

    def summed(value):
        return lax.psum_scatter(
            value.astype(jnp.bfloat16), AXES, scatter_dimension=0, tiled=True
        ).astype(jnp.float32)

    qkv_w, proj_w = whole(triple_projection_matrix), whole(attention_outward_matrix)
    fc1_w, fc2_w = whole(widening_matrix), whole(narrowing_matrix)
    par = Parameters(whole(pack_small(*small_parts, rows)), rows)
    indicator, strength = frame_scalars(horizon_indices, horizon_tallies)
    guesses = jnp.transpose(member_guesses[0], (1, 0, 2))
    lead_vector = jnp.sum(par.lead * indicator[None, :], axis=1)
    started, normed, joined = attention_input(
        tile_embeddings[0], lead_vector, par.gain[:, 0], par.bias[:, 0], par.offset, qkv_w
    )
    prob_full, attended = attention(joined)
    middle, normed_two = mlp_input(
        started, attended, proj_w, par.bias[:, 1], par.gain[:, 1], par.bias[:, 2]
    )
    pre_act, hidden, final_low = mlp(middle, normed_two, fc1_w, par.fc1, fc2_w, par.bias[:, 3])
    table = jnp.asarray([0, 1], jnp.int32)
    held_shape = (1, D, WIDE)
    combined, head_grads, d_parts, entropies = None, [], [], []
    head_w = whole(jnp.concatenate(head_chunks(gating_matrix), axis=1))
    for q in range(CHUNKS):
        halves = []
        for own in (False, True):
            combined, d_logits, d_part, entropy = head_pass(
                q,
                own,
                strength.reshape(1),
                table,
                final_low,
                [head_w],
                [(0, (0, 0), held_shape[1:], 0, 0, (0, 0))],
                held_shape,
                guesses,
                adjoint_of_mixture[0],
                combined,
            )
            flat = d_logits.transpose(1, 0, 2).reshape(TILE_COUNT, WIDE)
            halves.append(summed(transpose_times(final_low, flat)))
            d_parts.append(d_part)
            entropies.append(entropy)
        head_grads.append(halves)
    contribution = jnp.sum(sum(entropies)) * strength
    d_final, d_branch, d_pre = mlp_back(d_parts, pre_act, fc2_w)
    d_middle, d_attn, d_attended, gain_two, shift_two = mlp_input_back(
        d_final, d_pre, fc1_w, middle, par.gain[:, 1], par.bias[:, 2], proj_w
    )
    d_joined = attention_back(joined, prob_full, d_attended)
    d_started, gain_one, shift_one = attention_input_back(
        d_middle, d_joined, qkv_w, started, par.gain[:, 0], par.bias[:, 0]
    )
    small_grad = small_gradient(
        rows,
        indicator,
        contribution,
        d_started,
        d_joined,
        d_attn,
        d_branch,
        d_pre,
        (gain_one, gain_two),
        (shift_one, shift_two),
    )
    return (
        combined[None],
        lax.psum(contribution, AXES),
        d_started.astype(jnp.bfloat16)[None],
        summed(transpose_times(normed, d_joined)),
        summed(transpose_times(attended, d_attn)),
        summed(transpose_times(normed_two, d_pre)),
        summed(transpose_times(hidden, d_branch)),
        head_whole(*zip(*head_grads)),
        *small_outputs(summed(small_grad), rows),
    )


def paired_step(
    tile_embeddings,
    horizon_indices,
    horizon_tallies,
    member_guesses,
    adjoint_of_mixture,
    triple_projection_matrix,
    attention_outward_matrix,
    widening_matrix,
    narrowing_matrix,
    gating_matrix,
    *small_parts,
):
    rows = triple_projection_matrix.shape[0]
    core = lax.axis_index("fsdp") % 2
    table = places(True)
    marks = jnp.concatenate([core.reshape(1), places(False)[::2] // 2])
    head_marks = jnp.concatenate([core.reshape(1), table[::2] // 2])
    head_table = jnp.concatenate([table, core.reshape(1)])
    seq = Sequence(horizon_tallies)
    indicator, strength = frame_scalars(horizon_indices, horizon_tallies)

    first_own, second_own = seq.run(
        pack_trunk,
        triple_projection_matrix,
        attention_outward_matrix,
        widening_matrix,
        narrowing_matrix,
        *small_parts,
    )
    one, two = RoundFirst(seq, first_own, 1), RoundFirst(seq, second_own, -1)
    one.start()
    two.start()
    head_own = seq.run(pack_head, gating_matrix)
    over = across(head_own)
    one.arrive()
    one.start()
    two.arrive()
    two.start()
    one.arrive()
    one.start()
    over = seq.tie(over)
    one.batch(True)
    two.arrive()
    two.start()
    one.arrive()
    one.last()
    head_first = seq.run(lambda a, b: jnp.concatenate([a, b], axis=0), head_own, over)
    two.arrive()
    two.last()
    guesses = seq.run(
        lambda v: lax.optimization_barrier(jnp.transpose(v[0], (1, 0, 2))), member_guesses
    )
    one.arrive_last()
    two.arrive_last()
    three = AcrossFirst(seq, head_first)
    three.start()
    one.arrive_over()
    one.batch(False)
    adjoint = seq.run(lambda v: lax.optimization_barrier(v[0]), adjoint_of_mixture)
    one.arrive_over()
    two.batch(True)
    three.arrive()
    three.start()
    one.arrive_batches()
    whole_one = [((0, rows), (0, FIRST_WIDE), 0, 0, 0)]
    whole_two = [((0, 8 * rows), (0, D), 0, 0, 0)]
    index = horizon_indices
    sources_one, moves = plan_moves(one.collect(), whole_one)
    middle, normed, joined, attended, normed_two, par, fc1_b = seq.run(
        functools.partial(trunk_first, table, index, rows, moves), tile_embeddings[0], *sources_one
    )
    two.arrive_over()
    two.batch(False)
    three.arrive()
    three.start()
    two.arrive_over()
    two.arrive_batches()
    three.arrive()
    three.last()
    sources_two, moves_two = plan_moves(two.collect(), whole_two)
    hidden, slope, final_low = seq.run(
        functools.partial(trunk_second, table, rows, moves_two),
        middle,
        normed_two,
        par,
        fc1_b,
        *sources_two,
    )
    three.arrive_last()
    final_other = sibling(final_low)
    normed_other, attended_other = sibling(normed), sibling(attended)
    normed_two_other, hidden_other = sibling(normed_two), sibling(hidden)

    held_shape = (32, rows, WIDE)
    head_fields = [((0, rows), (0, WIDE), 0, 0, 0)]
    state = dict(combined=None, d_parts=[], entropies=[])

    def head(q, own, around):
        sources, moves = plan_moves(around.collect(), head_fields)
        before = () if state["combined"] is None else (state["combined"],)

        def function(final_low, before, *sources):
            return head_pass(
                q,
                own,
                strength.reshape(1),
                head_table,
                final_low,
                list(sources),
                moves,
                held_shape,
                guesses,
                adjoint,
                before[0] if before else None,
            )

        state["combined"], d_logits, d_part, entropy = seq.run(
            function, final_low, before, *sources
        )
        state["d_parts"].append(d_part)
        state["entropies"].append(entropy)
        return d_logits

    make_grad = functools.partial(head_grad, head_marks)
    send = sibling(head(0, False, three))
    own = head(0, True, three)
    sum_one = SumRoundFirst(seq, *seq.run(make_grad, final_low, final_other, own, send))
    send = sibling(head(1, False, three))
    sum_one.step(3)
    own = head(1, True, three)
    sum_one.step(2)
    moves_proj = plan_moves(one.collect(), [((0, rows), (3 * D, 4 * D), 0, 0, 0)])[1]
    moves_qkv = plan_moves(one.collect(), [((0, rows), (0, 3 * D), 0, 0, 0)])[1]
    d_branch, d_pre, d_middle, d_attn, d_attended, d_rows, d_fc1_b = seq.run(
        functools.partial(second_back, table, rows, moves_two, moves_proj, len(sources_two)),
        slope,
        middle,
        par,
        state["d_parts"],
        *sources_two,
        *sources_one,
    )
    d_attn_other, d_fc1_b_other = sibling(d_attn), sibling(d_fc1_b)
    d_branch_other, d_pre_other = sibling(d_branch), sibling(d_pre)
    sum_one.step(1)
    sum_two = SumRoundFirst(seq, *seq.run(make_grad, final_low, final_other, own, send))
    parts = seq.run(
        lambda *ins: ring_grad(
            second_grad_body,
            marks,
            ins,
            (16 * rows, D // 2),
            [(16, 8 * rows, D // 2), (16, 2 * rows, FF // 2)],
            "second_grad",
        ),
        *(hidden, hidden_other, d_branch, d_branch_other),
        *(normed_two, normed_two_other, d_pre, d_pre_other),
    )
    sum_one.arrive()
    sum_two.arrive()
    sum_three = SumAcrossFirst(seq, parts, 1)
    sum_three.go_across(0)
    sum_two.step(3)
    d_joined, tokens, small_grad = seq.run(
        functools.partial(first_back, table, index, strength.reshape(1), rows, moves_qkv),
        tile_embeddings[0],
        joined,
        par,
        d_middle,
        d_attended,
        d_rows,
        state["entropies"],
        *sources_one,
    )
    d_joined_other, small_other = sibling(d_joined), sibling(small_grad)
    sum_two.arrive()
    sum_three.arrive_across(0)
    sum_two.step(2)
    sum_three.go_across(1)
    sum_three.step(4)
    blocks = seq.run(
        lambda *ins: round_grad(
            first_grad_body,
            head_marks,
            ins,
            (2 * rows, 2 * D + 2 * LANES),
            [(16, 2 * rows, 3 * D // 2), (16, 2 * rows, D // 2), (16, 2 * rows, LANES)]
            + [(LANES, D), (32, LANES), (2 * rows, LANES)],
            "first_grad",
        ),
        *(normed, normed_other, d_joined, d_joined_other),
        *(attended, attended_other, d_attn, d_attn_other),
        *(small_grad, small_other, d_fc1_b, d_fc1_b_other),
    )
    sum_three.arrive()
    sum_four = SumRoundFirst(seq, *blocks)
    sum_three.step(3)
    sum_two.arrive()
    sum_two.step(1)
    sum_one.go_across()
    sum_four.arrive()
    sum_four.step(3)
    combined_result = seq.run(lambda v: lax.optimization_barrier(v[None]), state["combined"])
    total_one = sum_one.finish()
    sum_four.arrive()
    sum_four.step(2)
    sum_two.arrive()
    sum_three.arrive_across(1)
    sum_two.go_across()
    sum_three.step(2)
    sum_four.arrive()
    sum_four.step(1)
    grad_tokens = tokens[None]
    first = core == 0

    def finish(total, rows_of):
        low, high = rows_of(total, 0, rows), rows_of(total, 1, rows)
        own, other = jnp.where(first, low, high), jnp.where(first, high, low)
        met = sibling(other.astype(jnp.bfloat16)).astype(jnp.float32)
        return jnp.where(first, own, met), jnp.where(first, met, own)

    head_one = finish(total_one, low_or_high)
    sum_three.arrive()
    sum_three.step(1)
    sum_four.arrive()
    sum_four.go_across()
    head_two = finish(sum_two.finish(), low_or_high)
    out_head = head_whole(*zip(head_one, head_two))
    total = sum_three.finish()
    out_fc2 = jnp.concatenate(finish(total, fc2_rows), axis=1)
    out_fc1 = jnp.concatenate(finish(total, fc1_rows), axis=1)
    total = sum_four.finish()
    out_small = jnp.where(first, total[:rows, 2 * D :], total[rows:, 2 * D :])
    low, high = finish(total[:, : 2 * D], low_or_high)
    n = 3 * D // 2
    out_fc1_b = out_small[0, LANES : LANES + 4 * rows]
    return (
        combined_result,
        value_of(out_small[0, ROW_DIGIT : ROW_DIGIT + DIGITS]),
        grad_tokens,
        jnp.concatenate([low[:, :n], high[:, :n]], axis=1),
        jnp.concatenate([low[:, n:], high[:, n:]], axis=1),
        out_fc1,
        out_fc2,
        out_head,
        out_small[:, :LEADS],
        out_small[:, ROW_GAIN:ROW_BIAS],
        out_small[:, ROW_BIAS:ROW_QKV],
        out_small[:, ROW_QKV:ROW_DIGIT],
        out_fc1_b,
    )


def solution(mesh):
    split = P(AXES)
    paired = mesh.shape["dp"] == 2 and mesh.shape["fsdp"] == 16
    return jax.shard_map(
        paired_step if paired else plain_step,
        mesh=mesh,
        in_specs=(split, split, P()) + (split,) * 12,
        out_specs=(split, P()) + (split,) * 11,
        check_vma=False,
    )
```

```python
import functools

import jax
import jax.numpy as jnp
from jax import lax
from jax.experimental import pallas as pl
from jax.experimental.pallas import tpu as pltpu
from jax.sharding import PartitionSpec as P

D = 768
HEADS = 12
HD = 64
FF = 3072
MODEL_COUNT = 3
TILE_SAMPLES = 4416
LEADS = 40
TILE_COUNT = 256
EPS = 1e-06
LANES = 128
HALF = 2304
PADDED = 2 * HALF
VMEM = 56 * 1024 * 1024

AXES = ("dp", "fsdp")
RING = [(z, 0) for z in range(4)] + [(z, 1) for z in (3, 2, 1, 0)]


def ring_pairs(step):
    pairs = []
    for spot, (z, x) in enumerate(RING):
        to_z, to_x = RING[(spot + step) % 8]
        for core in range(2):
            pairs.append((z * 4 + x * 2 + core, to_z * 4 + to_x * 2 + core))
    return pairs


def forth(value):
    return lax.ppermute(value, "fsdp", ring_pairs(1))


def back(value):
    return lax.ppermute(value, "fsdp", ring_pairs(-1))


def across(value):
    return lax.ppermute(value, "dp", [(0, 1), (1, 0)])


def exchange_rows(value):
    return lax.all_to_all(value, "dp", 0, 0)


def sibling(value):
    return lax.ppermute(value, "fsdp", [(i, i ^ 1) for i in range(16)])


def places(relative):
    y = lax.axis_index("dp") if relative else 0
    f = lax.axis_index("fsdp")
    z, x, core = f // 4, (f // 2) % 2, f % 2
    spot = jnp.where(x == 0, z, 7 - z)
    i = lax.iota(jnp.int32, 32)
    seat = (spot + (i // 2) % 8) % 8
    pair = jnp.where(seat < 4, seat * 2, (7 - seat) * 2 + 1)
    return ((y + i // 16) % 2) * 16 + pair * 2 + (core + i) % 2


def slot(other_row, distance, other_core):
    return other_row * 16 + (distance % 8) * 2 + other_core


def plan_moves(found, fields):
    sources, moves = [], []
    for source, rows, where in found:
        at = [i for i, s in enumerate(sources) if s is source]
        if not at:
            at = [len(sources)]
            sources.append(source)
        for (f0, f1), (g0, g1), out, out_row, out_col in fields:
            moves.append(
                (at[0], (rows[0] + f0, g0), (f1 - f0, g1 - g0), where, out, (out_row, out_col))
            )
    return sources, moves


def place(sources, moves, shapes, table, shards):
    def body(table_ref, *refs):
        ins, outs = refs[: len(sources)], refs[len(sources) : len(sources) + len(shapes)]
        held, sems, out_sems = refs[len(sources) + len(shapes) : -2], refs[-2], refs[-1]
        run_moves(moves, table_ref, ins, held, sems)
        copies = [
            pltpu.make_async_copy(held[i], outs[i], out_sems.at[i]) for i in range(len(shapes))
        ]
        for copy in copies:
            copy.start()
        for copy in copies:
            copy.wait()

    whole = [(shards,) + s for s in shapes]
    return pl.pallas_call(
        body,
        grid_spec=pltpu.PrefetchScalarGridSpec(
            num_scalar_prefetch=1,
            grid=(1,),
            in_specs=[pl.BlockSpec(memory_space=pl.ANY)] * len(sources),
            out_specs=[pl.BlockSpec(memory_space=pl.ANY)] * len(shapes),
            scratch_shapes=[pltpu.VMEM(s, jnp.bfloat16) for s in whole]
            + [
                pltpu.SemaphoreType.DMA((len(moves),)),
                pltpu.SemaphoreType.DMA((len(shapes),)),
            ],
        ),
        out_shape=[jax.ShapeDtypeStruct(s, jnp.bfloat16) for s in whole],
        compiler_params=pltpu.CompilerParams(vmem_limit_bytes=VMEM),
        name="place",
    )(table, *sources)


def run_moves(moves, table_ref, ins, outs, sems, begin=0):
    copies = []
    for i, (at, (sr, sc), (nr, nc), where, out, (dr, dc)) in enumerate(moves):
        copy = pltpu.make_async_copy(
            ins[at].at[pl.ds(sr, nr), pl.ds(begin + sc, nc)],
            outs[out].at[table_ref[where], pl.ds(dr, nr), pl.ds(dc, nc)],
            sems.at[i],
        )
        copy.start()
        copies.append(copy)
    for copy in copies:
        copy.wait()


def add_low(*values):
    total = values[0].astype(jnp.float32)
    for value in values[1:]:
        total = total + value.astype(jnp.float32)
    return total.astype(jnp.bfloat16)


class Sequence:
    def __init__(self, token):
        self.token = token

    def tie(self, *values):
        out = lax.optimization_barrier((self.token,) + values)
        self.token = out[0]
        return out[1] if len(values) == 1 else out[1:]

    def run(self, function, *values):
        values = lax.optimization_barrier((self.token,) + values)
        self.token = values[0]
        return self.tie(function(*values[1:]))


class Around:
    def __init__(self, seq, first):
        self.seq, self.rights, self.lefts = seq, [first], [first]

    def start(self, right=True, left=True):
        if right:
            self.rights.append(forth(self.rights[-1]))
        if left:
            self.lefts.append(back(self.lefts[-1]))

    def arrive(self, right=True, left=True):
        ends = ([self.rights] if right else []) + ([self.lefts] if left else [])
        met = self.seq.tie(*[end[-1] for end in ends])
        for end, value in zip(ends, met if len(ends) > 1 else (met,)):
            end[-1] = value


class RoundFirst(Around):
    def __init__(self, seq, first, longer):
        super().__init__(seq, first)
        self.longer, self.found = longer, []

    def last(self):
        ends = self.rights if self.longer > 0 else self.lefts
        ends.append(forth(ends[-1]) if self.longer > 0 else back(ends[-1]))

    def arrive_last(self):
        self.arrive(self.longer > 0, self.longer < 0)

    def batch(self):
        rights, lefts = self.rights, self.lefts
        r = rights[0].shape[0]
        end = rights[4] if self.longer > 0 else lefts[4]
        parts = (rights[0], rights[1], lefts[1], rights[2], lefts[2], rights[3], lefts[3], end)
        distances = (0, -1, 1, -2, 2, -3, 3, 4)
        joint = self.seq.run(lambda *v: jnp.concatenate(v, axis=0), *parts)
        self.over = across(joint), r, distances
        self.found.append((joint, r, 0, 0, distances))
        self.found.append((sibling(joint), r, 0, 1, distances))

    def arrive_over(self):
        over, r, distances = self.over
        over = self.seq.tie(over)
        self.found.append((over, r, 1, 0, distances))
        self.found.append((sibling(over), r, 1, 1, distances))

    def arrive_batches(self):
        met = self.seq.tie(*[v[0] for v in self.found])
        self.found = [(m,) + v[1:] for m, v in zip(met, self.found)]

    def collect(self):
        return [
            (source, (i * r, (i + 1) * r), slot(other_row, k, other_core))
            for source, r, other_row, other_core, distances in self.found
            for i, k in enumerate(distances)
        ]


class AcrossFirst(Around):
    def __init__(self, seq, first):
        super().__init__(seq, first)
        self.found, self.settled = [], set()
        self.note(first, [(0, 0), (1, 0)])

    def note(self, joint, spots):
        self.found.append((joint, 0, spots))
        self.found.append((sibling(joint), 1, spots))

    def settle(self):
        late = [i for i, item in enumerate(self.found) if item[1] and i not in self.settled]
        met = self.seq.tie(*[self.found[i][0] for i in late])
        for i, value in zip(late, met if len(late) > 1 else (met,)):
            self.found[i] = (value,) + self.found[i][1:]
        self.settled.update(late)

    def arrive(self):
        super().arrive()
        k = len(self.rights) - 1
        self.note(self.rights[k], [(0, -k), (1, -k)])
        self.note(self.lefts[k], [(0, k), (1, k)])

    def last(self):
        r = self.rights[0].shape[0] // 2
        right, left = self.seq.run(lambda a, b: (a[:r], b[r:]), self.rights[3], self.lefts[3])
        self.far = [forth(right), back(left)]

    def arrive_last(self):
        self.far = list(self.seq.tie(*self.far))
        for row, array in enumerate(self.far):
            self.note(array, [(row, 4)])

    def collect(self):
        r = self.rights[0].shape[0] // 2
        return [
            (source, (i * r, (i + 1) * r), slot(row, k, other_core))
            for source, other_core, spots in self.found
            for i, (row, k) in enumerate(spots)
        ]


ORDER_FIRST = (4, 3, -3)
ORDER_LAST = (2, -2, 1, -1, 0)


class SumAcrossFirst:
    def __init__(self, seq, parts, longer):
        self.seq, self.longer, self.ready = seq, longer, {}
        self.parts = parts
        self.met = [None, None]
        self.right = self.left = None

    def go_across(self, part):
        self.met[part] = exchange_rows(self.parts[part])

    def arrive_across(self, part):
        met = self.seq.tie(self.met[part])
        for i, k in enumerate((ORDER_FIRST, ORDER_LAST)[part]):
            self.ready[k] = (met, i)

    def arrive(self):
        if self.right is None:
            self.left = self.seq.tie(self.left)
        elif self.left is None:
            self.right = self.seq.tie(self.right)
        else:
            self.right, self.left = self.seq.tie(self.right, self.left)

    def step(self, k):
        if k == 4:
            value = self.seq.run(lambda v: add_low(v[0, 0], v[1, 0]), self.ready[4][0])
            if self.longer > 0:
                self.right = forth(value)
            else:
                self.left = back(value)
            return
        (met, i), (_, j) = self.ready[k], self.ready[-k]

        def add(met, right, left):
            return add_low(met[0, i], met[1, i], *right), add_low(met[0, j], met[1, j], *left)

        right = () if self.right is None else (self.right,)
        left = () if self.left is None else (self.left,)
        go_right, go_left = self.seq.run(add, met, right, left)
        self.right, self.left = forth(go_right), back(go_left)

    def finish(self):
        met, i = self.ready[0]

        def add(met, right, left):
            return sum(v.astype(jnp.float32) for v in (met[0, i], met[1, i], right, left))

        return self.seq.run(add, met, self.right, self.left)


class SumRoundFirst:
    def __init__(self, seq, blocks, far_right, far_left):
        self.seq, self.blocks = seq, blocks
        self.right, self.left = forth(far_right), back(far_left)

    def arrive(self):
        self.right, self.left = self.seq.tie(self.right, self.left)

    def step(self, k):
        def add_part(one, two, right, left):
            r = right.shape[0]
            return (
                jnp.concatenate([add_low(one[:r], right), one[r:]], axis=0),
                jnp.concatenate([two[:r], add_low(two[r:], left)], axis=0),
            )

        if k == 3:
            values = self.blocks[k], self.blocks[-k], self.right, self.left
            go_right, go_left = self.seq.run(add_part, *values)
            self.right, self.left = forth(go_right), back(go_left)
        else:
            self.right = forth(self.seq.run(add_low, self.blocks[k], self.right))
            self.left = back(self.seq.run(add_low, self.blocks[-k], self.left))

    def add(self, k):
        self.right = self.seq.run(add_low, self.blocks[k], self.right)
        self.left = self.seq.run(add_low, self.blocks[-k], self.left)

    def send(self):
        self.arrive()
        self.right, self.left = forth(self.right), back(self.left)

    def go_across(self):
        def add(block, right, left):
            r = block.shape[0] // 2
            near = sum(v[:r].astype(jnp.float32) for v in (block, right, left))
            return near, add_low(block[r:], right[r:], left[r:])

        self.near, sent = self.seq.run(add, self.blocks[0], self.right, self.left)
        self.met = across(sent)

    def finish(self):
        return self.seq.run(lambda a, b: a + b.astype(jnp.float32), self.near, self.met)


def layer_norm(values, norm_gain, norm_shift):
    row_mean = jnp.mean(values, axis=-1, keepdims=True)
    centred = values - row_mean
    row_var = jnp.mean(centred * centred, axis=-1, keepdims=True)
    return centred * lax.rsqrt(row_var + EPS) * norm_gain + norm_shift


def exact_gelu(values):
    return jax.nn.gelu(values, approximate=False)


def plain_dot(left, right):
    return jnp.dot(left, right, preferred_element_type=jnp.float32)


def times_transpose(left, right):
    return lax.dot_general(
        left, right, (((1,), (1,)), ((), ())), preferred_element_type=jnp.float32
    )


def transpose_times(left, right):
    return lax.dot_general(
        left, right, (((0,), (0,)), ((), ())), preferred_element_type=jnp.float32
    )


CHUNKS = 1
CHUNK = HALF // CHUNKS
LIGHT = pl.CostEstimate(flops=0, transcendentals=0, bytes_accessed=0)
HEAD_TILE = 384
HALF_STEPS = CHUNK // HEAD_TILE
ROWS = 16
COLS = 384


def half_of(own, table_ref):
    core = table_ref[table_ref.shape[0] - 1]
    return core if own else 1 - core


def pixel_block(q, own, j, table_ref):
    return half_of(own, table_ref) * (CHUNKS * HALF_STEPS) + q * HALF_STEPS + j


def head_body(q, own, moves, weight_ref, table_ref, x_ref, guess_ref, adj_ref, *refs):
    ins, refs = refs[:-7], refs[-7:]
    comb_ref, dl_ref, df_ref, ent_ref, logit_ref, held_ref, sems = refs
    j = pl.program_id(0)
    strength = weight_ref[0]
    half = half_of(own, table_ref)
    first_pixel = half * HALF + q * CHUNK + j * HEAD_TILE

    @pl.when(j == 0)
    def _():
        df_ref[...] = jnp.zeros_like(df_ref)
        ent_ref[...] = jnp.zeros_like(ent_ref)
        begin = pl.multiple_of((2 * q + half) * WIDE, LANES)
        run_moves(moves, table_ref, ins, [held_ref], sems, begin)

    x = x_ref[...]

    def weight(e):
        begin = pl.multiple_of(e * CHUNK + j * HEAD_TILE, LANES)
        return held_ref[:, :, pl.ds(begin, HEAD_TILE)].reshape(D, HEAD_TILE)

    for e in range(MODEL_COUNT):
        logit_ref[e] = jnp.dot(x, weight(e), preferred_element_type=jnp.float32)

    for part in range(HEAD_TILE // COLS):
        cols = pl.ds(part * COLS, COLS)
        pixel = first_pixel + part * COLS + lax.broadcasted_iota(jnp.int32, (ROWS, COLS), 1)
        real = pixel < TILE_SAMPLES

        def chunk(i, total):
            rows = pl.ds(pl.multiple_of(i * ROWS, ROWS), ROWS)
            l0, l1, l2 = (logit_ref[e, rows, cols] for e in range(3))
            top = jnp.maximum(jnp.maximum(l0, l1), l2)
            l0, l1, l2 = l0 - top, l1 - top, l2 - top
            e0, e1, e2 = jnp.exp(l0), jnp.exp(l1), jnp.exp(l2)
            norm = e0 + e1 + e2
            inverse = 1.0 / norm
            log_norm = jnp.log(norm)
            b0, b1, b2 = e0 * inverse, e1 * inverse, e2 * inverse
            l0, l1, l2 = l0 - log_norm, l1 - log_norm, l2 - log_norm
            minus_h = b0 * l0 + b1 * l1 + b2 * l2
            g0, g1, g2 = (guess_ref[e, rows, cols].astype(jnp.float32) for e in range(3))
            mixed = b0 * g0 + b1 * g1 + b2 * g2
            comb_ref[rows, cols] = mixed.astype(jnp.bfloat16)
            adj = adj_ref[rows, cols].astype(jnp.float32)
            for e, (b, l, g) in enumerate(((b0, l0, g0), (b1, l1, g1), (b2, l2, g2))):
                d = b * (adj * (g - mixed) - strength * (l - minus_h))
                dl_ref[e, rows, cols] = jnp.where(real, d, 0.0).astype(jnp.bfloat16)
            return total - jnp.where(real, minus_h, 0.0)

        total = lax.fori_loop(
            0,
            TILE_COUNT // ROWS,
            chunk,
            jnp.zeros((ROWS, COLS), jnp.float32),
            unroll=True,
        )
        gathered = total[:, :LANES]
        for k in range(1, COLS // LANES):
            gathered = gathered + total[:, k * LANES : (k + 1) * LANES]
        ent_ref[...] += gathered[:8] + gathered[8:]

    part = None
    for e in range(MODEL_COUNT):
        piece = lax.dot_general(
            dl_ref[e], weight(e), (((1,), (1,)), ((), ())), preferred_element_type=jnp.float32
        )
        part = piece if part is None else part + piece
    df_ref[...] += part


def head_pass(q, own, strength, table, final_low, sources, moves, held_shape, guesses, adjoint, before):
    tile = HEAD_TILE
    extra = [] if before is None else [before]

    def body(*refs):
        refs = refs[:5] + refs[5 + len(extra) :]
        head_body(q, own, moves, *refs)

    d_spec = (MODEL_COUNT, TILE_COUNT, tile)
    return pl.pallas_call(
        body,
        grid_spec=pltpu.PrefetchScalarGridSpec(
            num_scalar_prefetch=2,
            grid=(HALF_STEPS,),
            in_specs=[
                pl.BlockSpec((TILE_COUNT, D), lambda j, s, t: (0, 0)),
                pl.BlockSpec(d_spec, lambda j, s, t: (0, 0, pixel_block(q, own, j, t))),
                pl.BlockSpec((TILE_COUNT, tile), lambda j, s, t: (0, pixel_block(q, own, j, t))),
            ]
            + [pl.BlockSpec(memory_space=pl.ANY)] * (len(extra) + len(sources)),
            out_specs=[
                pl.BlockSpec((TILE_COUNT, tile), lambda j, s, t: (0, pixel_block(q, own, j, t))),
                pl.BlockSpec(d_spec, lambda j, s, t: (0, 0, j)),
                pl.BlockSpec((TILE_COUNT, D), lambda j, s, t: (0, 0)),
                pl.BlockSpec((8, LANES), lambda j, s, t: (0, 0)),
            ],
            scratch_shapes=[
                pltpu.VMEM(d_spec, jnp.float32),
                pltpu.VMEM(held_shape, jnp.bfloat16),
                pltpu.SemaphoreType.DMA((len(moves),)),
            ],
        ),
        out_shape=[
            jax.ShapeDtypeStruct((TILE_COUNT, TILE_SAMPLES), jnp.bfloat16),
            jax.ShapeDtypeStruct((MODEL_COUNT, TILE_COUNT, CHUNK), jnp.bfloat16),
            jax.ShapeDtypeStruct((TILE_COUNT, D), jnp.float32),
            jax.ShapeDtypeStruct((8, LANES), jnp.float32),
        ],
        input_output_aliases={5: 0} if extra else {},
        compiler_params=pltpu.CompilerParams(
            dimension_semantics=("arbitrary",), vmem_limit_bytes=VMEM
        ),
        cost_estimate=LIGHT,
        name="head_pass",
    )(strength, table, final_low, guesses, adjoint, *extra, *sources)


def dot_tokens(left, right):
    return lax.dot_general(left, right, (((0,), (0,)), ((), ())), preferred_element_type=jnp.float32)


def chip_at(marks_ref, row, distance):
    return marks_ref[1 + row * 8 + distance % 8]


HEAD_ORDER = (0, 1, -1, 2, -2, 3, -3)


def head_grad_body(marks_ref, x_mine_ref, x_other_ref, d_mine_ref, d_other_ref, *refs):
    outs, right_ref, left_ref, sum_ref = refs[:7], refs[7], refs[8], refs[9]
    value = dot_tokens(x_mine_ref[...], d_mine_ref[0]) + dot_tokens(x_other_ref[...], d_other_ref[0])
    sum_ref[...] = value.reshape(sum_ref.shape)
    r = sum_ref.shape[1]
    for k, out in zip(HEAD_ORDER, outs):
        for row in (0, 1):
            block = sum_ref[chip_at(marks_ref, row, k)].astype(jnp.bfloat16)
            out[row * r : (row + 1) * r, :] = block
    right_ref[...] = sum_ref[chip_at(marks_ref, 0, 4)].astype(jnp.bfloat16)
    left_ref[...] = sum_ref[chip_at(marks_ref, 1, 4)].astype(jnp.bfloat16)


def head_grad(marks, x_mine, x_other, d_mine, d_other):
    tile = 1152
    steps = CHUNK // tile
    r = D // 16
    n = MODEL_COUNT * CHUNK
    tall = [2 * r] * 7 + [r] * 2
    outs = pl.pallas_call(
        head_grad_body,
        grid_spec=pltpu.PrefetchScalarGridSpec(
            num_scalar_prefetch=1,
            grid=(MODEL_COUNT, steps),
            in_specs=[
                pl.BlockSpec((TILE_COUNT, D), lambda e, j, c: (0, 0)),
                pl.BlockSpec((TILE_COUNT, D), lambda e, j, c: (0, 0)),
                pl.BlockSpec((1, TILE_COUNT, tile), lambda e, j, c: (e, 0, j)),
                pl.BlockSpec((1, TILE_COUNT, tile), lambda e, j, c: (e, 0, j)),
            ],
            out_specs=[pl.BlockSpec((h, tile), lambda e, j, c: (0, e * steps + j)) for h in tall],
            scratch_shapes=[pltpu.VMEM((16, r, tile), jnp.float32)],
        ),
        out_shape=[jax.ShapeDtypeStruct((h, n), jnp.bfloat16) for h in tall],
        compiler_params=pltpu.CompilerParams(
            dimension_semantics=("arbitrary", "arbitrary"), vmem_limit_bytes=VMEM
        ),
        cost_estimate=LIGHT,
        name="head_grad",
    )(marks, x_mine, x_other, d_mine, d_other)
    return dict(zip(HEAD_ORDER, outs[:7])), outs[7], outs[8]


def ring_rows(marks_ref, outs, write):
    for row in (0, 1):
        for out, order in zip(outs, (ORDER_FIRST, ORDER_LAST)):
            for i, k in enumerate(order):
                write(out, row, i, chip_at(marks_ref, row, k))


def core_half(ref, marks_ref):
    n = ref.shape[1] // 2
    return ref[:, pl.ds(pl.multiple_of(marks_ref[0] * n, LANES), n)]


def paired_product(marks_ref, x, x_other, d, d_other):
    return dot_tokens(x[...], core_half(d, marks_ref)) + dot_tokens(
        x_other[...], core_half(d_other, marks_ref)
    )


def second_grad_body(marks_ref, *refs):
    ins, outs, (fc2_ref, fc1_ref) = refs[:8], refs[8:10], refs[10:]
    fc2_ref[...] = paired_product(marks_ref, *ins[:4]).reshape(fc2_ref.shape)
    fc1_ref[...] = paired_product(marks_ref, *ins[4:]).reshape(fc1_ref.shape)
    r4, wide = fc2_ref.shape[1:]
    r = fc1_ref.shape[1]

    def write(out, row, i, chip):
        out[row, i, :r4, :] = fc2_ref[chip].astype(jnp.bfloat16)
        for k in range(4):
            block = fc1_ref[chip, :, k * wide : (k + 1) * wide].astype(jnp.bfloat16)
            out[row, i, r4 + k * r : r4 + (k + 1) * r, :] = block

    ring_rows(marks_ref, outs, write)


def first_grad_body(marks_ref, *refs):
    ins, outs, refs = refs[:12], refs[12:21], refs[21:]
    qkv_ref, proj_ref, small_ref, flat_ref, hidden_ref, block_ref = refs
    qkv_ref[...] = paired_product(marks_ref, *ins[:4]).reshape(qkv_ref.shape)
    proj_ref[...] = paired_product(marks_ref, *ins[4:8]).reshape(proj_ref.shape)
    flat_ref[...] = jnp.zeros_like(flat_ref)
    flat_ref[: ins[8].shape[0], :] = ins[8][...] + ins[9][...]
    small_ref[...] = flat_ref[...].T.reshape(small_ref.shape)
    shards = hidden_ref.shape[0]
    r, wide = qkv_ref.shape[1] // 2, FF // shards
    hidden_ref[...] = jnp.zeros_like(hidden_ref)
    for d in range(shards):
        cols = slice(d * wide, (d + 1) * wide)
        hidden_ref[d : d + 1, :wide] = ins[10][:, cols] + ins[11][:, cols]
    block_ref[...] = jnp.zeros_like(block_ref)
    n, m = qkv_ref.shape[2], qkv_ref.shape[2] + proj_ref.shape[2]

    def write(out, at, chip):
        rows = slice(at, at + 2 * r)
        out[rows, :n] = qkv_ref[chip].astype(jnp.bfloat16)
        out[rows, n:m] = proj_ref[chip].astype(jnp.bfloat16)
        out[rows, m : m + LANES] = small_ref[chip].astype(jnp.bfloat16)
        block_ref[0:1, :] = hidden_ref[pl.ds(2 * chip, 1), :]
        block_ref[r : r + 1, :] = hidden_ref[pl.ds(2 * chip + 1, 1), :]
        out[rows, m + LANES :] = block_ref[...].astype(jnp.bfloat16)

    for k, out in zip(HEAD_ORDER, outs):
        for row in (0, 1):
            write(out, row * 2 * r, chip_at(marks_ref, row, k))
    for row, out in enumerate(outs[7:]):
        write(out, 0, chip_at(marks_ref, row, 4))


def round_grad(body, marks, ins, block, scratch, name):
    r, n = block
    shapes = [(2 * r, n)] * 7 + [(r, n)] * 2
    outs = pl.pallas_call(
        body,
        grid_spec=pltpu.PrefetchScalarGridSpec(
            num_scalar_prefetch=1,
            grid=(1,),
            in_specs=[pl.BlockSpec(v.shape, lambda i, m: (0, 0)) for v in ins],
            out_specs=[pl.BlockSpec(s, lambda i, m: (0, 0)) for s in shapes],
            scratch_shapes=[pltpu.VMEM(s, jnp.float32) for s in scratch],
        ),
        out_shape=[jax.ShapeDtypeStruct(s, jnp.bfloat16) for s in shapes],
        compiler_params=pltpu.CompilerParams(vmem_limit_bytes=VMEM),
        cost_estimate=LIGHT,
        name=name,
    )(marks, *ins)
    return dict(zip(HEAD_ORDER, outs[:7])), outs[7], outs[8]


def ring_grad(body, marks, ins, block, scratch, name):
    shapes = [(2, 3) + block, (2, 5) + block]
    return pl.pallas_call(
        body,
        grid_spec=pltpu.PrefetchScalarGridSpec(
            num_scalar_prefetch=1,
            grid=(1,),
            in_specs=[pl.BlockSpec(v.shape, lambda i, m: (0, 0)) for v in ins],
            out_specs=[pl.BlockSpec(s, lambda i, m: (0, 0, 0, 0)) for s in shapes],
            scratch_shapes=[pltpu.VMEM(s, jnp.float32) for s in scratch],
        ),
        out_shape=[jax.ShapeDtypeStruct(s, jnp.bfloat16) for s in shapes],
        compiler_params=pltpu.CompilerParams(vmem_limit_bytes=VMEM),
        cost_estimate=LIGHT,
        name=name,
    )(marks, *ins)


def pack_small(lead_w, gains, biases, qkv_b, fc1_b, rows):
    value = jnp.concatenate([lead_w, gains, biases, qkv_b, fc1_b.reshape(4, rows).T], axis=1)
    return jnp.pad(value, ((0, 0), (0, LANES - value.shape[1])))


def split_small(small):
    at, found = 0, []
    for width in (LEADS, 2, 4, 2, 4):
        found.append(small[:, at : at + width])
        at += width
    return found


WIDE = MODEL_COUNT * CHUNK


def head_chunks(value):
    r = value.shape[0]
    value = value.reshape(r, MODEL_COUNT, TILE_SAMPLES)
    value = jnp.pad(value, ((0, 0), (0, 0), (0, PADDED - TILE_SAMPLES)))
    value = value.reshape(r, MODEL_COUNT, 2, CHUNKS, CHUNK).transpose(0, 2, 1, 3, 4)
    return [value[:, :, :, q].reshape(r, 2 * WIDE) for q in range(CHUNKS)]


def pack_trunk_body(qkv_ref, proj_ref, fc1_ref, fc2_ref, lead_ref, gain_ref, bias_ref, qkv_b_ref, fc1_b_ref, *refs):
    one_ref, two_ref, flat_ref, tall_ref = refs
    r = qkv_ref.shape[0]
    flat_ref[...] = jnp.zeros_like(flat_ref)
    at = LEADS
    for ref in (gain_ref, bias_ref, qkv_b_ref):
        rows = ref.shape[0]
        flat_ref[at : at + rows, :r] = ref[...].astype(jnp.float32)
        at += rows
    tall_ref[...] = flat_ref[...].T
    tall_ref[:r, :LEADS] = lead_ref[...].astype(jnp.float32)
    flat_ref[...] = jnp.zeros_like(flat_ref)
    flat_ref[0:1, : 4 * r] = fc1_b_ref[...].astype(jnp.float32)
    n = 4 * D
    one_ref[:, : 3 * D] = qkv_ref[...]
    one_ref[:, 3 * D : n] = proj_ref[...]
    one_ref[:, n : n + LANES] = tall_ref[:r, :].astype(jnp.bfloat16)
    one_ref[:, n + LANES :] = flat_ref[:r, :].astype(jnp.bfloat16)
    two_ref[: 4 * r, :] = fc2_ref[...]
    for k in range(4):
        two_ref[(4 + k) * r : (5 + k) * r, :] = fc1_ref[:, k * D : (k + 1) * D]


def pack_trunk(qkv, proj, fc1, fc2, lead_w, gains, biases, qkv_b, fc1_b):
    r = qkv.shape[0]
    return pl.pallas_call(
        pack_trunk_body,
        out_shape=[
            jax.ShapeDtypeStruct((r, 4 * D + 2 * LANES), jnp.bfloat16),
            jax.ShapeDtypeStruct((8 * r, D), jnp.bfloat16),
        ],
        scratch_shapes=[pltpu.VMEM((LANES, LANES), jnp.float32)] * 2,
        compiler_params=pltpu.CompilerParams(vmem_limit_bytes=VMEM),
        cost_estimate=LIGHT,
        name="pack_trunk",
    )(qkv, proj, fc1, fc2, lead_w, gains.T, biases.T, qkv_b.T, fc1_b.reshape(1, 4 * r))


def pack_head_body(head_ref, out):
    r = head_ref.shape[0]
    for q in range(CHUNKS):
        for h in range(2):
            first = h * HALF + q * CHUNK
            real = min(CHUNK, TILE_SAMPLES - first)
            for e in range(MODEL_COUNT):
                begin, at = e * TILE_SAMPLES + first, ((2 * q + h) * MODEL_COUNT + e) * CHUNK
                part = head_ref[:, begin : begin + real]
                if real < CHUNK:
                    part = jnp.concatenate([part, jnp.zeros((r, CHUNK - real), part.dtype)], axis=1)
                out[:, at : at + CHUNK] = part


def pack_head(head):
    return pl.pallas_call(
        pack_head_body,
        out_shape=jax.ShapeDtypeStruct((head.shape[0], 2 * CHUNKS * WIDE), jnp.bfloat16),
        compiler_params=pltpu.CompilerParams(vmem_limit_bytes=VMEM),
        cost_estimate=LIGHT,
        name="pack_head",
    )(head)


def head_whole(low, high):
    r = low[0].shape[0]
    parts = [v.reshape(r, MODEL_COUNT, CHUNK) for v in (*low, *high)]
    return jnp.concatenate(parts, axis=2)[:, :, :TILE_SAMPLES].reshape(r, MODEL_COUNT * TILE_SAMPLES)


DIGITS = 16
BASE = 8.0


def digits_of(value):
    powers = jnp.asarray([BASE**k for k in range(DIGITS + 1)], jnp.float32)
    floors = jnp.floor(value * 32.0 * powers)
    return floors[1:] - BASE * floors[:-1]


def value_of(digits):
    powers = jnp.asarray([BASE ** -(k + 1) / 32.0 for k in range(DIGITS)], jnp.float32)
    return jnp.sum(digits * powers)


SCALE = HD ** (-0.5)
ROW_GAIN, ROW_BIAS, ROW_QKV, ROW_DIGIT = LEADS, LEADS + 2, LEADS + 6, LEADS + 8
SMALL_ROWS = 64
FIRST_WIDE = 4 * D + 2 * LANES


def slab(ref, first, n):
    shards, rows = ref.shape[:2]
    return ref[:, :, first : first + n].reshape(shards * rows, n)


def dot_last(left, right):
    return lax.dot_general(left, right, (((1,), (1,)), ((), ())), preferred_element_type=jnp.float32)


def normalised(values):
    centred = values - jnp.mean(values, axis=-1, keepdims=True)
    inverse = lax.rsqrt(jnp.mean(centred * centred, axis=-1, keepdims=True) + EPS)
    return centred * inverse, inverse


def norm_back(values, d_out, gain):
    unit, inverse = normalised(values)
    d_unit = d_out * gain
    mean_one = jnp.mean(d_unit, axis=-1, keepdims=True)
    mean_two = jnp.mean(d_unit * unit, axis=-1, keepdims=True)
    d_values = inverse * (d_unit - mean_one - unit * mean_two)
    return (
        d_values,
        jnp.sum(d_out * unit, axis=0, keepdims=True),
        jnp.sum(d_out, axis=0, keepdims=True),
    )


def head_masks():
    lane = lax.broadcasted_iota(jnp.int32, (1, 2 * HD), 1)
    low = lane < HD
    return low, [m.astype(jnp.float32).astype(jnp.bfloat16) for m in (low, lane >= HD)]


def softmax_of(scores):
    expd = jnp.exp(scores - jnp.max(scores, axis=-1, keepdims=True))
    return expd * (1.0 / jnp.sum(expd, axis=-1, keepdims=True))


def trunk_first_body(moves, table_ref, index_ref, frame_ref, *refs):
    ins, refs = refs[:-9], refs[-9:]
    middle_ref, normed_ref, joined_ref, attended_ref, normed_two_ref, par_ref, fc1_b_ref = refs[:7]
    held_ref, sems = refs[7:]
    run_moves(moves, table_ref, ins, [held_ref], sems)
    par_ref[...] = slab(held_ref, 4 * D, LANES).astype(jnp.float32).T
    shards = held_ref.shape[0]
    wide = FF // shards
    for d in range(shards):
        row = held_ref[d, 0:1, 4 * D + LANES : 4 * D + LANES + wide]
        fc1_b_ref[:, d * wide : (d + 1) * wide] = row.astype(jnp.float32)

    def row(i):
        return par_ref[i : i + 1, :]

    started = frame_ref[...].astype(jnp.float32) + par_ref[pl.ds(index_ref[0], 1), :]
    normed = (normalised(started)[0] * row(ROW_GAIN) + row(ROW_BIAS)).astype(jnp.bfloat16)
    normed_ref[...] = normed
    for i, shift in enumerate((row(ROW_QKV), None, row(ROW_QKV + 1))):
        part = jnp.dot(normed, slab(held_ref, i * D, D), preferred_element_type=jnp.float32)
        part = part if shift is None else part + shift
        joined_ref[:, i * D : (i + 1) * D] = part.astype(jnp.bfloat16)
    low, masks = head_masks()
    for p in range(HEADS // 2):
        at = p * 2 * HD
        q, k, v = (joined_ref[:, i * D + at : i * D + at + 2 * HD] for i in range(3))
        outs = []
        for mask in masks:
            probs = softmax_of(dot_last(q * mask, k) * SCALE).astype(jnp.bfloat16)
            outs.append(jnp.dot(probs, v, preferred_element_type=jnp.float32))
        attended_ref[:, at : at + 2 * HD] = jnp.where(low, *outs).astype(jnp.bfloat16)
    middle = (
        started
        + jnp.dot(attended_ref[...], slab(held_ref, 3 * D, D), preferred_element_type=jnp.float32)
        + row(ROW_BIAS + 1)
    )
    middle_ref[...] = middle
    normed_two = normalised(middle)[0] * row(ROW_GAIN + 1) + row(ROW_BIAS + 2)
    normed_two_ref[...] = normed_two.astype(jnp.bfloat16)


def trunk_call(body, scalars, ins, sources, outs, scratch, name):
    any_spec = pl.BlockSpec(memory_space=pl.ANY)

    def whole(shape):
        return pl.BlockSpec(shape, lambda i, *s: (0,) * len(shape))

    return pl.pallas_call(
        body,
        grid_spec=pltpu.PrefetchScalarGridSpec(
            num_scalar_prefetch=len(scalars),
            grid=(1,),
            in_specs=[whole(v.shape) for v in ins] + [any_spec] * len(sources),
            out_specs=[whole(s) for s, _ in outs],
            scratch_shapes=scratch,
        ),
        out_shape=[jax.ShapeDtypeStruct(*o) for o in outs],
        compiler_params=pltpu.CompilerParams(vmem_limit_bytes=VMEM),
        cost_estimate=LIGHT,
        name=name,
    )(*scalars, *ins, *sources)


def trunk_first(table, index, rows, moves, frame, *sources):
    flat, low, full = (TILE_COUNT, D), jnp.bfloat16, jnp.float32
    return trunk_call(
        functools.partial(trunk_first_body, moves),
        (table, index),
        (frame,),
        sources,
        [
            (flat, full),
            (flat, low),
            ((TILE_COUNT, 3 * D), low),
            (flat, low),
            (flat, low),
            ((LANES, D), full),
            ((1, FF), full),
        ],
        [
            pltpu.VMEM((32, rows, FIRST_WIDE), low),
            pltpu.SemaphoreType.DMA((len(moves),)),
        ],
        "trunk_first",
    )


def trunk_second_body(moves, table_ref, middle_ref, normed_two_ref, par_ref, fc1_b_ref, *refs):
    ins, refs = refs[:-5], refs[-5:]
    hidden_ref, slope_ref, final_ref, held_ref, sems = refs
    run_moves(moves, table_ref, ins, [held_ref], sems)
    total = middle_ref[...] + par_ref[ROW_BIAS + 3 : ROW_BIAS + 4, :]
    normed_two = normed_two_ref[...]
    for k in range(4):
        cols = slice(k * D, (k + 1) * D)
        pre = jnp.dot(normed_two, widening(held_ref, k), preferred_element_type=jnp.float32)
        pre = pre + fc1_b_ref[:, cols]
        share = 0.5 * (1.0 + lax.erf(pre * (0.5**0.5)))
        density = jnp.exp(-0.5 * pre * pre) * ((0.5 / 3.141592653589793) ** 0.5)
        slope_ref[:, cols] = share + pre * density
        hidden = (pre * share).astype(jnp.bfloat16)
        hidden_ref[:, cols] = hidden
        weight = narrowing(held_ref, k)
        total += jnp.dot(hidden, weight, preferred_element_type=jnp.float32)
    final_ref[...] = total.astype(jnp.bfloat16)


def second_scratch(rows):
    return [pltpu.VMEM((32, 8 * rows, D), jnp.bfloat16)]


def narrowing(held_ref, k):
    shards, rows = held_ref.shape[:2]
    return held_ref[k * shards // 4 : (k + 1) * shards // 4, : rows // 2, :].reshape(D, D)


def widening(held_ref, k):
    rows = held_ref.shape[1] // 8
    return held_ref[:, (4 + k) * rows : (5 + k) * rows, :].reshape(D, D)


def trunk_second(table, rows, moves, middle, normed_two, par, fc1_b, *sources):
    return trunk_call(
        functools.partial(trunk_second_body, moves),
        (table,),
        (middle, normed_two, par, fc1_b),
        sources,
        [
            ((TILE_COUNT, FF), jnp.bfloat16),
            ((TILE_COUNT, FF), jnp.float32),
            ((TILE_COUNT, D), jnp.bfloat16),
        ],
        second_scratch(rows) + [pltpu.SemaphoreType.DMA((len(moves),))],
        "trunk_second",
    )


def second_back_body(moves_two, moves_one, n_two, table_ref, slope_ref, middle_ref, par_ref, *refs):
    d_parts, refs = refs[: 2 * CHUNKS], refs[2 * CHUNKS :]
    ins, refs = refs[:-11], refs[-11:]
    branch_ref, pre_ref, middle_d_ref, attn_ref, attended_ref, rows_ref, fc1_b_ref = refs[:7]
    held_ref, proj_ref, sems_two, sems_one = refs[7:]
    run_moves(moves_one, table_ref, ins[n_two:], [proj_ref], sems_one)
    run_moves(moves_two, table_ref, ins[:n_two], [held_ref], sems_two)
    d_final = d_parts[0][...]
    for part in d_parts[1:]:
        d_final = d_final + part[...]
    d_branch = d_final.astype(jnp.bfloat16)
    branch_ref[...] = d_branch
    d_normed = None
    for k in range(4):
        cols = slice(k * D, (k + 1) * D)
        d_hidden = dot_last(d_branch, narrowing(held_ref, k))
        d_pre = (d_hidden * slope_ref[:, cols]).astype(jnp.bfloat16)
        pre_ref[:, cols] = d_pre
        fc1_b_ref[:, cols] = jnp.sum(d_pre.astype(jnp.float32), axis=0, keepdims=True)
        part = dot_last(d_pre, widening(held_ref, k))
        d_normed = part if d_normed is None else d_normed + part
    gain = par_ref[ROW_GAIN + 1 : ROW_GAIN + 2, :]
    d_part, d_gain, d_shift = norm_back(middle_ref[...], d_normed, gain)
    d_middle = d_final + d_part
    middle_d_ref[...] = d_middle
    d_attn = d_middle.astype(jnp.bfloat16)
    attn_ref[...] = d_attn
    attended_ref[...] = dot_last(d_attn, slab(proj_ref, 0, D)).astype(jnp.bfloat16)
    sums = [jnp.sum(v.astype(jnp.float32), axis=0, keepdims=True) for v in (d_attn, d_branch)]
    rows_ref[...] = jnp.zeros_like(rows_ref)
    for i, value in enumerate((d_gain, d_shift, *sums)):
        rows_ref[i : i + 1, :] = value


def second_back(table, rows, moves_two, moves_one, n_two, slope, middle, par, d_parts, *sources):
    flat, low, full = (TILE_COUNT, D), jnp.bfloat16, jnp.float32
    return trunk_call(
        functools.partial(second_back_body, moves_two, moves_one, n_two),
        (table,),
        (slope, middle, par, *d_parts),
        sources,
        [
            (flat, low),
            ((TILE_COUNT, FF), low),
            (flat, full),
            (flat, low),
            (flat, low),
            ((8, D), full),
            ((1, FF), full),
        ],
        second_scratch(rows)
        + [
            pltpu.VMEM((32, rows, D), low),
            pltpu.SemaphoreType.DMA((len(moves_two),)),
            pltpu.SemaphoreType.DMA((len(moves_one),)),
        ],
        "second_back",
    )


def first_back_body(moves, n_ent, table_ref, index_ref, weight_ref, frame_ref, joined_ref, par_ref, middle_d_ref, attended_ref, rows_ref, *refs):
    ents, refs = refs[:n_ent], refs[n_ent:]
    ins, refs = refs[:-5], refs[-5:]
    d_joined_ref, tokens_ref, small_ref, qkv_ref, sems = refs
    run_moves(moves, table_ref, ins, [qkv_ref], sems)
    small_ref[...] = jnp.zeros_like(small_ref)
    _, masks = head_masks()
    for p in range(HEADS // 2):
        at = p * 2 * HD
        q, k, v = (joined_ref[:, i * D + at : i * D + at + 2 * HD] for i in range(3))
        d_out = attended_ref[:, at : at + 2 * HD]
        totals = [None] * 3
        for mask in masks:
            q_one, k_one, d_one = q * mask, k * mask, d_out * mask
            probs = softmax_of(dot_last(q_one, k) * SCALE)
            d_probs = dot_last(d_one, v)
            inner = jnp.sum(probs * d_probs, axis=-1, keepdims=True)
            d_scores = (probs * (d_probs - inner)).astype(jnp.bfloat16)
            parts = (
                jnp.dot(d_scores, k_one, preferred_element_type=jnp.float32),
                dot_tokens(d_scores, q_one),
                dot_tokens(probs.astype(jnp.bfloat16), d_one),
            )
            totals = [a if b is None else a + b for a, b in zip(parts, totals)]
        for i, scale in enumerate((SCALE, SCALE, 1.0)):
            d_joined_ref[:, i * D + at : i * D + at + 2 * HD] = (totals[i] * scale).astype(
                jnp.bfloat16
            )
    d_normed = None
    for i in range(3):
        block = d_joined_ref[:, i * D : (i + 1) * D]
        if i != 1:
            at = ROW_QKV + i // 2
            total = jnp.sum(block.astype(jnp.float32), axis=0, keepdims=True)
            small_ref[at : at + 1, :] = total
        part = dot_last(block, slab(qkv_ref, i * D, D))
        d_normed = part if d_normed is None else d_normed + part
    started = frame_ref[...].astype(jnp.float32) + par_ref[pl.ds(index_ref[0], 1), :]
    gain = par_ref[ROW_GAIN : ROW_GAIN + 1, :]
    d_part, d_gain, d_shift = norm_back(started, d_normed, gain)
    d_started = middle_d_ref[...] + d_part
    tokens_ref[...] = d_started.astype(jnp.bfloat16)
    small_ref[pl.ds(index_ref[0], 1), :] = jnp.sum(d_started, axis=0, keepdims=True)
    small_ref[ROW_GAIN : ROW_GAIN + 1, :] = d_gain
    small_ref[ROW_BIAS : ROW_BIAS + 1, :] = d_shift
    small_ref[ROW_GAIN + 1 : ROW_GAIN + 2, :] = rows_ref[0:1, :]
    small_ref[ROW_BIAS + 2 : ROW_BIAS + 3, :] = rows_ref[1:2, :]
    small_ref[ROW_BIAS + 1 : ROW_BIAS + 2, :] = rows_ref[2:3, :]
    small_ref[ROW_BIAS + 3 : ROW_BIAS + 4, :] = rows_ref[3:4, :]
    entropy = ents[0][...]
    for ent in ents[1:]:
        entropy = entropy + ent[...]
    entropy = jnp.sum(jnp.sum(entropy, axis=0, keepdims=True), axis=1, keepdims=True)
    value = jnp.broadcast_to(entropy * weight_ref[0] * 32.0, (1, D))
    before = jnp.floor(value)
    for k in range(DIGITS):
        value = value * BASE
        floor = jnp.floor(value)
        small_ref[ROW_DIGIT + k : ROW_DIGIT + k + 1, :] = floor - BASE * before
        before = floor


def first_back(table, index, strength, rows, moves, frame, joined, par, d_middle, d_attended, d_rows, ents, *sources):
    return trunk_call(
        functools.partial(first_back_body, moves, len(ents)),
        (table, index, strength),
        (frame, joined, par, d_middle, d_attended, d_rows, *ents),
        sources,
        [
            ((TILE_COUNT, 3 * D), jnp.bfloat16),
            ((TILE_COUNT, D), jnp.bfloat16),
            ((SMALL_ROWS, D), jnp.float32),
        ],
        [
            pltpu.VMEM((32, rows, 3 * D), jnp.bfloat16),
            pltpu.SemaphoreType.DMA((len(moves),)),
        ],
        "first_back",
    )


def low_or_high(value, core, rows):
    return value[core * rows : (core + 1) * rows]


def fc2_rows(value, core, rows):
    return value[core * 4 * rows : (core + 1) * 4 * rows]


def fc1_rows(value, core, rows):
    begin = 8 * rows + core * rows
    return jnp.concatenate(
        [value[begin + 2 * k * rows : begin + (2 * k + 1) * rows] for k in range(4)], axis=1
    )


class Parameters:
    def __init__(self, small_all, rows):
        lead_w, gain_all, bias_all, qkv_b, fc1_b = split_small(small_all)
        self.lead = lead_w.astype(jnp.float32)
        self.gain = gain_all.astype(jnp.float32)
        self.bias = bias_all.astype(jnp.float32)
        qkv_b = qkv_b.astype(jnp.float32)
        self.offset = jnp.concatenate([qkv_b[:, 0], jnp.zeros_like(qkv_b[:, 0]), qkv_b[:, 1]])
        self.fc1 = (
            fc1_b.astype(jnp.float32).reshape(D // rows, rows, 4).transpose(0, 2, 1).reshape(FF)
        )


    def parts(self):
        return self.lead, self.gain, self.bias, self.offset, self.fc1


def attention_input(frame, lead_vector, gain, bias, offset, qkv_w):
    started = frame.astype(jnp.float32) + lead_vector[None, :]
    normed = layer_norm(started, gain, bias).astype(jnp.bfloat16)
    joined = (plain_dot(normed, qkv_w) + offset).astype(jnp.bfloat16)
    return started, normed, joined


def heads_of(joined):
    return [joined[:, i * D : (i + 1) * D].reshape(TILE_COUNT, HEADS, HD) for i in range(3)]


def attention(joined):
    queries, keys, values = heads_of(joined)
    scores = jnp.einsum("qhd,khd->hqk", queries, keys, preferred_element_type=jnp.float32) * SCALE
    row_top = jnp.max(scores, axis=-1, keepdims=True)
    expd = jnp.exp(scores - row_top)
    prob_full = expd / jnp.sum(expd, axis=-1, keepdims=True)
    probs_low = prob_full.astype(jnp.bfloat16)
    attended = jnp.einsum("hqk,khd->qhd", probs_low, values, preferred_element_type=jnp.float32)
    return prob_full, attended.astype(jnp.bfloat16).reshape(TILE_COUNT, D)


def mlp_input(started, attended, proj_w, proj_bias, gain, bias):
    middle = started + plain_dot(attended, proj_w) + proj_bias
    return middle, layer_norm(middle, gain, bias).astype(jnp.bfloat16)


def mlp(middle, normed_two, fc1_w, fc1_b, fc2_w, fc2_b):
    pre_act = plain_dot(normed_two, fc1_w) + fc1_b
    hidden = exact_gelu(pre_act).astype(jnp.bfloat16)
    final_sum = middle + plain_dot(hidden, fc2_w) + fc2_b
    return pre_act, hidden, final_sum.astype(jnp.bfloat16)


def mlp_back(d_parts, pre_act, fc2_w):
    d_final = sum(d_parts)
    d_branch = d_final.astype(jnp.bfloat16)
    d_hidden = times_transpose(d_branch, fc2_w)
    _, gelu_back = jax.vjp(exact_gelu, pre_act)
    return d_final, d_branch, gelu_back(d_hidden)[0].astype(jnp.bfloat16)


def mlp_input_back(d_final, d_pre, fc1_w, middle, gain, bias, proj_w):
    d_normed_two = times_transpose(d_pre, fc1_w)
    _, norm_back = jax.vjp(layer_norm, middle, gain, bias)
    d_part, d_gain, d_shift = norm_back(d_normed_two)
    d_middle = d_final + d_part
    d_attn = d_middle.astype(jnp.bfloat16)
    d_attended = times_transpose(d_attn, proj_w).astype(jnp.bfloat16)
    return d_middle, d_attn, d_attended, d_gain, d_shift


def attention_back(joined, prob_full, d_attended):
    queries, keys, values = heads_of(joined)
    d_attended = d_attended.reshape(TILE_COUNT, HEADS, HD)
    probs_low = prob_full.astype(jnp.bfloat16)
    d_values = jnp.einsum("hqk,qhd->khd", probs_low, d_attended, preferred_element_type=jnp.float32)
    d_prob = jnp.einsum("qhd,khd->hqk", d_attended, values, preferred_element_type=jnp.float32)
    d_score = (
        prob_full * (d_prob - jnp.sum(prob_full * d_prob, axis=-1, keepdims=True))
    ).astype(jnp.bfloat16)
    d_queries = (
        jnp.einsum("hqk,khd->qhd", d_score, keys, preferred_element_type=jnp.float32) * SCALE
    )
    d_keys = (
        jnp.einsum("hqk,qhd->khd", d_score, queries, preferred_element_type=jnp.float32) * SCALE
    )
    return jnp.concatenate(
        [v.reshape(TILE_COUNT, D) for v in (d_queries, d_keys, d_values)], axis=1
    ).astype(jnp.bfloat16)


def attention_input_back(d_middle, d_joined, qkv_w, started, gain, bias):
    d_normed = times_transpose(d_joined, qkv_w)
    _, norm_back = jax.vjp(layer_norm, started, gain, bias)
    d_part, d_gain, d_shift = norm_back(d_normed)
    return d_middle + d_part, d_gain, d_shift


def small_gradient(rows, horizon_indicator, contribution, d_started, d_joined, d_attn, d_branch, d_pre, gains, shifts):
    def column_sum(value):
        return jnp.sum(value.astype(jnp.float32), axis=0)

    joined_sums = column_sum(d_joined)
    columns = jnp.stack(
        [
            *gains,
            shifts[0],
            column_sum(d_attn),
            shifts[1],
            column_sum(d_branch),
            joined_sums[:D],
            joined_sums[2 * D :],
        ],
        axis=1,
    )
    hidden_columns = column_sum(d_pre).reshape(D // rows, 4, rows).transpose(0, 2, 1).reshape(D, 4)
    return jnp.concatenate(
        [
            jnp.sum(d_started, axis=0)[:, None] * horizon_indicator[None, :],
            columns,
            hidden_columns,
            jnp.broadcast_to(digits_of(contribution)[None, :], (D, DIGITS)),
            jnp.zeros((D, LANES - LEADS - 12 - DIGITS), jnp.float32),
        ],
        axis=1,
    ).astype(jnp.bfloat16)


def small_outputs(value, rows):
    return (
        value[:, :LEADS],
        value[:, LEADS : LEADS + 2],
        value[:, LEADS + 2 : LEADS + 6],
        value[:, LEADS + 6 : LEADS + 8],
        value[:, LEADS + 8 : LEADS + 12].T.reshape(4 * rows),
    )


def frame_scalars(horizon_indices, horizon_tallies):
    indicator = (horizon_indices[0] == lax.iota(jnp.int32, LEADS)).astype(jnp.float32)
    frame_count = jnp.sum(indicator * horizon_tallies.astype(jnp.float32))
    return indicator, 1.0 / (frame_count * (LEADS * TILE_COUNT * TILE_SAMPLES))


def plain_step(
    tile_embeddings,
    horizon_indices,
    horizon_tallies,
    member_guesses,
    adjoint_of_mixture,
    triple_projection_matrix,
    attention_outward_matrix,
    widening_matrix,
    narrowing_matrix,
    gating_matrix,
    *small_parts,
):
    rows = triple_projection_matrix.shape[0]
    whole = functools.partial(lax.all_gather, axis_name=AXES, axis=0, tiled=True)

    def summed(value):
        return lax.psum_scatter(
            value.astype(jnp.bfloat16), AXES, scatter_dimension=0, tiled=True
        ).astype(jnp.float32)

    qkv_w, proj_w = whole(triple_projection_matrix), whole(attention_outward_matrix)
    fc1_w, fc2_w = whole(widening_matrix), whole(narrowing_matrix)
    par = Parameters(whole(pack_small(*small_parts, rows)), rows)
    indicator, strength = frame_scalars(horizon_indices, horizon_tallies)
    guesses = jnp.transpose(member_guesses[0], (1, 0, 2))
    lead_vector = jnp.sum(par.lead * indicator[None, :], axis=1)
    started, normed, joined = attention_input(
        tile_embeddings[0], lead_vector, par.gain[:, 0], par.bias[:, 0], par.offset, qkv_w
    )
    prob_full, attended = attention(joined)
    middle, normed_two = mlp_input(
        started, attended, proj_w, par.bias[:, 1], par.gain[:, 1], par.bias[:, 2]
    )
    pre_act, hidden, final_low = mlp(middle, normed_two, fc1_w, par.fc1, fc2_w, par.bias[:, 3])
    table = jnp.asarray([0, 1], jnp.int32)
    held_shape = (1, D, WIDE)
    combined, head_grads, d_parts, entropies = None, [], [], []
    head_w = whole(jnp.concatenate(head_chunks(gating_matrix), axis=1))
    for q in range(CHUNKS):
        halves = []
        for own in (False, True):
            combined, d_logits, d_part, entropy = head_pass(
                q,
                own,
                strength.reshape(1),
                table,
                final_low,
                [head_w],
                [(0, (0, 0), held_shape[1:], 0, 0, (0, 0))],
                held_shape,
                guesses,
                adjoint_of_mixture[0],
                combined,
            )
            flat = d_logits.transpose(1, 0, 2).reshape(TILE_COUNT, WIDE)
            halves.append(summed(transpose_times(final_low, flat)))
            d_parts.append(d_part)
            entropies.append(entropy)
        head_grads.append(halves)
    contribution = jnp.sum(sum(entropies)) * strength
    d_final, d_branch, d_pre = mlp_back(d_parts, pre_act, fc2_w)
    d_middle, d_attn, d_attended, gain_two, shift_two = mlp_input_back(
        d_final, d_pre, fc1_w, middle, par.gain[:, 1], par.bias[:, 2], proj_w
    )
    d_joined = attention_back(joined, prob_full, d_attended)
    d_started, gain_one, shift_one = attention_input_back(
        d_middle, d_joined, qkv_w, started, par.gain[:, 0], par.bias[:, 0]
    )
    small_grad = small_gradient(
        rows,
        indicator,
        contribution,
        d_started,
        d_joined,
        d_attn,
        d_branch,
        d_pre,
        (gain_one, gain_two),
        (shift_one, shift_two),
    )
    return (
        combined[None],
        lax.psum(contribution, AXES),
        d_started.astype(jnp.bfloat16)[None],
        summed(transpose_times(normed, d_joined)),
        summed(transpose_times(attended, d_attn)),
        summed(transpose_times(normed_two, d_pre)),
        summed(transpose_times(hidden, d_branch)),
        head_whole(*zip(*head_grads)),
        *small_outputs(summed(small_grad), rows),
    )


def paired_step(
    tile_embeddings,
    horizon_indices,
    horizon_tallies,
    member_guesses,
    adjoint_of_mixture,
    triple_projection_matrix,
    attention_outward_matrix,
    widening_matrix,
    narrowing_matrix,
    gating_matrix,
    *small_parts,
):
    rows = triple_projection_matrix.shape[0]
    core = lax.axis_index("fsdp") % 2
    table = places(True)
    marks = jnp.concatenate([core.reshape(1), places(False)[::2] // 2])
    head_marks = jnp.concatenate([core.reshape(1), table[::2] // 2])
    head_table = jnp.concatenate([table, core.reshape(1)])
    seq = Sequence(horizon_tallies)
    indicator, strength = frame_scalars(horizon_indices, horizon_tallies)

    first_own, second_own = seq.run(
        pack_trunk,
        triple_projection_matrix,
        attention_outward_matrix,
        widening_matrix,
        narrowing_matrix,
        *small_parts,
    )
    one, two = RoundFirst(seq, first_own, 1), RoundFirst(seq, second_own, -1)
    one.start()
    two.start()
    head_own = seq.run(pack_head, gating_matrix)
    over = across(head_own)
    one.arrive()
    one.start()
    two.arrive()
    two.start()
    one.arrive()
    one.start()
    two.arrive()
    two.start()
    over = seq.tie(over)
    one.arrive()
    one.last()
    two.arrive()
    two.last()
    one.arrive_last()
    one.batch()
    two.arrive_last()
    head_first = seq.run(lambda a, b: jnp.concatenate([a, b], axis=0), head_own, over)
    three = AcrossFirst(seq, head_first)
    three.start()
    guesses = seq.run(
        lambda v: lax.optimization_barrier(jnp.transpose(v[0], (1, 0, 2))), member_guesses
    )
    three.arrive()
    three.start()
    one.arrive_over()
    two.batch()
    one.arrive_batches()
    whole_one = [((0, rows), (0, FIRST_WIDE), 0, 0, 0)]
    whole_two = [((0, 8 * rows), (0, D), 0, 0, 0)]
    index = horizon_indices
    sources_one, moves = plan_moves(one.collect(), whole_one)
    middle, normed, joined, attended, normed_two, par, fc1_b = seq.run(
        functools.partial(trunk_first, table, index, rows, moves), tile_embeddings[0], *sources_one
    )
    three.settle()
    three.arrive()
    three.start()
    adjoint = seq.run(lambda v: lax.optimization_barrier(v[0]), adjoint_of_mixture)
    two.arrive_batches()
    three.settle()
    three.arrive()
    three.last()
    two.arrive_over()
    two.arrive_batches()
    sources_two, moves_two = plan_moves(two.collect(), whole_two)
    hidden, slope, final_low = seq.run(
        functools.partial(trunk_second, table, rows, moves_two),
        middle,
        normed_two,
        par,
        fc1_b,
        *sources_two,
    )
    three.settle()
    three.arrive_last()
    final_other = sibling(final_low)
    normed_other, attended_other = sibling(normed), sibling(attended)
    normed_two_other, hidden_other = sibling(normed_two), sibling(hidden)

    held_shape = (32, rows, WIDE)
    head_fields = [((0, rows), (0, WIDE), 0, 0, 0)]
    state = dict(combined=None, d_parts=[], entropies=[])

    def head(q, own, around):
        sources, moves = plan_moves(around.collect(), head_fields)
        before = () if state["combined"] is None else (state["combined"],)

        def function(final_low, before, *sources):
            return head_pass(
                q,
                own,
                strength.reshape(1),
                head_table,
                final_low,
                list(sources),
                moves,
                held_shape,
                guesses,
                adjoint,
                before[0] if before else None,
            )

        state["combined"], d_logits, d_part, entropy = seq.run(
            function, final_low, before, *sources
        )
        state["d_parts"].append(d_part)
        state["entropies"].append(entropy)
        return d_logits

    make_grad = functools.partial(head_grad, head_marks)
    send = sibling(head(0, False, three))
    own = head(0, True, three)
    sum_one = SumRoundFirst(seq, *seq.run(make_grad, final_low, final_other, own, send))
    moves_proj = plan_moves(one.collect(), [((0, rows), (3 * D, 4 * D), 0, 0, 0)])[1]
    moves_qkv = plan_moves(one.collect(), [((0, rows), (0, 3 * D), 0, 0, 0)])[1]
    d_branch, d_pre, d_middle, d_attn, d_attended, d_rows, d_fc1_b = seq.run(
        functools.partial(second_back, table, rows, moves_two, moves_proj, len(sources_two)),
        slope,
        middle,
        par,
        state["d_parts"],
        *sources_two,
        *sources_one,
    )
    d_attn_other, d_fc1_b_other = sibling(d_attn), sibling(d_fc1_b)
    d_branch_other, d_pre_other = sibling(d_branch), sibling(d_pre)
    sum_one.arrive()
    sum_one.step(3)
    d_branch_other, d_pre_other = seq.tie(d_branch_other, d_pre_other)
    parts = seq.run(
        lambda *ins: ring_grad(
            second_grad_body,
            marks,
            ins,
            (16 * rows, D // 2),
            [(16, 8 * rows, D // 2), (16, 2 * rows, FF // 2)],
            "second_grad",
        ),
        *(hidden, hidden_other, d_branch, d_branch_other),
        *(normed_two, normed_two_other, d_pre, d_pre_other),
    )
    sum_three = SumAcrossFirst(seq, parts, 1)
    sum_three.go_across(0)
    d_joined, tokens, small_grad = seq.run(
        functools.partial(first_back, table, index, strength.reshape(1), rows, moves_qkv),
        tile_embeddings[0],
        joined,
        par,
        d_middle,
        d_attended,
        d_rows,
        state["entropies"],
        *sources_one,
    )
    d_joined_other, small_other = sibling(d_joined), sibling(small_grad)
    sum_three.arrive_across(0)
    sum_one.arrive()
    sum_three.step(4)
    sum_one.add(2)
    sum_three.arrive()
    sum_three.step(3)
    sum_one.send()
    sum_three.go_across(1)
    blocks = seq.run(
        lambda *ins: round_grad(
            first_grad_body,
            head_marks,
            ins,
            (2 * rows, 2 * D + 2 * LANES),
            [(16, 2 * rows, 3 * D // 2), (16, 2 * rows, D // 2), (16, 2 * rows, LANES)]
            + [(LANES, D), (32, LANES), (2 * rows, LANES)],
            "first_grad",
        ),
        *(normed, normed_other, d_joined, d_joined_other),
        *(attended, attended_other, d_attn, d_attn_other),
        *(small_grad, small_other, d_fc1_b, d_fc1_b_other),
    )
    sum_four = SumRoundFirst(seq, *blocks)
    sum_one.arrive()
    sum_one.step(1)
    sum_four.arrive()
    sum_four.step(3)
    combined_result = seq.run(lambda v: lax.optimization_barrier(v[None]), state["combined"])
    grad_tokens = tokens[None]
    sum_three.arrive()
    sum_three.arrive_across(1)
    sum_three.step(2)
    sum_one.arrive()
    sum_one.go_across()
    sum_four.arrive()
    sum_four.step(2)
    sum_three.arrive()
    sum_three.step(1)
    sum_four.arrive()
    sum_four.step(1)
    first = core == 0

    def finish(total, rows_of):
        low, high = rows_of(total, 0, rows), rows_of(total, 1, rows)
        own, other = jnp.where(first, low, high), jnp.where(first, high, low)
        met = sibling(other.astype(jnp.bfloat16)).astype(jnp.float32)
        return jnp.where(first, own, met), jnp.where(first, met, own)

    low, high = finish(sum_one.finish(), low_or_high)
    out_head = head_whole([low], [high])
    sum_three.arrive()
    total = sum_three.finish()
    out_fc2 = jnp.concatenate(finish(total, fc2_rows), axis=1)
    out_fc1 = jnp.concatenate(finish(total, fc1_rows), axis=1)
    sum_four.arrive()
    sum_four.go_across()
    total = sum_four.finish()
    out_small = jnp.where(first, total[:rows, 2 * D :], total[rows:, 2 * D :])
    low, high = finish(total[:, : 2 * D], low_or_high)
    n = 3 * D // 2
    out_fc1_b = out_small[0, LANES : LANES + 4 * rows]
    cost = value_of(out_small[0, ROW_DIGIT : ROW_DIGIT + DIGITS])
    cost = jnp.where(seq.token[0] < 0, 0.0, cost)
    return (
        combined_result,
        cost,
        grad_tokens,
        jnp.concatenate([low[:, :n], high[:, :n]], axis=1),
        jnp.concatenate([low[:, n:], high[:, n:]], axis=1),
        out_fc1,
        out_fc2,
        out_head,
        out_small[:, :LEADS],
        out_small[:, ROW_GAIN:ROW_BIAS],
        out_small[:, ROW_BIAS:ROW_QKV],
        out_small[:, ROW_QKV:ROW_DIGIT],
        out_fc1_b,
    )


def solution(mesh):
    split = P(AXES)
    paired = mesh.shape["dp"] == 2 and mesh.shape["fsdp"] == 16
    return jax.shard_map(
        paired_step if paired else plain_step,
        mesh=mesh,
        in_specs=(split, split, P()) + (split,) * 12,
        out_specs=(split, P()) + (split,) * 11,
        check_vma=False,
    )
```

```python
import functools

import jax
import jax.numpy as jnp
from jax import lax
from jax.experimental import pallas as pl
from jax.experimental.pallas import tpu as pltpu
from jax.sharding import PartitionSpec as P

D = 768
HEADS = 12
HD = 64
FF = 3072
MODEL_COUNT = 3
TILE_SAMPLES = 4416
LEADS = 40
TILE_COUNT = 256
EPS = 1e-06
LANES = 128
HALF = 2304
PADDED = 2 * HALF
VMEM = 56 * 1024 * 1024

AXES = ("dp", "fsdp")
RING = [(z, 0) for z in range(4)] + [(z, 1) for z in (3, 2, 1, 0)]


def ring_pairs(step):
    pairs = []
    for spot, (z, x) in enumerate(RING):
        to_z, to_x = RING[(spot + step) % 8]
        for core in range(2):
            pairs.append((z * 4 + x * 2 + core, to_z * 4 + to_x * 2 + core))
    return pairs


def forth(value):
    return lax.ppermute(value, "fsdp", ring_pairs(1))


def back(value):
    return lax.ppermute(value, "fsdp", ring_pairs(-1))


def across(value):
    return lax.ppermute(value, "dp", [(0, 1), (1, 0)])


def exchange_rows(value):
    return lax.all_to_all(value, "dp", 0, 0)


def sibling(value):
    return lax.ppermute(value, "fsdp", [(i, i ^ 1) for i in range(16)])


def places(relative):
    y = lax.axis_index("dp") if relative else 0
    f = lax.axis_index("fsdp")
    z, x, core = f // 4, (f // 2) % 2, f % 2
    spot = jnp.where(x == 0, z, 7 - z)
    i = lax.iota(jnp.int32, 32)
    seat = (spot + (i // 2) % 8) % 8
    pair = jnp.where(seat < 4, seat * 2, (7 - seat) * 2 + 1)
    return ((y + i // 16) % 2) * 16 + pair * 2 + (core + i) % 2


def slot(other_row, distance, other_core):
    return other_row * 16 + (distance % 8) * 2 + other_core


def plan_moves(found, fields):
    sources, moves = [], []
    for source, rows, where in found:
        at = [i for i, s in enumerate(sources) if s is source]
        if not at:
            at = [len(sources)]
            sources.append(source)
        for (f0, f1), (g0, g1), out, out_row, out_col in fields:
            moves.append(
                (at[0], (rows[0] + f0, g0), (f1 - f0, g1 - g0), where, out, (out_row, out_col))
            )
    return sources, moves


def place(sources, moves, shapes, table, shards):
    def body(table_ref, *refs):
        ins, outs = refs[: len(sources)], refs[len(sources) : len(sources) + len(shapes)]
        held, sems, out_sems = refs[len(sources) + len(shapes) : -2], refs[-2], refs[-1]
        run_moves(moves, table_ref, ins, held, sems)
        copies = [
            pltpu.make_async_copy(held[i], outs[i], out_sems.at[i]) for i in range(len(shapes))
        ]
        for copy in copies:
            copy.start()
        for copy in copies:
            copy.wait()

    whole = [(shards,) + s for s in shapes]
    return pl.pallas_call(
        body,
        grid_spec=pltpu.PrefetchScalarGridSpec(
            num_scalar_prefetch=1,
            grid=(1,),
            in_specs=[pl.BlockSpec(memory_space=pl.ANY)] * len(sources),
            out_specs=[pl.BlockSpec(memory_space=pl.ANY)] * len(shapes),
            scratch_shapes=[pltpu.VMEM(s, jnp.bfloat16) for s in whole]
            + [
                pltpu.SemaphoreType.DMA((len(moves),)),
                pltpu.SemaphoreType.DMA((len(shapes),)),
            ],
        ),
        out_shape=[jax.ShapeDtypeStruct(s, jnp.bfloat16) for s in whole],
        compiler_params=pltpu.CompilerParams(vmem_limit_bytes=VMEM),
        name="place",
    )(table, *sources)


def run_moves(moves, table_ref, ins, outs, sems, begin=0):
    copies = []
    for i, (at, (sr, sc), (nr, nc), where, out, (dr, dc)) in enumerate(moves):
        copy = pltpu.make_async_copy(
            ins[at].at[pl.ds(sr, nr), pl.ds(begin + sc, nc)],
            outs[out].at[table_ref[where], pl.ds(dr, nr), pl.ds(dc, nc)],
            sems.at[i],
        )
        copy.start()
        copies.append(copy)
    for copy in copies:
        copy.wait()


def add_low(*values):
    total = values[0].astype(jnp.float32)
    for value in values[1:]:
        total = total + value.astype(jnp.float32)
    return total.astype(jnp.bfloat16)


class Sequence:
    def __init__(self, token):
        self.token = token

    def tie(self, *values):
        out = lax.optimization_barrier((self.token,) + values)
        self.token = out[0]
        return out[1] if len(values) == 1 else out[1:]

    def run(self, function, *values):
        values = lax.optimization_barrier((self.token,) + values)
        self.token = values[0]
        return self.tie(function(*values[1:]))


class Around:
    def __init__(self, seq, first):
        self.seq, self.rights, self.lefts = seq, [first], [first]

    def start(self, right=True, left=True):
        if right:
            self.rights.append(forth(self.rights[-1]))
        if left:
            self.lefts.append(back(self.lefts[-1]))

    def arrive(self, right=True, left=True):
        ends = ([self.rights] if right else []) + ([self.lefts] if left else [])
        met = self.seq.tie(*[end[-1] for end in ends])
        for end, value in zip(ends, met if len(ends) > 1 else (met,)):
            end[-1] = value


class RoundFirst(Around):
    def __init__(self, seq, first, longer):
        super().__init__(seq, first)
        self.longer, self.found = longer, []

    def last(self):
        ends = self.rights if self.longer > 0 else self.lefts
        ends.append(forth(ends[-1]) if self.longer > 0 else back(ends[-1]))

    def arrive_last(self):
        self.arrive(self.longer > 0, self.longer < 0)

    def batch(self):
        rights, lefts = self.rights, self.lefts
        r = rights[0].shape[0]
        end = rights[4] if self.longer > 0 else lefts[4]
        parts = (rights[0], rights[1], lefts[1], rights[2], lefts[2], rights[3], lefts[3], end)
        distances = (0, -1, 1, -2, 2, -3, 3, 4)
        joint = self.seq.run(lambda *v: jnp.concatenate(v, axis=0), *parts)
        self.over = across(joint), r, distances
        self.found.append((joint, r, 0, 0, distances))
        self.found.append((sibling(joint), r, 0, 1, distances))

    def arrive_over(self):
        over, r, distances = self.over
        over = self.seq.tie(over)
        self.found.append((over, r, 1, 0, distances))
        self.found.append((sibling(over), r, 1, 1, distances))

    def arrive_batches(self):
        met = self.seq.tie(*[v[0] for v in self.found])
        self.found = [(m,) + v[1:] for m, v in zip(met, self.found)]

    def collect(self):
        return [
            (source, (i * r, (i + 1) * r), slot(other_row, k, other_core))
            for source, r, other_row, other_core, distances in self.found
            for i, k in enumerate(distances)
        ]


class AcrossFirst(Around):
    def __init__(self, seq, first):
        super().__init__(seq, first)
        self.found, self.settled = [], set()
        self.note(first, [(0, 0), (1, 0)])

    def note(self, joint, spots):
        self.found.append((joint, 0, spots))
        self.found.append((sibling(joint), 1, spots))

    def settle(self):
        late = [i for i, item in enumerate(self.found) if item[1] and i not in self.settled]
        met = self.seq.tie(*[self.found[i][0] for i in late])
        for i, value in zip(late, met if len(late) > 1 else (met,)):
            self.found[i] = (value,) + self.found[i][1:]
        self.settled.update(late)

    def arrive(self):
        super().arrive()
        k = len(self.rights) - 1
        self.note(self.rights[k], [(0, -k), (1, -k)])
        self.note(self.lefts[k], [(0, k), (1, k)])

    def last(self):
        r = self.rights[0].shape[0] // 2
        right, left = self.seq.run(lambda a, b: (a[:r], b[r:]), self.rights[3], self.lefts[3])
        self.far = [forth(right), back(left)]

    def arrive_last(self):
        self.far = list(self.seq.tie(*self.far))
        for row, array in enumerate(self.far):
            self.note(array, [(row, 4)])

    def collect(self):
        r = self.rights[0].shape[0] // 2
        return [
            (source, (i * r, (i + 1) * r), slot(row, k, other_core))
            for source, other_core, spots in self.found
            for i, (row, k) in enumerate(spots)
        ]


ORDER_FIRST = (4, 3, -3)
ORDER_LAST = (2, -2, 1, -1, 0)


class SumAcrossFirst:
    def __init__(self, seq, parts, longer):
        self.seq, self.longer, self.ready = seq, longer, {}
        self.parts = parts
        self.met = [None, None]
        self.right = self.left = None

    def go_across(self, part):
        self.met[part] = exchange_rows(self.parts[part])

    def arrive_across(self, part):
        met = self.seq.tie(self.met[part])
        for i, k in enumerate((ORDER_FIRST, ORDER_LAST)[part]):
            self.ready[k] = (met, i)

    def arrive(self):
        if self.right is None:
            self.left = self.seq.tie(self.left)
        elif self.left is None:
            self.right = self.seq.tie(self.right)
        else:
            self.right, self.left = self.seq.tie(self.right, self.left)

    def step(self, k):
        if k == 4:
            value = self.seq.run(lambda v: add_low(v[0, 0], v[1, 0]), self.ready[4][0])
            if self.longer > 0:
                self.right = forth(value)
            else:
                self.left = back(value)
            return
        (met, i), (_, j) = self.ready[k], self.ready[-k]

        def add(met, right, left):
            return add_low(met[0, i], met[1, i], *right), add_low(met[0, j], met[1, j], *left)

        right = () if self.right is None else (self.right,)
        left = () if self.left is None else (self.left,)
        go_right, go_left = self.seq.run(add, met, right, left)
        self.right, self.left = forth(go_right), back(go_left)

    def finish(self):
        met, i = self.ready[0]

        def add(met, right, left):
            return sum(v.astype(jnp.float32) for v in (met[0, i], met[1, i], right, left))

        return self.seq.run(add, met, self.right, self.left)


class SumRoundFirst:
    def __init__(self, seq, blocks, far_right, far_left):
        self.seq, self.blocks = seq, blocks
        self.right, self.left = forth(far_right), back(far_left)

    def arrive(self):
        self.right, self.left = self.seq.tie(self.right, self.left)

    def step(self, k):
        def add_part(one, two, right, left):
            r = right.shape[0]
            return (
                jnp.concatenate([add_low(one[:r], right), one[r:]], axis=0),
                jnp.concatenate([two[:r], add_low(two[r:], left)], axis=0),
            )

        if k == 3:
            values = self.blocks[k], self.blocks[-k], self.right, self.left
            go_right, go_left = self.seq.run(add_part, *values)
            self.right, self.left = forth(go_right), back(go_left)
        else:
            self.right = forth(self.seq.run(add_low, self.blocks[k], self.right))
            self.left = back(self.seq.run(add_low, self.blocks[-k], self.left))

    def add(self, k):
        self.right = self.seq.run(add_low, self.blocks[k], self.right)
        self.left = self.seq.run(add_low, self.blocks[-k], self.left)

    def send(self):
        self.arrive()
        self.right, self.left = forth(self.right), back(self.left)

    def go_across(self):
        def add(block, right, left):
            r = block.shape[0] // 2
            near = sum(v[:r].astype(jnp.float32) for v in (block, right, left))
            return near, add_low(block[r:], right[r:], left[r:])

        self.near, sent = self.seq.run(add, self.blocks[0], self.right, self.left)
        self.met = across(sent)

    def finish(self):
        return self.seq.run(lambda a, b: a + b.astype(jnp.float32), self.near, self.met)


def layer_norm(values, norm_gain, norm_shift):
    row_mean = jnp.mean(values, axis=-1, keepdims=True)
    centred = values - row_mean
    row_var = jnp.mean(centred * centred, axis=-1, keepdims=True)
    return centred * lax.rsqrt(row_var + EPS) * norm_gain + norm_shift


def exact_gelu(values):
    return jax.nn.gelu(values, approximate=False)


def plain_dot(left, right):
    return jnp.dot(left, right, preferred_element_type=jnp.float32)


def times_transpose(left, right):
    return lax.dot_general(
        left, right, (((1,), (1,)), ((), ())), preferred_element_type=jnp.float32
    )


def transpose_times(left, right):
    return lax.dot_general(
        left, right, (((0,), (0,)), ((), ())), preferred_element_type=jnp.float32
    )


CHUNKS = 1
CHUNK = HALF // CHUNKS
LIGHT = pl.CostEstimate(flops=0, transcendentals=0, bytes_accessed=0)
HEAD_TILE = 384
HALF_STEPS = CHUNK // HEAD_TILE
ROWS = 16
COLS = 384


def half_of(own, table_ref):
    core = table_ref[table_ref.shape[0] - 1]
    return core if own else 1 - core


def pixel_block(q, own, j, table_ref):
    return half_of(own, table_ref) * (CHUNKS * HALF_STEPS) + q * HALF_STEPS + j


def head_body(q, own, moves, weight_ref, table_ref, x_ref, guess_ref, adj_ref, *refs):
    ins, refs = refs[:-7], refs[-7:]
    comb_ref, dl_ref, df_ref, ent_ref, logit_ref, held_ref, sems = refs
    j = pl.program_id(0)
    strength = weight_ref[0]
    half = half_of(own, table_ref)
    first_pixel = half * HALF + q * CHUNK + j * HEAD_TILE

    @pl.when(j == 0)
    def _():
        df_ref[...] = jnp.zeros_like(df_ref)
        ent_ref[...] = jnp.zeros_like(ent_ref)
        begin = pl.multiple_of((2 * q + half) * WIDE, LANES)
        run_moves(moves, table_ref, ins, [held_ref], sems, begin)

    x = x_ref[...]

    def weight(e):
        begin = pl.multiple_of(e * CHUNK + j * HEAD_TILE, LANES)
        return held_ref[:, :, pl.ds(begin, HEAD_TILE)].reshape(D, HEAD_TILE)

    for e in range(MODEL_COUNT):
        logit_ref[e] = jnp.dot(x, weight(e), preferred_element_type=jnp.float32)

    for part in range(HEAD_TILE // COLS):
        cols = pl.ds(part * COLS, COLS)
        pixel = first_pixel + part * COLS + lax.broadcasted_iota(jnp.int32, (ROWS, COLS), 1)
        real = pixel < TILE_SAMPLES

        def chunk(i, total):
            rows = pl.ds(pl.multiple_of(i * ROWS, ROWS), ROWS)
            l0, l1, l2 = (logit_ref[e, rows, cols] for e in range(3))
            top = jnp.maximum(jnp.maximum(l0, l1), l2)
            l0, l1, l2 = l0 - top, l1 - top, l2 - top
            e0, e1, e2 = jnp.exp(l0), jnp.exp(l1), jnp.exp(l2)
            norm = e0 + e1 + e2
            inverse = 1.0 / norm
            log_norm = jnp.log(norm)
            b0, b1, b2 = e0 * inverse, e1 * inverse, e2 * inverse
            l0, l1, l2 = l0 - log_norm, l1 - log_norm, l2 - log_norm
            minus_h = b0 * l0 + b1 * l1 + b2 * l2
            g0, g1, g2 = (guess_ref[e, rows, cols].astype(jnp.float32) for e in range(3))
            mixed = b0 * g0 + b1 * g1 + b2 * g2
            comb_ref[rows, cols] = mixed.astype(jnp.bfloat16)
            adj = adj_ref[rows, cols].astype(jnp.float32)
            for e, (b, l, g) in enumerate(((b0, l0, g0), (b1, l1, g1), (b2, l2, g2))):
                d = b * (adj * (g - mixed) - strength * (l - minus_h))
                dl_ref[e, rows, cols] = jnp.where(real, d, 0.0).astype(jnp.bfloat16)
            return total - jnp.where(real, minus_h, 0.0)

        total = lax.fori_loop(
            0,
            TILE_COUNT // ROWS,
            chunk,
            jnp.zeros((ROWS, COLS), jnp.float32),
            unroll=True,
        )
        gathered = total[:, :LANES]
        for k in range(1, COLS // LANES):
            gathered = gathered + total[:, k * LANES : (k + 1) * LANES]
        ent_ref[...] += gathered[:8] + gathered[8:]

    part = None
    for e in range(MODEL_COUNT):
        piece = lax.dot_general(
            dl_ref[e], weight(e), (((1,), (1,)), ((), ())), preferred_element_type=jnp.float32
        )
        part = piece if part is None else part + piece
    df_ref[...] += part


def head_pass(q, own, strength, table, final_low, sources, moves, held_shape, guesses, adjoint, before):
    tile = HEAD_TILE
    extra = [] if before is None else [before]

    def body(*refs):
        refs = refs[:5] + refs[5 + len(extra) :]
        head_body(q, own, moves, *refs)

    d_spec = (MODEL_COUNT, TILE_COUNT, tile)
    return pl.pallas_call(
        body,
        grid_spec=pltpu.PrefetchScalarGridSpec(
            num_scalar_prefetch=2,
            grid=(HALF_STEPS,),
            in_specs=[
                pl.BlockSpec((TILE_COUNT, D), lambda j, s, t: (0, 0)),
                pl.BlockSpec(d_spec, lambda j, s, t: (0, 0, pixel_block(q, own, j, t))),
                pl.BlockSpec((TILE_COUNT, tile), lambda j, s, t: (0, pixel_block(q, own, j, t))),
            ]
            + [pl.BlockSpec(memory_space=pl.ANY)] * (len(extra) + len(sources)),
            out_specs=[
                pl.BlockSpec((TILE_COUNT, tile), lambda j, s, t: (0, pixel_block(q, own, j, t))),
                pl.BlockSpec(d_spec, lambda j, s, t: (0, 0, j)),
                pl.BlockSpec((TILE_COUNT, D), lambda j, s, t: (0, 0)),
                pl.BlockSpec((8, LANES), lambda j, s, t: (0, 0)),
            ],
            scratch_shapes=[
                pltpu.VMEM(d_spec, jnp.float32),
                pltpu.VMEM(held_shape, jnp.bfloat16),
                pltpu.SemaphoreType.DMA((len(moves),)),
            ],
        ),
        out_shape=[
            jax.ShapeDtypeStruct((TILE_COUNT, TILE_SAMPLES), jnp.bfloat16),
            jax.ShapeDtypeStruct((MODEL_COUNT, TILE_COUNT, CHUNK), jnp.bfloat16),
            jax.ShapeDtypeStruct((TILE_COUNT, D), jnp.float32),
            jax.ShapeDtypeStruct((8, LANES), jnp.float32),
        ],
        input_output_aliases={5: 0} if extra else {},
        compiler_params=pltpu.CompilerParams(
            dimension_semantics=("arbitrary",), vmem_limit_bytes=VMEM
        ),
        cost_estimate=LIGHT,
        name="head_pass",
    )(strength, table, final_low, guesses, adjoint, *extra, *sources)


def flip_body(in_ref, out_ref):
    out_ref[...] = in_ref[...].T


def flip(value):
    tile = HEAD_TILE
    rows, n = value.shape
    return pl.pallas_call(
        flip_body,
        grid=(pl.cdiv(n, tile),),
        in_specs=[pl.BlockSpec((rows, tile), lambda j: (0, j))],
        out_specs=pl.BlockSpec((tile, rows), lambda j: (j, 0)),
        out_shape=jax.ShapeDtypeStruct((n, rows), value.dtype),
        compiler_params=pltpu.CompilerParams(vmem_limit_bytes=VMEM),
        cost_estimate=LIGHT,
        name="flip",
    )(value)


def dot_tokens(left, right):
    return lax.dot_general(left, right, (((0,), (0,)), ((), ())), preferred_element_type=jnp.float32)


def chip_at(marks_ref, row, distance):
    return marks_ref[1 + row * 8 + distance % 8]


HEAD_ORDER = (0, 1, -1, 2, -2, 3, -3)


def head_grad_body(marks_ref, x_mine_ref, x_other_ref, d_mine_ref, d_other_ref, *refs):
    outs, right_ref, left_ref, sum_ref = refs[:7], refs[7], refs[8], refs[9]
    value = dot_tokens(x_mine_ref[...], d_mine_ref[0]) + dot_tokens(x_other_ref[...], d_other_ref[0])
    sum_ref[...] = value.reshape(sum_ref.shape)
    r = sum_ref.shape[1]
    for k, out in zip(HEAD_ORDER, outs):
        for row in (0, 1):
            block = sum_ref[chip_at(marks_ref, row, k)].astype(jnp.bfloat16)
            out[row * r : (row + 1) * r, :] = block
    right_ref[...] = sum_ref[chip_at(marks_ref, 0, 4)].astype(jnp.bfloat16)
    left_ref[...] = sum_ref[chip_at(marks_ref, 1, 4)].astype(jnp.bfloat16)


def head_grad(marks, x_mine, x_other, d_mine, d_other):
    tile = 1152
    steps = CHUNK // tile
    r = D // 16
    n = MODEL_COUNT * CHUNK
    tall = [2 * r] * 7 + [r] * 2
    outs = pl.pallas_call(
        head_grad_body,
        grid_spec=pltpu.PrefetchScalarGridSpec(
            num_scalar_prefetch=1,
            grid=(MODEL_COUNT, steps),
            in_specs=[
                pl.BlockSpec((TILE_COUNT, D), lambda e, j, c: (0, 0)),
                pl.BlockSpec((TILE_COUNT, D), lambda e, j, c: (0, 0)),
                pl.BlockSpec((1, TILE_COUNT, tile), lambda e, j, c: (e, 0, j)),
                pl.BlockSpec((1, TILE_COUNT, tile), lambda e, j, c: (e, 0, j)),
            ],
            out_specs=[pl.BlockSpec((h, tile), lambda e, j, c: (0, e * steps + j)) for h in tall],
            scratch_shapes=[pltpu.VMEM((16, r, tile), jnp.float32)],
        ),
        out_shape=[jax.ShapeDtypeStruct((h, n), jnp.bfloat16) for h in tall],
        compiler_params=pltpu.CompilerParams(
            dimension_semantics=("arbitrary", "arbitrary"), vmem_limit_bytes=VMEM
        ),
        cost_estimate=LIGHT,
        name="head_grad",
    )(marks, x_mine, x_other, d_mine, d_other)
    return dict(zip(HEAD_ORDER, outs[:7])), outs[7], outs[8]


def ring_rows(marks_ref, outs, write):
    for row in (0, 1):
        for out, order in zip(outs, (ORDER_FIRST, ORDER_LAST)):
            for i, k in enumerate(order):
                write(out, row, i, chip_at(marks_ref, row, k))


def core_half(ref, marks_ref):
    n = ref.shape[1] // 2
    return ref[:, pl.ds(pl.multiple_of(marks_ref[0] * n, LANES), n)]


def paired_product(marks_ref, x, x_other, d, d_other):
    return dot_tokens(x[...], core_half(d, marks_ref)) + dot_tokens(
        x_other[...], core_half(d_other, marks_ref)
    )


def second_grad_body(marks_ref, *refs):
    ins, outs, (fc2_ref, fc1_ref) = refs[:8], refs[8:10], refs[10:]
    fc2_ref[...] = paired_product(marks_ref, *ins[:4]).reshape(fc2_ref.shape)
    fc1_ref[...] = paired_product(marks_ref, *ins[4:]).reshape(fc1_ref.shape)
    r4, wide = fc2_ref.shape[1:]
    r = fc1_ref.shape[1]

    def write(out, row, i, chip):
        out[row, i, :r4, :] = fc2_ref[chip].astype(jnp.bfloat16)
        for k in range(4):
            block = fc1_ref[chip, :, k * wide : (k + 1) * wide].astype(jnp.bfloat16)
            out[row, i, r4 + k * r : r4 + (k + 1) * r, :] = block

    ring_rows(marks_ref, outs, write)


def first_grad_body(marks_ref, *refs):
    ins, outs, refs = refs[:12], refs[12:21], refs[21:]
    qkv_ref, proj_ref, small_ref, flat_ref, hidden_ref, block_ref = refs
    qkv_ref[...] = paired_product(marks_ref, *ins[:4]).reshape(qkv_ref.shape)
    proj_ref[...] = paired_product(marks_ref, *ins[4:8]).reshape(proj_ref.shape)
    flat_ref[...] = jnp.zeros_like(flat_ref)
    flat_ref[: ins[8].shape[0], :] = ins[8][...] + ins[9][...]
    small_ref[...] = flat_ref[...].T.reshape(small_ref.shape)
    shards = hidden_ref.shape[0]
    r, wide = qkv_ref.shape[1] // 2, FF // shards
    hidden_ref[...] = jnp.zeros_like(hidden_ref)
    for d in range(shards):
        cols = slice(d * wide, (d + 1) * wide)
        hidden_ref[d : d + 1, :wide] = ins[10][:, cols] + ins[11][:, cols]
    block_ref[...] = jnp.zeros_like(block_ref)
    n, m = qkv_ref.shape[2], qkv_ref.shape[2] + proj_ref.shape[2]

    def write(out, at, chip):
        rows = slice(at, at + 2 * r)
        out[rows, :n] = qkv_ref[chip].astype(jnp.bfloat16)
        out[rows, n:m] = proj_ref[chip].astype(jnp.bfloat16)
        out[rows, m : m + LANES] = small_ref[chip].astype(jnp.bfloat16)
        block_ref[0:1, :] = hidden_ref[pl.ds(2 * chip, 1), :]
        block_ref[r : r + 1, :] = hidden_ref[pl.ds(2 * chip + 1, 1), :]
        out[rows, m + LANES :] = block_ref[...].astype(jnp.bfloat16)

    for k, out in zip(HEAD_ORDER, outs):
        for row in (0, 1):
            write(out, row * 2 * r, chip_at(marks_ref, row, k))
    for row, out in enumerate(outs[7:]):
        write(out, 0, chip_at(marks_ref, row, 4))


def round_grad(body, marks, ins, block, scratch, name):
    r, n = block
    shapes = [(2 * r, n)] * 7 + [(r, n)] * 2
    outs = pl.pallas_call(
        body,
        grid_spec=pltpu.PrefetchScalarGridSpec(
            num_scalar_prefetch=1,
            grid=(1,),
            in_specs=[pl.BlockSpec(v.shape, lambda i, m: (0, 0)) for v in ins],
            out_specs=[pl.BlockSpec(s, lambda i, m: (0, 0)) for s in shapes],
            scratch_shapes=[pltpu.VMEM(s, jnp.float32) for s in scratch],
        ),
        out_shape=[jax.ShapeDtypeStruct(s, jnp.bfloat16) for s in shapes],
        compiler_params=pltpu.CompilerParams(vmem_limit_bytes=VMEM),
        cost_estimate=LIGHT,
        name=name,
    )(marks, *ins)
    return dict(zip(HEAD_ORDER, outs[:7])), outs[7], outs[8]


def ring_grad(body, marks, ins, block, scratch, name):
    shapes = [(2, 3) + block, (2, 5) + block]
    return pl.pallas_call(
        body,
        grid_spec=pltpu.PrefetchScalarGridSpec(
            num_scalar_prefetch=1,
            grid=(1,),
            in_specs=[pl.BlockSpec(v.shape, lambda i, m: (0, 0)) for v in ins],
            out_specs=[pl.BlockSpec(s, lambda i, m: (0, 0, 0, 0)) for s in shapes],
            scratch_shapes=[pltpu.VMEM(s, jnp.float32) for s in scratch],
        ),
        out_shape=[jax.ShapeDtypeStruct(s, jnp.bfloat16) for s in shapes],
        compiler_params=pltpu.CompilerParams(vmem_limit_bytes=VMEM),
        cost_estimate=LIGHT,
        name=name,
    )(marks, *ins)


def pack_small(lead_w, gains, biases, qkv_b, fc1_b, rows):
    value = jnp.concatenate([lead_w, gains, biases, qkv_b, fc1_b.reshape(4, rows).T], axis=1)
    return jnp.pad(value, ((0, 0), (0, LANES - value.shape[1])))


def split_small(small):
    at, found = 0, []
    for width in (LEADS, 2, 4, 2, 4):
        found.append(small[:, at : at + width])
        at += width
    return found


WIDE = MODEL_COUNT * CHUNK


def head_chunks(value):
    r = value.shape[0]
    value = value.reshape(r, MODEL_COUNT, TILE_SAMPLES)
    value = jnp.pad(value, ((0, 0), (0, 0), (0, PADDED - TILE_SAMPLES)))
    value = value.reshape(r, MODEL_COUNT, 2, CHUNKS, CHUNK).transpose(0, 2, 1, 3, 4)
    return [value[:, :, :, q].reshape(r, 2 * WIDE) for q in range(CHUNKS)]


def pack_trunk_body(qkv_ref, proj_ref, fc1_ref, fc2_ref, lead_ref, gain_ref, bias_ref, qkv_b_ref, fc1_b_ref, *refs):
    one_ref, two_ref, flat_ref, tall_ref = refs
    r = qkv_ref.shape[0]
    flat_ref[...] = jnp.zeros_like(flat_ref)
    at = LEADS
    for ref in (gain_ref, bias_ref, qkv_b_ref):
        rows = ref.shape[0]
        flat_ref[at : at + rows, :r] = ref[...].astype(jnp.float32)
        at += rows
    tall_ref[...] = flat_ref[...].T
    tall_ref[:r, :LEADS] = lead_ref[...].astype(jnp.float32)
    flat_ref[...] = jnp.zeros_like(flat_ref)
    flat_ref[0:1, : 4 * r] = fc1_b_ref[...].astype(jnp.float32)
    n = 4 * D
    one_ref[:, : 3 * D] = qkv_ref[...]
    one_ref[:, 3 * D : n] = proj_ref[...]
    one_ref[:, n : n + LANES] = tall_ref[:r, :].astype(jnp.bfloat16)
    one_ref[:, n + LANES :] = flat_ref[:r, :].astype(jnp.bfloat16)
    two_ref[: 4 * r, :] = fc2_ref[...]
    for k in range(4):
        two_ref[(4 + k) * r : (5 + k) * r, :] = fc1_ref[:, k * D : (k + 1) * D]


def pack_trunk(qkv, proj, fc1, fc2, lead_w, gains, biases, qkv_b, fc1_b):
    r = qkv.shape[0]
    return pl.pallas_call(
        pack_trunk_body,
        out_shape=[
            jax.ShapeDtypeStruct((r, 4 * D + 2 * LANES), jnp.bfloat16),
            jax.ShapeDtypeStruct((8 * r, D), jnp.bfloat16),
        ],
        scratch_shapes=[pltpu.VMEM((LANES, LANES), jnp.float32)] * 2,
        compiler_params=pltpu.CompilerParams(vmem_limit_bytes=VMEM),
        cost_estimate=LIGHT,
        name="pack_trunk",
    )(qkv, proj, fc1, fc2, lead_w, gains.T, biases.T, qkv_b.T, fc1_b.reshape(1, 4 * r))


def pack_head_body(head_ref, out):
    r = head_ref.shape[0]
    for q in range(CHUNKS):
        for h in range(2):
            first = h * HALF + q * CHUNK
            real = min(CHUNK, TILE_SAMPLES - first)
            for e in range(MODEL_COUNT):
                begin, at = e * TILE_SAMPLES + first, ((2 * q + h) * MODEL_COUNT + e) * CHUNK
                part = head_ref[:, begin : begin + real]
                if real < CHUNK:
                    part = jnp.concatenate([part, jnp.zeros((r, CHUNK - real), part.dtype)], axis=1)
                out[:, at : at + CHUNK] = part


def pack_head(head):
    return pl.pallas_call(
        pack_head_body,
        out_shape=jax.ShapeDtypeStruct((head.shape[0], 2 * CHUNKS * WIDE), jnp.bfloat16),
        compiler_params=pltpu.CompilerParams(vmem_limit_bytes=VMEM),
        cost_estimate=LIGHT,
        name="pack_head",
    )(head)


def head_whole(low, high):
    r = low[0].shape[0]
    parts = [v.reshape(r, MODEL_COUNT, CHUNK) for v in (*low, *high)]
    return jnp.concatenate(parts, axis=2)[:, :, :TILE_SAMPLES].reshape(r, MODEL_COUNT * TILE_SAMPLES)


DIGITS = 16
BASE = 8.0


def digits_of(value):
    powers = jnp.asarray([BASE**k for k in range(DIGITS + 1)], jnp.float32)
    floors = jnp.floor(value * 32.0 * powers)
    return floors[1:] - BASE * floors[:-1]


def value_of(digits):
    powers = jnp.asarray([BASE ** -(k + 1) / 32.0 for k in range(DIGITS)], jnp.float32)
    return jnp.sum(digits * powers)


SCALE = HD ** (-0.5)
ROW_GAIN, ROW_BIAS, ROW_QKV, ROW_DIGIT = LEADS, LEADS + 2, LEADS + 6, LEADS + 8
SMALL_ROWS = 64
FIRST_WIDE = 4 * D + 2 * LANES


def slab(ref, first, n):
    shards, rows = ref.shape[:2]
    return ref[:, :, first : first + n].reshape(shards * rows, n)


def dot_last(left, right):
    return lax.dot_general(left, right, (((1,), (1,)), ((), ())), preferred_element_type=jnp.float32)


def normalised(values):
    centred = values - jnp.mean(values, axis=-1, keepdims=True)
    inverse = lax.rsqrt(jnp.mean(centred * centred, axis=-1, keepdims=True) + EPS)
    return centred * inverse, inverse


def norm_back(values, d_out, gain):
    unit, inverse = normalised(values)
    d_unit = d_out * gain
    mean_one = jnp.mean(d_unit, axis=-1, keepdims=True)
    mean_two = jnp.mean(d_unit * unit, axis=-1, keepdims=True)
    d_values = inverse * (d_unit - mean_one - unit * mean_two)
    return (
        d_values,
        jnp.sum(d_out * unit, axis=0, keepdims=True),
        jnp.sum(d_out, axis=0, keepdims=True),
    )


def head_masks():
    lane = lax.broadcasted_iota(jnp.int32, (1, 2 * HD), 1)
    low = lane < HD
    return low, [m.astype(jnp.float32).astype(jnp.bfloat16) for m in (low, lane >= HD)]


def softmax_of(scores):
    expd = jnp.exp(scores - jnp.max(scores, axis=-1, keepdims=True))
    return expd * (1.0 / jnp.sum(expd, axis=-1, keepdims=True))


def trunk_first_body(moves, table_ref, index_ref, frame_ref, *refs):
    ins, refs = refs[:-9], refs[-9:]
    middle_ref, normed_ref, joined_ref, attended_ref, normed_two_ref, par_ref, fc1_b_ref = refs[:7]
    held_ref, sems = refs[7:]
    run_moves(moves, table_ref, ins, [held_ref], sems)
    par_ref[...] = slab(held_ref, 4 * D, LANES).astype(jnp.float32).T
    shards = held_ref.shape[0]
    wide = FF // shards
    for d in range(shards):
        row = held_ref[d, 0:1, 4 * D + LANES : 4 * D + LANES + wide]
        fc1_b_ref[:, d * wide : (d + 1) * wide] = row.astype(jnp.float32)

    def row(i):
        return par_ref[i : i + 1, :]

    started = frame_ref[...].astype(jnp.float32) + par_ref[pl.ds(index_ref[0], 1), :]
    normed = (normalised(started)[0] * row(ROW_GAIN) + row(ROW_BIAS)).astype(jnp.bfloat16)
    normed_ref[...] = normed
    for i, shift in enumerate((row(ROW_QKV), None, row(ROW_QKV + 1))):
        part = jnp.dot(normed, slab(held_ref, i * D, D), preferred_element_type=jnp.float32)
        part = part if shift is None else part + shift
        joined_ref[:, i * D : (i + 1) * D] = part.astype(jnp.bfloat16)
    low, masks = head_masks()
    for p in range(HEADS // 2):
        at = p * 2 * HD
        q, k, v = (joined_ref[:, i * D + at : i * D + at + 2 * HD] for i in range(3))
        outs = []
        for mask in masks:
            probs = softmax_of(dot_last(q * mask, k) * SCALE).astype(jnp.bfloat16)
            outs.append(jnp.dot(probs, v, preferred_element_type=jnp.float32))
        attended_ref[:, at : at + 2 * HD] = jnp.where(low, *outs).astype(jnp.bfloat16)
    middle = (
        started
        + jnp.dot(attended_ref[...], slab(held_ref, 3 * D, D), preferred_element_type=jnp.float32)
        + row(ROW_BIAS + 1)
    )
    middle_ref[...] = middle
    normed_two = normalised(middle)[0] * row(ROW_GAIN + 1) + row(ROW_BIAS + 2)
    normed_two_ref[...] = normed_two.astype(jnp.bfloat16)


def trunk_call(body, scalars, ins, sources, outs, scratch, name):
    any_spec = pl.BlockSpec(memory_space=pl.ANY)

    def whole(shape):
        return pl.BlockSpec(shape, lambda i, *s: (0,) * len(shape))

    return pl.pallas_call(
        body,
        grid_spec=pltpu.PrefetchScalarGridSpec(
            num_scalar_prefetch=len(scalars),
            grid=(1,),
            in_specs=[whole(v.shape) for v in ins] + [any_spec] * len(sources),
            out_specs=[whole(s) for s, _ in outs],
            scratch_shapes=scratch,
        ),
        out_shape=[jax.ShapeDtypeStruct(*o) for o in outs],
        compiler_params=pltpu.CompilerParams(vmem_limit_bytes=VMEM),
        cost_estimate=LIGHT,
        name=name,
    )(*scalars, *ins, *sources)


def trunk_first(table, index, rows, moves, frame, *sources):
    flat, low, full = (TILE_COUNT, D), jnp.bfloat16, jnp.float32
    return trunk_call(
        functools.partial(trunk_first_body, moves),
        (table, index),
        (frame,),
        sources,
        [
            (flat, full),
            (flat, low),
            ((TILE_COUNT, 3 * D), low),
            (flat, low),
            (flat, low),
            ((LANES, D), full),
            ((1, FF), full),
        ],
        [
            pltpu.VMEM((32, rows, FIRST_WIDE), low),
            pltpu.SemaphoreType.DMA((len(moves),)),
        ],
        "trunk_first",
    )


def trunk_second_body(moves, table_ref, middle_ref, normed_two_ref, par_ref, fc1_b_ref, *refs):
    ins, refs = refs[:-5], refs[-5:]
    hidden_ref, slope_ref, final_ref, held_ref, sems = refs
    run_moves(moves, table_ref, ins, [held_ref], sems)
    total = middle_ref[...] + par_ref[ROW_BIAS + 3 : ROW_BIAS + 4, :]
    normed_two = normed_two_ref[...]
    for k in range(4):
        cols = slice(k * D, (k + 1) * D)
        pre = jnp.dot(normed_two, widening(held_ref, k), preferred_element_type=jnp.float32)
        pre = pre + fc1_b_ref[:, cols]
        share = 0.5 * (1.0 + lax.erf(pre * (0.5**0.5)))
        density = jnp.exp(-0.5 * pre * pre) * ((0.5 / 3.141592653589793) ** 0.5)
        slope_ref[:, cols] = share + pre * density
        hidden = (pre * share).astype(jnp.bfloat16)
        hidden_ref[:, cols] = hidden
        weight = narrowing(held_ref, k)
        total += jnp.dot(hidden, weight, preferred_element_type=jnp.float32)
    final_ref[...] = total.astype(jnp.bfloat16)


def second_scratch(rows):
    return [pltpu.VMEM((32, 8 * rows, D), jnp.bfloat16)]


def narrowing(held_ref, k):
    shards, rows = held_ref.shape[:2]
    return held_ref[k * shards // 4 : (k + 1) * shards // 4, : rows // 2, :].reshape(D, D)


def widening(held_ref, k):
    rows = held_ref.shape[1] // 8
    return held_ref[:, (4 + k) * rows : (5 + k) * rows, :].reshape(D, D)


def trunk_second(table, rows, moves, middle, normed_two, par, fc1_b, *sources):
    return trunk_call(
        functools.partial(trunk_second_body, moves),
        (table,),
        (middle, normed_two, par, fc1_b),
        sources,
        [
            ((TILE_COUNT, FF), jnp.bfloat16),
            ((TILE_COUNT, FF), jnp.float32),
            ((TILE_COUNT, D), jnp.bfloat16),
        ],
        second_scratch(rows) + [pltpu.SemaphoreType.DMA((len(moves),))],
        "trunk_second",
    )


def second_back_body(moves_two, moves_one, n_two, table_ref, slope_ref, middle_ref, par_ref, *refs):
    d_parts, refs = refs[: 2 * CHUNKS], refs[2 * CHUNKS :]
    ins, refs = refs[:-11], refs[-11:]
    branch_ref, pre_ref, middle_d_ref, attn_ref, attended_ref, rows_ref, fc1_b_ref = refs[:7]
    held_ref, proj_ref, sems_two, sems_one = refs[7:]
    run_moves(moves_one, table_ref, ins[n_two:], [proj_ref], sems_one)
    run_moves(moves_two, table_ref, ins[:n_two], [held_ref], sems_two)
    d_final = d_parts[0][...]
    for part in d_parts[1:]:
        d_final = d_final + part[...]
    d_branch = d_final.astype(jnp.bfloat16)
    branch_ref[...] = d_branch
    d_normed = None
    for k in range(4):
        cols = slice(k * D, (k + 1) * D)
        d_hidden = dot_last(d_branch, narrowing(held_ref, k))
        d_pre = (d_hidden * slope_ref[:, cols]).astype(jnp.bfloat16)
        pre_ref[:, cols] = d_pre
        fc1_b_ref[:, cols] = jnp.sum(d_pre.astype(jnp.float32), axis=0, keepdims=True)
        part = dot_last(d_pre, widening(held_ref, k))
        d_normed = part if d_normed is None else d_normed + part
    gain = par_ref[ROW_GAIN + 1 : ROW_GAIN + 2, :]
    d_part, d_gain, d_shift = norm_back(middle_ref[...], d_normed, gain)
    d_middle = d_final + d_part
    middle_d_ref[...] = d_middle
    d_attn = d_middle.astype(jnp.bfloat16)
    attn_ref[...] = d_attn
    attended_ref[...] = dot_last(d_attn, slab(proj_ref, 0, D)).astype(jnp.bfloat16)
    sums = [jnp.sum(v.astype(jnp.float32), axis=0, keepdims=True) for v in (d_attn, d_branch)]
    rows_ref[...] = jnp.zeros_like(rows_ref)
    for i, value in enumerate((d_gain, d_shift, *sums)):
        rows_ref[i : i + 1, :] = value


def second_back(table, rows, moves_two, moves_one, n_two, slope, middle, par, d_parts, *sources):
    flat, low, full = (TILE_COUNT, D), jnp.bfloat16, jnp.float32
    return trunk_call(
        functools.partial(second_back_body, moves_two, moves_one, n_two),
        (table,),
        (slope, middle, par, *d_parts),
        sources,
        [
            (flat, low),
            ((TILE_COUNT, FF), low),
            (flat, full),
            (flat, low),
            (flat, low),
            ((8, D), full),
            ((1, FF), full),
        ],
        second_scratch(rows)
        + [
            pltpu.VMEM((32, rows, D), low),
            pltpu.SemaphoreType.DMA((len(moves_two),)),
            pltpu.SemaphoreType.DMA((len(moves_one),)),
        ],
        "second_back",
    )


def first_back_body(moves, n_ent, table_ref, index_ref, weight_ref, frame_ref, joined_ref, par_ref, middle_d_ref, attended_ref, rows_ref, *refs):
    ents, refs = refs[:n_ent], refs[n_ent:]
    ins, refs = refs[:-5], refs[-5:]
    d_joined_ref, tokens_ref, small_ref, qkv_ref, sems = refs
    run_moves(moves, table_ref, ins, [qkv_ref], sems)
    small_ref[...] = jnp.zeros_like(small_ref)
    _, masks = head_masks()
    for p in range(HEADS // 2):
        at = p * 2 * HD
        q, k, v = (joined_ref[:, i * D + at : i * D + at + 2 * HD] for i in range(3))
        d_out = attended_ref[:, at : at + 2 * HD]
        totals = [None] * 3
        for mask in masks:
            q_one, k_one, d_one = q * mask, k * mask, d_out * mask
            probs = softmax_of(dot_last(q_one, k) * SCALE)
            d_probs = dot_last(d_one, v)
            inner = jnp.sum(probs * d_probs, axis=-1, keepdims=True)
            d_scores = (probs * (d_probs - inner)).astype(jnp.bfloat16)
            parts = (
                jnp.dot(d_scores, k_one, preferred_element_type=jnp.float32),
                dot_tokens(d_scores, q_one),
                dot_tokens(probs.astype(jnp.bfloat16), d_one),
            )
            totals = [a if b is None else a + b for a, b in zip(parts, totals)]
        for i, scale in enumerate((SCALE, SCALE, 1.0)):
            d_joined_ref[:, i * D + at : i * D + at + 2 * HD] = (totals[i] * scale).astype(
                jnp.bfloat16
            )
    d_normed = None
    for i in range(3):
        block = d_joined_ref[:, i * D : (i + 1) * D]
        if i != 1:
            at = ROW_QKV + i // 2
            total = jnp.sum(block.astype(jnp.float32), axis=0, keepdims=True)
            small_ref[at : at + 1, :] = total
        part = dot_last(block, slab(qkv_ref, i * D, D))
        d_normed = part if d_normed is None else d_normed + part
    started = frame_ref[...].astype(jnp.float32) + par_ref[pl.ds(index_ref[0], 1), :]
    gain = par_ref[ROW_GAIN : ROW_GAIN + 1, :]
    d_part, d_gain, d_shift = norm_back(started, d_normed, gain)
    d_started = middle_d_ref[...] + d_part
    tokens_ref[...] = d_started.astype(jnp.bfloat16)
    small_ref[pl.ds(index_ref[0], 1), :] = jnp.sum(d_started, axis=0, keepdims=True)
    small_ref[ROW_GAIN : ROW_GAIN + 1, :] = d_gain
    small_ref[ROW_BIAS : ROW_BIAS + 1, :] = d_shift
    small_ref[ROW_GAIN + 1 : ROW_GAIN + 2, :] = rows_ref[0:1, :]
    small_ref[ROW_BIAS + 2 : ROW_BIAS + 3, :] = rows_ref[1:2, :]
    small_ref[ROW_BIAS + 1 : ROW_BIAS + 2, :] = rows_ref[2:3, :]
    small_ref[ROW_BIAS + 3 : ROW_BIAS + 4, :] = rows_ref[3:4, :]
    entropy = ents[0][...]
    for ent in ents[1:]:
        entropy = entropy + ent[...]
    entropy = jnp.sum(jnp.sum(entropy, axis=0, keepdims=True), axis=1, keepdims=True)
    value = jnp.broadcast_to(entropy * weight_ref[0] * 32.0, (1, D))
    before = jnp.floor(value)
    for k in range(DIGITS):
        value = value * BASE
        floor = jnp.floor(value)
        small_ref[ROW_DIGIT + k : ROW_DIGIT + k + 1, :] = floor - BASE * before
        before = floor


def first_back(table, index, strength, rows, moves, frame, joined, par, d_middle, d_attended, d_rows, ents, *sources):
    return trunk_call(
        functools.partial(first_back_body, moves, len(ents)),
        (table, index, strength),
        (frame, joined, par, d_middle, d_attended, d_rows, *ents),
        sources,
        [
            ((TILE_COUNT, 3 * D), jnp.bfloat16),
            ((TILE_COUNT, D), jnp.bfloat16),
            ((SMALL_ROWS, D), jnp.float32),
        ],
        [
            pltpu.VMEM((32, rows, 3 * D), jnp.bfloat16),
            pltpu.SemaphoreType.DMA((len(moves),)),
        ],
        "first_back",
    )


def low_or_high(value, core, rows):
    return value[core * rows : (core + 1) * rows]


def fc2_rows(value, core, rows):
    return value[core * 4 * rows : (core + 1) * 4 * rows]


def fc1_rows(value, core, rows):
    begin = 8 * rows + core * rows
    return jnp.concatenate(
        [value[begin + 2 * k * rows : begin + (2 * k + 1) * rows] for k in range(4)], axis=1
    )


class Parameters:
    def __init__(self, small_all, rows):
        lead_w, gain_all, bias_all, qkv_b, fc1_b = split_small(small_all)
        self.lead = lead_w.astype(jnp.float32)
        self.gain = gain_all.astype(jnp.float32)
        self.bias = bias_all.astype(jnp.float32)
        qkv_b = qkv_b.astype(jnp.float32)
        self.offset = jnp.concatenate([qkv_b[:, 0], jnp.zeros_like(qkv_b[:, 0]), qkv_b[:, 1]])
        self.fc1 = (
            fc1_b.astype(jnp.float32).reshape(D // rows, rows, 4).transpose(0, 2, 1).reshape(FF)
        )


    def parts(self):
        return self.lead, self.gain, self.bias, self.offset, self.fc1


def attention_input(frame, lead_vector, gain, bias, offset, qkv_w):
    started = frame.astype(jnp.float32) + lead_vector[None, :]
    normed = layer_norm(started, gain, bias).astype(jnp.bfloat16)
    joined = (plain_dot(normed, qkv_w) + offset).astype(jnp.bfloat16)
    return started, normed, joined


def heads_of(joined):
    return [joined[:, i * D : (i + 1) * D].reshape(TILE_COUNT, HEADS, HD) for i in range(3)]


def attention(joined):
    queries, keys, values = heads_of(joined)
    scores = jnp.einsum("qhd,khd->hqk", queries, keys, preferred_element_type=jnp.float32) * SCALE
    row_top = jnp.max(scores, axis=-1, keepdims=True)
    expd = jnp.exp(scores - row_top)
    prob_full = expd / jnp.sum(expd, axis=-1, keepdims=True)
    probs_low = prob_full.astype(jnp.bfloat16)
    attended = jnp.einsum("hqk,khd->qhd", probs_low, values, preferred_element_type=jnp.float32)
    return prob_full, attended.astype(jnp.bfloat16).reshape(TILE_COUNT, D)


def mlp_input(started, attended, proj_w, proj_bias, gain, bias):
    middle = started + plain_dot(attended, proj_w) + proj_bias
    return middle, layer_norm(middle, gain, bias).astype(jnp.bfloat16)


def mlp(middle, normed_two, fc1_w, fc1_b, fc2_w, fc2_b):
    pre_act = plain_dot(normed_two, fc1_w) + fc1_b
    hidden = exact_gelu(pre_act).astype(jnp.bfloat16)
    final_sum = middle + plain_dot(hidden, fc2_w) + fc2_b
    return pre_act, hidden, final_sum.astype(jnp.bfloat16)


def mlp_back(d_parts, pre_act, fc2_w):
    d_final = sum(d_parts)
    d_branch = d_final.astype(jnp.bfloat16)
    d_hidden = times_transpose(d_branch, fc2_w)
    _, gelu_back = jax.vjp(exact_gelu, pre_act)
    return d_final, d_branch, gelu_back(d_hidden)[0].astype(jnp.bfloat16)


def mlp_input_back(d_final, d_pre, fc1_w, middle, gain, bias, proj_w):
    d_normed_two = times_transpose(d_pre, fc1_w)
    _, norm_back = jax.vjp(layer_norm, middle, gain, bias)
    d_part, d_gain, d_shift = norm_back(d_normed_two)
    d_middle = d_final + d_part
    d_attn = d_middle.astype(jnp.bfloat16)
    d_attended = times_transpose(d_attn, proj_w).astype(jnp.bfloat16)
    return d_middle, d_attn, d_attended, d_gain, d_shift


def attention_back(joined, prob_full, d_attended):
    queries, keys, values = heads_of(joined)
    d_attended = d_attended.reshape(TILE_COUNT, HEADS, HD)
    probs_low = prob_full.astype(jnp.bfloat16)
    d_values = jnp.einsum("hqk,qhd->khd", probs_low, d_attended, preferred_element_type=jnp.float32)
    d_prob = jnp.einsum("qhd,khd->hqk", d_attended, values, preferred_element_type=jnp.float32)
    d_score = (
        prob_full * (d_prob - jnp.sum(prob_full * d_prob, axis=-1, keepdims=True))
    ).astype(jnp.bfloat16)
    d_queries = (
        jnp.einsum("hqk,khd->qhd", d_score, keys, preferred_element_type=jnp.float32) * SCALE
    )
    d_keys = (
        jnp.einsum("hqk,qhd->khd", d_score, queries, preferred_element_type=jnp.float32) * SCALE
    )
    return jnp.concatenate(
        [v.reshape(TILE_COUNT, D) for v in (d_queries, d_keys, d_values)], axis=1
    ).astype(jnp.bfloat16)


def attention_input_back(d_middle, d_joined, qkv_w, started, gain, bias):
    d_normed = times_transpose(d_joined, qkv_w)
    _, norm_back = jax.vjp(layer_norm, started, gain, bias)
    d_part, d_gain, d_shift = norm_back(d_normed)
    return d_middle + d_part, d_gain, d_shift


def small_gradient(rows, horizon_indicator, contribution, d_started, d_joined, d_attn, d_branch, d_pre, gains, shifts):
    def column_sum(value):
        return jnp.sum(value.astype(jnp.float32), axis=0)

    joined_sums = column_sum(d_joined)
    columns = jnp.stack(
        [
            *gains,
            shifts[0],
            column_sum(d_attn),
            shifts[1],
            column_sum(d_branch),
            joined_sums[:D],
            joined_sums[2 * D :],
        ],
        axis=1,
    )
    hidden_columns = column_sum(d_pre).reshape(D // rows, 4, rows).transpose(0, 2, 1).reshape(D, 4)
    return jnp.concatenate(
        [
            jnp.sum(d_started, axis=0)[:, None] * horizon_indicator[None, :],
            columns,
            hidden_columns,
            jnp.broadcast_to(digits_of(contribution)[None, :], (D, DIGITS)),
            jnp.zeros((D, LANES - LEADS - 12 - DIGITS), jnp.float32),
        ],
        axis=1,
    ).astype(jnp.bfloat16)


def small_outputs(value, rows):
    return (
        value[:, :LEADS],
        value[:, LEADS : LEADS + 2],
        value[:, LEADS + 2 : LEADS + 6],
        value[:, LEADS + 6 : LEADS + 8],
        value[:, LEADS + 8 : LEADS + 12].T.reshape(4 * rows),
    )


def frame_scalars(horizon_indices, horizon_tallies):
    indicator = (horizon_indices[0] == lax.iota(jnp.int32, LEADS)).astype(jnp.float32)
    frame_count = jnp.sum(indicator * horizon_tallies.astype(jnp.float32))
    return indicator, 1.0 / (frame_count * (LEADS * TILE_COUNT * TILE_SAMPLES))


def plain_step(
    tile_embeddings,
    horizon_indices,
    horizon_tallies,
    member_guesses,
    adjoint_of_mixture,
    triple_projection_matrix,
    attention_outward_matrix,
    widening_matrix,
    narrowing_matrix,
    gating_matrix,
    *small_parts,
):
    rows = triple_projection_matrix.shape[0]
    whole = functools.partial(lax.all_gather, axis_name=AXES, axis=0, tiled=True)

    def summed(value):
        return lax.psum_scatter(
            value.astype(jnp.bfloat16), AXES, scatter_dimension=0, tiled=True
        ).astype(jnp.float32)

    qkv_w, proj_w = whole(triple_projection_matrix), whole(attention_outward_matrix)
    fc1_w, fc2_w = whole(widening_matrix), whole(narrowing_matrix)
    par = Parameters(whole(pack_small(*small_parts, rows)), rows)
    indicator, strength = frame_scalars(horizon_indices, horizon_tallies)
    guesses = jnp.transpose(member_guesses[0], (1, 0, 2))
    lead_vector = jnp.sum(par.lead * indicator[None, :], axis=1)
    started, normed, joined = attention_input(
        tile_embeddings[0], lead_vector, par.gain[:, 0], par.bias[:, 0], par.offset, qkv_w
    )
    prob_full, attended = attention(joined)
    middle, normed_two = mlp_input(
        started, attended, proj_w, par.bias[:, 1], par.gain[:, 1], par.bias[:, 2]
    )
    pre_act, hidden, final_low = mlp(middle, normed_two, fc1_w, par.fc1, fc2_w, par.bias[:, 3])
    table = jnp.asarray([0, 1], jnp.int32)
    held_shape = (1, D, WIDE)
    combined, head_grads, d_parts, entropies = None, [], [], []
    head_w = whole(jnp.concatenate(head_chunks(gating_matrix), axis=1))
    for q in range(CHUNKS):
        halves = []
        for own in (False, True):
            combined, d_logits, d_part, entropy = head_pass(
                q,
                own,
                strength.reshape(1),
                table,
                final_low,
                [head_w],
                [(0, (0, 0), held_shape[1:], 0, 0, (0, 0))],
                held_shape,
                guesses,
                adjoint_of_mixture[0],
                combined,
            )
            flat = d_logits.transpose(1, 0, 2).reshape(TILE_COUNT, WIDE)
            halves.append(summed(transpose_times(final_low, flat)))
            d_parts.append(d_part)
            entropies.append(entropy)
        head_grads.append(halves)
    contribution = jnp.sum(sum(entropies)) * strength
    d_final, d_branch, d_pre = mlp_back(d_parts, pre_act, fc2_w)
    d_middle, d_attn, d_attended, gain_two, shift_two = mlp_input_back(
        d_final, d_pre, fc1_w, middle, par.gain[:, 1], par.bias[:, 2], proj_w
    )
    d_joined = attention_back(joined, prob_full, d_attended)
    d_started, gain_one, shift_one = attention_input_back(
        d_middle, d_joined, qkv_w, started, par.gain[:, 0], par.bias[:, 0]
    )
    small_grad = small_gradient(
        rows,
        indicator,
        contribution,
        d_started,
        d_joined,
        d_attn,
        d_branch,
        d_pre,
        (gain_one, gain_two),
        (shift_one, shift_two),
    )
    return (
        combined[None],
        lax.psum(contribution, AXES),
        d_started.astype(jnp.bfloat16)[None],
        summed(transpose_times(normed, d_joined)),
        summed(transpose_times(attended, d_attn)),
        summed(transpose_times(normed_two, d_pre)),
        summed(transpose_times(hidden, d_branch)),
        head_whole(*zip(*head_grads)),
        *small_outputs(summed(small_grad), rows),
    )


def paired_step(
    tile_embeddings,
    horizon_indices,
    horizon_tallies,
    member_guesses,
    adjoint_of_mixture,
    triple_projection_matrix,
    attention_outward_matrix,
    widening_matrix,
    narrowing_matrix,
    gating_matrix,
    *small_parts,
):
    rows = triple_projection_matrix.shape[0]
    core = lax.axis_index("fsdp") % 2
    table = places(True)
    marks = jnp.concatenate([core.reshape(1), places(False)[::2] // 2])
    head_marks = jnp.concatenate([core.reshape(1), table[::2] // 2])
    head_table = jnp.concatenate([table, core.reshape(1)])
    seq = Sequence(horizon_tallies)
    indicator, strength = frame_scalars(horizon_indices, horizon_tallies)

    first_own, second_own = seq.run(
        pack_trunk,
        triple_projection_matrix,
        attention_outward_matrix,
        widening_matrix,
        narrowing_matrix,
        *small_parts,
    )
    one, two = RoundFirst(seq, first_own, 1), RoundFirst(seq, second_own, -1)
    one.start()
    two.start()
    head_own = seq.run(pack_head, gating_matrix)
    over = across(head_own)
    one.arrive()
    one.start()
    two.arrive()
    two.start()
    one.arrive()
    one.start()
    two.arrive()
    two.start()
    over = seq.tie(over)
    one.arrive()
    one.last()
    two.arrive()
    two.last()
    one.arrive_last()
    one.batch()
    two.arrive_last()
    head_first = seq.run(lambda a, b: jnp.concatenate([a, b], axis=0), head_own, over)
    three = AcrossFirst(seq, head_first)
    three.start()
    guesses = seq.run(
        lambda v: lax.optimization_barrier(jnp.transpose(v[0], (1, 0, 2))), member_guesses
    )
    two.batch()
    three.arrive()
    three.start()
    one.arrive_over()
    one.arrive_batches()
    whole_one = [((0, rows), (0, FIRST_WIDE), 0, 0, 0)]
    whole_two = [((0, 8 * rows), (0, D), 0, 0, 0)]
    index = horizon_indices
    sources_one, moves = plan_moves(one.collect(), whole_one)
    middle, normed, joined, attended, normed_two, par, fc1_b = seq.run(
        functools.partial(trunk_first, table, index, rows, moves), tile_embeddings[0], *sources_one
    )
    three.settle()
    three.arrive()
    three.start()
    adjoint = seq.run(lambda v: lax.optimization_barrier(v[0]), adjoint_of_mixture)
    two.arrive_batches()
    three.settle()
    three.arrive()
    three.last()
    two.arrive_over()
    two.arrive_batches()
    sources_two, moves_two = plan_moves(two.collect(), whole_two)
    hidden, slope, final_low = seq.run(
        functools.partial(trunk_second, table, rows, moves_two),
        middle,
        normed_two,
        par,
        fc1_b,
        *sources_two,
    )
    three.settle()
    three.arrive_last()
    final_other = sibling(final_low)
    normed_other, attended_other = sibling(normed), sibling(attended)
    normed_two_other, hidden_other = sibling(normed_two), sibling(hidden)

    held_shape = (32, rows, WIDE)
    head_fields = [((0, rows), (0, WIDE), 0, 0, 0)]
    state = dict(combined=None, d_parts=[], entropies=[])

    def head(q, own, around):
        sources, moves = plan_moves(around.collect(), head_fields)
        before = () if state["combined"] is None else (state["combined"],)

        def function(final_low, before, *sources):
            return head_pass(
                q,
                own,
                strength.reshape(1),
                head_table,
                final_low,
                list(sources),
                moves,
                held_shape,
                guesses,
                adjoint,
                before[0] if before else None,
            )

        state["combined"], d_logits, d_part, entropy = seq.run(
            function, final_low, before, *sources
        )
        state["d_parts"].append(d_part)
        state["entropies"].append(entropy)
        return d_logits

    make_grad = functools.partial(head_grad, head_marks)
    send = sibling(head(0, False, three))
    own = head(0, True, three)
    sum_one = SumRoundFirst(seq, *seq.run(make_grad, final_low, final_other, own, send))
    normed_other, attended_other, normed_two_other, hidden_other = seq.tie(
        normed_other, attended_other, normed_two_other, hidden_other
    )
    moves_proj = plan_moves(one.collect(), [((0, rows), (3 * D, 4 * D), 0, 0, 0)])[1]
    moves_qkv = plan_moves(one.collect(), [((0, rows), (0, 3 * D), 0, 0, 0)])[1]
    d_branch, d_pre, d_middle, d_attn, d_attended, d_rows, d_fc1_b = seq.run(
        functools.partial(second_back, table, rows, moves_two, moves_proj, len(sources_two)),
        slope,
        middle,
        par,
        state["d_parts"],
        *sources_two,
        *sources_one,
    )
    d_attn_other, d_fc1_b_other = sibling(d_attn), sibling(d_fc1_b)
    d_branch_other, d_pre_other = sibling(d_branch), sibling(d_pre)
    sum_one.arrive()
    sum_one.step(3)
    d_branch_other, d_pre_other, d_attn_other, d_fc1_b_other = seq.tie(
        d_branch_other, d_pre_other, d_attn_other, d_fc1_b_other
    )
    parts = seq.run(
        lambda *ins: ring_grad(
            second_grad_body,
            marks,
            ins,
            (16 * rows, D // 2),
            [(16, 8 * rows, D // 2), (16, 2 * rows, FF // 2)],
            "second_grad",
        ),
        *(hidden, hidden_other, d_branch, d_branch_other),
        *(normed_two, normed_two_other, d_pre, d_pre_other),
    )
    sum_three = SumAcrossFirst(seq, parts, 1)
    sum_three.go_across(0)
    d_joined, tokens, small_grad = seq.run(
        functools.partial(first_back, table, index, strength.reshape(1), rows, moves_qkv),
        tile_embeddings[0],
        joined,
        par,
        d_middle,
        d_attended,
        d_rows,
        state["entropies"],
        *sources_one,
    )
    d_joined_other, small_other = sibling(d_joined), sibling(small_grad)
    sum_one.arrive()
    sum_one.step(2)
    blocks = seq.run(
        lambda *ins: round_grad(
            first_grad_body,
            head_marks,
            ins,
            (2 * rows, 2 * D + 2 * LANES),
            [(16, 2 * rows, 3 * D // 2), (16, 2 * rows, D // 2), (16, 2 * rows, LANES)]
            + [(LANES, D), (32, LANES), (2 * rows, LANES)],
            "first_grad",
        ),
        *(normed, normed_other, d_joined, d_joined_other),
        *(attended, attended_other, d_attn, d_attn_other),
        *(small_grad, small_other, d_fc1_b, d_fc1_b_other),
    )
    sum_four = SumRoundFirst(seq, *blocks)
    sum_three.arrive_across(0)
    sum_three.step(4)
    sum_three.go_across(1)
    sum_one.arrive()
    sum_one.step(1)
    sum_four.arrive()
    sum_four.step(3)
    sum_three.arrive()
    sum_three.step(3)
    combined_result = seq.run(flip, state["combined"]).T[None]
    grad_tokens = tokens[None]
    sum_one.arrive()
    sum_one.go_across()
    sum_four.arrive()
    sum_four.step(2)
    sum_three.arrive()
    sum_three.arrive_across(1)
    sum_three.step(2)
    sum_four.arrive()
    sum_four.step(1)
    sum_three.arrive()
    sum_three.step(1)
    first = core == 0

    def finish(total, rows_of):
        low, high = rows_of(total, 0, rows), rows_of(total, 1, rows)
        own, other = jnp.where(first, low, high), jnp.where(first, high, low)
        met = sibling(other.astype(jnp.bfloat16)).astype(jnp.float32)
        return jnp.where(first, own, met), jnp.where(first, met, own)

    low, high = finish(sum_one.finish(), low_or_high)
    sum_four.arrive()
    sum_four.go_across()
    sum_three.arrive()
    total = sum_three.finish()
    out_fc2 = jnp.concatenate(finish(total, fc2_rows), axis=1)
    out_fc1 = jnp.concatenate(finish(total, fc1_rows), axis=1)
    out_head = head_whole([low], [high])
    total = sum_four.finish()
    out_small = jnp.where(first, total[:rows, 2 * D :], total[rows:, 2 * D :])
    low, high = finish(total[:, : 2 * D], low_or_high)
    n = 3 * D // 2
    out_fc1_b = out_small[0, LANES : LANES + 4 * rows]
    cost = value_of(out_small[0, ROW_DIGIT : ROW_DIGIT + DIGITS])
    cost = jnp.where(seq.token[0] < 0, 0.0, cost)
    return (
        combined_result,
        cost,
        grad_tokens,
        jnp.concatenate([low[:, :n], high[:, :n]], axis=1),
        jnp.concatenate([low[:, n:], high[:, n:]], axis=1),
        out_fc1,
        out_fc2,
        out_head,
        out_small[:, :LEADS],
        out_small[:, ROW_GAIN:ROW_BIAS],
        out_small[:, ROW_BIAS:ROW_QKV],
        out_small[:, ROW_QKV:ROW_DIGIT],
        out_fc1_b,
    )


def solution(mesh):
    split = P(AXES)
    paired = mesh.shape["dp"] == 2 and mesh.shape["fsdp"] == 16
    return jax.shard_map(
        paired_step if paired else plain_step,
        mesh=mesh,
        in_specs=(split, split, P()) + (split,) * 12,
        out_specs=(split, P()) + (split,) * 11,
        check_vma=False,
    )
```

```python
import functools

import jax
import jax.numpy as jnp
from jax import lax
from jax.experimental import pallas as pl
from jax.experimental.pallas import tpu as pltpu
from jax.sharding import PartitionSpec as P

D = 768
HEADS = 12
HD = 64
FF = 3072
MODEL_COUNT = 3
TILE_SAMPLES = 4416
LEADS = 40
TILE_COUNT = 256
EPS = 1e-06
LANES = 128
HALF = 2304
PADDED = 2 * HALF
VMEM = 56 * 1024 * 1024

AXES = ("dp", "fsdp")
RING = [(z, 0) for z in range(4)] + [(z, 1) for z in (3, 2, 1, 0)]


def ring_pairs(step):
    pairs = []
    for spot, (z, x) in enumerate(RING):
        to_z, to_x = RING[(spot + step) % 8]
        for core in range(2):
            pairs.append((z * 4 + x * 2 + core, to_z * 4 + to_x * 2 + core))
    return pairs


def forth(value):
    return lax.ppermute(value, "fsdp", ring_pairs(1))


def back(value):
    return lax.ppermute(value, "fsdp", ring_pairs(-1))


def across(value):
    return lax.ppermute(value, "dp", [(0, 1), (1, 0)])


def exchange_rows(value):
    return lax.all_to_all(value, "dp", 0, 0)


def sibling(value):
    return lax.ppermute(value, "fsdp", [(i, i ^ 1) for i in range(16)])


def places(relative):
    y = lax.axis_index("dp") if relative else 0
    f = lax.axis_index("fsdp")
    z, x, core = f // 4, (f // 2) % 2, f % 2
    spot = jnp.where(x == 0, z, 7 - z)
    i = lax.iota(jnp.int32, 32)
    seat = (spot + (i // 2) % 8) % 8
    pair = jnp.where(seat < 4, seat * 2, (7 - seat) * 2 + 1)
    return ((y + i // 16) % 2) * 16 + pair * 2 + (core + i) % 2


def slot(other_row, distance, other_core):
    return other_row * 16 + (distance % 8) * 2 + other_core


def plan_moves(found, fields):
    sources, moves = [], []
    for source, rows, where in found:
        at = [i for i, s in enumerate(sources) if s is source]
        if not at:
            at = [len(sources)]
            sources.append(source)
        for (f0, f1), (g0, g1), out, out_row, out_col in fields:
            moves.append(
                (at[0], (rows[0] + f0, g0), (f1 - f0, g1 - g0), where, out, (out_row, out_col))
            )
    return sources, moves


def place(sources, moves, shapes, table, shards):
    def body(table_ref, *refs):
        ins, outs = refs[: len(sources)], refs[len(sources) : len(sources) + len(shapes)]
        held, sems, out_sems = refs[len(sources) + len(shapes) : -2], refs[-2], refs[-1]
        run_moves(moves, table_ref, ins, held, sems)
        copies = [
            pltpu.make_async_copy(held[i], outs[i], out_sems.at[i]) for i in range(len(shapes))
        ]
        for copy in copies:
            copy.start()
        for copy in copies:
            copy.wait()

    whole = [(shards,) + s for s in shapes]
    return pl.pallas_call(
        body,
        grid_spec=pltpu.PrefetchScalarGridSpec(
            num_scalar_prefetch=1,
            grid=(1,),
            in_specs=[pl.BlockSpec(memory_space=pl.ANY)] * len(sources),
            out_specs=[pl.BlockSpec(memory_space=pl.ANY)] * len(shapes),
            scratch_shapes=[pltpu.VMEM(s, jnp.bfloat16) for s in whole]
            + [
                pltpu.SemaphoreType.DMA((len(moves),)),
                pltpu.SemaphoreType.DMA((len(shapes),)),
            ],
        ),
        out_shape=[jax.ShapeDtypeStruct(s, jnp.bfloat16) for s in whole],
        compiler_params=pltpu.CompilerParams(vmem_limit_bytes=VMEM),
        name="place",
    )(table, *sources)


def run_moves(moves, table_ref, ins, outs, sems, begin=0):
    copies = []
    for i, (at, (sr, sc), (nr, nc), where, out, (dr, dc)) in enumerate(moves):
        copy = pltpu.make_async_copy(
            ins[at].at[pl.ds(sr, nr), pl.ds(begin + sc, nc)],
            outs[out].at[table_ref[where], pl.ds(dr, nr), pl.ds(dc, nc)],
            sems.at[i],
        )
        copy.start()
        copies.append(copy)
    for copy in copies:
        copy.wait()


def add_low(*values):
    total = values[0].astype(jnp.float32)
    for value in values[1:]:
        total = total + value.astype(jnp.float32)
    return total.astype(jnp.bfloat16)


class Sequence:
    def __init__(self, token):
        self.token = token

    def tie(self, *values):
        out = lax.optimization_barrier((self.token,) + values)
        self.token = out[0]
        return out[1] if len(values) == 1 else out[1:]

    def run(self, function, *values):
        values = lax.optimization_barrier((self.token,) + values)
        self.token = values[0]
        return self.tie(function(*values[1:]))


class Around:
    def __init__(self, seq, first):
        self.seq, self.rights, self.lefts = seq, [first], [first]

    def start(self, right=True, left=True):
        if right:
            self.rights.append(forth(self.rights[-1]))
        if left:
            self.lefts.append(back(self.lefts[-1]))

    def arrive(self, right=True, left=True):
        ends = ([self.rights] if right else []) + ([self.lefts] if left else [])
        met = self.seq.tie(*[end[-1] for end in ends])
        for end, value in zip(ends, met if len(ends) > 1 else (met,)):
            end[-1] = value


class RoundFirst(Around):
    def __init__(self, seq, first, longer):
        super().__init__(seq, first)
        self.longer, self.found = longer, []

    def last(self):
        ends = self.rights if self.longer > 0 else self.lefts
        ends.append(forth(ends[-1]) if self.longer > 0 else back(ends[-1]))

    def arrive_last(self):
        self.arrive(self.longer > 0, self.longer < 0)

    def batch(self):
        rights, lefts = self.rights, self.lefts
        r = rights[0].shape[0]
        end = rights[4] if self.longer > 0 else lefts[4]
        parts = (rights[0], rights[1], lefts[1], rights[2], lefts[2], rights[3], lefts[3], end)
        distances = (0, -1, 1, -2, 2, -3, 3, 4)
        joint = self.seq.run(lambda *v: jnp.concatenate(v, axis=0), *parts)
        self.over = across(joint), r, distances
        self.found.append((joint, r, 0, 0, distances))
        self.found.append((sibling(joint), r, 0, 1, distances))

    def arrive_over(self):
        over, r, distances = self.over
        over = self.seq.tie(over)
        self.found.append((over, r, 1, 0, distances))
        self.found.append((sibling(over), r, 1, 1, distances))

    def arrive_batches(self):
        met = self.seq.tie(*[v[0] for v in self.found])
        self.found = [(m,) + v[1:] for m, v in zip(met, self.found)]

    def collect(self):
        return [
            (source, (i * r, (i + 1) * r), slot(other_row, k, other_core))
            for source, r, other_row, other_core, distances in self.found
            for i, k in enumerate(distances)
        ]


class AcrossFirst(Around):
    def __init__(self, seq, first):
        super().__init__(seq, first)
        self.found, self.settled = [], set()
        self.note(first, [(0, 0), (1, 0)])

    def note(self, joint, spots):
        self.found.append((joint, 0, spots))
        self.found.append((sibling(joint), 1, spots))

    def settle(self):
        late = [i for i, item in enumerate(self.found) if item[1] and i not in self.settled]
        met = self.seq.tie(*[self.found[i][0] for i in late])
        for i, value in zip(late, met if len(late) > 1 else (met,)):
            self.found[i] = (value,) + self.found[i][1:]
        self.settled.update(late)

    def arrive(self):
        super().arrive()
        k = len(self.rights) - 1
        self.note(self.rights[k], [(0, -k), (1, -k)])
        self.note(self.lefts[k], [(0, k), (1, k)])

    def last(self):
        r = self.rights[0].shape[0] // 2
        right, left = self.seq.run(lambda a, b: (a[:r], b[r:]), self.rights[3], self.lefts[3])
        self.far = [forth(right), back(left)]

    def arrive_last(self):
        self.far = list(self.seq.tie(*self.far))
        for row, array in enumerate(self.far):
            self.note(array, [(row, 4)])

    def collect(self):
        r = self.rights[0].shape[0] // 2
        return [
            (source, (i * r, (i + 1) * r), slot(row, k, other_core))
            for source, other_core, spots in self.found
            for i, (row, k) in enumerate(spots)
        ]


ORDER_FIRST = (4, 3, -3)
ORDER_LAST = (2, -2, 1, -1, 0)


class SumAcrossFirst:
    def __init__(self, seq, parts, longer):
        self.seq, self.longer, self.ready = seq, longer, {}
        self.parts = parts
        self.met = [None, None]
        self.right = self.left = None

    def go_across(self, part):
        self.met[part] = exchange_rows(self.parts[part])

    def arrive_across(self, part):
        met = self.seq.tie(self.met[part])
        for i, k in enumerate((ORDER_FIRST, ORDER_LAST)[part]):
            self.ready[k] = (met, i)

    def arrive(self):
        if self.right is None:
            self.left = self.seq.tie(self.left)
        elif self.left is None:
            self.right = self.seq.tie(self.right)
        else:
            self.right, self.left = self.seq.tie(self.right, self.left)

    def step(self, k):
        if k == 4:
            value = self.seq.run(lambda v: add_low(v[0, 0], v[1, 0]), self.ready[4][0])
            if self.longer > 0:
                self.right = forth(value)
            else:
                self.left = back(value)
            return
        (met, i), (_, j) = self.ready[k], self.ready[-k]

        def add(met, right, left):
            return add_low(met[0, i], met[1, i], *right), add_low(met[0, j], met[1, j], *left)

        right = () if self.right is None else (self.right,)
        left = () if self.left is None else (self.left,)
        go_right, go_left = self.seq.run(add, met, right, left)
        self.right, self.left = forth(go_right), back(go_left)

    def finish(self):
        met, i = self.ready[0]

        def add(met, right, left):
            return sum(v.astype(jnp.float32) for v in (met[0, i], met[1, i], right, left))

        return self.seq.run(add, met, self.right, self.left)


class SumRoundFirst:
    def __init__(self, seq, blocks, far_right, far_left):
        self.seq, self.blocks = seq, blocks
        self.right, self.left = forth(far_right), back(far_left)

    def arrive(self):
        self.right, self.left = self.seq.tie(self.right, self.left)

    def step(self, k):
        def add_part(one, two, right, left):
            r = right.shape[0]
            return (
                jnp.concatenate([add_low(one[:r], right), one[r:]], axis=0),
                jnp.concatenate([two[:r], add_low(two[r:], left)], axis=0),
            )

        if k == 3:
            values = self.blocks[k], self.blocks[-k], self.right, self.left
            go_right, go_left = self.seq.run(add_part, *values)
            self.right, self.left = forth(go_right), back(go_left)
        else:
            self.right = forth(self.seq.run(add_low, self.blocks[k], self.right))
            self.left = back(self.seq.run(add_low, self.blocks[-k], self.left))

    def add(self, k):
        self.right = self.seq.run(add_low, self.blocks[k], self.right)
        self.left = self.seq.run(add_low, self.blocks[-k], self.left)

    def send(self):
        self.arrive()
        self.right, self.left = forth(self.right), back(self.left)

    def go_across(self):
        def add(block, right, left):
            r = block.shape[0] // 2
            near = sum(v[:r].astype(jnp.float32) for v in (block, right, left))
            return near, add_low(block[r:], right[r:], left[r:])

        self.near, sent = self.seq.run(add, self.blocks[0], self.right, self.left)
        self.met = across(sent)

    def finish(self):
        return self.seq.run(lambda a, b: a + b.astype(jnp.float32), self.near, self.met)


def layer_norm(values, norm_gain, norm_shift):
    row_mean = jnp.mean(values, axis=-1, keepdims=True)
    centred = values - row_mean
    row_var = jnp.mean(centred * centred, axis=-1, keepdims=True)
    return centred * lax.rsqrt(row_var + EPS) * norm_gain + norm_shift


def exact_gelu(values):
    return jax.nn.gelu(values, approximate=False)


def plain_dot(left, right):
    return jnp.dot(left, right, preferred_element_type=jnp.float32)


def times_transpose(left, right):
    return lax.dot_general(
        left, right, (((1,), (1,)), ((), ())), preferred_element_type=jnp.float32
    )


def transpose_times(left, right):
    return lax.dot_general(
        left, right, (((0,), (0,)), ((), ())), preferred_element_type=jnp.float32
    )


CHUNKS = 1
CHUNK = HALF // CHUNKS
LIGHT = pl.CostEstimate(flops=0, transcendentals=0, bytes_accessed=0)
HEAD_TILE = 768
HALF_STEPS = CHUNK // HEAD_TILE
ROWS = 16
COLS = 384


def half_of(own, table_ref):
    core = table_ref[table_ref.shape[0] - 1]
    return core if own else 1 - core


def pixel_block(q, own, j, table_ref):
    return half_of(own, table_ref) * (CHUNKS * HALF_STEPS) + q * HALF_STEPS + j


def head_body(q, own, moves, weight_ref, table_ref, x_ref, guess_ref, adj_ref, *refs):
    ins, refs = refs[:-7], refs[-7:]
    comb_ref, dl_ref, df_ref, ent_ref, logit_ref, held_ref, sems = refs
    j = pl.program_id(0)
    strength = weight_ref[0]
    half = half_of(own, table_ref)
    first_pixel = half * HALF + q * CHUNK + j * HEAD_TILE

    @pl.when(j == 0)
    def _():
        df_ref[...] = jnp.zeros_like(df_ref)
        ent_ref[...] = jnp.zeros_like(ent_ref)
        begin = pl.multiple_of((2 * q + half) * WIDE, LANES)
        run_moves(moves, table_ref, ins, [held_ref], sems, begin)

    x = x_ref[...]

    def weight(e):
        begin = pl.multiple_of(e * CHUNK + j * HEAD_TILE, LANES)
        return held_ref[:, :, pl.ds(begin, HEAD_TILE)].reshape(D, HEAD_TILE)

    for e in range(MODEL_COUNT):
        logit_ref[e] = jnp.dot(x, weight(e), preferred_element_type=jnp.float32)

    for part in range(HEAD_TILE // COLS):
        cols = pl.ds(part * COLS, COLS)
        pixel = first_pixel + part * COLS + lax.broadcasted_iota(jnp.int32, (ROWS, COLS), 1)
        real = pixel < TILE_SAMPLES

        def chunk(i, total):
            rows = pl.ds(pl.multiple_of(i * ROWS, ROWS), ROWS)
            l0, l1, l2 = (logit_ref[e, rows, cols] for e in range(3))
            top = jnp.maximum(jnp.maximum(l0, l1), l2)
            l0, l1, l2 = l0 - top, l1 - top, l2 - top
            e0, e1, e2 = jnp.exp(l0), jnp.exp(l1), jnp.exp(l2)
            norm = e0 + e1 + e2
            inverse = 1.0 / norm
            log_norm = jnp.log(norm)
            b0, b1, b2 = e0 * inverse, e1 * inverse, e2 * inverse
            l0, l1, l2 = l0 - log_norm, l1 - log_norm, l2 - log_norm
            minus_h = b0 * l0 + b1 * l1 + b2 * l2
            g0, g1, g2 = (guess_ref[e, rows, cols].astype(jnp.float32) for e in range(3))
            mixed = b0 * g0 + b1 * g1 + b2 * g2
            comb_ref[rows, cols] = mixed.astype(jnp.bfloat16)
            adj = adj_ref[rows, cols].astype(jnp.float32)
            for e, (b, l, g) in enumerate(((b0, l0, g0), (b1, l1, g1), (b2, l2, g2))):
                d = b * (adj * (g - mixed) - strength * (l - minus_h))
                dl_ref[e, rows, cols] = jnp.where(real, d, 0.0).astype(jnp.bfloat16)
            return total - jnp.where(real, minus_h, 0.0)

        total = lax.fori_loop(
            0,
            TILE_COUNT // ROWS,
            chunk,
            jnp.zeros((ROWS, COLS), jnp.float32),
            unroll=True,
        )
        gathered = total[:, :LANES]
        for k in range(1, COLS // LANES):
            gathered = gathered + total[:, k * LANES : (k + 1) * LANES]
        ent_ref[...] += gathered[:8] + gathered[8:]

    part = None
    for e in range(MODEL_COUNT):
        piece = lax.dot_general(
            dl_ref[e], weight(e), (((1,), (1,)), ((), ())), preferred_element_type=jnp.float32
        )
        part = piece if part is None else part + piece
    df_ref[...] += part


def head_pass(q, own, strength, table, final_low, sources, moves, held_shape, guesses, adjoint, before):
    tile = HEAD_TILE
    extra = [] if before is None else [before]

    def body(*refs):
        refs = refs[:5] + refs[5 + len(extra) :]
        head_body(q, own, moves, *refs)

    d_spec = (MODEL_COUNT, TILE_COUNT, tile)
    return pl.pallas_call(
        body,
        grid_spec=pltpu.PrefetchScalarGridSpec(
            num_scalar_prefetch=2,
            grid=(HALF_STEPS,),
            in_specs=[
                pl.BlockSpec((TILE_COUNT, D), lambda j, s, t: (0, 0)),
                pl.BlockSpec(d_spec, lambda j, s, t: (0, 0, pixel_block(q, own, j, t))),
                pl.BlockSpec((TILE_COUNT, tile), lambda j, s, t: (0, pixel_block(q, own, j, t))),
            ]
            + [pl.BlockSpec(memory_space=pl.ANY)] * (len(extra) + len(sources)),
            out_specs=[
                pl.BlockSpec((TILE_COUNT, tile), lambda j, s, t: (0, pixel_block(q, own, j, t))),
                pl.BlockSpec(d_spec, lambda j, s, t: (0, 0, j)),
                pl.BlockSpec((TILE_COUNT, D), lambda j, s, t: (0, 0)),
                pl.BlockSpec((8, LANES), lambda j, s, t: (0, 0)),
            ],
            scratch_shapes=[
                pltpu.VMEM(d_spec, jnp.float32),
                pltpu.VMEM(held_shape, jnp.bfloat16),
                pltpu.SemaphoreType.DMA((len(moves),)),
            ],
        ),
        out_shape=[
            jax.ShapeDtypeStruct((TILE_COUNT, TILE_SAMPLES), jnp.bfloat16),
            jax.ShapeDtypeStruct((MODEL_COUNT, TILE_COUNT, CHUNK), jnp.bfloat16),
            jax.ShapeDtypeStruct((TILE_COUNT, D), jnp.float32),
            jax.ShapeDtypeStruct((8, LANES), jnp.float32),
        ],
        input_output_aliases={5: 0} if extra else {},
        compiler_params=pltpu.CompilerParams(
            dimension_semantics=("arbitrary",), vmem_limit_bytes=VMEM
        ),
        cost_estimate=LIGHT,
        name="head_pass",
    )(strength, table, final_low, guesses, adjoint, *extra, *sources)


def flip_body(in_ref, out_ref):
    out_ref[...] = in_ref[...].T


def flip(value):
    tile = HEAD_TILE
    rows, n = value.shape
    return pl.pallas_call(
        flip_body,
        grid=(pl.cdiv(n, tile),),
        in_specs=[pl.BlockSpec((rows, tile), lambda j: (0, j))],
        out_specs=pl.BlockSpec((tile, rows), lambda j: (j, 0)),
        out_shape=jax.ShapeDtypeStruct((n, rows), value.dtype),
        compiler_params=pltpu.CompilerParams(vmem_limit_bytes=VMEM),
        cost_estimate=LIGHT,
        name="flip",
    )(value)


def dot_tokens(left, right):
    return lax.dot_general(left, right, (((0,), (0,)), ((), ())), preferred_element_type=jnp.float32)


def chip_at(marks_ref, row, distance):
    return marks_ref[1 + row * 8 + distance % 8]


HEAD_ORDER = (0, 1, -1, 2, -2, 3, -3)


def head_grad_body(marks_ref, x_mine_ref, x_other_ref, d_mine_ref, d_other_ref, *refs):
    outs, right_ref, left_ref, sum_ref = refs[:7], refs[7], refs[8], refs[9]
    value = dot_tokens(x_mine_ref[...], d_mine_ref[0]) + dot_tokens(x_other_ref[...], d_other_ref[0])
    sum_ref[...] = value.reshape(sum_ref.shape)
    r = sum_ref.shape[1]
    for k, out in zip(HEAD_ORDER, outs):
        for row in (0, 1):
            block = sum_ref[chip_at(marks_ref, row, k)].astype(jnp.bfloat16)
            out[row * r : (row + 1) * r, :] = block
    right_ref[...] = sum_ref[chip_at(marks_ref, 0, 4)].astype(jnp.bfloat16)
    left_ref[...] = sum_ref[chip_at(marks_ref, 1, 4)].astype(jnp.bfloat16)


def head_grad(marks, x_mine, x_other, d_mine, d_other):
    tile = 1152
    steps = CHUNK // tile
    r = D // 16
    n = MODEL_COUNT * CHUNK
    tall = [2 * r] * 7 + [r] * 2
    outs = pl.pallas_call(
        head_grad_body,
        grid_spec=pltpu.PrefetchScalarGridSpec(
            num_scalar_prefetch=1,
            grid=(MODEL_COUNT, steps),
            in_specs=[
                pl.BlockSpec((TILE_COUNT, D), lambda e, j, c: (0, 0)),
                pl.BlockSpec((TILE_COUNT, D), lambda e, j, c: (0, 0)),
                pl.BlockSpec((1, TILE_COUNT, tile), lambda e, j, c: (e, 0, j)),
                pl.BlockSpec((1, TILE_COUNT, tile), lambda e, j, c: (e, 0, j)),
            ],
            out_specs=[pl.BlockSpec((h, tile), lambda e, j, c: (0, e * steps + j)) for h in tall],
            scratch_shapes=[pltpu.VMEM((16, r, tile), jnp.float32)],
        ),
        out_shape=[jax.ShapeDtypeStruct((h, n), jnp.bfloat16) for h in tall],
        compiler_params=pltpu.CompilerParams(
            dimension_semantics=("arbitrary", "arbitrary"), vmem_limit_bytes=VMEM
        ),
        cost_estimate=LIGHT,
        name="head_grad",
    )(marks, x_mine, x_other, d_mine, d_other)
    return dict(zip(HEAD_ORDER, outs[:7])), outs[7], outs[8]


def ring_rows(marks_ref, outs, write):
    for row in (0, 1):
        for out, order in zip(outs, (ORDER_FIRST, ORDER_LAST)):
            for i, k in enumerate(order):
                write(out, row, i, chip_at(marks_ref, row, k))


def core_half(ref, marks_ref):
    n = ref.shape[1] // 2
    return ref[:, pl.ds(pl.multiple_of(marks_ref[0] * n, LANES), n)]


def paired_product(marks_ref, x, x_other, d, d_other):
    return dot_tokens(x[...], core_half(d, marks_ref)) + dot_tokens(
        x_other[...], core_half(d_other, marks_ref)
    )


def second_grad_body(marks_ref, *refs):
    ins, outs, (fc2_ref, fc1_ref) = refs[:8], refs[8:10], refs[10:]
    fc2_ref[...] = paired_product(marks_ref, *ins[:4]).reshape(fc2_ref.shape)
    fc1_ref[...] = paired_product(marks_ref, *ins[4:]).reshape(fc1_ref.shape)
    r4, wide = fc2_ref.shape[1:]
    r = fc1_ref.shape[1]

    def write(out, row, i, chip):
        out[row, i, :r4, :] = fc2_ref[chip].astype(jnp.bfloat16)
        for k in range(4):
            block = fc1_ref[chip, :, k * wide : (k + 1) * wide].astype(jnp.bfloat16)
            out[row, i, r4 + k * r : r4 + (k + 1) * r, :] = block

    ring_rows(marks_ref, outs, write)


def first_grad_body(marks_ref, *refs):
    ins, outs, refs = refs[:12], refs[12:21], refs[21:]
    qkv_ref, proj_ref, small_ref, flat_ref, hidden_ref, block_ref = refs
    qkv_ref[...] = paired_product(marks_ref, *ins[:4]).reshape(qkv_ref.shape)
    proj_ref[...] = paired_product(marks_ref, *ins[4:8]).reshape(proj_ref.shape)
    flat_ref[...] = jnp.zeros_like(flat_ref)
    flat_ref[: ins[8].shape[0], :] = ins[8][...] + ins[9][...]
    small_ref[...] = flat_ref[...].T.reshape(small_ref.shape)
    shards = hidden_ref.shape[0]
    r, wide = qkv_ref.shape[1] // 2, FF // shards
    hidden_ref[...] = jnp.zeros_like(hidden_ref)
    for d in range(shards):
        cols = slice(d * wide, (d + 1) * wide)
        hidden_ref[d : d + 1, :wide] = ins[10][:, cols] + ins[11][:, cols]
    block_ref[...] = jnp.zeros_like(block_ref)
    n, m = qkv_ref.shape[2], qkv_ref.shape[2] + proj_ref.shape[2]

    def write(out, at, chip):
        rows = slice(at, at + 2 * r)
        out[rows, :n] = qkv_ref[chip].astype(jnp.bfloat16)
        out[rows, n:m] = proj_ref[chip].astype(jnp.bfloat16)
        out[rows, m : m + LANES] = small_ref[chip].astype(jnp.bfloat16)
        block_ref[0:1, :] = hidden_ref[pl.ds(2 * chip, 1), :]
        block_ref[r : r + 1, :] = hidden_ref[pl.ds(2 * chip + 1, 1), :]
        out[rows, m + LANES :] = block_ref[...].astype(jnp.bfloat16)

    for k, out in zip(HEAD_ORDER, outs):
        for row in (0, 1):
            write(out, row * 2 * r, chip_at(marks_ref, row, k))
    for row, out in enumerate(outs[7:]):
        write(out, 0, chip_at(marks_ref, row, 4))


def round_grad(body, marks, ins, block, scratch, name):
    r, n = block
    shapes = [(2 * r, n)] * 7 + [(r, n)] * 2
    outs = pl.pallas_call(
        body,
        grid_spec=pltpu.PrefetchScalarGridSpec(
            num_scalar_prefetch=1,
            grid=(1,),
            in_specs=[pl.BlockSpec(v.shape, lambda i, m: (0, 0)) for v in ins],
            out_specs=[pl.BlockSpec(s, lambda i, m: (0, 0)) for s in shapes],
            scratch_shapes=[pltpu.VMEM(s, jnp.float32) for s in scratch],
        ),
        out_shape=[jax.ShapeDtypeStruct(s, jnp.bfloat16) for s in shapes],
        compiler_params=pltpu.CompilerParams(vmem_limit_bytes=VMEM),
        cost_estimate=LIGHT,
        name=name,
    )(marks, *ins)
    return dict(zip(HEAD_ORDER, outs[:7])), outs[7], outs[8]


def ring_grad(body, marks, ins, block, scratch, name):
    shapes = [(2, 3) + block, (2, 5) + block]
    return pl.pallas_call(
        body,
        grid_spec=pltpu.PrefetchScalarGridSpec(
            num_scalar_prefetch=1,
            grid=(1,),
            in_specs=[pl.BlockSpec(v.shape, lambda i, m: (0, 0)) for v in ins],
            out_specs=[pl.BlockSpec(s, lambda i, m: (0, 0, 0, 0)) for s in shapes],
            scratch_shapes=[pltpu.VMEM(s, jnp.float32) for s in scratch],
        ),
        out_shape=[jax.ShapeDtypeStruct(s, jnp.bfloat16) for s in shapes],
        compiler_params=pltpu.CompilerParams(vmem_limit_bytes=VMEM),
        cost_estimate=LIGHT,
        name=name,
    )(marks, *ins)


def pack_small(lead_w, gains, biases, qkv_b, fc1_b, rows):
    value = jnp.concatenate([lead_w, gains, biases, qkv_b, fc1_b.reshape(4, rows).T], axis=1)
    return jnp.pad(value, ((0, 0), (0, LANES - value.shape[1])))


def split_small(small):
    at, found = 0, []
    for width in (LEADS, 2, 4, 2, 4):
        found.append(small[:, at : at + width])
        at += width
    return found


WIDE = MODEL_COUNT * CHUNK


def head_chunks(value):
    r = value.shape[0]
    value = value.reshape(r, MODEL_COUNT, TILE_SAMPLES)
    value = jnp.pad(value, ((0, 0), (0, 0), (0, PADDED - TILE_SAMPLES)))
    value = value.reshape(r, MODEL_COUNT, 2, CHUNKS, CHUNK).transpose(0, 2, 1, 3, 4)
    return [value[:, :, :, q].reshape(r, 2 * WIDE) for q in range(CHUNKS)]


def pack_trunk_body(qkv_ref, proj_ref, fc1_ref, fc2_ref, lead_ref, gain_ref, bias_ref, qkv_b_ref, fc1_b_ref, *refs):
    one_ref, two_ref, flat_ref, tall_ref = refs
    r = qkv_ref.shape[0]
    flat_ref[...] = jnp.zeros_like(flat_ref)
    at = LEADS
    for ref in (gain_ref, bias_ref, qkv_b_ref):
        rows = ref.shape[0]
        flat_ref[at : at + rows, :r] = ref[...].astype(jnp.float32)
        at += rows
    tall_ref[...] = flat_ref[...].T
    tall_ref[:r, :LEADS] = lead_ref[...].astype(jnp.float32)
    flat_ref[...] = jnp.zeros_like(flat_ref)
    flat_ref[0:1, : 4 * r] = fc1_b_ref[...].astype(jnp.float32)
    n = 4 * D
    one_ref[:, : 3 * D] = qkv_ref[...]
    one_ref[:, 3 * D : n] = proj_ref[...]
    one_ref[:, n : n + LANES] = tall_ref[:r, :].astype(jnp.bfloat16)
    one_ref[:, n + LANES :] = flat_ref[:r, :].astype(jnp.bfloat16)
    two_ref[: 4 * r, :] = fc2_ref[...]
    for k in range(4):
        two_ref[(4 + k) * r : (5 + k) * r, :] = fc1_ref[:, k * D : (k + 1) * D]


def pack_trunk(qkv, proj, fc1, fc2, lead_w, gains, biases, qkv_b, fc1_b):
    r = qkv.shape[0]
    return pl.pallas_call(
        pack_trunk_body,
        out_shape=[
            jax.ShapeDtypeStruct((r, 4 * D + 2 * LANES), jnp.bfloat16),
            jax.ShapeDtypeStruct((8 * r, D), jnp.bfloat16),
        ],
        scratch_shapes=[pltpu.VMEM((LANES, LANES), jnp.float32)] * 2,
        compiler_params=pltpu.CompilerParams(vmem_limit_bytes=VMEM),
        cost_estimate=LIGHT,
        name="pack_trunk",
    )(qkv, proj, fc1, fc2, lead_w, gains.T, biases.T, qkv_b.T, fc1_b.reshape(1, 4 * r))


def pack_head_body(head_ref, out):
    r = head_ref.shape[0]
    for q in range(CHUNKS):
        for h in range(2):
            first = h * HALF + q * CHUNK
            real = min(CHUNK, TILE_SAMPLES - first)
            for e in range(MODEL_COUNT):
                begin, at = e * TILE_SAMPLES + first, ((2 * q + h) * MODEL_COUNT + e) * CHUNK
                part = head_ref[:, begin : begin + real]
                if real < CHUNK:
                    part = jnp.concatenate([part, jnp.zeros((r, CHUNK - real), part.dtype)], axis=1)
                out[:, at : at + CHUNK] = part


def pack_head(head):
    return pl.pallas_call(
        pack_head_body,
        out_shape=jax.ShapeDtypeStruct((head.shape[0], 2 * CHUNKS * WIDE), jnp.bfloat16),
        compiler_params=pltpu.CompilerParams(vmem_limit_bytes=VMEM),
        cost_estimate=LIGHT,
        name="pack_head",
    )(head)


def head_whole(low, high):
    r = low[0].shape[0]
    parts = [v.reshape(r, MODEL_COUNT, CHUNK) for v in (*low, *high)]
    return jnp.concatenate(parts, axis=2)[:, :, :TILE_SAMPLES].reshape(r, MODEL_COUNT * TILE_SAMPLES)


DIGITS = 16
BASE = 8.0


def digits_of(value):
    powers = jnp.asarray([BASE**k for k in range(DIGITS + 1)], jnp.float32)
    floors = jnp.floor(value * 32.0 * powers)
    return floors[1:] - BASE * floors[:-1]


def value_of(digits):
    powers = jnp.asarray([BASE ** -(k + 1) / 32.0 for k in range(DIGITS)], jnp.float32)
    return jnp.sum(digits * powers)


SCALE = HD ** (-0.5)
ROW_GAIN, ROW_BIAS, ROW_QKV, ROW_DIGIT = LEADS, LEADS + 2, LEADS + 6, LEADS + 8
SMALL_ROWS = 64
FIRST_WIDE = 4 * D + 2 * LANES


def slab(ref, first, n):
    shards, rows = ref.shape[:2]
    return ref[:, :, first : first + n].reshape(shards * rows, n)


def dot_last(left, right):
    return lax.dot_general(left, right, (((1,), (1,)), ((), ())), preferred_element_type=jnp.float32)


def normalised(values):
    centred = values - jnp.mean(values, axis=-1, keepdims=True)
    inverse = lax.rsqrt(jnp.mean(centred * centred, axis=-1, keepdims=True) + EPS)
    return centred * inverse, inverse


def norm_back(values, d_out, gain):
    unit, inverse = normalised(values)
    d_unit = d_out * gain
    mean_one = jnp.mean(d_unit, axis=-1, keepdims=True)
    mean_two = jnp.mean(d_unit * unit, axis=-1, keepdims=True)
    d_values = inverse * (d_unit - mean_one - unit * mean_two)
    return (
        d_values,
        jnp.sum(d_out * unit, axis=0, keepdims=True),
        jnp.sum(d_out, axis=0, keepdims=True),
    )


def head_masks():
    lane = lax.broadcasted_iota(jnp.int32, (1, 2 * HD), 1)
    low = lane < HD
    return low, [m.astype(jnp.float32).astype(jnp.bfloat16) for m in (low, lane >= HD)]


def softmax_of(scores):
    expd = jnp.exp(scores - jnp.max(scores, axis=-1, keepdims=True))
    return expd * (1.0 / jnp.sum(expd, axis=-1, keepdims=True))


def trunk_first_body(moves, table_ref, index_ref, frame_ref, *refs):
    ins, refs = refs[:-9], refs[-9:]
    middle_ref, normed_ref, joined_ref, attended_ref, normed_two_ref, par_ref, fc1_b_ref = refs[:7]
    held_ref, sems = refs[7:]
    run_moves(moves, table_ref, ins, [held_ref], sems)
    par_ref[...] = slab(held_ref, 4 * D, LANES).astype(jnp.float32).T
    shards = held_ref.shape[0]
    wide = FF // shards
    for d in range(shards):
        row = held_ref[d, 0:1, 4 * D + LANES : 4 * D + LANES + wide]
        fc1_b_ref[:, d * wide : (d + 1) * wide] = row.astype(jnp.float32)

    def row(i):
        return par_ref[i : i + 1, :]

    started = frame_ref[...].astype(jnp.float32) + par_ref[pl.ds(index_ref[0], 1), :]
    normed = (normalised(started)[0] * row(ROW_GAIN) + row(ROW_BIAS)).astype(jnp.bfloat16)
    normed_ref[...] = normed
    for i, shift in enumerate((row(ROW_QKV), None, row(ROW_QKV + 1))):
        part = jnp.dot(normed, slab(held_ref, i * D, D), preferred_element_type=jnp.float32)
        part = part if shift is None else part + shift
        joined_ref[:, i * D : (i + 1) * D] = part.astype(jnp.bfloat16)
    low, masks = head_masks()
    for p in range(HEADS // 2):
        at = p * 2 * HD
        q, k, v = (joined_ref[:, i * D + at : i * D + at + 2 * HD] for i in range(3))
        outs = []
        for mask in masks:
            probs = softmax_of(dot_last(q * mask, k) * SCALE).astype(jnp.bfloat16)
            outs.append(jnp.dot(probs, v, preferred_element_type=jnp.float32))
        attended_ref[:, at : at + 2 * HD] = jnp.where(low, *outs).astype(jnp.bfloat16)
    middle = (
        started
        + jnp.dot(attended_ref[...], slab(held_ref, 3 * D, D), preferred_element_type=jnp.float32)
        + row(ROW_BIAS + 1)
    )
    middle_ref[...] = middle
    normed_two = normalised(middle)[0] * row(ROW_GAIN + 1) + row(ROW_BIAS + 2)
    normed_two_ref[...] = normed_two.astype(jnp.bfloat16)


def trunk_call(body, scalars, ins, sources, outs, scratch, name):
    any_spec = pl.BlockSpec(memory_space=pl.ANY)

    def whole(shape):
        return pl.BlockSpec(shape, lambda i, *s: (0,) * len(shape))

    return pl.pallas_call(
        body,
        grid_spec=pltpu.PrefetchScalarGridSpec(
            num_scalar_prefetch=len(scalars),
            grid=(1,),
            in_specs=[whole(v.shape) for v in ins] + [any_spec] * len(sources),
            out_specs=[whole(s) for s, _ in outs],
            scratch_shapes=scratch,
        ),
        out_shape=[jax.ShapeDtypeStruct(*o) for o in outs],
        compiler_params=pltpu.CompilerParams(vmem_limit_bytes=VMEM),
        cost_estimate=LIGHT,
        name=name,
    )(*scalars, *ins, *sources)


def trunk_first(table, index, rows, moves, frame, *sources):
    flat, low, full = (TILE_COUNT, D), jnp.bfloat16, jnp.float32
    return trunk_call(
        functools.partial(trunk_first_body, moves),
        (table, index),
        (frame,),
        sources,
        [
            (flat, full),
            (flat, low),
            ((TILE_COUNT, 3 * D), low),
            (flat, low),
            (flat, low),
            ((LANES, D), full),
            ((1, FF), full),
        ],
        [
            pltpu.VMEM((32, rows, FIRST_WIDE), low),
            pltpu.SemaphoreType.DMA((len(moves),)),
        ],
        "trunk_first",
    )


def trunk_second_body(moves, table_ref, middle_ref, normed_two_ref, par_ref, fc1_b_ref, *refs):
    ins, refs = refs[:-5], refs[-5:]
    hidden_ref, slope_ref, final_ref, held_ref, sems = refs
    run_moves(moves, table_ref, ins, [held_ref], sems)
    total = middle_ref[...] + par_ref[ROW_BIAS + 3 : ROW_BIAS + 4, :]
    normed_two = normed_two_ref[...]
    for k in range(4):
        cols = slice(k * D, (k + 1) * D)
        pre = jnp.dot(normed_two, widening(held_ref, k), preferred_element_type=jnp.float32)
        pre = pre + fc1_b_ref[:, cols]
        share = 0.5 * (1.0 + lax.erf(pre * (0.5**0.5)))
        density = jnp.exp(-0.5 * pre * pre) * ((0.5 / 3.141592653589793) ** 0.5)
        slope_ref[:, cols] = share + pre * density
        hidden = (pre * share).astype(jnp.bfloat16)
        hidden_ref[:, cols] = hidden
        weight = narrowing(held_ref, k)
        total += jnp.dot(hidden, weight, preferred_element_type=jnp.float32)
    final_ref[...] = total.astype(jnp.bfloat16)


def second_scratch(rows):
    return [pltpu.VMEM((32, 8 * rows, D), jnp.bfloat16)]


def narrowing(held_ref, k):
    shards, rows = held_ref.shape[:2]
    return held_ref[k * shards // 4 : (k + 1) * shards // 4, : rows // 2, :].reshape(D, D)


def widening(held_ref, k):
    rows = held_ref.shape[1] // 8
    return held_ref[:, (4 + k) * rows : (5 + k) * rows, :].reshape(D, D)


def trunk_second(table, rows, moves, middle, normed_two, par, fc1_b, *sources):
    return trunk_call(
        functools.partial(trunk_second_body, moves),
        (table,),
        (middle, normed_two, par, fc1_b),
        sources,
        [
            ((TILE_COUNT, FF), jnp.bfloat16),
            ((TILE_COUNT, FF), jnp.float32),
            ((TILE_COUNT, D), jnp.bfloat16),
        ],
        second_scratch(rows) + [pltpu.SemaphoreType.DMA((len(moves),))],
        "trunk_second",
    )


def second_back_body(moves_two, moves_one, n_two, table_ref, slope_ref, middle_ref, par_ref, *refs):
    d_parts, refs = refs[: 2 * CHUNKS], refs[2 * CHUNKS :]
    ins, refs = refs[:-11], refs[-11:]
    branch_ref, pre_ref, middle_d_ref, attn_ref, attended_ref, rows_ref, fc1_b_ref = refs[:7]
    held_ref, proj_ref, sems_two, sems_one = refs[7:]
    run_moves(moves_one, table_ref, ins[n_two:], [proj_ref], sems_one)
    run_moves(moves_two, table_ref, ins[:n_two], [held_ref], sems_two)
    d_final = d_parts[0][...]
    for part in d_parts[1:]:
        d_final = d_final + part[...]
    d_branch = d_final.astype(jnp.bfloat16)
    branch_ref[...] = d_branch
    d_normed = None
    for k in range(4):
        cols = slice(k * D, (k + 1) * D)
        d_hidden = dot_last(d_branch, narrowing(held_ref, k))
        d_pre = (d_hidden * slope_ref[:, cols]).astype(jnp.bfloat16)
        pre_ref[:, cols] = d_pre
        fc1_b_ref[:, cols] = jnp.sum(d_pre.astype(jnp.float32), axis=0, keepdims=True)
        part = dot_last(d_pre, widening(held_ref, k))
        d_normed = part if d_normed is None else d_normed + part
    gain = par_ref[ROW_GAIN + 1 : ROW_GAIN + 2, :]
    d_part, d_gain, d_shift = norm_back(middle_ref[...], d_normed, gain)
    d_middle = d_final + d_part
    middle_d_ref[...] = d_middle
    d_attn = d_middle.astype(jnp.bfloat16)
    attn_ref[...] = d_attn
    attended_ref[...] = dot_last(d_attn, slab(proj_ref, 0, D)).astype(jnp.bfloat16)
    sums = [jnp.sum(v.astype(jnp.float32), axis=0, keepdims=True) for v in (d_attn, d_branch)]
    rows_ref[...] = jnp.zeros_like(rows_ref)
    for i, value in enumerate((d_gain, d_shift, *sums)):
        rows_ref[i : i + 1, :] = value


def second_back(table, rows, moves_two, moves_one, n_two, slope, middle, par, d_parts, *sources):
    flat, low, full = (TILE_COUNT, D), jnp.bfloat16, jnp.float32
    return trunk_call(
        functools.partial(second_back_body, moves_two, moves_one, n_two),
        (table,),
        (slope, middle, par, *d_parts),
        sources,
        [
            (flat, low),
            ((TILE_COUNT, FF), low),
            (flat, full),
            (flat, low),
            (flat, low),
            ((8, D), full),
            ((1, FF), full),
        ],
        second_scratch(rows)
        + [
            pltpu.VMEM((32, rows, D), low),
            pltpu.SemaphoreType.DMA((len(moves_two),)),
            pltpu.SemaphoreType.DMA((len(moves_one),)),
        ],
        "second_back",
    )


def first_back_body(moves, n_ent, table_ref, index_ref, weight_ref, frame_ref, joined_ref, par_ref, middle_d_ref, attended_ref, rows_ref, *refs):
    ents, refs = refs[:n_ent], refs[n_ent:]
    ins, refs = refs[:-5], refs[-5:]
    d_joined_ref, tokens_ref, small_ref, qkv_ref, sems = refs
    run_moves(moves, table_ref, ins, [qkv_ref], sems)
    small_ref[...] = jnp.zeros_like(small_ref)
    _, masks = head_masks()
    for p in range(HEADS // 2):
        at = p * 2 * HD
        q, k, v = (joined_ref[:, i * D + at : i * D + at + 2 * HD] for i in range(3))
        d_out = attended_ref[:, at : at + 2 * HD]
        totals = [None] * 3
        for mask in masks:
            q_one, k_one, d_one = q * mask, k * mask, d_out * mask
            probs = softmax_of(dot_last(q_one, k) * SCALE)
            d_probs = dot_last(d_one, v)
            inner = jnp.sum(probs * d_probs, axis=-1, keepdims=True)
            d_scores = (probs * (d_probs - inner)).astype(jnp.bfloat16)
            parts = (
                jnp.dot(d_scores, k_one, preferred_element_type=jnp.float32),
                dot_tokens(d_scores, q_one),
                dot_tokens(probs.astype(jnp.bfloat16), d_one),
            )
            totals = [a if b is None else a + b for a, b in zip(parts, totals)]
        for i, scale in enumerate((SCALE, SCALE, 1.0)):
            d_joined_ref[:, i * D + at : i * D + at + 2 * HD] = (totals[i] * scale).astype(
                jnp.bfloat16
            )
    d_normed = None
    for i in range(3):
        block = d_joined_ref[:, i * D : (i + 1) * D]
        if i != 1:
            at = ROW_QKV + i // 2
            total = jnp.sum(block.astype(jnp.float32), axis=0, keepdims=True)
            small_ref[at : at + 1, :] = total
        part = dot_last(block, slab(qkv_ref, i * D, D))
        d_normed = part if d_normed is None else d_normed + part
    started = frame_ref[...].astype(jnp.float32) + par_ref[pl.ds(index_ref[0], 1), :]
    gain = par_ref[ROW_GAIN : ROW_GAIN + 1, :]
    d_part, d_gain, d_shift = norm_back(started, d_normed, gain)
    d_started = middle_d_ref[...] + d_part
    tokens_ref[...] = d_started.astype(jnp.bfloat16)
    small_ref[pl.ds(index_ref[0], 1), :] = jnp.sum(d_started, axis=0, keepdims=True)
    small_ref[ROW_GAIN : ROW_GAIN + 1, :] = d_gain
    small_ref[ROW_BIAS : ROW_BIAS + 1, :] = d_shift
    small_ref[ROW_GAIN + 1 : ROW_GAIN + 2, :] = rows_ref[0:1, :]
    small_ref[ROW_BIAS + 2 : ROW_BIAS + 3, :] = rows_ref[1:2, :]
    small_ref[ROW_BIAS + 1 : ROW_BIAS + 2, :] = rows_ref[2:3, :]
    small_ref[ROW_BIAS + 3 : ROW_BIAS + 4, :] = rows_ref[3:4, :]
    entropy = ents[0][...]
    for ent in ents[1:]:
        entropy = entropy + ent[...]
    entropy = jnp.sum(jnp.sum(entropy, axis=0, keepdims=True), axis=1, keepdims=True)
    value = jnp.broadcast_to(entropy * weight_ref[0] * 32.0, (1, D))
    before = jnp.floor(value)
    for k in range(DIGITS):
        value = value * BASE
        floor = jnp.floor(value)
        small_ref[ROW_DIGIT + k : ROW_DIGIT + k + 1, :] = floor - BASE * before
        before = floor


def first_back(table, index, strength, rows, moves, frame, joined, par, d_middle, d_attended, d_rows, ents, *sources):
    return trunk_call(
        functools.partial(first_back_body, moves, len(ents)),
        (table, index, strength),
        (frame, joined, par, d_middle, d_attended, d_rows, *ents),
        sources,
        [
            ((TILE_COUNT, 3 * D), jnp.bfloat16),
            ((TILE_COUNT, D), jnp.bfloat16),
            ((SMALL_ROWS, D), jnp.float32),
        ],
        [
            pltpu.VMEM((32, rows, 3 * D), jnp.bfloat16),
            pltpu.SemaphoreType.DMA((len(moves),)),
        ],
        "first_back",
    )


def low_or_high(value, core, rows):
    return value[core * rows : (core + 1) * rows]


def fc2_rows(value, core, rows):
    return value[core * 4 * rows : (core + 1) * 4 * rows]


def fc1_rows(value, core, rows):
    begin = 8 * rows + core * rows
    return jnp.concatenate(
        [value[begin + 2 * k * rows : begin + (2 * k + 1) * rows] for k in range(4)], axis=1
    )


class Parameters:
    def __init__(self, small_all, rows):
        lead_w, gain_all, bias_all, qkv_b, fc1_b = split_small(small_all)
        self.lead = lead_w.astype(jnp.float32)
        self.gain = gain_all.astype(jnp.float32)
        self.bias = bias_all.astype(jnp.float32)
        qkv_b = qkv_b.astype(jnp.float32)
        self.offset = jnp.concatenate([qkv_b[:, 0], jnp.zeros_like(qkv_b[:, 0]), qkv_b[:, 1]])
        self.fc1 = (
            fc1_b.astype(jnp.float32).reshape(D // rows, rows, 4).transpose(0, 2, 1).reshape(FF)
        )


    def parts(self):
        return self.lead, self.gain, self.bias, self.offset, self.fc1


def attention_input(frame, lead_vector, gain, bias, offset, qkv_w):
    started = frame.astype(jnp.float32) + lead_vector[None, :]
    normed = layer_norm(started, gain, bias).astype(jnp.bfloat16)
    joined = (plain_dot(normed, qkv_w) + offset).astype(jnp.bfloat16)
    return started, normed, joined


def heads_of(joined):
    return [joined[:, i * D : (i + 1) * D].reshape(TILE_COUNT, HEADS, HD) for i in range(3)]


def attention(joined):
    queries, keys, values = heads_of(joined)
    scores = jnp.einsum("qhd,khd->hqk", queries, keys, preferred_element_type=jnp.float32) * SCALE
    row_top = jnp.max(scores, axis=-1, keepdims=True)
    expd = jnp.exp(scores - row_top)
    prob_full = expd / jnp.sum(expd, axis=-1, keepdims=True)
    probs_low = prob_full.astype(jnp.bfloat16)
    attended = jnp.einsum("hqk,khd->qhd", probs_low, values, preferred_element_type=jnp.float32)
    return prob_full, attended.astype(jnp.bfloat16).reshape(TILE_COUNT, D)


def mlp_input(started, attended, proj_w, proj_bias, gain, bias):
    middle = started + plain_dot(attended, proj_w) + proj_bias
    return middle, layer_norm(middle, gain, bias).astype(jnp.bfloat16)


def mlp(middle, normed_two, fc1_w, fc1_b, fc2_w, fc2_b):
    pre_act = plain_dot(normed_two, fc1_w) + fc1_b
    hidden = exact_gelu(pre_act).astype(jnp.bfloat16)
    final_sum = middle + plain_dot(hidden, fc2_w) + fc2_b
    return pre_act, hidden, final_sum.astype(jnp.bfloat16)


def mlp_back(d_parts, pre_act, fc2_w):
    d_final = sum(d_parts)
    d_branch = d_final.astype(jnp.bfloat16)
    d_hidden = times_transpose(d_branch, fc2_w)
    _, gelu_back = jax.vjp(exact_gelu, pre_act)
    return d_final, d_branch, gelu_back(d_hidden)[0].astype(jnp.bfloat16)


def mlp_input_back(d_final, d_pre, fc1_w, middle, gain, bias, proj_w):
    d_normed_two = times_transpose(d_pre, fc1_w)
    _, norm_back = jax.vjp(layer_norm, middle, gain, bias)
    d_part, d_gain, d_shift = norm_back(d_normed_two)
    d_middle = d_final + d_part
    d_attn = d_middle.astype(jnp.bfloat16)
    d_attended = times_transpose(d_attn, proj_w).astype(jnp.bfloat16)
    return d_middle, d_attn, d_attended, d_gain, d_shift


def attention_back(joined, prob_full, d_attended):
    queries, keys, values = heads_of(joined)
    d_attended = d_attended.reshape(TILE_COUNT, HEADS, HD)
    probs_low = prob_full.astype(jnp.bfloat16)
    d_values = jnp.einsum("hqk,qhd->khd", probs_low, d_attended, preferred_element_type=jnp.float32)
    d_prob = jnp.einsum("qhd,khd->hqk", d_attended, values, preferred_element_type=jnp.float32)
    d_score = (
        prob_full * (d_prob - jnp.sum(prob_full * d_prob, axis=-1, keepdims=True))
    ).astype(jnp.bfloat16)
    d_queries = (
        jnp.einsum("hqk,khd->qhd", d_score, keys, preferred_element_type=jnp.float32) * SCALE
    )
    d_keys = (
        jnp.einsum("hqk,qhd->khd", d_score, queries, preferred_element_type=jnp.float32) * SCALE
    )
    return jnp.concatenate(
        [v.reshape(TILE_COUNT, D) for v in (d_queries, d_keys, d_values)], axis=1
    ).astype(jnp.bfloat16)


def attention_input_back(d_middle, d_joined, qkv_w, started, gain, bias):
    d_normed = times_transpose(d_joined, qkv_w)
    _, norm_back = jax.vjp(layer_norm, started, gain, bias)
    d_part, d_gain, d_shift = norm_back(d_normed)
    return d_middle + d_part, d_gain, d_shift


def small_gradient(rows, horizon_indicator, contribution, d_started, d_joined, d_attn, d_branch, d_pre, gains, shifts):
    def column_sum(value):
        return jnp.sum(value.astype(jnp.float32), axis=0)

    joined_sums = column_sum(d_joined)
    columns = jnp.stack(
        [
            *gains,
            shifts[0],
            column_sum(d_attn),
            shifts[1],
            column_sum(d_branch),
            joined_sums[:D],
            joined_sums[2 * D :],
        ],
        axis=1,
    )
    hidden_columns = column_sum(d_pre).reshape(D // rows, 4, rows).transpose(0, 2, 1).reshape(D, 4)
    return jnp.concatenate(
        [
            jnp.sum(d_started, axis=0)[:, None] * horizon_indicator[None, :],
            columns,
            hidden_columns,
            jnp.broadcast_to(digits_of(contribution)[None, :], (D, DIGITS)),
            jnp.zeros((D, LANES - LEADS - 12 - DIGITS), jnp.float32),
        ],
        axis=1,
    ).astype(jnp.bfloat16)


def small_outputs(value, rows):
    return (
        value[:, :LEADS],
        value[:, LEADS : LEADS + 2],
        value[:, LEADS + 2 : LEADS + 6],
        value[:, LEADS + 6 : LEADS + 8],
        value[:, LEADS + 8 : LEADS + 12].T.reshape(4 * rows),
    )


def frame_scalars(horizon_indices, horizon_tallies):
    indicator = (horizon_indices[0] == lax.iota(jnp.int32, LEADS)).astype(jnp.float32)
    frame_count = jnp.sum(indicator * horizon_tallies.astype(jnp.float32))
    return indicator, 1.0 / (frame_count * (LEADS * TILE_COUNT * TILE_SAMPLES))


def plain_step(
    tile_embeddings,
    horizon_indices,
    horizon_tallies,
    member_guesses,
    adjoint_of_mixture,
    triple_projection_matrix,
    attention_outward_matrix,
    widening_matrix,
    narrowing_matrix,
    gating_matrix,
    *small_parts,
):
    rows = triple_projection_matrix.shape[0]
    whole = functools.partial(lax.all_gather, axis_name=AXES, axis=0, tiled=True)

    def summed(value):
        return lax.psum_scatter(
            value.astype(jnp.bfloat16), AXES, scatter_dimension=0, tiled=True
        ).astype(jnp.float32)

    qkv_w, proj_w = whole(triple_projection_matrix), whole(attention_outward_matrix)
    fc1_w, fc2_w = whole(widening_matrix), whole(narrowing_matrix)
    par = Parameters(whole(pack_small(*small_parts, rows)), rows)
    indicator, strength = frame_scalars(horizon_indices, horizon_tallies)
    guesses = jnp.transpose(member_guesses[0], (1, 0, 2))
    lead_vector = jnp.sum(par.lead * indicator[None, :], axis=1)
    started, normed, joined = attention_input(
        tile_embeddings[0], lead_vector, par.gain[:, 0], par.bias[:, 0], par.offset, qkv_w
    )
    prob_full, attended = attention(joined)
    middle, normed_two = mlp_input(
        started, attended, proj_w, par.bias[:, 1], par.gain[:, 1], par.bias[:, 2]
    )
    pre_act, hidden, final_low = mlp(middle, normed_two, fc1_w, par.fc1, fc2_w, par.bias[:, 3])
    table = jnp.asarray([0, 1], jnp.int32)
    held_shape = (1, D, WIDE)
    combined, head_grads, d_parts, entropies = None, [], [], []
    head_w = whole(jnp.concatenate(head_chunks(gating_matrix), axis=1))
    for q in range(CHUNKS):
        halves = []
        for own in (False, True):
            combined, d_logits, d_part, entropy = head_pass(
                q,
                own,
                strength.reshape(1),
                table,
                final_low,
                [head_w],
                [(0, (0, 0), held_shape[1:], 0, 0, (0, 0))],
                held_shape,
                guesses,
                adjoint_of_mixture[0],
                combined,
            )
            flat = d_logits.transpose(1, 0, 2).reshape(TILE_COUNT, WIDE)
            halves.append(summed(transpose_times(final_low, flat)))
            d_parts.append(d_part)
            entropies.append(entropy)
        head_grads.append(halves)
    contribution = jnp.sum(sum(entropies)) * strength
    d_final, d_branch, d_pre = mlp_back(d_parts, pre_act, fc2_w)
    d_middle, d_attn, d_attended, gain_two, shift_two = mlp_input_back(
        d_final, d_pre, fc1_w, middle, par.gain[:, 1], par.bias[:, 2], proj_w
    )
    d_joined = attention_back(joined, prob_full, d_attended)
    d_started, gain_one, shift_one = attention_input_back(
        d_middle, d_joined, qkv_w, started, par.gain[:, 0], par.bias[:, 0]
    )
    small_grad = small_gradient(
        rows,
        indicator,
        contribution,
        d_started,
        d_joined,
        d_attn,
        d_branch,
        d_pre,
        (gain_one, gain_two),
        (shift_one, shift_two),
    )
    return (
        combined[None],
        lax.psum(contribution, AXES),
        d_started.astype(jnp.bfloat16)[None],
        summed(transpose_times(normed, d_joined)),
        summed(transpose_times(attended, d_attn)),
        summed(transpose_times(normed_two, d_pre)),
        summed(transpose_times(hidden, d_branch)),
        head_whole(*zip(*head_grads)),
        *small_outputs(summed(small_grad), rows),
    )


def paired_step(
    tile_embeddings,
    horizon_indices,
    horizon_tallies,
    member_guesses,
    adjoint_of_mixture,
    triple_projection_matrix,
    attention_outward_matrix,
    widening_matrix,
    narrowing_matrix,
    gating_matrix,
    *small_parts,
):
    rows = triple_projection_matrix.shape[0]
    core = lax.axis_index("fsdp") % 2
    table = places(True)
    marks = jnp.concatenate([core.reshape(1), places(False)[::2] // 2])
    head_marks = jnp.concatenate([core.reshape(1), table[::2] // 2])
    head_table = jnp.concatenate([table, core.reshape(1)])
    seq = Sequence(horizon_tallies)
    indicator, strength = frame_scalars(horizon_indices, horizon_tallies)

    first_own, second_own = seq.run(
        pack_trunk,
        triple_projection_matrix,
        attention_outward_matrix,
        widening_matrix,
        narrowing_matrix,
        *small_parts,
    )
    one, two = RoundFirst(seq, first_own, 1), RoundFirst(seq, second_own, -1)
    one.start()
    two.start()
    one.arrive()
    one.start()
    head_own = seq.run(pack_head, gating_matrix)
    over = across(head_own)
    two.arrive()
    two.start()
    one.arrive()
    one.start()
    two.arrive()
    two.start()
    over = seq.tie(over)
    one.arrive()
    one.last()
    two.arrive()
    two.last()
    one.arrive_last()
    one.batch()
    two.arrive_last()
    head_first = seq.run(lambda a, b: jnp.concatenate([a, b], axis=0), head_own, over)
    three = AcrossFirst(seq, head_first)
    three.start()
    guesses = seq.run(
        lambda v: lax.optimization_barrier(jnp.transpose(v[0], (1, 0, 2))), member_guesses
    )
    two.batch()
    three.arrive()
    three.start()
    one.arrive_over()
    one.arrive_batches()
    whole_one = [((0, rows), (0, FIRST_WIDE), 0, 0, 0)]
    whole_two = [((0, 8 * rows), (0, D), 0, 0, 0)]
    index = horizon_indices
    sources_one, moves = plan_moves(one.collect(), whole_one)
    middle, normed, joined, attended, normed_two, par, fc1_b = seq.run(
        functools.partial(trunk_first, table, index, rows, moves), tile_embeddings[0], *sources_one
    )
    three.settle()
    three.arrive()
    three.start()
    adjoint = seq.run(lambda v: lax.optimization_barrier(v[0]), adjoint_of_mixture)
    two.arrive_batches()
    three.settle()
    three.arrive()
    three.last()
    two.arrive_over()
    two.arrive_batches()
    sources_two, moves_two = plan_moves(two.collect(), whole_two)
    hidden, slope, final_low = seq.run(
        functools.partial(trunk_second, table, rows, moves_two),
        middle,
        normed_two,
        par,
        fc1_b,
        *sources_two,
    )
    three.settle()
    three.arrive_last()
    final_other = sibling(final_low)
    normed_other, attended_other = sibling(normed), sibling(attended)
    normed_two_other, hidden_other = sibling(normed_two), sibling(hidden)

    held_shape = (32, rows, WIDE)
    head_fields = [((0, rows), (0, WIDE), 0, 0, 0)]
    state = dict(combined=None, d_parts=[], entropies=[])

    def head(q, own, around):
        sources, moves = plan_moves(around.collect(), head_fields)
        before = () if state["combined"] is None else (state["combined"],)

        def function(final_low, before, *sources):
            return head_pass(
                q,
                own,
                strength.reshape(1),
                head_table,
                final_low,
                list(sources),
                moves,
                held_shape,
                guesses,
                adjoint,
                before[0] if before else None,
            )

        state["combined"], d_logits, d_part, entropy = seq.run(
            function, final_low, before, *sources
        )
        state["d_parts"].append(d_part)
        state["entropies"].append(entropy)
        return d_logits

    make_grad = functools.partial(head_grad, head_marks)
    send = sibling(head(0, False, three))
    own = head(0, True, three)
    sum_one = SumRoundFirst(seq, *seq.run(make_grad, final_low, final_other, own, send))
    normed_other, attended_other, normed_two_other, hidden_other = seq.tie(
        normed_other, attended_other, normed_two_other, hidden_other
    )
    moves_proj = plan_moves(one.collect(), [((0, rows), (3 * D, 4 * D), 0, 0, 0)])[1]
    moves_qkv = plan_moves(one.collect(), [((0, rows), (0, 3 * D), 0, 0, 0)])[1]
    d_branch, d_pre, d_middle, d_attn, d_attended, d_rows, d_fc1_b = seq.run(
        functools.partial(second_back, table, rows, moves_two, moves_proj, len(sources_two)),
        slope,
        middle,
        par,
        state["d_parts"],
        *sources_two,
        *sources_one,
    )
    d_attn_other, d_fc1_b_other = sibling(d_attn), sibling(d_fc1_b)
    d_branch_other, d_pre_other = sibling(d_branch), sibling(d_pre)
    sum_one.arrive()
    sum_one.step(3)
    d_branch_other, d_pre_other, d_attn_other, d_fc1_b_other = seq.tie(
        d_branch_other, d_pre_other, d_attn_other, d_fc1_b_other
    )
    parts = seq.run(
        lambda *ins: ring_grad(
            second_grad_body,
            marks,
            ins,
            (16 * rows, D // 2),
            [(16, 8 * rows, D // 2), (16, 2 * rows, FF // 2)],
            "second_grad",
        ),
        *(hidden, hidden_other, d_branch, d_branch_other),
        *(normed_two, normed_two_other, d_pre, d_pre_other),
    )
    sum_three = SumAcrossFirst(seq, parts, 1)
    sum_three.go_across(0)
    d_joined, tokens, small_grad = seq.run(
        functools.partial(first_back, table, index, strength.reshape(1), rows, moves_qkv),
        tile_embeddings[0],
        joined,
        par,
        d_middle,
        d_attended,
        d_rows,
        state["entropies"],
        *sources_one,
    )
    d_joined_other, small_other = sibling(d_joined), sibling(small_grad)
    sum_one.arrive()
    sum_one.step(2)
    blocks = seq.run(
        lambda *ins: round_grad(
            first_grad_body,
            head_marks,
            ins,
            (2 * rows, 2 * D + 2 * LANES),
            [(16, 2 * rows, 3 * D // 2), (16, 2 * rows, D // 2), (16, 2 * rows, LANES)]
            + [(LANES, D), (32, LANES), (2 * rows, LANES)],
            "first_grad",
        ),
        *(normed, normed_other, d_joined, d_joined_other),
        *(attended, attended_other, d_attn, d_attn_other),
        *(small_grad, small_other, d_fc1_b, d_fc1_b_other),
    )
    sum_four = SumRoundFirst(seq, *blocks)
    sum_three.arrive_across(0)
    sum_three.step(4)
    sum_three.go_across(1)
    sum_one.arrive()
    sum_one.step(1)
    sum_four.arrive()
    sum_four.step(3)
    sum_three.arrive()
    sum_three.step(3)
    combined_result = seq.run(flip, state["combined"]).T[None]
    grad_tokens = tokens[None]
    sum_one.arrive()
    sum_one.go_across()
    sum_four.arrive()
    sum_four.step(2)
    sum_three.arrive()
    sum_three.arrive_across(1)
    sum_three.step(2)
    sum_four.arrive()
    sum_four.step(1)
    sum_three.arrive()
    sum_three.step(1)
    first = core == 0

    def finish(total, rows_of):
        low, high = rows_of(total, 0, rows), rows_of(total, 1, rows)
        own, other = jnp.where(first, low, high), jnp.where(first, high, low)
        met = sibling(other.astype(jnp.bfloat16)).astype(jnp.float32)
        return jnp.where(first, own, met), jnp.where(first, met, own)

    low, high = finish(sum_one.finish(), low_or_high)
    sum_four.arrive()
    sum_four.go_across()
    sum_three.arrive()
    total = sum_three.finish()
    out_fc2 = jnp.concatenate(finish(total, fc2_rows), axis=1)
    out_fc1 = jnp.concatenate(finish(total, fc1_rows), axis=1)
    out_head = head_whole([low], [high])
    total = sum_four.finish()
    out_small = jnp.where(first, total[:rows, 2 * D :], total[rows:, 2 * D :])
    low, high = finish(total[:, : 2 * D], low_or_high)
    n = 3 * D // 2
    out_fc1_b = out_small[0, LANES : LANES + 4 * rows]
    cost = value_of(out_small[0, ROW_DIGIT : ROW_DIGIT + DIGITS])
    cost = jnp.where(seq.token[0] < 0, 0.0, cost)
    return (
        combined_result,
        cost,
        grad_tokens,
        jnp.concatenate([low[:, :n], high[:, :n]], axis=1),
        jnp.concatenate([low[:, n:], high[:, n:]], axis=1),
        out_fc1,
        out_fc2,
        out_head,
        out_small[:, :LEADS],
        out_small[:, ROW_GAIN:ROW_BIAS],
        out_small[:, ROW_BIAS:ROW_QKV],
        out_small[:, ROW_QKV:ROW_DIGIT],
        out_fc1_b,
    )


def solution(mesh):
    split = P(AXES)
    paired = mesh.shape["dp"] == 2 and mesh.shape["fsdp"] == 16
    return jax.shard_map(
        paired_step if paired else plain_step,
        mesh=mesh,
        in_specs=(split, split, P()) + (split,) * 12,
        out_specs=(split, P()) + (split,) * 11,
        check_vma=False,
    )
```

```python
import functools

import jax
import jax.numpy as jnp
from jax import lax
from jax.experimental import pallas as pl
from jax.experimental.pallas import tpu as pltpu
from jax.sharding import PartitionSpec as P

D = 768
HEADS = 12
HD = 64
FF = 3072
MODEL_COUNT = 3
TILE_SAMPLES = 4416
LEADS = 40
TILE_COUNT = 256
EPS = 1e-06
LANES = 128
HALF = 2304
PADDED = 2 * HALF
VMEM = 56 * 1024 * 1024

AXES = ("dp", "fsdp")
RING = [(z, 0) for z in range(4)] + [(z, 1) for z in (3, 2, 1, 0)]


def ring_pairs(step):
    pairs = []
    for spot, (z, x) in enumerate(RING):
        to_z, to_x = RING[(spot + step) % 8]
        for core in range(2):
            pairs.append((z * 4 + x * 2 + core, to_z * 4 + to_x * 2 + core))
    return pairs


def forth(value):
    return lax.ppermute(value, "fsdp", ring_pairs(1))


def back(value):
    return lax.ppermute(value, "fsdp", ring_pairs(-1))


def across(value):
    return lax.ppermute(value, "dp", [(0, 1), (1, 0)])


def exchange_rows(value):
    return lax.all_to_all(value, "dp", 0, 0)


def sibling(value):
    return lax.ppermute(value, "fsdp", [(i, i ^ 1) for i in range(16)])


def places(relative):
    y = lax.axis_index("dp") if relative else 0
    f = lax.axis_index("fsdp")
    z, x, core = f // 4, (f // 2) % 2, f % 2
    spot = jnp.where(x == 0, z, 7 - z)
    i = lax.iota(jnp.int32, 32)
    seat = (spot + (i // 2) % 8) % 8
    pair = jnp.where(seat < 4, seat * 2, (7 - seat) * 2 + 1)
    return ((y + i // 16) % 2) * 16 + pair * 2 + (core + i) % 2


def slot(other_row, distance, other_core):
    return other_row * 16 + (distance % 8) * 2 + other_core


def plan_moves(found, fields):
    sources, moves = [], []
    for source, rows, where in found:
        at = [i for i, s in enumerate(sources) if s is source]
        if not at:
            at = [len(sources)]
            sources.append(source)
        for (f0, f1), (g0, g1), out, out_row, out_col in fields:
            moves.append(
                (at[0], (rows[0] + f0, g0), (f1 - f0, g1 - g0), where, out, (out_row, out_col))
            )
    return sources, moves


def place(sources, moves, shapes, table, shards):
    def body(table_ref, *refs):
        ins, outs = refs[: len(sources)], refs[len(sources) : len(sources) + len(shapes)]
        held, sems, out_sems = refs[len(sources) + len(shapes) : -2], refs[-2], refs[-1]
        run_moves(moves, table_ref, ins, held, sems)
        copies = [
            pltpu.make_async_copy(held[i], outs[i], out_sems.at[i]) for i in range(len(shapes))
        ]
        for copy in copies:
            copy.start()
        for copy in copies:
            copy.wait()

    whole = [(shards,) + s for s in shapes]
    return pl.pallas_call(
        body,
        grid_spec=pltpu.PrefetchScalarGridSpec(
            num_scalar_prefetch=1,
            grid=(1,),
            in_specs=[pl.BlockSpec(memory_space=pl.ANY)] * len(sources),
            out_specs=[pl.BlockSpec(memory_space=pl.ANY)] * len(shapes),
            scratch_shapes=[pltpu.VMEM(s, jnp.bfloat16) for s in whole]
            + [
                pltpu.SemaphoreType.DMA((len(moves),)),
                pltpu.SemaphoreType.DMA((len(shapes),)),
            ],
        ),
        out_shape=[jax.ShapeDtypeStruct(s, jnp.bfloat16) for s in whole],
        compiler_params=pltpu.CompilerParams(vmem_limit_bytes=VMEM),
        name="place",
    )(table, *sources)


def run_moves(moves, table_ref, ins, outs, sems, begin=0):
    copies = []
    for i, (at, (sr, sc), (nr, nc), where, out, (dr, dc)) in enumerate(moves):
        copy = pltpu.make_async_copy(
            ins[at].at[pl.ds(sr, nr), pl.ds(begin + sc, nc)],
            outs[out].at[table_ref[where], pl.ds(dr, nr), pl.ds(dc, nc)],
            sems.at[i],
        )
        copy.start()
        copies.append(copy)
    for copy in copies:
        copy.wait()


def add_low(*values):
    total = values[0].astype(jnp.float32)
    for value in values[1:]:
        total = total + value.astype(jnp.float32)
    return total.astype(jnp.bfloat16)


class Sequence:
    def __init__(self, token):
        self.token = token

    def tie(self, *values):
        out = lax.optimization_barrier((self.token,) + values)
        self.token = out[0]
        return out[1] if len(values) == 1 else out[1:]

    def run(self, function, *values):
        values = lax.optimization_barrier((self.token,) + values)
        self.token = values[0]
        return self.tie(function(*values[1:]))


class Around:
    def __init__(self, seq, first):
        self.seq, self.rights, self.lefts = seq, [first], [first]

    def start(self, right=True, left=True):
        if right:
            self.rights.append(forth(self.rights[-1]))
        if left:
            self.lefts.append(back(self.lefts[-1]))

    def arrive(self, right=True, left=True):
        ends = ([self.rights] if right else []) + ([self.lefts] if left else [])
        met = self.seq.tie(*[end[-1] for end in ends])
        for end, value in zip(ends, met if len(ends) > 1 else (met,)):
            end[-1] = value


class RoundFirst(Around):
    def __init__(self, seq, first, longer):
        super().__init__(seq, first)
        self.longer, self.found = longer, []

    def last(self):
        ends = self.rights if self.longer > 0 else self.lefts
        ends.append(forth(ends[-1]) if self.longer > 0 else back(ends[-1]))

    def arrive_last(self):
        self.arrive(self.longer > 0, self.longer < 0)

    def batch(self):
        rights, lefts = self.rights, self.lefts
        r = rights[0].shape[0]
        end = rights[4] if self.longer > 0 else lefts[4]
        parts = (rights[0], rights[1], lefts[1], rights[2], lefts[2], rights[3], lefts[3], end)
        distances = (0, -1, 1, -2, 2, -3, 3, 4)
        joint = self.seq.run(lambda *v: jnp.concatenate(v, axis=0), *parts)
        self.over = across(joint), r, distances
        self.found.append((joint, r, 0, 0, distances))
        self.found.append((sibling(joint), r, 0, 1, distances))

    def arrive_over(self):
        over, r, distances = self.over
        over = self.seq.tie(over)
        self.found.append((over, r, 1, 0, distances))
        self.found.append((sibling(over), r, 1, 1, distances))

    def arrive_batches(self):
        met = self.seq.tie(*[v[0] for v in self.found])
        self.found = [(m,) + v[1:] for m, v in zip(met, self.found)]

    def collect(self):
        return [
            (source, (i * r, (i + 1) * r), slot(other_row, k, other_core))
            for source, r, other_row, other_core, distances in self.found
            for i, k in enumerate(distances)
        ]


class AcrossFirst(Around):
    def __init__(self, seq, first):
        super().__init__(seq, first)
        self.found, self.settled = [], set()
        self.note(first, [(0, 0), (1, 0)])

    def note(self, joint, spots):
        self.found.append((joint, 0, spots))
        self.found.append((sibling(joint), 1, spots))

    def settle(self):
        late = [i for i, item in enumerate(self.found) if item[1] and i not in self.settled]
        met = self.seq.tie(*[self.found[i][0] for i in late])
        for i, value in zip(late, met if len(late) > 1 else (met,)):
            self.found[i] = (value,) + self.found[i][1:]
        self.settled.update(late)

    def arrive(self):
        super().arrive()
        k = len(self.rights) - 1
        self.note(self.rights[k], [(0, -k), (1, -k)])
        self.note(self.lefts[k], [(0, k), (1, k)])

    def last(self):
        r = self.rights[0].shape[0] // 2
        right, left = self.seq.run(lambda a, b: (a[:r], b[r:]), self.rights[3], self.lefts[3])
        self.far = [forth(right), back(left)]

    def arrive_last(self):
        self.far = list(self.seq.tie(*self.far))
        for row, array in enumerate(self.far):
            self.note(array, [(row, 4)])

    def collect(self):
        r = self.rights[0].shape[0] // 2
        return [
            (source, (i * r, (i + 1) * r), slot(row, k, other_core))
            for source, other_core, spots in self.found
            for i, (row, k) in enumerate(spots)
        ]


ORDER_FIRST = (4, 3, -3)
ORDER_LAST = (2, -2, 1, -1, 0)


class SumAcrossFirst:
    def __init__(self, seq, parts, longer):
        self.seq, self.longer, self.ready = seq, longer, {}
        self.parts = parts
        self.met = [None, None]
        self.right = self.left = None

    def go_across(self, part):
        self.met[part] = exchange_rows(self.parts[part])

    def arrive_across(self, part):
        met = self.seq.tie(self.met[part])
        for i, k in enumerate((ORDER_FIRST, ORDER_LAST)[part]):
            self.ready[k] = (met, i)

    def arrive(self):
        if self.right is None:
            self.left = self.seq.tie(self.left)
        elif self.left is None:
            self.right = self.seq.tie(self.right)
        else:
            self.right, self.left = self.seq.tie(self.right, self.left)

    def step(self, k):
        if k == 4:
            value = self.seq.run(lambda v: add_low(v[0, 0], v[1, 0]), self.ready[4][0])
            if self.longer > 0:
                self.right = forth(value)
            else:
                self.left = back(value)
            return
        (met, i), (_, j) = self.ready[k], self.ready[-k]

        def add(met, right, left):
            return add_low(met[0, i], met[1, i], *right), add_low(met[0, j], met[1, j], *left)

        right = () if self.right is None else (self.right,)
        left = () if self.left is None else (self.left,)
        go_right, go_left = self.seq.run(add, met, right, left)
        self.right, self.left = forth(go_right), back(go_left)

    def finish(self):
        met, i = self.ready[0]

        def add(met, right, left):
            return sum(v.astype(jnp.float32) for v in (met[0, i], met[1, i], right, left))

        return self.seq.run(add, met, self.right, self.left)


class SumRoundFirst:
    def __init__(self, seq, blocks, far_right, far_left):
        self.seq, self.blocks = seq, blocks
        self.right, self.left = forth(far_right), back(far_left)

    def arrive(self):
        self.right, self.left = self.seq.tie(self.right, self.left)

    def step(self, k):
        def add_part(one, two, right, left):
            r = right.shape[0]
            return (
                jnp.concatenate([add_low(one[:r], right), one[r:]], axis=0),
                jnp.concatenate([two[:r], add_low(two[r:], left)], axis=0),
            )

        if k == 3:
            values = self.blocks[k], self.blocks[-k], self.right, self.left
            go_right, go_left = self.seq.run(add_part, *values)
            self.right, self.left = forth(go_right), back(go_left)
        else:
            self.right = forth(self.seq.run(add_low, self.blocks[k], self.right))
            self.left = back(self.seq.run(add_low, self.blocks[-k], self.left))

    def add(self, k):
        self.right = self.seq.run(add_low, self.blocks[k], self.right)
        self.left = self.seq.run(add_low, self.blocks[-k], self.left)

    def send(self):
        self.arrive()
        self.right, self.left = forth(self.right), back(self.left)

    def go_across(self):
        def add(block, right, left):
            r = block.shape[0] // 2
            near = sum(v[:r].astype(jnp.float32) for v in (block, right, left))
            return near, add_low(block[r:], right[r:], left[r:])

        self.near, sent = self.seq.run(add, self.blocks[0], self.right, self.left)
        self.met = across(sent)

    def finish(self):
        return self.seq.run(lambda a, b: a + b.astype(jnp.float32), self.near, self.met)


def layer_norm(values, norm_gain, norm_shift):
    row_mean = jnp.mean(values, axis=-1, keepdims=True)
    centred = values - row_mean
    row_var = jnp.mean(centred * centred, axis=-1, keepdims=True)
    return centred * lax.rsqrt(row_var + EPS) * norm_gain + norm_shift


def exact_gelu(values):
    return jax.nn.gelu(values, approximate=False)


def plain_dot(left, right):
    return jnp.dot(left, right, preferred_element_type=jnp.float32)


def times_transpose(left, right):
    return lax.dot_general(
        left, right, (((1,), (1,)), ((), ())), preferred_element_type=jnp.float32
    )


def transpose_times(left, right):
    return lax.dot_general(
        left, right, (((0,), (0,)), ((), ())), preferred_element_type=jnp.float32
    )


CHUNKS = 1
CHUNK = HALF // CHUNKS
LIGHT = pl.CostEstimate(flops=0, transcendentals=0, bytes_accessed=0)
HEAD_TILE = 768
HALF_STEPS = CHUNK // HEAD_TILE
ROWS = 16
COLS = 384


def half_of(own, table_ref):
    core = table_ref[table_ref.shape[0] - 1]
    return core if own else 1 - core


def pixel_block(q, own, j, table_ref):
    return half_of(own, table_ref) * (CHUNKS * HALF_STEPS) + q * HALF_STEPS + j


def head_body(q, own, moves, weight_ref, table_ref, x_ref, guess_ref, adj_ref, *refs):
    ins, refs = refs[:-7], refs[-7:]
    comb_ref, dl_ref, df_ref, ent_ref, logit_ref, held_ref, sems = refs
    j = pl.program_id(0)
    strength = weight_ref[0]
    half = half_of(own, table_ref)
    first_pixel = half * HALF + q * CHUNK + j * HEAD_TILE

    @pl.when(j == 0)
    def _():
        df_ref[...] = jnp.zeros_like(df_ref)
        ent_ref[...] = jnp.zeros_like(ent_ref)
        begin = pl.multiple_of((2 * q + half) * WIDE, LANES)
        run_moves(moves, table_ref, ins, [held_ref], sems, begin)

    x = x_ref[...]

    def weight(e):
        begin = pl.multiple_of(e * CHUNK + j * HEAD_TILE, LANES)
        return held_ref[:, :, pl.ds(begin, HEAD_TILE)].reshape(D, HEAD_TILE)

    for e in range(MODEL_COUNT):
        logit_ref[e] = jnp.dot(x, weight(e), preferred_element_type=jnp.float32)

    for part in range(HEAD_TILE // COLS):
        cols = pl.ds(part * COLS, COLS)
        pixel = first_pixel + part * COLS + lax.broadcasted_iota(jnp.int32, (ROWS, COLS), 1)
        real = pixel < TILE_SAMPLES

        def chunk(i, total):
            rows = pl.ds(pl.multiple_of(i * ROWS, ROWS), ROWS)
            l0, l1, l2 = (logit_ref[e, rows, cols] for e in range(3))
            top = jnp.maximum(jnp.maximum(l0, l1), l2)
            l0, l1, l2 = l0 - top, l1 - top, l2 - top
            e0, e1, e2 = jnp.exp(l0), jnp.exp(l1), jnp.exp(l2)
            norm = e0 + e1 + e2
            inverse = 1.0 / norm
            log_norm = jnp.log(norm)
            b0, b1, b2 = e0 * inverse, e1 * inverse, e2 * inverse
            l0, l1, l2 = l0 - log_norm, l1 - log_norm, l2 - log_norm
            minus_h = b0 * l0 + b1 * l1 + b2 * l2
            g0, g1, g2 = (guess_ref[e, rows, cols].astype(jnp.float32) for e in range(3))
            mixed = b0 * g0 + b1 * g1 + b2 * g2
            comb_ref[rows, cols] = mixed.astype(jnp.bfloat16)
            adj = adj_ref[rows, cols].astype(jnp.float32)
            for e, (b, l, g) in enumerate(((b0, l0, g0), (b1, l1, g1), (b2, l2, g2))):
                d = b * (adj * (g - mixed) - strength * (l - minus_h))
                dl_ref[e, rows, cols] = jnp.where(real, d, 0.0).astype(jnp.bfloat16)
            return total - jnp.where(real, minus_h, 0.0)

        total = lax.fori_loop(
            0,
            TILE_COUNT // ROWS,
            chunk,
            jnp.zeros((ROWS, COLS), jnp.float32),
            unroll=True,
        )
        gathered = total[:, :LANES]
        for k in range(1, COLS // LANES):
            gathered = gathered + total[:, k * LANES : (k + 1) * LANES]
        ent_ref[...] += gathered[:8] + gathered[8:]

    part = None
    for e in range(MODEL_COUNT):
        piece = lax.dot_general(
            dl_ref[e], weight(e), (((1,), (1,)), ((), ())), preferred_element_type=jnp.float32
        )
        part = piece if part is None else part + piece
    df_ref[...] += part


def head_pass(q, own, strength, table, final_low, sources, moves, held_shape, guesses, adjoint, before):
    tile = HEAD_TILE
    extra = [] if before is None else [before]

    def body(*refs):
        refs = refs[:5] + refs[5 + len(extra) :]
        head_body(q, own, moves, *refs)

    d_spec = (MODEL_COUNT, TILE_COUNT, tile)
    return pl.pallas_call(
        body,
        grid_spec=pltpu.PrefetchScalarGridSpec(
            num_scalar_prefetch=2,
            grid=(HALF_STEPS,),
            in_specs=[
                pl.BlockSpec((TILE_COUNT, D), lambda j, s, t: (0, 0)),
                pl.BlockSpec(d_spec, lambda j, s, t: (0, 0, pixel_block(q, own, j, t))),
                pl.BlockSpec((TILE_COUNT, tile), lambda j, s, t: (0, pixel_block(q, own, j, t))),
            ]
            + [pl.BlockSpec(memory_space=pl.ANY)] * (len(extra) + len(sources)),
            out_specs=[
                pl.BlockSpec((TILE_COUNT, tile), lambda j, s, t: (0, pixel_block(q, own, j, t))),
                pl.BlockSpec(d_spec, lambda j, s, t: (0, 0, j)),
                pl.BlockSpec((TILE_COUNT, D), lambda j, s, t: (0, 0)),
                pl.BlockSpec((8, LANES), lambda j, s, t: (0, 0)),
            ],
            scratch_shapes=[
                pltpu.VMEM(d_spec, jnp.float32),
                pltpu.VMEM(held_shape, jnp.bfloat16),
                pltpu.SemaphoreType.DMA((len(moves),)),
            ],
        ),
        out_shape=[
            jax.ShapeDtypeStruct((TILE_COUNT, TILE_SAMPLES), jnp.bfloat16),
            jax.ShapeDtypeStruct((MODEL_COUNT, TILE_COUNT, CHUNK), jnp.bfloat16),
            jax.ShapeDtypeStruct((TILE_COUNT, D), jnp.float32),
            jax.ShapeDtypeStruct((8, LANES), jnp.float32),
        ],
        input_output_aliases={5: 0} if extra else {},
        compiler_params=pltpu.CompilerParams(
            dimension_semantics=("arbitrary",), vmem_limit_bytes=VMEM
        ),
        cost_estimate=LIGHT,
        name="head_pass",
    )(strength, table, final_low, guesses, adjoint, *extra, *sources)


def flip_body(in_ref, out_ref):
    out_ref[...] = in_ref[...].T


def flip(value):
    tile = HEAD_TILE
    rows, n = value.shape
    return pl.pallas_call(
        flip_body,
        grid=(pl.cdiv(n, tile),),
        in_specs=[pl.BlockSpec((rows, tile), lambda j: (0, j))],
        out_specs=pl.BlockSpec((tile, rows), lambda j: (j, 0)),
        out_shape=jax.ShapeDtypeStruct((n, rows), value.dtype),
        compiler_params=pltpu.CompilerParams(vmem_limit_bytes=VMEM),
        cost_estimate=LIGHT,
        name="flip",
    )(value)


def head_join_body(low_ref, high_ref, out_ref):
    rest = TILE_SAMPLES - HALF
    for e in range(MODEL_COUNT):
        at = e * TILE_SAMPLES
        out_ref[:, at : at + HALF] = low_ref[:, e * HALF : (e + 1) * HALF]
        out_ref[:, at + HALF : at + TILE_SAMPLES] = high_ref[:, e * HALF : e * HALF + rest]


def head_join(low, high):
    return pl.pallas_call(
        head_join_body,
        out_shape=jax.ShapeDtypeStruct((low.shape[0], MODEL_COUNT * TILE_SAMPLES), low.dtype),
        compiler_params=pltpu.CompilerParams(vmem_limit_bytes=VMEM),
        cost_estimate=LIGHT,
        name="head_join",
    )(low, high)


def small_join_body(small_ref, lead_ref, gain_ref, bias_ref, qkv_ref, flat_ref, tall_ref):
    r = small_ref.shape[0]
    flat_ref[...] = jnp.zeros_like(flat_ref)
    flat_ref[:r, :] = small_ref[:, :LANES]
    tall_ref[...] = flat_ref[...].T
    lead_ref[...] = small_ref[:, :LEADS]
    gain_ref[...] = tall_ref[ROW_GAIN:ROW_BIAS, :r]
    bias_ref[...] = tall_ref[ROW_BIAS:ROW_QKV, :r]
    qkv_ref[...] = tall_ref[ROW_QKV:ROW_DIGIT, :r]


def small_join(small):
    r = small.shape[0]
    return pl.pallas_call(
        small_join_body,
        out_shape=[jax.ShapeDtypeStruct(s, small.dtype) for s in ((r, LEADS), (2, r), (4, r), (2, r))],
        scratch_shapes=[pltpu.VMEM((LANES, LANES), jnp.float32)] * 2,
        compiler_params=pltpu.CompilerParams(vmem_limit_bytes=VMEM),
        cost_estimate=LIGHT,
        name="small_join",
    )(small)


def dot_tokens(left, right):
    return lax.dot_general(left, right, (((0,), (0,)), ((), ())), preferred_element_type=jnp.float32)


def chip_at(marks_ref, row, distance):
    return marks_ref[1 + row * 8 + distance % 8]


HEAD_ORDER = (0, 1, -1, 2, -2, 3, -3)


def head_grad_body(marks_ref, x_mine_ref, x_other_ref, d_mine_ref, d_other_ref, *refs):
    outs, right_ref, left_ref, sum_ref = refs[:7], refs[7], refs[8], refs[9]
    value = dot_tokens(x_mine_ref[...], d_mine_ref[0]) + dot_tokens(x_other_ref[...], d_other_ref[0])
    sum_ref[...] = value.reshape(sum_ref.shape)
    r = sum_ref.shape[1]
    for k, out in zip(HEAD_ORDER, outs):
        for row in (0, 1):
            block = sum_ref[chip_at(marks_ref, row, k)].astype(jnp.bfloat16)
            out[row * r : (row + 1) * r, :] = block
    right_ref[...] = sum_ref[chip_at(marks_ref, 0, 4)].astype(jnp.bfloat16)
    left_ref[...] = sum_ref[chip_at(marks_ref, 1, 4)].astype(jnp.bfloat16)


def head_grad(marks, x_mine, x_other, d_mine, d_other):
    tile = CHUNK
    steps = CHUNK // tile
    r = D // 16
    n = MODEL_COUNT * CHUNK
    tall = [2 * r] * 7 + [r] * 2
    outs = pl.pallas_call(
        head_grad_body,
        grid_spec=pltpu.PrefetchScalarGridSpec(
            num_scalar_prefetch=1,
            grid=(MODEL_COUNT, steps),
            in_specs=[
                pl.BlockSpec((TILE_COUNT, D), lambda e, j, c: (0, 0)),
                pl.BlockSpec((TILE_COUNT, D), lambda e, j, c: (0, 0)),
                pl.BlockSpec((1, TILE_COUNT, tile), lambda e, j, c: (e, 0, j)),
                pl.BlockSpec((1, TILE_COUNT, tile), lambda e, j, c: (e, 0, j)),
            ],
            out_specs=[pl.BlockSpec((h, tile), lambda e, j, c: (0, e * steps + j)) for h in tall],
            scratch_shapes=[pltpu.VMEM((16, r, tile), jnp.float32)],
        ),
        out_shape=[jax.ShapeDtypeStruct((h, n), jnp.bfloat16) for h in tall],
        compiler_params=pltpu.CompilerParams(
            dimension_semantics=("arbitrary", "arbitrary"), vmem_limit_bytes=VMEM
        ),
        cost_estimate=LIGHT,
        name="head_grad",
    )(marks, x_mine, x_other, d_mine, d_other)
    return dict(zip(HEAD_ORDER, outs[:7])), outs[7], outs[8]


def ring_rows(marks_ref, outs, write):
    for row in (0, 1):
        for out, order in zip(outs, (ORDER_FIRST, ORDER_LAST)):
            for i, k in enumerate(order):
                write(out, row, i, chip_at(marks_ref, row, k))


def core_half(ref, marks_ref):
    n = ref.shape[1] // 2
    return ref[:, pl.ds(pl.multiple_of(marks_ref[0] * n, LANES), n)]


def paired_product(marks_ref, x, x_other, d, d_other):
    return dot_tokens(x[...], core_half(d, marks_ref)) + dot_tokens(
        x_other[...], core_half(d_other, marks_ref)
    )


def second_grad_body(marks_ref, *refs):
    ins, outs, (fc2_ref, fc1_ref) = refs[:8], refs[8:10], refs[10:]
    fc2_ref[...] = paired_product(marks_ref, *ins[:4]).reshape(fc2_ref.shape)
    fc1_ref[...] = paired_product(marks_ref, *ins[4:]).reshape(fc1_ref.shape)
    r4, wide = fc2_ref.shape[1:]
    r = fc1_ref.shape[1]

    def write(out, row, i, chip):
        out[row, i, :r4, :] = fc2_ref[chip].astype(jnp.bfloat16)
        for k in range(4):
            block = fc1_ref[chip, :, k * wide : (k + 1) * wide].astype(jnp.bfloat16)
            out[row, i, r4 + k * r : r4 + (k + 1) * r, :] = block

    ring_rows(marks_ref, outs, write)


def first_grad_body(marks_ref, *refs):
    ins, outs, refs = refs[:12], refs[12:21], refs[21:]
    qkv_ref, proj_ref, small_ref, flat_ref, hidden_ref, block_ref = refs
    qkv_ref[...] = paired_product(marks_ref, *ins[:4]).reshape(qkv_ref.shape)
    proj_ref[...] = paired_product(marks_ref, *ins[4:8]).reshape(proj_ref.shape)
    flat_ref[...] = jnp.zeros_like(flat_ref)
    flat_ref[: ins[8].shape[0], :] = ins[8][...] + ins[9][...]
    small_ref[...] = flat_ref[...].T.reshape(small_ref.shape)
    shards = hidden_ref.shape[0]
    r, wide = qkv_ref.shape[1] // 2, FF // shards
    hidden_ref[...] = jnp.zeros_like(hidden_ref)
    for d in range(shards):
        cols = slice(d * wide, (d + 1) * wide)
        hidden_ref[d : d + 1, :wide] = ins[10][:, cols] + ins[11][:, cols]
    block_ref[...] = jnp.zeros_like(block_ref)
    n, m = qkv_ref.shape[2], qkv_ref.shape[2] + proj_ref.shape[2]

    def write(out, at, chip):
        rows = slice(at, at + 2 * r)
        out[rows, :n] = qkv_ref[chip].astype(jnp.bfloat16)
        out[rows, n:m] = proj_ref[chip].astype(jnp.bfloat16)
        out[rows, m : m + LANES] = small_ref[chip].astype(jnp.bfloat16)
        block_ref[0:1, :] = hidden_ref[pl.ds(2 * chip, 1), :]
        block_ref[r : r + 1, :] = hidden_ref[pl.ds(2 * chip + 1, 1), :]
        out[rows, m + LANES :] = block_ref[...].astype(jnp.bfloat16)

    for k, out in zip(HEAD_ORDER, outs):
        for row in (0, 1):
            write(out, row * 2 * r, chip_at(marks_ref, row, k))
    for row, out in enumerate(outs[7:]):
        write(out, 0, chip_at(marks_ref, row, 4))


def round_grad(body, marks, ins, block, scratch, name):
    r, n = block
    shapes = [(2 * r, n)] * 7 + [(r, n)] * 2
    outs = pl.pallas_call(
        body,
        grid_spec=pltpu.PrefetchScalarGridSpec(
            num_scalar_prefetch=1,
            grid=(1,),
            in_specs=[pl.BlockSpec(v.shape, lambda i, m: (0, 0)) for v in ins],
            out_specs=[pl.BlockSpec(s, lambda i, m: (0, 0)) for s in shapes],
            scratch_shapes=[pltpu.VMEM(s, jnp.float32) for s in scratch],
        ),
        out_shape=[jax.ShapeDtypeStruct(s, jnp.bfloat16) for s in shapes],
        compiler_params=pltpu.CompilerParams(vmem_limit_bytes=VMEM),
        cost_estimate=LIGHT,
        name=name,
    )(marks, *ins)
    return dict(zip(HEAD_ORDER, outs[:7])), outs[7], outs[8]


def ring_grad(body, marks, ins, block, scratch, name):
    shapes = [(2, 3) + block, (2, 5) + block]
    return pl.pallas_call(
        body,
        grid_spec=pltpu.PrefetchScalarGridSpec(
            num_scalar_prefetch=1,
            grid=(1,),
            in_specs=[pl.BlockSpec(v.shape, lambda i, m: (0, 0)) for v in ins],
            out_specs=[pl.BlockSpec(s, lambda i, m: (0, 0, 0, 0)) for s in shapes],
            scratch_shapes=[pltpu.VMEM(s, jnp.float32) for s in scratch],
        ),
        out_shape=[jax.ShapeDtypeStruct(s, jnp.bfloat16) for s in shapes],
        compiler_params=pltpu.CompilerParams(vmem_limit_bytes=VMEM),
        cost_estimate=LIGHT,
        name=name,
    )(marks, *ins)


def pack_small(lead_w, gains, biases, qkv_b, fc1_b, rows):
    value = jnp.concatenate([lead_w, gains, biases, qkv_b, fc1_b.reshape(4, rows).T], axis=1)
    return jnp.pad(value, ((0, 0), (0, LANES - value.shape[1])))


def split_small(small):
    at, found = 0, []
    for width in (LEADS, 2, 4, 2, 4):
        found.append(small[:, at : at + width])
        at += width
    return found


WIDE = MODEL_COUNT * CHUNK


def head_chunks(value):
    r = value.shape[0]
    value = value.reshape(r, MODEL_COUNT, TILE_SAMPLES)
    value = jnp.pad(value, ((0, 0), (0, 0), (0, PADDED - TILE_SAMPLES)))
    value = value.reshape(r, MODEL_COUNT, 2, CHUNKS, CHUNK).transpose(0, 2, 1, 3, 4)
    return [value[:, :, :, q].reshape(r, 2 * WIDE) for q in range(CHUNKS)]


def pack_trunk_body(qkv_ref, proj_ref, fc1_ref, fc2_ref, lead_ref, gain_ref, bias_ref, qkv_b_ref, fc1_b_ref, *refs):
    one_ref, two_ref, flat_ref, tall_ref = refs
    r = qkv_ref.shape[0]
    flat_ref[...] = jnp.zeros_like(flat_ref)
    at = LEADS
    for ref in (gain_ref, bias_ref, qkv_b_ref):
        rows = ref.shape[0]
        flat_ref[at : at + rows, :r] = ref[...].astype(jnp.float32)
        at += rows
    tall_ref[...] = flat_ref[...].T
    tall_ref[:r, :LEADS] = lead_ref[...].astype(jnp.float32)
    flat_ref[...] = jnp.zeros_like(flat_ref)
    flat_ref[0:1, : 4 * r] = fc1_b_ref[...].astype(jnp.float32)
    n = 4 * D
    one_ref[:, : 3 * D] = qkv_ref[...]
    one_ref[:, 3 * D : n] = proj_ref[...]
    one_ref[:, n : n + LANES] = tall_ref[:r, :].astype(jnp.bfloat16)
    one_ref[:, n + LANES :] = flat_ref[:r, :].astype(jnp.bfloat16)
    two_ref[: 4 * r, :] = fc2_ref[...]
    for k in range(4):
        two_ref[(4 + k) * r : (5 + k) * r, :] = fc1_ref[:, k * D : (k + 1) * D]


def pack_trunk(qkv, proj, fc1, fc2, lead_w, gains, biases, qkv_b, fc1_b):
    r = qkv.shape[0]
    return pl.pallas_call(
        pack_trunk_body,
        out_shape=[
            jax.ShapeDtypeStruct((r, 4 * D + 2 * LANES), jnp.bfloat16),
            jax.ShapeDtypeStruct((8 * r, D), jnp.bfloat16),
        ],
        scratch_shapes=[pltpu.VMEM((LANES, LANES), jnp.float32)] * 2,
        compiler_params=pltpu.CompilerParams(vmem_limit_bytes=VMEM),
        cost_estimate=LIGHT,
        name="pack_trunk",
    )(qkv, proj, fc1, fc2, lead_w, gains.T, biases.T, qkv_b.T, fc1_b.reshape(1, 4 * r))


def pack_head_body(head_ref, out):
    r = head_ref.shape[0]
    for q in range(CHUNKS):
        for h in range(2):
            first = h * HALF + q * CHUNK
            real = min(CHUNK, TILE_SAMPLES - first)
            for e in range(MODEL_COUNT):
                begin, at = e * TILE_SAMPLES + first, ((2 * q + h) * MODEL_COUNT + e) * CHUNK
                part = head_ref[:, begin : begin + real]
                if real < CHUNK:
                    part = jnp.concatenate([part, jnp.zeros((r, CHUNK - real), part.dtype)], axis=1)
                out[:, at : at + CHUNK] = part


def pack_head(head):
    return pl.pallas_call(
        pack_head_body,
        out_shape=jax.ShapeDtypeStruct((head.shape[0], 2 * CHUNKS * WIDE), jnp.bfloat16),
        compiler_params=pltpu.CompilerParams(vmem_limit_bytes=VMEM),
        cost_estimate=LIGHT,
        name="pack_head",
    )(head)


def head_whole(low, high):
    r = low[0].shape[0]
    parts = [v.reshape(r, MODEL_COUNT, CHUNK) for v in (*low, *high)]
    return jnp.concatenate(parts, axis=2)[:, :, :TILE_SAMPLES].reshape(r, MODEL_COUNT * TILE_SAMPLES)


DIGITS = 16
BASE = 8.0


def digits_of(value):
    powers = jnp.asarray([BASE**k for k in range(DIGITS + 1)], jnp.float32)
    floors = jnp.floor(value * 32.0 * powers)
    return floors[1:] - BASE * floors[:-1]


def value_of(digits):
    powers = jnp.asarray([BASE ** -(k + 1) / 32.0 for k in range(DIGITS)], jnp.float32)
    return jnp.sum(digits * powers)


SCALE = HD ** (-0.5)
ROW_GAIN, ROW_BIAS, ROW_QKV, ROW_DIGIT = LEADS, LEADS + 2, LEADS + 6, LEADS + 8
SMALL_ROWS = 64
FIRST_WIDE = 4 * D + 2 * LANES


def slab(ref, first, n):
    shards, rows = ref.shape[:2]
    return ref[:, :, first : first + n].reshape(shards * rows, n)


def dot_last(left, right):
    return lax.dot_general(left, right, (((1,), (1,)), ((), ())), preferred_element_type=jnp.float32)


def normalised(values):
    centred = values - jnp.mean(values, axis=-1, keepdims=True)
    inverse = lax.rsqrt(jnp.mean(centred * centred, axis=-1, keepdims=True) + EPS)
    return centred * inverse, inverse


def norm_back(values, d_out, gain):
    unit, inverse = normalised(values)
    d_unit = d_out * gain
    mean_one = jnp.mean(d_unit, axis=-1, keepdims=True)
    mean_two = jnp.mean(d_unit * unit, axis=-1, keepdims=True)
    d_values = inverse * (d_unit - mean_one - unit * mean_two)
    return (
        d_values,
        jnp.sum(d_out * unit, axis=0, keepdims=True),
        jnp.sum(d_out, axis=0, keepdims=True),
    )


def head_masks():
    lane = lax.broadcasted_iota(jnp.int32, (1, 2 * HD), 1)
    low = lane < HD
    return low, [m.astype(jnp.float32).astype(jnp.bfloat16) for m in (low, lane >= HD)]


def softmax_of(scores):
    expd = jnp.exp(scores - jnp.max(scores, axis=-1, keepdims=True))
    return expd * (1.0 / jnp.sum(expd, axis=-1, keepdims=True))


def trunk_first_body(moves, table_ref, index_ref, frame_ref, *refs):
    ins, refs = refs[:-9], refs[-9:]
    middle_ref, normed_ref, joined_ref, attended_ref, normed_two_ref, par_ref, fc1_b_ref = refs[:7]
    held_ref, sems = refs[7:]
    run_moves(moves, table_ref, ins, [held_ref], sems)
    par_ref[...] = slab(held_ref, 4 * D, LANES).astype(jnp.float32).T
    shards = held_ref.shape[0]
    wide = FF // shards
    for d in range(shards):
        row = held_ref[d, 0:1, 4 * D + LANES : 4 * D + LANES + wide]
        fc1_b_ref[:, d * wide : (d + 1) * wide] = row.astype(jnp.float32)

    def row(i):
        return par_ref[i : i + 1, :]

    started = frame_ref[...].astype(jnp.float32) + par_ref[pl.ds(index_ref[0], 1), :]
    normed = (normalised(started)[0] * row(ROW_GAIN) + row(ROW_BIAS)).astype(jnp.bfloat16)
    normed_ref[...] = normed
    for i, shift in enumerate((row(ROW_QKV), None, row(ROW_QKV + 1))):
        part = jnp.dot(normed, slab(held_ref, i * D, D), preferred_element_type=jnp.float32)
        part = part if shift is None else part + shift
        joined_ref[:, i * D : (i + 1) * D] = part.astype(jnp.bfloat16)
    low, masks = head_masks()
    for p in range(HEADS // 2):
        at = p * 2 * HD
        q, k, v = (joined_ref[:, i * D + at : i * D + at + 2 * HD] for i in range(3))
        outs = []
        for mask in masks:
            probs = softmax_of(dot_last(q * mask, k) * SCALE).astype(jnp.bfloat16)
            outs.append(jnp.dot(probs, v, preferred_element_type=jnp.float32))
        attended_ref[:, at : at + 2 * HD] = jnp.where(low, *outs).astype(jnp.bfloat16)
    middle = (
        started
        + jnp.dot(attended_ref[...], slab(held_ref, 3 * D, D), preferred_element_type=jnp.float32)
        + row(ROW_BIAS + 1)
    )
    middle_ref[...] = middle
    normed_two = normalised(middle)[0] * row(ROW_GAIN + 1) + row(ROW_BIAS + 2)
    normed_two_ref[...] = normed_two.astype(jnp.bfloat16)


def trunk_call(body, scalars, ins, sources, outs, scratch, name):
    any_spec = pl.BlockSpec(memory_space=pl.ANY)

    def whole(shape):
        return pl.BlockSpec(shape, lambda i, *s: (0,) * len(shape))

    return pl.pallas_call(
        body,
        grid_spec=pltpu.PrefetchScalarGridSpec(
            num_scalar_prefetch=len(scalars),
            grid=(1,),
            in_specs=[whole(v.shape) for v in ins] + [any_spec] * len(sources),
            out_specs=[whole(s) for s, _ in outs],
            scratch_shapes=scratch,
        ),
        out_shape=[jax.ShapeDtypeStruct(*o) for o in outs],
        compiler_params=pltpu.CompilerParams(vmem_limit_bytes=VMEM),
        cost_estimate=LIGHT,
        name=name,
    )(*scalars, *ins, *sources)


def trunk_first(table, index, rows, moves, frame, *sources):
    flat, low, full = (TILE_COUNT, D), jnp.bfloat16, jnp.float32
    return trunk_call(
        functools.partial(trunk_first_body, moves),
        (table, index),
        (frame,),
        sources,
        [
            (flat, full),
            (flat, low),
            ((TILE_COUNT, 3 * D), low),
            (flat, low),
            (flat, low),
            ((LANES, D), full),
            ((1, FF), full),
        ],
        [
            pltpu.VMEM((32, rows, FIRST_WIDE), low),
            pltpu.SemaphoreType.DMA((len(moves),)),
        ],
        "trunk_first",
    )


def trunk_second_body(moves, table_ref, middle_ref, normed_two_ref, par_ref, fc1_b_ref, *refs):
    ins, refs = refs[:-5], refs[-5:]
    hidden_ref, slope_ref, final_ref, held_ref, sems = refs
    run_moves(moves, table_ref, ins, [held_ref], sems)
    total = middle_ref[...] + par_ref[ROW_BIAS + 3 : ROW_BIAS + 4, :]
    normed_two = normed_two_ref[...]
    for k in range(4):
        cols = slice(k * D, (k + 1) * D)
        pre = jnp.dot(normed_two, widening(held_ref, k), preferred_element_type=jnp.float32)
        pre = pre + fc1_b_ref[:, cols]
        share = 0.5 * (1.0 + lax.erf(pre * (0.5**0.5)))
        density = jnp.exp(-0.5 * pre * pre) * ((0.5 / 3.141592653589793) ** 0.5)
        slope_ref[:, cols] = share + pre * density
        hidden = (pre * share).astype(jnp.bfloat16)
        hidden_ref[:, cols] = hidden
        weight = narrowing(held_ref, k)
        total += jnp.dot(hidden, weight, preferred_element_type=jnp.float32)
    final_ref[...] = total.astype(jnp.bfloat16)


def second_scratch(rows):
    return [pltpu.VMEM((32, 8 * rows, D), jnp.bfloat16)]


def narrowing(held_ref, k):
    shards, rows = held_ref.shape[:2]
    return held_ref[k * shards // 4 : (k + 1) * shards // 4, : rows // 2, :].reshape(D, D)


def widening(held_ref, k):
    rows = held_ref.shape[1] // 8
    return held_ref[:, (4 + k) * rows : (5 + k) * rows, :].reshape(D, D)


def trunk_second(table, rows, moves, middle, normed_two, par, fc1_b, *sources):
    return trunk_call(
        functools.partial(trunk_second_body, moves),
        (table,),
        (middle, normed_two, par, fc1_b),
        sources,
        [
            ((TILE_COUNT, FF), jnp.bfloat16),
            ((TILE_COUNT, FF), jnp.float32),
            ((TILE_COUNT, D), jnp.bfloat16),
        ],
        second_scratch(rows) + [pltpu.SemaphoreType.DMA((len(moves),))],
        "trunk_second",
    )


def second_back_body(moves_two, moves_one, n_two, table_ref, slope_ref, middle_ref, par_ref, *refs):
    d_parts, refs = refs[: 2 * CHUNKS], refs[2 * CHUNKS :]
    ins, refs = refs[:-11], refs[-11:]
    branch_ref, pre_ref, middle_d_ref, attn_ref, attended_ref, rows_ref, fc1_b_ref = refs[:7]
    held_ref, proj_ref, sems_two, sems_one = refs[7:]
    run_moves(moves_one, table_ref, ins[n_two:], [proj_ref], sems_one)
    run_moves(moves_two, table_ref, ins[:n_two], [held_ref], sems_two)
    d_final = d_parts[0][...]
    for part in d_parts[1:]:
        d_final = d_final + part[...]
    d_branch = d_final.astype(jnp.bfloat16)
    branch_ref[...] = d_branch
    d_normed = None
    for k in range(4):
        cols = slice(k * D, (k + 1) * D)
        d_hidden = dot_last(d_branch, narrowing(held_ref, k))
        d_pre = (d_hidden * slope_ref[:, cols]).astype(jnp.bfloat16)
        pre_ref[:, cols] = d_pre
        fc1_b_ref[:, cols] = jnp.sum(d_pre.astype(jnp.float32), axis=0, keepdims=True)
        part = dot_last(d_pre, widening(held_ref, k))
        d_normed = part if d_normed is None else d_normed + part
    gain = par_ref[ROW_GAIN + 1 : ROW_GAIN + 2, :]
    d_part, d_gain, d_shift = norm_back(middle_ref[...], d_normed, gain)
    d_middle = d_final + d_part
    middle_d_ref[...] = d_middle
    d_attn = d_middle.astype(jnp.bfloat16)
    attn_ref[...] = d_attn
    attended_ref[...] = dot_last(d_attn, slab(proj_ref, 0, D)).astype(jnp.bfloat16)
    sums = [jnp.sum(v.astype(jnp.float32), axis=0, keepdims=True) for v in (d_attn, d_branch)]
    rows_ref[...] = jnp.zeros_like(rows_ref)
    for i, value in enumerate((d_gain, d_shift, *sums)):
        rows_ref[i : i + 1, :] = value


def second_back(table, rows, moves_two, moves_one, n_two, slope, middle, par, d_parts, *sources):
    flat, low, full = (TILE_COUNT, D), jnp.bfloat16, jnp.float32
    return trunk_call(
        functools.partial(second_back_body, moves_two, moves_one, n_two),
        (table,),
        (slope, middle, par, *d_parts),
        sources,
        [
            (flat, low),
            ((TILE_COUNT, FF), low),
            (flat, full),
            (flat, low),
            (flat, low),
            ((8, D), full),
            ((1, FF), full),
        ],
        second_scratch(rows)
        + [
            pltpu.VMEM((32, rows, D), low),
            pltpu.SemaphoreType.DMA((len(moves_two),)),
            pltpu.SemaphoreType.DMA((len(moves_one),)),
        ],
        "second_back",
    )


def first_back_body(moves, n_ent, table_ref, index_ref, weight_ref, frame_ref, joined_ref, par_ref, middle_d_ref, attended_ref, rows_ref, *refs):
    ents, refs = refs[:n_ent], refs[n_ent:]
    ins, refs = refs[:-5], refs[-5:]
    d_joined_ref, tokens_ref, small_ref, qkv_ref, sems = refs
    run_moves(moves, table_ref, ins, [qkv_ref], sems)
    small_ref[...] = jnp.zeros_like(small_ref)
    _, masks = head_masks()
    for p in range(HEADS // 2):
        at = p * 2 * HD
        q, k, v = (joined_ref[:, i * D + at : i * D + at + 2 * HD] for i in range(3))
        d_out = attended_ref[:, at : at + 2 * HD]
        totals = [None] * 3
        for mask in masks:
            q_one, k_one, d_one = q * mask, k * mask, d_out * mask
            probs = softmax_of(dot_last(q_one, k) * SCALE)
            d_probs = dot_last(d_one, v)
            inner = jnp.sum(probs * d_probs, axis=-1, keepdims=True)
            d_scores = (probs * (d_probs - inner)).astype(jnp.bfloat16)
            parts = (
                jnp.dot(d_scores, k_one, preferred_element_type=jnp.float32),
                dot_tokens(d_scores, q_one),
                dot_tokens(probs.astype(jnp.bfloat16), d_one),
            )
            totals = [a if b is None else a + b for a, b in zip(parts, totals)]
        for i, scale in enumerate((SCALE, SCALE, 1.0)):
            d_joined_ref[:, i * D + at : i * D + at + 2 * HD] = (totals[i] * scale).astype(
                jnp.bfloat16
            )
    d_normed = None
    for i in range(3):
        block = d_joined_ref[:, i * D : (i + 1) * D]
        if i != 1:
            at = ROW_QKV + i // 2
            total = jnp.sum(block.astype(jnp.float32), axis=0, keepdims=True)
            small_ref[at : at + 1, :] = total
        part = dot_last(block, slab(qkv_ref, i * D, D))
        d_normed = part if d_normed is None else d_normed + part
    started = frame_ref[...].astype(jnp.float32) + par_ref[pl.ds(index_ref[0], 1), :]
    gain = par_ref[ROW_GAIN : ROW_GAIN + 1, :]
    d_part, d_gain, d_shift = norm_back(started, d_normed, gain)
    d_started = middle_d_ref[...] + d_part
    tokens_ref[...] = d_started.astype(jnp.bfloat16)
    small_ref[pl.ds(index_ref[0], 1), :] = jnp.sum(d_started, axis=0, keepdims=True)
    small_ref[ROW_GAIN : ROW_GAIN + 1, :] = d_gain
    small_ref[ROW_BIAS : ROW_BIAS + 1, :] = d_shift
    small_ref[ROW_GAIN + 1 : ROW_GAIN + 2, :] = rows_ref[0:1, :]
    small_ref[ROW_BIAS + 2 : ROW_BIAS + 3, :] = rows_ref[1:2, :]
    small_ref[ROW_BIAS + 1 : ROW_BIAS + 2, :] = rows_ref[2:3, :]
    small_ref[ROW_BIAS + 3 : ROW_BIAS + 4, :] = rows_ref[3:4, :]
    entropy = ents[0][...]
    for ent in ents[1:]:
        entropy = entropy + ent[...]
    entropy = jnp.sum(jnp.sum(entropy, axis=0, keepdims=True), axis=1, keepdims=True)
    value = jnp.broadcast_to(entropy * weight_ref[0] * 32.0, (1, D))
    before = jnp.floor(value)
    for k in range(DIGITS):
        value = value * BASE
        floor = jnp.floor(value)
        small_ref[ROW_DIGIT + k : ROW_DIGIT + k + 1, :] = floor - BASE * before
        before = floor


def first_back(table, index, strength, rows, moves, frame, joined, par, d_middle, d_attended, d_rows, ents, *sources):
    return trunk_call(
        functools.partial(first_back_body, moves, len(ents)),
        (table, index, strength),
        (frame, joined, par, d_middle, d_attended, d_rows, *ents),
        sources,
        [
            ((TILE_COUNT, 3 * D), jnp.bfloat16),
            ((TILE_COUNT, D), jnp.bfloat16),
            ((SMALL_ROWS, D), jnp.float32),
        ],
        [
            pltpu.VMEM((32, rows, 3 * D), jnp.bfloat16),
            pltpu.SemaphoreType.DMA((len(moves),)),
        ],
        "first_back",
    )


def low_or_high(value, core, rows):
    return value[core * rows : (core + 1) * rows]


def fc2_rows(value, core, rows):
    return value[core * 4 * rows : (core + 1) * 4 * rows]


def fc1_rows(value, core, rows):
    begin = 8 * rows + core * rows
    return jnp.concatenate(
        [value[begin + 2 * k * rows : begin + (2 * k + 1) * rows] for k in range(4)], axis=1
    )


class Parameters:
    def __init__(self, small_all, rows):
        lead_w, gain_all, bias_all, qkv_b, fc1_b = split_small(small_all)
        self.lead = lead_w.astype(jnp.float32)
        self.gain = gain_all.astype(jnp.float32)
        self.bias = bias_all.astype(jnp.float32)
        qkv_b = qkv_b.astype(jnp.float32)
        self.offset = jnp.concatenate([qkv_b[:, 0], jnp.zeros_like(qkv_b[:, 0]), qkv_b[:, 1]])
        self.fc1 = (
            fc1_b.astype(jnp.float32).reshape(D // rows, rows, 4).transpose(0, 2, 1).reshape(FF)
        )


    def parts(self):
        return self.lead, self.gain, self.bias, self.offset, self.fc1


def attention_input(frame, lead_vector, gain, bias, offset, qkv_w):
    started = frame.astype(jnp.float32) + lead_vector[None, :]
    normed = layer_norm(started, gain, bias).astype(jnp.bfloat16)
    joined = (plain_dot(normed, qkv_w) + offset).astype(jnp.bfloat16)
    return started, normed, joined


def heads_of(joined):
    return [joined[:, i * D : (i + 1) * D].reshape(TILE_COUNT, HEADS, HD) for i in range(3)]


def attention(joined):
    queries, keys, values = heads_of(joined)
    scores = jnp.einsum("qhd,khd->hqk", queries, keys, preferred_element_type=jnp.float32) * SCALE
    row_top = jnp.max(scores, axis=-1, keepdims=True)
    expd = jnp.exp(scores - row_top)
    prob_full = expd / jnp.sum(expd, axis=-1, keepdims=True)
    probs_low = prob_full.astype(jnp.bfloat16)
    attended = jnp.einsum("hqk,khd->qhd", probs_low, values, preferred_element_type=jnp.float32)
    return prob_full, attended.astype(jnp.bfloat16).reshape(TILE_COUNT, D)


def mlp_input(started, attended, proj_w, proj_bias, gain, bias):
    middle = started + plain_dot(attended, proj_w) + proj_bias
    return middle, layer_norm(middle, gain, bias).astype(jnp.bfloat16)


def mlp(middle, normed_two, fc1_w, fc1_b, fc2_w, fc2_b):
    pre_act = plain_dot(normed_two, fc1_w) + fc1_b
    hidden = exact_gelu(pre_act).astype(jnp.bfloat16)
    final_sum = middle + plain_dot(hidden, fc2_w) + fc2_b
    return pre_act, hidden, final_sum.astype(jnp.bfloat16)


def mlp_back(d_parts, pre_act, fc2_w):
    d_final = sum(d_parts)
    d_branch = d_final.astype(jnp.bfloat16)
    d_hidden = times_transpose(d_branch, fc2_w)
    _, gelu_back = jax.vjp(exact_gelu, pre_act)
    return d_final, d_branch, gelu_back(d_hidden)[0].astype(jnp.bfloat16)


def mlp_input_back(d_final, d_pre, fc1_w, middle, gain, bias, proj_w):
    d_normed_two = times_transpose(d_pre, fc1_w)
    _, norm_back = jax.vjp(layer_norm, middle, gain, bias)
    d_part, d_gain, d_shift = norm_back(d_normed_two)
    d_middle = d_final + d_part
    d_attn = d_middle.astype(jnp.bfloat16)
    d_attended = times_transpose(d_attn, proj_w).astype(jnp.bfloat16)
    return d_middle, d_attn, d_attended, d_gain, d_shift


def attention_back(joined, prob_full, d_attended):
    queries, keys, values = heads_of(joined)
    d_attended = d_attended.reshape(TILE_COUNT, HEADS, HD)
    probs_low = prob_full.astype(jnp.bfloat16)
    d_values = jnp.einsum("hqk,qhd->khd", probs_low, d_attended, preferred_element_type=jnp.float32)
    d_prob = jnp.einsum("qhd,khd->hqk", d_attended, values, preferred_element_type=jnp.float32)
    d_score = (
        prob_full * (d_prob - jnp.sum(prob_full * d_prob, axis=-1, keepdims=True))
    ).astype(jnp.bfloat16)
    d_queries = (
        jnp.einsum("hqk,khd->qhd", d_score, keys, preferred_element_type=jnp.float32) * SCALE
    )
    d_keys = (
        jnp.einsum("hqk,qhd->khd", d_score, queries, preferred_element_type=jnp.float32) * SCALE
    )
    return jnp.concatenate(
        [v.reshape(TILE_COUNT, D) for v in (d_queries, d_keys, d_values)], axis=1
    ).astype(jnp.bfloat16)


def attention_input_back(d_middle, d_joined, qkv_w, started, gain, bias):
    d_normed = times_transpose(d_joined, qkv_w)
    _, norm_back = jax.vjp(layer_norm, started, gain, bias)
    d_part, d_gain, d_shift = norm_back(d_normed)
    return d_middle + d_part, d_gain, d_shift


def small_gradient(rows, horizon_indicator, contribution, d_started, d_joined, d_attn, d_branch, d_pre, gains, shifts):
    def column_sum(value):
        return jnp.sum(value.astype(jnp.float32), axis=0)

    joined_sums = column_sum(d_joined)
    columns = jnp.stack(
        [
            *gains,
            shifts[0],
            column_sum(d_attn),
            shifts[1],
            column_sum(d_branch),
            joined_sums[:D],
            joined_sums[2 * D :],
        ],
        axis=1,
    )
    hidden_columns = column_sum(d_pre).reshape(D // rows, 4, rows).transpose(0, 2, 1).reshape(D, 4)
    return jnp.concatenate(
        [
            jnp.sum(d_started, axis=0)[:, None] * horizon_indicator[None, :],
            columns,
            hidden_columns,
            jnp.broadcast_to(digits_of(contribution)[None, :], (D, DIGITS)),
            jnp.zeros((D, LANES - LEADS - 12 - DIGITS), jnp.float32),
        ],
        axis=1,
    ).astype(jnp.bfloat16)


def small_outputs(value, rows):
    return (
        value[:, :LEADS],
        value[:, LEADS : LEADS + 2],
        value[:, LEADS + 2 : LEADS + 6],
        value[:, LEADS + 6 : LEADS + 8],
        value[:, LEADS + 8 : LEADS + 12].T.reshape(4 * rows),
    )


def frame_scalars(horizon_indices, horizon_tallies):
    indicator = (horizon_indices[0] == lax.iota(jnp.int32, LEADS)).astype(jnp.float32)
    frame_count = jnp.sum(indicator * horizon_tallies.astype(jnp.float32))
    return indicator, 1.0 / (frame_count * (LEADS * TILE_COUNT * TILE_SAMPLES))


def plain_step(
    tile_embeddings,
    horizon_indices,
    horizon_tallies,
    member_guesses,
    adjoint_of_mixture,
    triple_projection_matrix,
    attention_outward_matrix,
    widening_matrix,
    narrowing_matrix,
    gating_matrix,
    *small_parts,
):
    rows = triple_projection_matrix.shape[0]
    whole = functools.partial(lax.all_gather, axis_name=AXES, axis=0, tiled=True)

    def summed(value):
        return lax.psum_scatter(
            value.astype(jnp.bfloat16), AXES, scatter_dimension=0, tiled=True
        ).astype(jnp.float32)

    qkv_w, proj_w = whole(triple_projection_matrix), whole(attention_outward_matrix)
    fc1_w, fc2_w = whole(widening_matrix), whole(narrowing_matrix)
    par = Parameters(whole(pack_small(*small_parts, rows)), rows)
    indicator, strength = frame_scalars(horizon_indices, horizon_tallies)
    guesses = jnp.transpose(member_guesses[0], (1, 0, 2))
    lead_vector = jnp.sum(par.lead * indicator[None, :], axis=1)
    started, normed, joined = attention_input(
        tile_embeddings[0], lead_vector, par.gain[:, 0], par.bias[:, 0], par.offset, qkv_w
    )
    prob_full, attended = attention(joined)
    middle, normed_two = mlp_input(
        started, attended, proj_w, par.bias[:, 1], par.gain[:, 1], par.bias[:, 2]
    )
    pre_act, hidden, final_low = mlp(middle, normed_two, fc1_w, par.fc1, fc2_w, par.bias[:, 3])
    table = jnp.asarray([0, 1], jnp.int32)
    held_shape = (1, D, WIDE)
    combined, head_grads, d_parts, entropies = None, [], [], []
    head_w = whole(jnp.concatenate(head_chunks(gating_matrix), axis=1))
    for q in range(CHUNKS):
        halves = []
        for own in (False, True):
            combined, d_logits, d_part, entropy = head_pass(
                q,
                own,
                strength.reshape(1),
                table,
                final_low,
                [head_w],
                [(0, (0, 0), held_shape[1:], 0, 0, (0, 0))],
                held_shape,
                guesses,
                adjoint_of_mixture[0],
                combined,
            )
            flat = d_logits.transpose(1, 0, 2).reshape(TILE_COUNT, WIDE)
            halves.append(summed(transpose_times(final_low, flat)))
            d_parts.append(d_part)
            entropies.append(entropy)
        head_grads.append(halves)
    contribution = jnp.sum(sum(entropies)) * strength
    d_final, d_branch, d_pre = mlp_back(d_parts, pre_act, fc2_w)
    d_middle, d_attn, d_attended, gain_two, shift_two = mlp_input_back(
        d_final, d_pre, fc1_w, middle, par.gain[:, 1], par.bias[:, 2], proj_w
    )
    d_joined = attention_back(joined, prob_full, d_attended)
    d_started, gain_one, shift_one = attention_input_back(
        d_middle, d_joined, qkv_w, started, par.gain[:, 0], par.bias[:, 0]
    )
    small_grad = small_gradient(
        rows,
        indicator,
        contribution,
        d_started,
        d_joined,
        d_attn,
        d_branch,
        d_pre,
        (gain_one, gain_two),
        (shift_one, shift_two),
    )
    return (
        combined[None],
        lax.psum(contribution, AXES),
        d_started.astype(jnp.bfloat16)[None],
        summed(transpose_times(normed, d_joined)),
        summed(transpose_times(attended, d_attn)),
        summed(transpose_times(normed_two, d_pre)),
        summed(transpose_times(hidden, d_branch)),
        head_whole(*zip(*head_grads)),
        *small_outputs(summed(small_grad), rows),
    )


def paired_step(
    tile_embeddings,
    horizon_indices,
    horizon_tallies,
    member_guesses,
    adjoint_of_mixture,
    triple_projection_matrix,
    attention_outward_matrix,
    widening_matrix,
    narrowing_matrix,
    gating_matrix,
    *small_parts,
):
    rows = triple_projection_matrix.shape[0]
    core = lax.axis_index("fsdp") % 2
    table = places(True)
    marks = jnp.concatenate([core.reshape(1), places(False)[::2] // 2])
    head_marks = jnp.concatenate([core.reshape(1), table[::2] // 2])
    head_table = jnp.concatenate([table, core.reshape(1)])
    seq = Sequence(horizon_tallies)
    indicator, strength = frame_scalars(horizon_indices, horizon_tallies)

    first_own, second_own = seq.run(
        pack_trunk,
        triple_projection_matrix,
        attention_outward_matrix,
        widening_matrix,
        narrowing_matrix,
        *small_parts,
    )
    one, two = RoundFirst(seq, first_own, 1), RoundFirst(seq, second_own, -1)
    one.start()
    two.start()
    one.arrive()
    one.start()
    head_own = seq.run(pack_head, gating_matrix)
    over = across(head_own)
    two.arrive()
    two.start()
    one.arrive()
    one.start()
    two.arrive()
    two.start()
    over = seq.tie(over)
    one.arrive()
    one.last()
    two.arrive()
    two.last()
    one.arrive_last()
    one.batch()
    two.arrive_last()
    head_first = seq.run(lambda a, b: jnp.concatenate([a, b], axis=0), head_own, over)
    three = AcrossFirst(seq, head_first)
    three.start()
    guesses = seq.run(
        lambda v: lax.optimization_barrier(jnp.transpose(v[0], (1, 0, 2))), member_guesses
    )
    two.batch()
    three.arrive()
    three.start()
    one.arrive_over()
    one.arrive_batches()
    whole_one = [((0, rows), (0, FIRST_WIDE), 0, 0, 0)]
    whole_two = [((0, 8 * rows), (0, D), 0, 0, 0)]
    index = horizon_indices
    sources_one, moves = plan_moves(one.collect(), whole_one)
    middle, normed, joined, attended, normed_two, par, fc1_b = seq.run(
        functools.partial(trunk_first, table, index, rows, moves), tile_embeddings[0], *sources_one
    )
    three.settle()
    three.arrive()
    three.start()
    adjoint = seq.run(lambda v: lax.optimization_barrier(v[0]), adjoint_of_mixture)
    two.arrive_batches()
    three.settle()
    three.arrive()
    three.last()
    two.arrive_over()
    two.arrive_batches()
    sources_two, moves_two = plan_moves(two.collect(), whole_two)
    hidden, slope, final_low = seq.run(
        functools.partial(trunk_second, table, rows, moves_two),
        middle,
        normed_two,
        par,
        fc1_b,
        *sources_two,
    )
    three.settle()
    three.arrive_last()
    final_other = sibling(final_low)
    normed_other, attended_other = sibling(normed), sibling(attended)
    normed_two_other, hidden_other = sibling(normed_two), sibling(hidden)

    held_shape = (32, rows, WIDE)
    head_fields = [((0, rows), (0, WIDE), 0, 0, 0)]
    state = dict(combined=None, d_parts=[], entropies=[])

    def head(q, own, around):
        sources, moves = plan_moves(around.collect(), head_fields)
        before = () if state["combined"] is None else (state["combined"],)

        def function(final_low, before, *sources):
            return head_pass(
                q,
                own,
                strength.reshape(1),
                head_table,
                final_low,
                list(sources),
                moves,
                held_shape,
                guesses,
                adjoint,
                before[0] if before else None,
            )

        state["combined"], d_logits, d_part, entropy = seq.run(
            function, final_low, before, *sources
        )
        state["d_parts"].append(d_part)
        state["entropies"].append(entropy)
        return d_logits

    make_grad = functools.partial(head_grad, head_marks)
    send = sibling(head(0, False, three))
    own = head(0, True, three)
    sum_one = SumRoundFirst(seq, *seq.run(make_grad, final_low, final_other, own, send))
    moves_proj = plan_moves(one.collect(), [((0, rows), (3 * D, 4 * D), 0, 0, 0)])[1]
    moves_qkv = plan_moves(one.collect(), [((0, rows), (0, 3 * D), 0, 0, 0)])[1]
    d_branch, d_pre, d_middle, d_attn, d_attended, d_rows, d_fc1_b = seq.run(
        functools.partial(second_back, table, rows, moves_two, moves_proj, len(sources_two)),
        slope,
        middle,
        par,
        state["d_parts"],
        *sources_two,
        *sources_one,
    )
    d_attn_other, d_fc1_b_other = sibling(d_attn), sibling(d_fc1_b)
    d_branch_other, d_pre_other = sibling(d_branch), sibling(d_pre)
    normed_other, attended_other, normed_two_other, hidden_other = seq.tie(
        normed_other, attended_other, normed_two_other, hidden_other
    )
    sum_one.arrive()
    sum_one.step(3)
    d_branch_other, d_pre_other, d_attn_other, d_fc1_b_other = seq.tie(
        d_branch_other, d_pre_other, d_attn_other, d_fc1_b_other
    )
    parts = seq.run(
        lambda *ins: ring_grad(
            second_grad_body,
            marks,
            ins,
            (16 * rows, D // 2),
            [(16, 8 * rows, D // 2), (16, 2 * rows, FF // 2)],
            "second_grad",
        ),
        *(hidden, hidden_other, d_branch, d_branch_other),
        *(normed_two, normed_two_other, d_pre, d_pre_other),
    )
    sum_three = SumAcrossFirst(seq, parts, 1)
    sum_three.go_across(0)
    d_joined, tokens, small_grad = seq.run(
        functools.partial(first_back, table, index, strength.reshape(1), rows, moves_qkv),
        tile_embeddings[0],
        joined,
        par,
        d_middle,
        d_attended,
        d_rows,
        state["entropies"],
        *sources_one,
    )
    d_joined_other, small_other = sibling(d_joined), sibling(small_grad)
    sum_one.arrive()
    sum_one.step(2)
    blocks = seq.run(
        lambda *ins: round_grad(
            first_grad_body,
            head_marks,
            ins,
            (2 * rows, 2 * D + 2 * LANES),
            [(16, 2 * rows, 3 * D // 2), (16, 2 * rows, D // 2), (16, 2 * rows, LANES)]
            + [(LANES, D), (32, LANES), (2 * rows, LANES)],
            "first_grad",
        ),
        *(normed, normed_other, d_joined, d_joined_other),
        *(attended, attended_other, d_attn, d_attn_other),
        *(small_grad, small_other, d_fc1_b, d_fc1_b_other),
    )
    sum_four = SumRoundFirst(seq, *blocks)
    sum_three.arrive_across(0)
    sum_three.step(4)
    sum_three.go_across(1)
    sum_one.arrive()
    sum_one.step(1)
    sum_four.arrive()
    sum_four.step(3)
    sum_three.arrive()
    sum_three.step(3)
    combined_result = seq.run(flip, state["combined"]).T[None]
    grad_tokens = tokens[None]
    sum_one.arrive()
    sum_one.go_across()
    sum_four.arrive()
    sum_four.step(2)
    sum_three.arrive()
    sum_three.arrive_across(1)
    sum_three.step(2)
    sum_four.arrive()
    sum_four.step(1)
    sum_three.arrive()
    sum_three.step(1)
    first = core == 0

    def finish(total, rows_of):
        low, high = rows_of(total, 0, rows), rows_of(total, 1, rows)
        own, other = jnp.where(first, low, high), jnp.where(first, high, low)
        met = sibling(other.astype(jnp.bfloat16)).astype(jnp.float32)
        return jnp.where(first, own, met), jnp.where(first, met, own)

    low, high = finish(sum_one.finish(), low_or_high)
    sum_four.arrive()
    sum_four.go_across()
    sum_three.arrive()
    total = sum_three.finish()
    out_fc2 = jnp.concatenate(finish(total, fc2_rows), axis=1)
    out_fc1 = jnp.concatenate(finish(total, fc1_rows), axis=1)
    out_head = seq.run(head_join, low, high)
    total = sum_four.finish()
    out_small = jnp.where(first, total[:rows, 2 * D :], total[rows:, 2 * D :])
    low, high = finish(total[:, : 2 * D], low_or_high)
    n = 3 * D // 2
    out_fc1_b = out_small[0, LANES : LANES + 4 * rows]
    out_lead, out_gains, out_biases, out_qkv_b = small_join(out_small)
    cost = value_of(out_small[0, ROW_DIGIT : ROW_DIGIT + DIGITS])
    cost = jnp.where(seq.token[0] < 0, 0.0, cost)
    return (
        combined_result,
        cost,
        grad_tokens,
        jnp.concatenate([low[:, :n], high[:, :n]], axis=1),
        jnp.concatenate([low[:, n:], high[:, n:]], axis=1),
        out_fc1,
        out_fc2,
        out_head,
        out_lead,
        out_gains.T,
        out_biases.T,
        out_qkv_b.T,
        out_fc1_b,
    )


def solution(mesh):
    split = P(AXES)
    paired = mesh.shape["dp"] == 2 and mesh.shape["fsdp"] == 16
    return jax.shard_map(
        paired_step if paired else plain_step,
        mesh=mesh,
        in_specs=(split, split, P()) + (split,) * 12,
        out_specs=(split, P()) + (split,) * 11,
        check_vma=False,
    )
```

```python
import functools

import jax
import jax.numpy as jnp
from jax import lax
from jax.experimental import pallas as pl
from jax.experimental.pallas import tpu as pltpu
from jax.sharding import PartitionSpec as P

D = 768
HEADS = 12
HD = 64
FF = 3072
MODEL_COUNT = 3
TILE_SAMPLES = 4416
LEADS = 40
TILE_COUNT = 256
EPS = 1e-06
LANES = 128
HALF = 2304
PADDED = 2 * HALF
VMEM = 56 * 1024 * 1024

AXES = ("dp", "fsdp")
RING = [(z, 0) for z in range(4)] + [(z, 1) for z in (3, 2, 1, 0)]


def ring_pairs(step):
    pairs = []
    for spot, (z, x) in enumerate(RING):
        to_z, to_x = RING[(spot + step) % 8]
        for core in range(2):
            pairs.append((z * 4 + x * 2 + core, to_z * 4 + to_x * 2 + core))
    return pairs


def forth(value):
    return lax.ppermute(value, "fsdp", ring_pairs(1))


def back(value):
    return lax.ppermute(value, "fsdp", ring_pairs(-1))


def across(value):
    return lax.ppermute(value, "dp", [(0, 1), (1, 0)])


def exchange_rows(value):
    return lax.all_to_all(value, "dp", 0, 0)


def sibling(value):
    return lax.ppermute(value, "fsdp", [(i, i ^ 1) for i in range(16)])


def places(relative):
    y = lax.axis_index("dp") if relative else 0
    f = lax.axis_index("fsdp")
    z, x, core = f // 4, (f // 2) % 2, f % 2
    spot = jnp.where(x == 0, z, 7 - z)
    i = lax.iota(jnp.int32, 32)
    seat = (spot + (i // 2) % 8) % 8
    pair = jnp.where(seat < 4, seat * 2, (7 - seat) * 2 + 1)
    return ((y + i // 16) % 2) * 16 + pair * 2 + (core + i) % 2


def slot(other_row, distance, other_core):
    return other_row * 16 + (distance % 8) * 2 + other_core


def plan_moves(found, fields):
    sources, moves = [], []
    for source, rows, where in found:
        at = [i for i, s in enumerate(sources) if s is source]
        if not at:
            at = [len(sources)]
            sources.append(source)
        for (f0, f1), (g0, g1), out, out_row, out_col in fields:
            moves.append(
                (at[0], (rows[0] + f0, g0), (f1 - f0, g1 - g0), where, out, (out_row, out_col))
            )
    return sources, moves


def place(sources, moves, shapes, table, shards):
    def body(table_ref, *refs):
        ins, outs = refs[: len(sources)], refs[len(sources) : len(sources) + len(shapes)]
        held, sems, out_sems = refs[len(sources) + len(shapes) : -2], refs[-2], refs[-1]
        run_moves(moves, table_ref, ins, held, sems)
        copies = [
            pltpu.make_async_copy(held[i], outs[i], out_sems.at[i]) for i in range(len(shapes))
        ]
        for copy in copies:
            copy.start()
        for copy in copies:
            copy.wait()

    whole = [(shards,) + s for s in shapes]
    return pl.pallas_call(
        body,
        grid_spec=pltpu.PrefetchScalarGridSpec(
            num_scalar_prefetch=1,
            grid=(1,),
            in_specs=[pl.BlockSpec(memory_space=pl.ANY)] * len(sources),
            out_specs=[pl.BlockSpec(memory_space=pl.ANY)] * len(shapes),
            scratch_shapes=[pltpu.VMEM(s, jnp.bfloat16) for s in whole]
            + [
                pltpu.SemaphoreType.DMA((len(moves),)),
                pltpu.SemaphoreType.DMA((len(shapes),)),
            ],
        ),
        out_shape=[jax.ShapeDtypeStruct(s, jnp.bfloat16) for s in whole],
        compiler_params=pltpu.CompilerParams(vmem_limit_bytes=VMEM),
        name="place",
    )(table, *sources)


def run_moves(moves, table_ref, ins, outs, sems, begin=0):
    copies = []
    for i, (at, (sr, sc), (nr, nc), where, out, (dr, dc)) in enumerate(moves):
        copy = pltpu.make_async_copy(
            ins[at].at[pl.ds(sr, nr), pl.ds(begin + sc, nc)],
            outs[out].at[table_ref[where], pl.ds(dr, nr), pl.ds(dc, nc)],
            sems.at[i],
        )
        copy.start()
        copies.append(copy)
    for copy in copies:
        copy.wait()


def add_low(*values):
    total = values[0].astype(jnp.float32)
    for value in values[1:]:
        total = total + value.astype(jnp.float32)
    return total.astype(jnp.bfloat16)


class Sequence:
    def __init__(self, token):
        self.token = token

    def tie(self, *values):
        out = lax.optimization_barrier((self.token,) + values)
        self.token = out[0]
        return out[1] if len(values) == 1 else out[1:]

    def run(self, function, *values):
        values = lax.optimization_barrier((self.token,) + values)
        self.token = values[0]
        return self.tie(function(*values[1:]))


class Around:
    def __init__(self, seq, first):
        self.seq, self.rights, self.lefts = seq, [first], [first]

    def start(self, right=True, left=True):
        if right:
            self.rights.append(forth(self.rights[-1]))
        if left:
            self.lefts.append(back(self.lefts[-1]))

    def arrive(self, right=True, left=True):
        ends = ([self.rights] if right else []) + ([self.lefts] if left else [])
        met = self.seq.tie(*[end[-1] for end in ends])
        for end, value in zip(ends, met if len(ends) > 1 else (met,)):
            end[-1] = value


class RoundFirst(Around):
    def __init__(self, seq, first, longer):
        super().__init__(seq, first)
        self.longer, self.found = longer, []

    def last(self):
        ends = self.rights if self.longer > 0 else self.lefts
        ends.append(forth(ends[-1]) if self.longer > 0 else back(ends[-1]))

    def arrive_last(self):
        self.arrive(self.longer > 0, self.longer < 0)

    def batch(self):
        rights, lefts = self.rights, self.lefts
        r = rights[0].shape[0]
        end = rights[4] if self.longer > 0 else lefts[4]
        parts = (rights[0], rights[1], lefts[1], rights[2], lefts[2], rights[3], lefts[3], end)
        distances = (0, -1, 1, -2, 2, -3, 3, 4)
        joint = self.seq.run(lambda *v: jnp.concatenate(v, axis=0), *parts)
        self.over = across(joint), r, distances
        self.found.append((joint, r, 0, 0, distances))
        self.found.append((sibling(joint), r, 0, 1, distances))

    def arrive_over(self):
        over, r, distances = self.over
        over = self.seq.tie(over)
        self.found.append((over, r, 1, 0, distances))
        self.found.append((sibling(over), r, 1, 1, distances))

    def arrive_batches(self):
        met = self.seq.tie(*[v[0] for v in self.found])
        self.found = [(m,) + v[1:] for m, v in zip(met, self.found)]

    def collect(self):
        return [
            (source, (i * r, (i + 1) * r), slot(other_row, k, other_core))
            for source, r, other_row, other_core, distances in self.found
            for i, k in enumerate(distances)
        ]


class AcrossFirst(Around):
    def __init__(self, seq, first):
        super().__init__(seq, first)
        self.found, self.settled = [], set()
        self.note(first, [(0, 0), (1, 0)])

    def note(self, joint, spots):
        self.found.append((joint, 0, spots))
        self.found.append((sibling(joint), 1, spots))

    def settle(self):
        late = [i for i, item in enumerate(self.found) if item[1] and i not in self.settled]
        met = self.seq.tie(*[self.found[i][0] for i in late])
        for i, value in zip(late, met if len(late) > 1 else (met,)):
            self.found[i] = (value,) + self.found[i][1:]
        self.settled.update(late)

    def arrive(self):
        super().arrive()
        k = len(self.rights) - 1
        self.note(self.rights[k], [(0, -k), (1, -k)])
        self.note(self.lefts[k], [(0, k), (1, k)])

    def last(self):
        r = self.rights[0].shape[0] // 2
        right, left = self.seq.run(lambda a, b: (a[:r], b[r:]), self.rights[3], self.lefts[3])
        self.far = [forth(right), back(left)]

    def arrive_last(self):
        self.far = list(self.seq.tie(*self.far))
        for row, array in enumerate(self.far):
            self.note(array, [(row, 4)])

    def collect(self):
        r = self.rights[0].shape[0] // 2
        return [
            (source, (i * r, (i + 1) * r), slot(row, k, other_core))
            for source, other_core, spots in self.found
            for i, (row, k) in enumerate(spots)
        ]


ORDER_FIRST = (4, 3, -3)
ORDER_LAST = (2, -2, 1, -1, 0)


class SumAcrossFirst:
    def __init__(self, seq, parts, longer):
        self.seq, self.longer, self.ready = seq, longer, {}
        self.parts = parts
        self.met = [None, None]
        self.right = self.left = None

    def go_across(self, part):
        self.met[part] = exchange_rows(self.parts[part])

    def arrive_across(self, part):
        met = self.seq.tie(self.met[part])
        for i, k in enumerate((ORDER_FIRST, ORDER_LAST)[part]):
            self.ready[k] = (met, i)

    def arrive(self):
        if self.right is None:
            self.left = self.seq.tie(self.left)
        elif self.left is None:
            self.right = self.seq.tie(self.right)
        else:
            self.right, self.left = self.seq.tie(self.right, self.left)

    def step(self, k):
        if k == 4:
            value = self.seq.run(lambda v: add_low(v[0, 0], v[1, 0]), self.ready[4][0])
            if self.longer > 0:
                self.right = forth(value)
            else:
                self.left = back(value)
            return
        (met, i), (_, j) = self.ready[k], self.ready[-k]

        def add(met, right, left):
            return add_low(met[0, i], met[1, i], *right), add_low(met[0, j], met[1, j], *left)

        right = () if self.right is None else (self.right,)
        left = () if self.left is None else (self.left,)
        go_right, go_left = self.seq.run(add, met, right, left)
        self.right, self.left = forth(go_right), back(go_left)

    def finish(self):
        met, i = self.ready[0]

        def add(met, right, left):
            return sum(v.astype(jnp.float32) for v in (met[0, i], met[1, i], right, left))

        return self.seq.run(add, met, self.right, self.left)


class SumRoundFirst:
    def __init__(self, seq, blocks, far_right, far_left):
        self.seq, self.blocks = seq, blocks
        self.right, self.left = forth(far_right), back(far_left)

    def arrive(self):
        self.right, self.left = self.seq.tie(self.right, self.left)

    def step(self, k):
        def add_part(one, two, right, left):
            r = right.shape[0]
            return (
                jnp.concatenate([add_low(one[:r], right), one[r:]], axis=0),
                jnp.concatenate([two[:r], add_low(two[r:], left)], axis=0),
            )

        if k == 3:
            values = self.blocks[k], self.blocks[-k], self.right, self.left
            go_right, go_left = self.seq.run(add_part, *values)
            self.right, self.left = forth(go_right), back(go_left)
        else:
            self.right = forth(self.seq.run(add_low, self.blocks[k], self.right))
            self.left = back(self.seq.run(add_low, self.blocks[-k], self.left))

    def add(self, k):
        self.right = self.seq.run(add_low, self.blocks[k], self.right)
        self.left = self.seq.run(add_low, self.blocks[-k], self.left)

    def send(self):
        self.arrive()
        self.right, self.left = forth(self.right), back(self.left)

    def go_across(self):
        def add(block, right, left):
            r = block.shape[0] // 2
            near = sum(v[:r].astype(jnp.float32) for v in (block, right, left))
            return near, add_low(block[r:], right[r:], left[r:])

        self.near, sent = self.seq.run(add, self.blocks[0], self.right, self.left)
        self.met = across(sent)

    def finish(self):
        return self.seq.run(lambda a, b: a + b.astype(jnp.float32), self.near, self.met)


def layer_norm(values, norm_gain, norm_shift):
    row_mean = jnp.mean(values, axis=-1, keepdims=True)
    centred = values - row_mean
    row_var = jnp.mean(centred * centred, axis=-1, keepdims=True)
    return centred * lax.rsqrt(row_var + EPS) * norm_gain + norm_shift


def exact_gelu(values):
    return jax.nn.gelu(values, approximate=False)


def plain_dot(left, right):
    return jnp.dot(left, right, preferred_element_type=jnp.float32)


def times_transpose(left, right):
    return lax.dot_general(
        left, right, (((1,), (1,)), ((), ())), preferred_element_type=jnp.float32
    )


def transpose_times(left, right):
    return lax.dot_general(
        left, right, (((0,), (0,)), ((), ())), preferred_element_type=jnp.float32
    )


CHUNKS = 1
CHUNK = HALF // CHUNKS
LIGHT = pl.CostEstimate(flops=0, transcendentals=0, bytes_accessed=0)
HEAD_TILE = 768
HALF_STEPS = CHUNK // HEAD_TILE
ROWS = 16
COLS = 384


def half_of(own, table_ref):
    core = table_ref[table_ref.shape[0] - 1]
    return core if own else 1 - core


def pixel_block(q, own, j, table_ref):
    return half_of(own, table_ref) * (CHUNKS * HALF_STEPS) + q * HALF_STEPS + j


def head_body(q, own, moves, weight_ref, table_ref, x_ref, guess_ref, adj_ref, *refs):
    ins, refs = refs[:-7], refs[-7:]
    comb_ref, dl_ref, df_ref, ent_ref, logit_ref, held_ref, sems = refs
    j = pl.program_id(0)
    strength = weight_ref[0]
    half = half_of(own, table_ref)
    first_pixel = half * HALF + q * CHUNK + j * HEAD_TILE

    @pl.when(j == 0)
    def _():
        df_ref[...] = jnp.zeros_like(df_ref)
        ent_ref[...] = jnp.zeros_like(ent_ref)
        begin = pl.multiple_of((2 * q + half) * WIDE, LANES)
        run_moves(moves, table_ref, ins, [held_ref], sems, begin)

    x = x_ref[...]

    def weight(e):
        begin = pl.multiple_of(e * CHUNK + j * HEAD_TILE, LANES)
        return held_ref[:, :, pl.ds(begin, HEAD_TILE)].reshape(D, HEAD_TILE)

    for e in range(MODEL_COUNT):
        logit_ref[e] = jnp.dot(x, weight(e), preferred_element_type=jnp.float32)

    for part in range(HEAD_TILE // COLS):
        cols = pl.ds(part * COLS, COLS)
        pixel = first_pixel + part * COLS + lax.broadcasted_iota(jnp.int32, (ROWS, COLS), 1)
        real = pixel < TILE_SAMPLES

        def chunk(i, total):
            rows = pl.ds(pl.multiple_of(i * ROWS, ROWS), ROWS)
            l0, l1, l2 = (logit_ref[e, rows, cols] for e in range(3))
            top = jnp.maximum(jnp.maximum(l0, l1), l2)
            l0, l1, l2 = l0 - top, l1 - top, l2 - top
            e0, e1, e2 = jnp.exp(l0), jnp.exp(l1), jnp.exp(l2)
            norm = e0 + e1 + e2
            inverse = 1.0 / norm
            log_norm = jnp.log(norm)
            b0, b1, b2 = e0 * inverse, e1 * inverse, e2 * inverse
            l0, l1, l2 = l0 - log_norm, l1 - log_norm, l2 - log_norm
            minus_h = b0 * l0 + b1 * l1 + b2 * l2
            g0, g1, g2 = (guess_ref[e, rows, cols].astype(jnp.float32) for e in range(3))
            mixed = b0 * g0 + b1 * g1 + b2 * g2
            comb_ref[rows, cols] = mixed.astype(jnp.bfloat16)
            adj = adj_ref[rows, cols].astype(jnp.float32)
            for e, (b, l, g) in enumerate(((b0, l0, g0), (b1, l1, g1), (b2, l2, g2))):
                d = b * (adj * (g - mixed) - strength * (l - minus_h))
                dl_ref[e, rows, cols] = jnp.where(real, d, 0.0).astype(jnp.bfloat16)
            return total - jnp.where(real, minus_h, 0.0)

        total = lax.fori_loop(
            0,
            TILE_COUNT // ROWS,
            chunk,
            jnp.zeros((ROWS, COLS), jnp.float32),
            unroll=True,
        )
        gathered = total[:, :LANES]
        for k in range(1, COLS // LANES):
            gathered = gathered + total[:, k * LANES : (k + 1) * LANES]
        ent_ref[...] += gathered[:8] + gathered[8:]

    part = None
    for e in range(MODEL_COUNT):
        piece = lax.dot_general(
            dl_ref[e], weight(e), (((1,), (1,)), ((), ())), preferred_element_type=jnp.float32
        )
        part = piece if part is None else part + piece
    df_ref[...] += part


def head_pass(q, own, strength, table, final_low, sources, moves, held_shape, guesses, adjoint, before):
    tile = HEAD_TILE
    extra = [] if before is None else [before]

    def body(*refs):
        refs = refs[:5] + refs[5 + len(extra) :]
        head_body(q, own, moves, *refs)

    d_spec = (MODEL_COUNT, TILE_COUNT, tile)
    return pl.pallas_call(
        body,
        grid_spec=pltpu.PrefetchScalarGridSpec(
            num_scalar_prefetch=2,
            grid=(HALF_STEPS,),
            in_specs=[
                pl.BlockSpec((TILE_COUNT, D), lambda j, s, t: (0, 0)),
                pl.BlockSpec(d_spec, lambda j, s, t: (0, 0, pixel_block(q, own, j, t))),
                pl.BlockSpec((TILE_COUNT, tile), lambda j, s, t: (0, pixel_block(q, own, j, t))),
            ]
            + [pl.BlockSpec(memory_space=pl.ANY)] * (len(extra) + len(sources)),
            out_specs=[
                pl.BlockSpec((TILE_COUNT, tile), lambda j, s, t: (0, pixel_block(q, own, j, t))),
                pl.BlockSpec(d_spec, lambda j, s, t: (0, 0, j)),
                pl.BlockSpec((TILE_COUNT, D), lambda j, s, t: (0, 0)),
                pl.BlockSpec((8, LANES), lambda j, s, t: (0, 0)),
            ],
            scratch_shapes=[
                pltpu.VMEM(d_spec, jnp.float32),
                pltpu.VMEM(held_shape, jnp.bfloat16),
                pltpu.SemaphoreType.DMA((len(moves),)),
            ],
        ),
        out_shape=[
            jax.ShapeDtypeStruct((TILE_COUNT, TILE_SAMPLES), jnp.bfloat16),
            jax.ShapeDtypeStruct((MODEL_COUNT, TILE_COUNT, CHUNK), jnp.bfloat16),
            jax.ShapeDtypeStruct((TILE_COUNT, D), jnp.float32),
            jax.ShapeDtypeStruct((8, LANES), jnp.float32),
        ],
        input_output_aliases={5: 0} if extra else {},
        compiler_params=pltpu.CompilerParams(
            dimension_semantics=("arbitrary",), vmem_limit_bytes=VMEM
        ),
        cost_estimate=LIGHT,
        name="head_pass",
    )(strength, table, final_low, guesses, adjoint, *extra, *sources)


def flip_body(in_ref, out_ref):
    out_ref[...] = in_ref[...].T


def flip(value):
    tile = HEAD_TILE
    rows, n = value.shape
    return pl.pallas_call(
        flip_body,
        grid=(pl.cdiv(n, tile),),
        in_specs=[pl.BlockSpec((rows, tile), lambda j: (0, j))],
        out_specs=pl.BlockSpec((tile, rows), lambda j: (j, 0)),
        out_shape=jax.ShapeDtypeStruct((n, rows), value.dtype),
        compiler_params=pltpu.CompilerParams(vmem_limit_bytes=VMEM),
        cost_estimate=LIGHT,
        name="flip",
    )(value)


def head_join_body(low_ref, high_ref, out_ref):
    rest = TILE_SAMPLES - HALF
    for e in range(MODEL_COUNT):
        at = e * TILE_SAMPLES
        out_ref[:, at : at + HALF] = low_ref[:, e * HALF : (e + 1) * HALF]
        out_ref[:, at + HALF : at + TILE_SAMPLES] = high_ref[:, e * HALF : e * HALF + rest]


def head_join(low, high):
    return pl.pallas_call(
        head_join_body,
        out_shape=jax.ShapeDtypeStruct((low.shape[0], MODEL_COUNT * TILE_SAMPLES), low.dtype),
        compiler_params=pltpu.CompilerParams(vmem_limit_bytes=VMEM),
        cost_estimate=LIGHT,
        name="head_join",
    )(low, high)


def small_join_body(small_ref, lead_ref, gain_ref, bias_ref, qkv_ref, flat_ref, tall_ref):
    r = small_ref.shape[0]
    flat_ref[...] = jnp.zeros_like(flat_ref)
    flat_ref[:r, :] = small_ref[:, :LANES]
    tall_ref[...] = flat_ref[...].T
    lead_ref[...] = small_ref[:, :LEADS]
    gain_ref[...] = tall_ref[ROW_GAIN:ROW_BIAS, :r]
    bias_ref[...] = tall_ref[ROW_BIAS:ROW_QKV, :r]
    qkv_ref[...] = tall_ref[ROW_QKV:ROW_DIGIT, :r]


def small_join(small):
    r = small.shape[0]
    return pl.pallas_call(
        small_join_body,
        out_shape=[jax.ShapeDtypeStruct(s, small.dtype) for s in ((r, LEADS), (2, r), (4, r), (2, r))],
        scratch_shapes=[pltpu.VMEM((LANES, LANES), jnp.float32)] * 2,
        compiler_params=pltpu.CompilerParams(vmem_limit_bytes=VMEM),
        cost_estimate=LIGHT,
        name="small_join",
    )(small)


def dot_tokens(left, right):
    return lax.dot_general(left, right, (((0,), (0,)), ((), ())), preferred_element_type=jnp.float32)


def chip_at(marks_ref, row, distance):
    return marks_ref[1 + row * 8 + distance % 8]


HEAD_ORDER = (0, 1, -1, 2, -2, 3, -3)


def head_grad_body(marks_ref, x_mine_ref, x_other_ref, d_mine_ref, d_other_ref, *refs):
    outs, right_ref, left_ref, sum_ref = refs[:7], refs[7], refs[8], refs[9]
    value = dot_tokens(x_mine_ref[...], d_mine_ref[0]) + dot_tokens(x_other_ref[...], d_other_ref[0])
    sum_ref[...] = value.reshape(sum_ref.shape)
    r = sum_ref.shape[1]
    for k, out in zip(HEAD_ORDER, outs):
        for row in (0, 1):
            block = sum_ref[chip_at(marks_ref, row, k)].astype(jnp.bfloat16)
            out[row * r : (row + 1) * r, :] = block
    right_ref[...] = sum_ref[chip_at(marks_ref, 0, 4)].astype(jnp.bfloat16)
    left_ref[...] = sum_ref[chip_at(marks_ref, 1, 4)].astype(jnp.bfloat16)


def head_grad(marks, x_mine, x_other, d_mine, d_other):
    tile = CHUNK
    steps = CHUNK // tile
    r = D // 16
    n = MODEL_COUNT * CHUNK
    tall = [2 * r] * 7 + [r] * 2
    outs = pl.pallas_call(
        head_grad_body,
        grid_spec=pltpu.PrefetchScalarGridSpec(
            num_scalar_prefetch=1,
            grid=(MODEL_COUNT, steps),
            in_specs=[
                pl.BlockSpec((TILE_COUNT, D), lambda e, j, c: (0, 0)),
                pl.BlockSpec((TILE_COUNT, D), lambda e, j, c: (0, 0)),
                pl.BlockSpec((1, TILE_COUNT, tile), lambda e, j, c: (e, 0, j)),
                pl.BlockSpec((1, TILE_COUNT, tile), lambda e, j, c: (e, 0, j)),
            ],
            out_specs=[pl.BlockSpec((h, tile), lambda e, j, c: (0, e * steps + j)) for h in tall],
            scratch_shapes=[pltpu.VMEM((16, r, tile), jnp.float32)],
        ),
        out_shape=[jax.ShapeDtypeStruct((h, n), jnp.bfloat16) for h in tall],
        compiler_params=pltpu.CompilerParams(
            dimension_semantics=("arbitrary", "arbitrary"), vmem_limit_bytes=VMEM
        ),
        cost_estimate=LIGHT,
        name="head_grad",
    )(marks, x_mine, x_other, d_mine, d_other)
    return dict(zip(HEAD_ORDER, outs[:7])), outs[7], outs[8]


def ring_rows(marks_ref, outs, write):
    for row in (0, 1):
        for out, order in zip(outs, (ORDER_FIRST, ORDER_LAST)):
            for i, k in enumerate(order):
                write(out, row, i, chip_at(marks_ref, row, k))


def core_half(ref, marks_ref):
    n = ref.shape[1] // 2
    return ref[:, pl.ds(pl.multiple_of(marks_ref[0] * n, LANES), n)]


def paired_product(marks_ref, x, x_other, d, d_other):
    return dot_tokens(x[...], core_half(d, marks_ref)) + dot_tokens(
        x_other[...], core_half(d_other, marks_ref)
    )


def second_grad_body(marks_ref, *refs):
    ins, outs, (fc2_ref, fc1_ref) = refs[:8], refs[8:10], refs[10:]
    fc2_ref[...] = paired_product(marks_ref, *ins[:4]).reshape(fc2_ref.shape)
    fc1_ref[...] = paired_product(marks_ref, *ins[4:]).reshape(fc1_ref.shape)
    r4, wide = fc2_ref.shape[1:]
    r = fc1_ref.shape[1]

    def write(out, row, i, chip):
        out[row, i, :r4, :] = fc2_ref[chip].astype(jnp.bfloat16)
        for k in range(4):
            block = fc1_ref[chip, :, k * wide : (k + 1) * wide].astype(jnp.bfloat16)
            out[row, i, r4 + k * r : r4 + (k + 1) * r, :] = block

    ring_rows(marks_ref, outs, write)


def first_grad_body(marks_ref, *refs):
    ins, outs, refs = refs[:12], refs[12:21], refs[21:]
    qkv_ref, proj_ref, small_ref, flat_ref, hidden_ref, block_ref = refs
    qkv_ref[...] = paired_product(marks_ref, *ins[:4]).reshape(qkv_ref.shape)
    proj_ref[...] = paired_product(marks_ref, *ins[4:8]).reshape(proj_ref.shape)
    flat_ref[...] = jnp.zeros_like(flat_ref)
    flat_ref[: ins[8].shape[0], :] = ins[8][...] + ins[9][...]
    small_ref[...] = flat_ref[...].T.reshape(small_ref.shape)
    shards = hidden_ref.shape[0]
    r, wide = qkv_ref.shape[1] // 2, FF // shards
    hidden_ref[...] = jnp.zeros_like(hidden_ref)
    for d in range(shards):
        cols = slice(d * wide, (d + 1) * wide)
        hidden_ref[d : d + 1, :wide] = ins[10][:, cols] + ins[11][:, cols]
    block_ref[...] = jnp.zeros_like(block_ref)
    n, m = qkv_ref.shape[2], qkv_ref.shape[2] + proj_ref.shape[2]

    def write(out, at, chip):
        rows = slice(at, at + 2 * r)
        out[rows, :n] = qkv_ref[chip].astype(jnp.bfloat16)
        out[rows, n:m] = proj_ref[chip].astype(jnp.bfloat16)
        out[rows, m : m + LANES] = small_ref[chip].astype(jnp.bfloat16)
        block_ref[0:1, :] = hidden_ref[pl.ds(2 * chip, 1), :]
        block_ref[r : r + 1, :] = hidden_ref[pl.ds(2 * chip + 1, 1), :]
        out[rows, m + LANES :] = block_ref[...].astype(jnp.bfloat16)

    for k, out in zip(HEAD_ORDER, outs):
        for row in (0, 1):
            write(out, row * 2 * r, chip_at(marks_ref, row, k))
    for row, out in enumerate(outs[7:]):
        write(out, 0, chip_at(marks_ref, row, 4))


def round_grad(body, marks, ins, block, scratch, name):
    r, n = block
    shapes = [(2 * r, n)] * 7 + [(r, n)] * 2
    outs = pl.pallas_call(
        body,
        grid_spec=pltpu.PrefetchScalarGridSpec(
            num_scalar_prefetch=1,
            grid=(1,),
            in_specs=[pl.BlockSpec(v.shape, lambda i, m: (0, 0)) for v in ins],
            out_specs=[pl.BlockSpec(s, lambda i, m: (0, 0)) for s in shapes],
            scratch_shapes=[pltpu.VMEM(s, jnp.float32) for s in scratch],
        ),
        out_shape=[jax.ShapeDtypeStruct(s, jnp.bfloat16) for s in shapes],
        compiler_params=pltpu.CompilerParams(vmem_limit_bytes=VMEM),
        cost_estimate=LIGHT,
        name=name,
    )(marks, *ins)
    return dict(zip(HEAD_ORDER, outs[:7])), outs[7], outs[8]


def ring_grad(body, marks, ins, block, scratch, name):
    shapes = [(2, 3) + block, (2, 5) + block]
    return pl.pallas_call(
        body,
        grid_spec=pltpu.PrefetchScalarGridSpec(
            num_scalar_prefetch=1,
            grid=(1,),
            in_specs=[pl.BlockSpec(v.shape, lambda i, m: (0, 0)) for v in ins],
            out_specs=[pl.BlockSpec(s, lambda i, m: (0, 0, 0, 0)) for s in shapes],
            scratch_shapes=[pltpu.VMEM(s, jnp.float32) for s in scratch],
        ),
        out_shape=[jax.ShapeDtypeStruct(s, jnp.bfloat16) for s in shapes],
        compiler_params=pltpu.CompilerParams(vmem_limit_bytes=VMEM),
        cost_estimate=LIGHT,
        name=name,
    )(marks, *ins)


def pack_small(lead_w, gains, biases, qkv_b, fc1_b, rows):
    value = jnp.concatenate([lead_w, gains, biases, qkv_b, fc1_b.reshape(4, rows).T], axis=1)
    return jnp.pad(value, ((0, 0), (0, LANES - value.shape[1])))


def split_small(small):
    at, found = 0, []
    for width in (LEADS, 2, 4, 2, 4):
        found.append(small[:, at : at + width])
        at += width
    return found


WIDE = MODEL_COUNT * CHUNK


def head_chunks(value):
    r = value.shape[0]
    value = value.reshape(r, MODEL_COUNT, TILE_SAMPLES)
    value = jnp.pad(value, ((0, 0), (0, 0), (0, PADDED - TILE_SAMPLES)))
    value = value.reshape(r, MODEL_COUNT, 2, CHUNKS, CHUNK).transpose(0, 2, 1, 3, 4)
    return [value[:, :, :, q].reshape(r, 2 * WIDE) for q in range(CHUNKS)]


def pack_trunk_body(qkv_ref, proj_ref, fc1_ref, fc2_ref, lead_ref, gain_ref, bias_ref, qkv_b_ref, fc1_b_ref, *refs):
    one_ref, two_ref, flat_ref, tall_ref = refs
    r = qkv_ref.shape[0]
    flat_ref[...] = jnp.zeros_like(flat_ref)
    at = LEADS
    for ref in (gain_ref, bias_ref, qkv_b_ref):
        rows = ref.shape[0]
        flat_ref[at : at + rows, :r] = ref[...].astype(jnp.float32)
        at += rows
    tall_ref[...] = flat_ref[...].T
    tall_ref[:r, :LEADS] = lead_ref[...].astype(jnp.float32)
    flat_ref[...] = jnp.zeros_like(flat_ref)
    flat_ref[0:1, : 4 * r] = fc1_b_ref[...].astype(jnp.float32)
    n = 4 * D
    one_ref[:, : 3 * D] = qkv_ref[...]
    one_ref[:, 3 * D : n] = proj_ref[...]
    one_ref[:, n : n + LANES] = tall_ref[:r, :].astype(jnp.bfloat16)
    one_ref[:, n + LANES :] = flat_ref[:r, :].astype(jnp.bfloat16)
    two_ref[: 4 * r, :] = fc2_ref[...]
    for k in range(4):
        two_ref[(4 + k) * r : (5 + k) * r, :] = fc1_ref[:, k * D : (k + 1) * D]


def pack_trunk(qkv, proj, fc1, fc2, lead_w, gains, biases, qkv_b, fc1_b):
    r = qkv.shape[0]
    return pl.pallas_call(
        pack_trunk_body,
        out_shape=[
            jax.ShapeDtypeStruct((r, 4 * D + 2 * LANES), jnp.bfloat16),
            jax.ShapeDtypeStruct((8 * r, D), jnp.bfloat16),
        ],
        scratch_shapes=[pltpu.VMEM((LANES, LANES), jnp.float32)] * 2,
        compiler_params=pltpu.CompilerParams(vmem_limit_bytes=VMEM),
        cost_estimate=LIGHT,
        name="pack_trunk",
    )(qkv, proj, fc1, fc2, lead_w, gains.T, biases.T, qkv_b.T, fc1_b.reshape(1, 4 * r))


def pack_head_body(head_ref, out):
    r = head_ref.shape[0]
    for q in range(CHUNKS):
        for h in range(2):
            first = h * HALF + q * CHUNK
            real = min(CHUNK, TILE_SAMPLES - first)
            for e in range(MODEL_COUNT):
                begin, at = e * TILE_SAMPLES + first, ((2 * q + h) * MODEL_COUNT + e) * CHUNK
                part = head_ref[:, begin : begin + real]
                if real < CHUNK:
                    part = jnp.concatenate([part, jnp.zeros((r, CHUNK - real), part.dtype)], axis=1)
                out[:, at : at + CHUNK] = part


def pack_head(head):
    return pl.pallas_call(
        pack_head_body,
        out_shape=jax.ShapeDtypeStruct((head.shape[0], 2 * CHUNKS * WIDE), jnp.bfloat16),
        compiler_params=pltpu.CompilerParams(vmem_limit_bytes=VMEM),
        cost_estimate=LIGHT,
        name="pack_head",
    )(head)


def head_whole(low, high):
    r = low[0].shape[0]
    parts = [v.reshape(r, MODEL_COUNT, CHUNK) for v in (*low, *high)]
    return jnp.concatenate(parts, axis=2)[:, :, :TILE_SAMPLES].reshape(r, MODEL_COUNT * TILE_SAMPLES)


DIGITS = 16
BASE = 8.0


def digits_of(value):
    powers = jnp.asarray([BASE**k for k in range(DIGITS + 1)], jnp.float32)
    floors = jnp.floor(value * 32.0 * powers)
    return floors[1:] - BASE * floors[:-1]


def value_of(digits):
    powers = jnp.asarray([BASE ** -(k + 1) / 32.0 for k in range(DIGITS)], jnp.float32)
    return jnp.sum(digits * powers)


SCALE = HD ** (-0.5)
ROW_GAIN, ROW_BIAS, ROW_QKV, ROW_DIGIT = LEADS, LEADS + 2, LEADS + 6, LEADS + 8
SMALL_ROWS = 64
FIRST_WIDE = 4 * D + 2 * LANES


def slab(ref, first, n):
    shards, rows = ref.shape[:2]
    return ref[:, :, first : first + n].reshape(shards * rows, n)


def dot_last(left, right):
    return lax.dot_general(left, right, (((1,), (1,)), ((), ())), preferred_element_type=jnp.float32)


def normalised(values):
    centred = values - jnp.mean(values, axis=-1, keepdims=True)
    inverse = lax.rsqrt(jnp.mean(centred * centred, axis=-1, keepdims=True) + EPS)
    return centred * inverse, inverse


def norm_back(values, d_out, gain):
    unit, inverse = normalised(values)
    d_unit = d_out * gain
    mean_one = jnp.mean(d_unit, axis=-1, keepdims=True)
    mean_two = jnp.mean(d_unit * unit, axis=-1, keepdims=True)
    d_values = inverse * (d_unit - mean_one - unit * mean_two)
    return (
        d_values,
        jnp.sum(d_out * unit, axis=0, keepdims=True),
        jnp.sum(d_out, axis=0, keepdims=True),
    )


def head_masks():
    lane = lax.broadcasted_iota(jnp.int32, (1, 2 * HD), 1)
    low = lane < HD
    return low, [m.astype(jnp.float32).astype(jnp.bfloat16) for m in (low, lane >= HD)]


def softmax_of(scores):
    expd = jnp.exp(scores - jnp.max(scores, axis=-1, keepdims=True))
    return expd * (1.0 / jnp.sum(expd, axis=-1, keepdims=True))


def trunk_first_body(moves, table_ref, index_ref, frame_ref, *refs):
    ins, refs = refs[:-9], refs[-9:]
    middle_ref, normed_ref, joined_ref, attended_ref, normed_two_ref, par_ref, fc1_b_ref = refs[:7]
    held_ref, sems = refs[7:]
    run_moves(moves, table_ref, ins, [held_ref], sems)
    par_ref[...] = slab(held_ref, 4 * D, LANES).astype(jnp.float32).T
    shards = held_ref.shape[0]
    wide = FF // shards
    for d in range(shards):
        row = held_ref[d, 0:1, 4 * D + LANES : 4 * D + LANES + wide]
        fc1_b_ref[:, d * wide : (d + 1) * wide] = row.astype(jnp.float32)

    def row(i):
        return par_ref[i : i + 1, :]

    started = frame_ref[...].astype(jnp.float32) + par_ref[pl.ds(index_ref[0], 1), :]
    normed = (normalised(started)[0] * row(ROW_GAIN) + row(ROW_BIAS)).astype(jnp.bfloat16)
    normed_ref[...] = normed
    for i, shift in enumerate((row(ROW_QKV), None, row(ROW_QKV + 1))):
        part = jnp.dot(normed, slab(held_ref, i * D, D), preferred_element_type=jnp.float32)
        part = part if shift is None else part + shift
        joined_ref[:, i * D : (i + 1) * D] = part.astype(jnp.bfloat16)
    low, masks = head_masks()
    for p in range(HEADS // 2):
        at = p * 2 * HD
        q, k, v = (joined_ref[:, i * D + at : i * D + at + 2 * HD] for i in range(3))
        outs = []
        for mask in masks:
            probs = softmax_of(dot_last(q * mask, k) * SCALE).astype(jnp.bfloat16)
            outs.append(jnp.dot(probs, v, preferred_element_type=jnp.float32))
        attended_ref[:, at : at + 2 * HD] = jnp.where(low, *outs).astype(jnp.bfloat16)
    middle = (
        started
        + jnp.dot(attended_ref[...], slab(held_ref, 3 * D, D), preferred_element_type=jnp.float32)
        + row(ROW_BIAS + 1)
    )
    middle_ref[...] = middle
    normed_two = normalised(middle)[0] * row(ROW_GAIN + 1) + row(ROW_BIAS + 2)
    normed_two_ref[...] = normed_two.astype(jnp.bfloat16)


def trunk_call(body, scalars, ins, sources, outs, scratch, name):
    any_spec = pl.BlockSpec(memory_space=pl.ANY)

    def whole(shape):
        return pl.BlockSpec(shape, lambda i, *s: (0,) * len(shape))

    return pl.pallas_call(
        body,
        grid_spec=pltpu.PrefetchScalarGridSpec(
            num_scalar_prefetch=len(scalars),
            grid=(1,),
            in_specs=[whole(v.shape) for v in ins] + [any_spec] * len(sources),
            out_specs=[whole(s) for s, _ in outs],
            scratch_shapes=scratch,
        ),
        out_shape=[jax.ShapeDtypeStruct(*o) for o in outs],
        compiler_params=pltpu.CompilerParams(vmem_limit_bytes=VMEM),
        cost_estimate=LIGHT,
        name=name,
    )(*scalars, *ins, *sources)


def trunk_first(table, index, rows, moves, frame, *sources):
    flat, low, full = (TILE_COUNT, D), jnp.bfloat16, jnp.float32
    return trunk_call(
        functools.partial(trunk_first_body, moves),
        (table, index),
        (frame,),
        sources,
        [
            (flat, full),
            (flat, low),
            ((TILE_COUNT, 3 * D), low),
            (flat, low),
            (flat, low),
            ((LANES, D), full),
            ((1, FF), full),
        ],
        [
            pltpu.VMEM((32, rows, FIRST_WIDE), low),
            pltpu.SemaphoreType.DMA((len(moves),)),
        ],
        "trunk_first",
    )


def trunk_second_body(moves, table_ref, middle_ref, normed_two_ref, par_ref, fc1_b_ref, *refs):
    ins, refs = refs[:-5], refs[-5:]
    hidden_ref, slope_ref, final_ref, held_ref, sems = refs
    run_moves(moves, table_ref, ins, [held_ref], sems)
    total = middle_ref[...] + par_ref[ROW_BIAS + 3 : ROW_BIAS + 4, :]
    normed_two = normed_two_ref[...]
    for k in range(4):
        cols = slice(k * D, (k + 1) * D)
        pre = jnp.dot(normed_two, widening(held_ref, k), preferred_element_type=jnp.float32)
        pre = pre + fc1_b_ref[:, cols]
        share = 0.5 * (1.0 + lax.erf(pre * (0.5**0.5)))
        density = jnp.exp(-0.5 * pre * pre) * ((0.5 / 3.141592653589793) ** 0.5)
        slope_ref[:, cols] = share + pre * density
        hidden = (pre * share).astype(jnp.bfloat16)
        hidden_ref[:, cols] = hidden
        weight = narrowing(held_ref, k)
        total += jnp.dot(hidden, weight, preferred_element_type=jnp.float32)
    final_ref[...] = total.astype(jnp.bfloat16)


def second_scratch(rows):
    return [pltpu.VMEM((32, 8 * rows, D), jnp.bfloat16)]


def narrowing(held_ref, k):
    shards, rows = held_ref.shape[:2]
    return held_ref[k * shards // 4 : (k + 1) * shards // 4, : rows // 2, :].reshape(D, D)


def widening(held_ref, k):
    rows = held_ref.shape[1] // 8
    return held_ref[:, (4 + k) * rows : (5 + k) * rows, :].reshape(D, D)


def trunk_second(table, rows, moves, middle, normed_two, par, fc1_b, *sources):
    return trunk_call(
        functools.partial(trunk_second_body, moves),
        (table,),
        (middle, normed_two, par, fc1_b),
        sources,
        [
            ((TILE_COUNT, FF), jnp.bfloat16),
            ((TILE_COUNT, FF), jnp.float32),
            ((TILE_COUNT, D), jnp.bfloat16),
        ],
        second_scratch(rows) + [pltpu.SemaphoreType.DMA((len(moves),))],
        "trunk_second",
    )


def second_back_body(moves_two, moves_one, n_two, table_ref, slope_ref, middle_ref, par_ref, *refs):
    d_parts, refs = refs[: 2 * CHUNKS], refs[2 * CHUNKS :]
    ins, refs = refs[:-11], refs[-11:]
    branch_ref, pre_ref, middle_d_ref, attn_ref, attended_ref, rows_ref, fc1_b_ref = refs[:7]
    held_ref, proj_ref, sems_two, sems_one = refs[7:]
    run_moves(moves_one, table_ref, ins[n_two:], [proj_ref], sems_one)
    run_moves(moves_two, table_ref, ins[:n_two], [held_ref], sems_two)
    d_final = d_parts[0][...]
    for part in d_parts[1:]:
        d_final = d_final + part[...]
    d_branch = d_final.astype(jnp.bfloat16)
    branch_ref[...] = d_branch
    d_normed = None
    for k in range(4):
        cols = slice(k * D, (k + 1) * D)
        d_hidden = dot_last(d_branch, narrowing(held_ref, k))
        d_pre = (d_hidden * slope_ref[:, cols]).astype(jnp.bfloat16)
        pre_ref[:, cols] = d_pre
        fc1_b_ref[:, cols] = jnp.sum(d_pre.astype(jnp.float32), axis=0, keepdims=True)
        part = dot_last(d_pre, widening(held_ref, k))
        d_normed = part if d_normed is None else d_normed + part
    gain = par_ref[ROW_GAIN + 1 : ROW_GAIN + 2, :]
    d_part, d_gain, d_shift = norm_back(middle_ref[...], d_normed, gain)
    d_middle = d_final + d_part
    middle_d_ref[...] = d_middle
    d_attn = d_middle.astype(jnp.bfloat16)
    attn_ref[...] = d_attn
    attended_ref[...] = dot_last(d_attn, slab(proj_ref, 0, D)).astype(jnp.bfloat16)
    sums = [jnp.sum(v.astype(jnp.float32), axis=0, keepdims=True) for v in (d_attn, d_branch)]
    rows_ref[...] = jnp.zeros_like(rows_ref)
    for i, value in enumerate((d_gain, d_shift, *sums)):
        rows_ref[i : i + 1, :] = value


def second_back(table, rows, moves_two, moves_one, n_two, slope, middle, par, d_parts, *sources):
    flat, low, full = (TILE_COUNT, D), jnp.bfloat16, jnp.float32
    return trunk_call(
        functools.partial(second_back_body, moves_two, moves_one, n_two),
        (table,),
        (slope, middle, par, *d_parts),
        sources,
        [
            (flat, low),
            ((TILE_COUNT, FF), low),
            (flat, full),
            (flat, low),
            (flat, low),
            ((8, D), full),
            ((1, FF), full),
        ],
        second_scratch(rows)
        + [
            pltpu.VMEM((32, rows, D), low),
            pltpu.SemaphoreType.DMA((len(moves_two),)),
            pltpu.SemaphoreType.DMA((len(moves_one),)),
        ],
        "second_back",
    )


def first_back_body(moves, n_ent, table_ref, index_ref, weight_ref, frame_ref, joined_ref, par_ref, middle_d_ref, attended_ref, rows_ref, *refs):
    ents, refs = refs[:n_ent], refs[n_ent:]
    ins, refs = refs[:-5], refs[-5:]
    d_joined_ref, tokens_ref, small_ref, qkv_ref, sems = refs
    run_moves(moves, table_ref, ins, [qkv_ref], sems)
    small_ref[...] = jnp.zeros_like(small_ref)
    _, masks = head_masks()
    for p in range(HEADS // 2):
        at = p * 2 * HD
        q, k, v = (joined_ref[:, i * D + at : i * D + at + 2 * HD] for i in range(3))
        d_out = attended_ref[:, at : at + 2 * HD]
        totals = [None] * 3
        for mask in masks:
            q_one, k_one, d_one = q * mask, k * mask, d_out * mask
            probs = softmax_of(dot_last(q_one, k) * SCALE)
            d_probs = dot_last(d_one, v)
            inner = jnp.sum(probs * d_probs, axis=-1, keepdims=True)
            d_scores = (probs * (d_probs - inner)).astype(jnp.bfloat16)
            parts = (
                jnp.dot(d_scores, k_one, preferred_element_type=jnp.float32),
                dot_tokens(d_scores, q_one),
                dot_tokens(probs.astype(jnp.bfloat16), d_one),
            )
            totals = [a if b is None else a + b for a, b in zip(parts, totals)]
        for i, scale in enumerate((SCALE, SCALE, 1.0)):
            d_joined_ref[:, i * D + at : i * D + at + 2 * HD] = (totals[i] * scale).astype(
                jnp.bfloat16
            )
    d_normed = None
    for i in range(3):
        block = d_joined_ref[:, i * D : (i + 1) * D]
        if i != 1:
            at = ROW_QKV + i // 2
            total = jnp.sum(block.astype(jnp.float32), axis=0, keepdims=True)
            small_ref[at : at + 1, :] = total
        part = dot_last(block, slab(qkv_ref, i * D, D))
        d_normed = part if d_normed is None else d_normed + part
    started = frame_ref[...].astype(jnp.float32) + par_ref[pl.ds(index_ref[0], 1), :]
    gain = par_ref[ROW_GAIN : ROW_GAIN + 1, :]
    d_part, d_gain, d_shift = norm_back(started, d_normed, gain)
    d_started = middle_d_ref[...] + d_part
    tokens_ref[...] = d_started.astype(jnp.bfloat16)
    small_ref[pl.ds(index_ref[0], 1), :] = jnp.sum(d_started, axis=0, keepdims=True)
    small_ref[ROW_GAIN : ROW_GAIN + 1, :] = d_gain
    small_ref[ROW_BIAS : ROW_BIAS + 1, :] = d_shift
    small_ref[ROW_GAIN + 1 : ROW_GAIN + 2, :] = rows_ref[0:1, :]
    small_ref[ROW_BIAS + 2 : ROW_BIAS + 3, :] = rows_ref[1:2, :]
    small_ref[ROW_BIAS + 1 : ROW_BIAS + 2, :] = rows_ref[2:3, :]
    small_ref[ROW_BIAS + 3 : ROW_BIAS + 4, :] = rows_ref[3:4, :]
    entropy = ents[0][...]
    for ent in ents[1:]:
        entropy = entropy + ent[...]
    entropy = jnp.sum(jnp.sum(entropy, axis=0, keepdims=True), axis=1, keepdims=True)
    value = jnp.broadcast_to(entropy * weight_ref[0] * 32.0, (1, D))
    before = jnp.floor(value)
    for k in range(DIGITS):
        value = value * BASE
        floor = jnp.floor(value)
        small_ref[ROW_DIGIT + k : ROW_DIGIT + k + 1, :] = floor - BASE * before
        before = floor


def first_back(table, index, strength, rows, moves, frame, joined, par, d_middle, d_attended, d_rows, ents, *sources):
    return trunk_call(
        functools.partial(first_back_body, moves, len(ents)),
        (table, index, strength),
        (frame, joined, par, d_middle, d_attended, d_rows, *ents),
        sources,
        [
            ((TILE_COUNT, 3 * D), jnp.bfloat16),
            ((TILE_COUNT, D), jnp.bfloat16),
            ((SMALL_ROWS, D), jnp.float32),
        ],
        [
            pltpu.VMEM((32, rows, 3 * D), jnp.bfloat16),
            pltpu.SemaphoreType.DMA((len(moves),)),
        ],
        "first_back",
    )


def low_or_high(value, core, rows):
    return value[core * rows : (core + 1) * rows]


def fc2_rows(value, core, rows):
    return value[core * 4 * rows : (core + 1) * 4 * rows]


def fc1_rows(value, core, rows):
    begin = 8 * rows + core * rows
    return jnp.concatenate(
        [value[begin + 2 * k * rows : begin + (2 * k + 1) * rows] for k in range(4)], axis=1
    )


class Parameters:
    def __init__(self, small_all, rows):
        lead_w, gain_all, bias_all, qkv_b, fc1_b = split_small(small_all)
        self.lead = lead_w.astype(jnp.float32)
        self.gain = gain_all.astype(jnp.float32)
        self.bias = bias_all.astype(jnp.float32)
        qkv_b = qkv_b.astype(jnp.float32)
        self.offset = jnp.concatenate([qkv_b[:, 0], jnp.zeros_like(qkv_b[:, 0]), qkv_b[:, 1]])
        self.fc1 = (
            fc1_b.astype(jnp.float32).reshape(D // rows, rows, 4).transpose(0, 2, 1).reshape(FF)
        )


    def parts(self):
        return self.lead, self.gain, self.bias, self.offset, self.fc1


def attention_input(frame, lead_vector, gain, bias, offset, qkv_w):
    started = frame.astype(jnp.float32) + lead_vector[None, :]
    normed = layer_norm(started, gain, bias).astype(jnp.bfloat16)
    joined = (plain_dot(normed, qkv_w) + offset).astype(jnp.bfloat16)
    return started, normed, joined


def heads_of(joined):
    return [joined[:, i * D : (i + 1) * D].reshape(TILE_COUNT, HEADS, HD) for i in range(3)]


def attention(joined):
    queries, keys, values = heads_of(joined)
    scores = jnp.einsum("qhd,khd->hqk", queries, keys, preferred_element_type=jnp.float32) * SCALE
    row_top = jnp.max(scores, axis=-1, keepdims=True)
    expd = jnp.exp(scores - row_top)
    prob_full = expd / jnp.sum(expd, axis=-1, keepdims=True)
    probs_low = prob_full.astype(jnp.bfloat16)
    attended = jnp.einsum("hqk,khd->qhd", probs_low, values, preferred_element_type=jnp.float32)
    return prob_full, attended.astype(jnp.bfloat16).reshape(TILE_COUNT, D)


def mlp_input(started, attended, proj_w, proj_bias, gain, bias):
    middle = started + plain_dot(attended, proj_w) + proj_bias
    return middle, layer_norm(middle, gain, bias).astype(jnp.bfloat16)


def mlp(middle, normed_two, fc1_w, fc1_b, fc2_w, fc2_b):
    pre_act = plain_dot(normed_two, fc1_w) + fc1_b
    hidden = exact_gelu(pre_act).astype(jnp.bfloat16)
    final_sum = middle + plain_dot(hidden, fc2_w) + fc2_b
    return pre_act, hidden, final_sum.astype(jnp.bfloat16)


def mlp_back(d_parts, pre_act, fc2_w):
    d_final = sum(d_parts)
    d_branch = d_final.astype(jnp.bfloat16)
    d_hidden = times_transpose(d_branch, fc2_w)
    _, gelu_back = jax.vjp(exact_gelu, pre_act)
    return d_final, d_branch, gelu_back(d_hidden)[0].astype(jnp.bfloat16)


def mlp_input_back(d_final, d_pre, fc1_w, middle, gain, bias, proj_w):
    d_normed_two = times_transpose(d_pre, fc1_w)
    _, norm_back = jax.vjp(layer_norm, middle, gain, bias)
    d_part, d_gain, d_shift = norm_back(d_normed_two)
    d_middle = d_final + d_part
    d_attn = d_middle.astype(jnp.bfloat16)
    d_attended = times_transpose(d_attn, proj_w).astype(jnp.bfloat16)
    return d_middle, d_attn, d_attended, d_gain, d_shift


def attention_back(joined, prob_full, d_attended):
    queries, keys, values = heads_of(joined)
    d_attended = d_attended.reshape(TILE_COUNT, HEADS, HD)
    probs_low = prob_full.astype(jnp.bfloat16)
    d_values = jnp.einsum("hqk,qhd->khd", probs_low, d_attended, preferred_element_type=jnp.float32)
    d_prob = jnp.einsum("qhd,khd->hqk", d_attended, values, preferred_element_type=jnp.float32)
    d_score = (
        prob_full * (d_prob - jnp.sum(prob_full * d_prob, axis=-1, keepdims=True))
    ).astype(jnp.bfloat16)
    d_queries = (
        jnp.einsum("hqk,khd->qhd", d_score, keys, preferred_element_type=jnp.float32) * SCALE
    )
    d_keys = (
        jnp.einsum("hqk,qhd->khd", d_score, queries, preferred_element_type=jnp.float32) * SCALE
    )
    return jnp.concatenate(
        [v.reshape(TILE_COUNT, D) for v in (d_queries, d_keys, d_values)], axis=1
    ).astype(jnp.bfloat16)


def attention_input_back(d_middle, d_joined, qkv_w, started, gain, bias):
    d_normed = times_transpose(d_joined, qkv_w)
    _, norm_back = jax.vjp(layer_norm, started, gain, bias)
    d_part, d_gain, d_shift = norm_back(d_normed)
    return d_middle + d_part, d_gain, d_shift


def small_gradient(rows, horizon_indicator, contribution, d_started, d_joined, d_attn, d_branch, d_pre, gains, shifts):
    def column_sum(value):
        return jnp.sum(value.astype(jnp.float32), axis=0)

    joined_sums = column_sum(d_joined)
    columns = jnp.stack(
        [
            *gains,
            shifts[0],
            column_sum(d_attn),
            shifts[1],
            column_sum(d_branch),
            joined_sums[:D],
            joined_sums[2 * D :],
        ],
        axis=1,
    )
    hidden_columns = column_sum(d_pre).reshape(D // rows, 4, rows).transpose(0, 2, 1).reshape(D, 4)
    return jnp.concatenate(
        [
            jnp.sum(d_started, axis=0)[:, None] * horizon_indicator[None, :],
            columns,
            hidden_columns,
            jnp.broadcast_to(digits_of(contribution)[None, :], (D, DIGITS)),
            jnp.zeros((D, LANES - LEADS - 12 - DIGITS), jnp.float32),
        ],
        axis=1,
    ).astype(jnp.bfloat16)


def small_outputs(value, rows):
    return (
        value[:, :LEADS],
        value[:, LEADS : LEADS + 2],
        value[:, LEADS + 2 : LEADS + 6],
        value[:, LEADS + 6 : LEADS + 8],
        value[:, LEADS + 8 : LEADS + 12].T.reshape(4 * rows),
    )


def frame_scalars(horizon_indices, horizon_tallies):
    indicator = (horizon_indices[0] == lax.iota(jnp.int32, LEADS)).astype(jnp.float32)
    frame_count = jnp.sum(indicator * horizon_tallies.astype(jnp.float32))
    return indicator, 1.0 / (frame_count * (LEADS * TILE_COUNT * TILE_SAMPLES))


def plain_step(
    tile_embeddings,
    horizon_indices,
    horizon_tallies,
    member_guesses,
    adjoint_of_mixture,
    triple_projection_matrix,
    attention_outward_matrix,
    widening_matrix,
    narrowing_matrix,
    gating_matrix,
    *small_parts,
):
    rows = triple_projection_matrix.shape[0]
    whole = functools.partial(lax.all_gather, axis_name=AXES, axis=0, tiled=True)

    def summed(value):
        return lax.psum_scatter(
            value.astype(jnp.bfloat16), AXES, scatter_dimension=0, tiled=True
        ).astype(jnp.float32)

    qkv_w, proj_w = whole(triple_projection_matrix), whole(attention_outward_matrix)
    fc1_w, fc2_w = whole(widening_matrix), whole(narrowing_matrix)
    par = Parameters(whole(pack_small(*small_parts, rows)), rows)
    indicator, strength = frame_scalars(horizon_indices, horizon_tallies)
    guesses = jnp.transpose(member_guesses[0], (1, 0, 2))
    lead_vector = jnp.sum(par.lead * indicator[None, :], axis=1)
    started, normed, joined = attention_input(
        tile_embeddings[0], lead_vector, par.gain[:, 0], par.bias[:, 0], par.offset, qkv_w
    )
    prob_full, attended = attention(joined)
    middle, normed_two = mlp_input(
        started, attended, proj_w, par.bias[:, 1], par.gain[:, 1], par.bias[:, 2]
    )
    pre_act, hidden, final_low = mlp(middle, normed_two, fc1_w, par.fc1, fc2_w, par.bias[:, 3])
    table = jnp.asarray([0, 1], jnp.int32)
    held_shape = (1, D, WIDE)
    combined, head_grads, d_parts, entropies = None, [], [], []
    head_w = whole(jnp.concatenate(head_chunks(gating_matrix), axis=1))
    for q in range(CHUNKS):
        halves = []
        for own in (False, True):
            combined, d_logits, d_part, entropy = head_pass(
                q,
                own,
                strength.reshape(1),
                table,
                final_low,
                [head_w],
                [(0, (0, 0), held_shape[1:], 0, 0, (0, 0))],
                held_shape,
                guesses,
                adjoint_of_mixture[0],
                combined,
            )
            flat = d_logits.transpose(1, 0, 2).reshape(TILE_COUNT, WIDE)
            halves.append(summed(transpose_times(final_low, flat)))
            d_parts.append(d_part)
            entropies.append(entropy)
        head_grads.append(halves)
    contribution = jnp.sum(sum(entropies)) * strength
    d_final, d_branch, d_pre = mlp_back(d_parts, pre_act, fc2_w)
    d_middle, d_attn, d_attended, gain_two, shift_two = mlp_input_back(
        d_final, d_pre, fc1_w, middle, par.gain[:, 1], par.bias[:, 2], proj_w
    )
    d_joined = attention_back(joined, prob_full, d_attended)
    d_started, gain_one, shift_one = attention_input_back(
        d_middle, d_joined, qkv_w, started, par.gain[:, 0], par.bias[:, 0]
    )
    small_grad = small_gradient(
        rows,
        indicator,
        contribution,
        d_started,
        d_joined,
        d_attn,
        d_branch,
        d_pre,
        (gain_one, gain_two),
        (shift_one, shift_two),
    )
    return (
        combined[None],
        lax.psum(contribution, AXES),
        d_started.astype(jnp.bfloat16)[None],
        summed(transpose_times(normed, d_joined)),
        summed(transpose_times(attended, d_attn)),
        summed(transpose_times(normed_two, d_pre)),
        summed(transpose_times(hidden, d_branch)),
        head_whole(*zip(*head_grads)),
        *small_outputs(summed(small_grad), rows),
    )


def paired_step(
    tile_embeddings,
    horizon_indices,
    horizon_tallies,
    member_guesses,
    adjoint_of_mixture,
    triple_projection_matrix,
    attention_outward_matrix,
    widening_matrix,
    narrowing_matrix,
    gating_matrix,
    *small_parts,
):
    rows = triple_projection_matrix.shape[0]
    core = lax.axis_index("fsdp") % 2
    table = places(True)
    marks = jnp.concatenate([core.reshape(1), places(False)[::2] // 2])
    head_marks = jnp.concatenate([core.reshape(1), table[::2] // 2])
    head_table = jnp.concatenate([table, core.reshape(1)])
    seq = Sequence(horizon_tallies)
    indicator, strength = frame_scalars(horizon_indices, horizon_tallies)

    first_own, second_own = seq.run(
        pack_trunk,
        triple_projection_matrix,
        attention_outward_matrix,
        widening_matrix,
        narrowing_matrix,
        *small_parts,
    )
    one, two = RoundFirst(seq, first_own, 1), RoundFirst(seq, second_own, -1)
    one.start()
    two.start()
    one.arrive()
    one.start()
    head_own = seq.run(pack_head, gating_matrix)
    over = across(head_own)
    two.arrive()
    two.start()
    one.arrive()
    one.start()
    two.arrive()
    two.start()
    over = seq.tie(over)
    one.arrive()
    one.last()
    two.arrive()
    two.last()
    one.arrive_last()
    one.batch()
    two.arrive_last()
    head_first = seq.run(lambda a, b: jnp.concatenate([a, b], axis=0), head_own, over)
    three = AcrossFirst(seq, head_first)
    three.start()
    guesses = seq.run(
        lambda v: lax.optimization_barrier(jnp.transpose(v[0], (1, 0, 2))), member_guesses
    )
    two.batch()
    three.arrive()
    three.start()
    one.arrive_over()
    one.arrive_batches()
    whole_one = [((0, rows), (0, FIRST_WIDE), 0, 0, 0)]
    whole_two = [((0, 8 * rows), (0, D), 0, 0, 0)]
    index = horizon_indices
    sources_one, moves = plan_moves(one.collect(), whole_one)
    middle, normed, joined, attended, normed_two, par, fc1_b = seq.run(
        functools.partial(trunk_first, table, index, rows, moves), tile_embeddings[0], *sources_one
    )
    three.settle()
    three.arrive()
    three.start()
    adjoint = seq.run(lambda v: lax.optimization_barrier(v[0]), adjoint_of_mixture)
    two.arrive_batches()
    three.settle()
    three.arrive()
    three.last()
    two.arrive_over()
    two.arrive_batches()
    sources_two, moves_two = plan_moves(two.collect(), whole_two)
    hidden, slope, final_low = seq.run(
        functools.partial(trunk_second, table, rows, moves_two),
        middle,
        normed_two,
        par,
        fc1_b,
        *sources_two,
    )
    three.settle()
    three.arrive_last()
    final_other = sibling(final_low)
    normed_other, attended_other = sibling(normed), sibling(attended)
    normed_two_other, hidden_other = sibling(normed_two), sibling(hidden)

    held_shape = (32, rows, WIDE)
    head_fields = [((0, rows), (0, WIDE), 0, 0, 0)]
    state = dict(combined=None, d_parts=[], entropies=[])

    def head(q, own, around):
        sources, moves = plan_moves(around.collect(), head_fields)
        before = () if state["combined"] is None else (state["combined"],)

        def function(final_low, before, *sources):
            return head_pass(
                q,
                own,
                strength.reshape(1),
                head_table,
                final_low,
                list(sources),
                moves,
                held_shape,
                guesses,
                adjoint,
                before[0] if before else None,
            )

        state["combined"], d_logits, d_part, entropy = seq.run(
            function, final_low, before, *sources
        )
        state["d_parts"].append(d_part)
        state["entropies"].append(entropy)
        return d_logits

    make_grad = functools.partial(head_grad, head_marks)
    send = sibling(head(0, False, three))
    own = head(0, True, three)
    sum_one = SumRoundFirst(seq, *seq.run(make_grad, final_low, final_other, own, send))
    moves_proj = plan_moves(one.collect(), [((0, rows), (3 * D, 4 * D), 0, 0, 0)])[1]
    moves_qkv = plan_moves(one.collect(), [((0, rows), (0, 3 * D), 0, 0, 0)])[1]
    d_branch, d_pre, d_middle, d_attn, d_attended, d_rows, d_fc1_b = seq.run(
        functools.partial(second_back, table, rows, moves_two, moves_proj, len(sources_two)),
        slope,
        middle,
        par,
        state["d_parts"],
        *sources_two,
        *sources_one,
    )
    d_attn_other, d_fc1_b_other = sibling(d_attn), sibling(d_fc1_b)
    d_branch_other, d_pre_other = sibling(d_branch), sibling(d_pre)
    normed_other, attended_other, normed_two_other, hidden_other = seq.tie(
        normed_other, attended_other, normed_two_other, hidden_other
    )
    sum_one.arrive()
    sum_one.step(3)
    d_branch_other, d_pre_other, d_attn_other, d_fc1_b_other = seq.tie(
        d_branch_other, d_pre_other, d_attn_other, d_fc1_b_other
    )
    parts = seq.run(
        lambda *ins: ring_grad(
            second_grad_body,
            marks,
            ins,
            (16 * rows, D // 2),
            [(16, 8 * rows, D // 2), (16, 2 * rows, FF // 2)],
            "second_grad",
        ),
        *(hidden, hidden_other, d_branch, d_branch_other),
        *(normed_two, normed_two_other, d_pre, d_pre_other),
    )
    sum_three = SumAcrossFirst(seq, parts, 1)
    sum_three.go_across(0)
    d_joined, tokens, small_grad = seq.run(
        functools.partial(first_back, table, index, strength.reshape(1), rows, moves_qkv),
        tile_embeddings[0],
        joined,
        par,
        d_middle,
        d_attended,
        d_rows,
        state["entropies"],
        *sources_one,
    )
    d_joined_other, small_other = sibling(d_joined), sibling(small_grad)
    sum_one.arrive()
    sum_one.step(2)
    blocks = seq.run(
        lambda *ins: round_grad(
            first_grad_body,
            head_marks,
            ins,
            (2 * rows, 2 * D + 2 * LANES),
            [(16, 2 * rows, 3 * D // 2), (16, 2 * rows, D // 2), (16, 2 * rows, LANES)]
            + [(LANES, D), (32, LANES), (2 * rows, LANES)],
            "first_grad",
        ),
        *(normed, normed_other, d_joined, d_joined_other),
        *(attended, attended_other, d_attn, d_attn_other),
        *(small_grad, small_other, d_fc1_b, d_fc1_b_other),
    )
    sum_four = SumRoundFirst(seq, *blocks)
    sum_three.arrive_across(0)
    sum_three.step(4)
    sum_one.arrive()
    sum_one.step(1)
    sum_three.go_across(1)
    sum_four.arrive()
    sum_four.step(3)
    sum_three.arrive()
    sum_three.step(3)
    combined_result = seq.run(flip, state["combined"]).T[None]
    grad_tokens = tokens[None]
    sum_one.arrive()
    sum_one.go_across()
    sum_four.arrive()
    sum_four.step(2)
    sum_three.arrive()
    sum_three.arrive_across(1)
    sum_three.step(2)
    sum_four.arrive()
    sum_four.step(1)
    sum_three.arrive()
    sum_three.step(1)
    first = core == 0

    def finish(total, rows_of):
        low, high = rows_of(total, 0, rows), rows_of(total, 1, rows)
        own, other = jnp.where(first, low, high), jnp.where(first, high, low)
        met = sibling(other.astype(jnp.bfloat16)).astype(jnp.float32)
        return jnp.where(first, own, met), jnp.where(first, met, own)

    low, high = finish(sum_one.finish(), low_or_high)
    sum_four.arrive()
    sum_four.go_across()
    sum_three.arrive()
    total = sum_three.finish()
    out_fc2 = jnp.concatenate(finish(total, fc2_rows), axis=1)
    out_fc1 = jnp.concatenate(finish(total, fc1_rows), axis=1)
    out_head = seq.run(head_join, low, high)
    total = sum_four.finish()
    out_small = jnp.where(first, total[:rows, 2 * D :], total[rows:, 2 * D :])
    low, high = finish(total[:, : 2 * D], low_or_high)
    n = 3 * D // 2
    out_fc1_b = out_small[0, LANES : LANES + 4 * rows]
    out_lead, out_gains, out_biases, out_qkv_b = small_join(out_small)
    cost = value_of(out_small[0, ROW_DIGIT : ROW_DIGIT + DIGITS])
    cost = jnp.where(seq.token[0] < 0, 0.0, cost)
    return (
        combined_result,
        cost,
        grad_tokens,
        jnp.concatenate([low[:, :n], high[:, :n]], axis=1),
        jnp.concatenate([low[:, n:], high[:, n:]], axis=1),
        out_fc1,
        out_fc2,
        out_head,
        out_lead,
        out_gains.T,
        out_biases.T,
        out_qkv_b.T,
        out_fc1_b,
    )


def solution(mesh):
    split = P(AXES)
    paired = mesh.shape["dp"] == 2 and mesh.shape["fsdp"] == 16
    return jax.shard_map(
        paired_step if paired else plain_step,
        mesh=mesh,
        in_specs=(split, split, P()) + (split,) * 12,
        out_specs=(split, P()) + (split,) * 11,
        check_vma=False,
    )
```
